32 devices in a mesh: seq: 2 (over x), fsdp: 16 (over z, y, core).
Axes of the slice: x: 2, y: 2, z: 4, core: 2. Of those that a mesh axis runs over, the one named last changes fastest.
Arguments:
- inputs: bfloat16 [16, 1024, 1536], P('fsdp', 'seq'), may hold values from -6 to 6
- text_states: bfloat16 [16, 64, 1536], P('fsdp'), may hold values from -6 to 6
- adapter_index: int32 [16], P('fsdp'), may hold values from 0 to 7
- norm_gains: float32 [3, 1536], replicated, may hold values from 0.25 to 1.75
- norm_biases: float32 [3, 1536], replicated, may hold values from -1.8 to 1.8
- self_in: bfloat16 [1536, 4608], P('fsdp'), may hold values from -0.15625 to 0.15625
- self_out: bfloat16 [1536, 1536], P('fsdp'), may hold values from -2.5 to 2.5
- cross_query: bfloat16 [1536, 1536], P('fsdp'), may hold values from -0.15625 to 0.15625
- cross_text: bfloat16 [1536, 3072], P('fsdp'), may hold values from -0.15625 to 0.15625
- cross_out: bfloat16 [1536, 1536], P('fsdp'), may hold values from -0.875 to 0.875
- hidden_in: bfloat16 [1536, 6144], P('fsdp'), may hold values from -0.15625 to 0.15625
- hidden_out: bfloat16 [6144, 1536], P('fsdp'), may hold values from -0.078125 to 0.078125
- adapter_down: bfloat16 [8, 16, 19968], P(None, None, 'fsdp'), may hold values from -0.15625 to 0.15625
- adapter_up: bfloat16 [8, 16, 19968], P(None, None, 'fsdp'), may hold values from -0.75 to 0.75
- cotangent: bfloat16 [16, 1024, 1536], P('fsdp', 'seq'), may hold values from -6 to 6
Outputs:
- output: bfloat16 [16, 1024, 1536], P('fsdp', 'seq')
- grad_input: float32 [16, 1024, 1536], P('fsdp', 'seq')
- grad_text: float32 [16, 64, 1536], P('fsdp')
- grad_down: float32 [8, 16, 19968], P(None, None, 'fsdp')
- grad_up: float32 [8, 16, 19968], P(None, None, 'fsdp')
The draws below stay inside these ranges and needn't reach their ends.
All inputs are finite; a program needn't handle non-finite values.
Results may differ from the reference program's by a relative error of at most 0.022.
Values may be sent and summed in bfloat16 or wider, within the bound.
No kernel may reach another device: no remote copies, remote signals or barrier semaphores. Data moves between devices by JAX's collectives and lax.ppermute only.
A program may use at most 448 MiB of HBM per device.

```python
import jax
import jax.numpy as jnp
from jax import lax

D = 1536
HEAD = 64
FF = 6144
RANK = 16
ADAPTERS = 8
TXT = 64
FRAMES = 1024
CLIPS = 16
SUMW = 19968


def with_ends(values, key, least, largest):
    spot = [jax.random.randint(jax.random.fold_in(key, axis), (), 0, length) for axis, length in enumerate(values.shape)]
    widest = values.shape.index(max(values.shape))
    next_to = spot[:widest] + [(spot[widest] + 1) % values.shape[widest]] + spot[widest + 1:]
    return values.at[tuple(spot)].set(least).at[tuple(next_to)].set(largest)


def block_levels(key, extent, cuts, smallest, largest):
    loudness, own = 1.0, jax.random.fold_in(key, 6)
    for axis_at, blocks in cuts:
        draws = jnp.exp(jax.random.uniform(jax.random.fold_in(own, axis_at), (blocks,), jnp.float32, smallest / len(cuts), largest / len(cuts)))
        loudness = loudness * jnp.repeat(draws, extent[axis_at] // blocks).reshape([-1 if axis == axis_at else 1 for axis in range(len(extent))])
    return loudness


def bell_draw(stream_key, dims, scale, most, split=(), kind=jnp.bfloat16):
    array = jax.random.normal(stream_key, dims, jnp.float32) * scale
    if len(split) > 0:
        array = block_levels(stream_key, dims, split, -0.22, 0.18) * array
    return jnp.clip(array, min=-most, max=most).astype(kind)


def setup_inputs(seed: int = 0) -> dict:
    keys = jax.random.split(jax.random.key(seed), 16)
    return {
        "inputs": bell_draw(keys[0], (CLIPS, FRAMES, D), 1.0, 6.0, ((0, 16), (1, 2))),
        "text_states": bell_draw(keys[1], (CLIPS, TXT, D), 1.0, 6.0, ((0, 16),)),
        "adapter_index": with_ends(jax.random.randint(keys[2], (CLIPS,), 0, ADAPTERS), jax.random.fold_in(keys[2], 1), 0, ADAPTERS - 1).astype(jnp.int32),
        "norm_gains": jnp.clip(1.0 + 0.15 * jax.random.normal(keys[3], (3, D), jnp.float32), 0.25, 1.75),
        "norm_biases": bell_draw(keys[4], (3, D), 0.3, 1.8, (), jnp.float32),
        "self_in": bell_draw(keys[5], (D, 3 * D), D ** -0.5, 0.15625, ((0, 16),)),
        "self_out": bell_draw(keys[6], (D, D), (max(D // 256, 1)) ** -0.5, 2.5, ((0, 16),)),
        "cross_query": bell_draw(keys[7], (D, D), D ** -0.5, 0.15625, ((0, 16),)),
        "cross_text": bell_draw(keys[8], (D, 2 * D), D ** -0.5, 0.15625, ((0, 16),)),
        "cross_out": bell_draw(keys[9], (D, D), (max(D // 32, 1)) ** -0.5, 0.875, ((0, 16),)),
        "hidden_in": bell_draw(keys[10], (D, FF), D ** -0.5, 0.15625, ((0, 16),)),
        "hidden_out": bell_draw(keys[11], (FF, D), FF ** -0.5, 0.078125, ((0, 16),)),
        "adapter_down": bell_draw(keys[12], (ADAPTERS, RANK, SUMW), D ** -0.5, 0.15625, ((2, 16),)),
        "adapter_up": bell_draw(keys[13], (ADAPTERS, RANK, SUMW), (4 * RANK) ** -0.5, 0.75, ((2, 16),)),
        "cotangent": bell_draw(keys[14], (CLIPS, FRAMES, D), 1.0, 6.0, ((0, 16), (1, 2))),
    }


precise = lax.Precision.HIGHEST

@jax.custom_vjp
def low(v):
    return lax.optimization_barrier(v.astype(jnp.bfloat16)).astype(jnp.float32)

@jax.custom_vjp
def low_back(v):
    return v

def low_keep(v):
    return (low(v), None)

def low_pass(kept, grad):
    return (grad,)

def back_keep(v):
    return (v, None)

def back_low(kept, grad):
    return (low(grad),)
low.defvjp(low_keep, low_pass)
low_back.defvjp(back_keep, back_low)

def rounded(value):
    return low_back(low(value))

def layer_norm(values, gains, biases):
    centered = values - lax.optimization_barrier(jnp.mean(values, -1, keepdims=True))
    variance = lax.optimization_barrier(jnp.mean(centered * centered, -1, keepdims=True))
    return centered * lax.rsqrt(variance + 1e-05) * gains + biases

def adapter_slices(down_rows, upper_rows, index):
    in_cuts = [0, 3 * D, 4 * D, 5 * D, 7 * D, 8 * D, 9 * D, 9 * D + FF]
    out_cuts = [0, 3 * D, 4 * D, 5 * D, 7 * D, 8 * D, 8 * D + FF, 9 * D + FF]
    return (down_rows[..., in_cuts[index]:in_cuts[index + 1]], upper_rows[..., out_cuts[index]:out_cuts[index + 1]])

def project(inputs, weight, pieces, part_count):
    down_rows, upper_rows = pieces
    row_count, in_width = inputs.shape
    rank_size = down_rows.shape[0]
    down_split = down_rows.reshape(rank_size, part_count, in_width)
    upper_split = upper_rows.reshape(rank_size, part_count, -1)
    latent = rounded(jnp.einsum('ti,rpi->tpr', inputs, down_split, precision=precise))
    adapted = jnp.einsum('tpr,rpo->tpo', latent, upper_split, precision=precise).reshape(row_count, -1)
    return jnp.dot(inputs, weight, precision=precise) + adapted

def self_attend(queries, key_rows, values):
    frame_count, model_width = queries.shape
    head_count = model_width // HEAD
    score_scale = float(HEAD) ** (-0.5)
    block_rows = min(512, frame_count)
    block_count = frame_count // block_rows
    query_split = queries.reshape(frame_count, head_count, HEAD)
    key_split = key_rows.reshape(frame_count, head_count, HEAD)
    value_split = values.reshape(frame_count, head_count, HEAD)

    def one_block(block_index):
        row_start = block_index * block_rows
        query_block = lax.dynamic_slice_in_dim(query_split, row_start, block_rows, 0)
        scores = low_back(jnp.einsum('qhe,khe->hqk', query_block, key_split, precision=precise) * score_scale)
        row_pos = row_start + lax.broadcasted_iota(jnp.int32, (block_rows, frame_count), 0)
        col_pos = lax.broadcasted_iota(jnp.int32, (block_rows, frame_count), 1)
        scores = jnp.where(col_pos <= row_pos, scores, -1e+30)
        row_top = lax.optimization_barrier(jnp.max(scores, -1, keepdims=True))
        raised = jnp.exp(scores - row_top)
        prob_block = raised / lax.optimization_barrier(jnp.sum(raised, -1, keepdims=True))
        mixed = jnp.einsum('hqk,khe->qhe', low(prob_block), value_split, precision=precise)
        return mixed.reshape(block_rows, model_width)
    blocks = lax.map(jax.checkpoint(one_block), jnp.arange(block_count, dtype=jnp.int32))
    return rounded(blocks.reshape(frame_count, model_width))

def cross_attend(queries, key_rows, values):
    row_count, model_width = queries.shape
    head_count = model_width // HEAD
    score_scale = float(HEAD) ** (-0.5)
    query_split = queries.reshape(row_count, head_count, HEAD)
    key_split = key_rows.reshape(key_rows.shape[0], head_count, HEAD)
    value_split = values.reshape(values.shape[0], head_count, HEAD)
    scores = low_back(jnp.einsum('qhe,khe->hqk', query_split, key_split, precision=precise) * score_scale)
    row_top = lax.optimization_barrier(jnp.max(scores, -1, keepdims=True))
    raised = jnp.exp(scores - row_top)
    prob_all = raised / lax.optimization_barrier(jnp.sum(raised, -1, keepdims=True))
    mixed = jnp.einsum('hqk,khe->qhe', low(prob_all), value_split, precision=precise)
    return rounded(mixed.reshape(row_count, model_width))

def clip_layer(frame_rows, text_rows, down_rows, upper_rows, matrices, norm_gains, norm_biases):
    self_in, self_out, cross_query, cross_text, cross_out, hidden_in, hidden_out = matrices
    normed1 = low(layer_norm(frame_rows, norm_gains[0], norm_biases[0]))
    triple = rounded(project(normed1, self_in, adapter_slices(down_rows, upper_rows, 0), 3))
    attended = self_attend(triple[:, :D], triple[:, D:2 * D], triple[:, 2 * D:])
    resid1 = frame_rows + low_back(project(attended, self_out, adapter_slices(down_rows, upper_rows, 1), 1))
    normed2 = low(layer_norm(resid1, norm_gains[1], norm_biases[1]))
    cross_queries = rounded(project(normed2, cross_query, adapter_slices(down_rows, upper_rows, 2), 1))
    memory = rounded(project(text_rows, cross_text, adapter_slices(down_rows, upper_rows, 3), 2))
    cross_attended = cross_attend(cross_queries, memory[:, :D], memory[:, D:])
    resid2 = resid1 + low_back(project(cross_attended, cross_out, adapter_slices(down_rows, upper_rows, 4), 1))
    normed3 = low(layer_norm(resid2, norm_gains[2], norm_biases[2]))
    pre_act = low_back(project(normed3, hidden_in, adapter_slices(down_rows, upper_rows, 5), 1))
    activated = low(jax.nn.gelu(pre_act, approximate=False))
    return resid2 + low_back(project(activated, hidden_out, adapter_slices(down_rows, upper_rows, 6), 1))

def reference(inputs, text_states, adapter_index, norm_gains, norm_biases, self_in, self_out, cross_query, cross_text, cross_out, hidden_in, hidden_out, adapter_down, adapter_up, cotangent):
    matrices = tuple((item.astype(jnp.float32) for item in (self_in, self_out, cross_query, cross_text, cross_out, hidden_in, hidden_out)))
    picker = (adapter_index[:, None] == jnp.arange(ADAPTERS, dtype=jnp.int32)[None, :]).astype(jnp.float32)

    def forward(frames, texts, down_table, upper_table):
        down_pick = jnp.einsum('ca,arw->crw', picker, down_table, precision=precise)
        upper_pick = jnp.einsum('ca,arw->crw', picker, upper_table, precision=precise)

        def one_clip(clip_args):
            frame_rows, text_rows, down_rows, upper_rows = clip_args
            return clip_layer(frame_rows, text_rows, down_rows, upper_rows, matrices, norm_gains, norm_biases)
        return lax.map(jax.checkpoint(one_clip), (frames, texts, down_pick, upper_pick))
    result, pull_back = jax.vjp(forward, inputs.astype(jnp.float32), text_states.astype(jnp.float32), adapter_down.astype(jnp.float32), adapter_up.astype(jnp.float32))
    grads = pull_back(cotangent.astype(jnp.float32))
    return (result.astype(jnp.bfloat16), grads[0], grads[1], grads[2], grads[3])
```

```python
from functools import partial

import jax
import jax.numpy as jnp
from jax import lax
from jax.experimental import pallas as pl
from jax.experimental.pallas import tpu as pltpu
from jax.sharding import PartitionSpec as P

HEAD = 64
LANES = 128
QB = 256
BF = jnp.bfloat16
F32 = jnp.float32
SCALE = float(HEAD) ** (-0.5)
SQRT_HALF = 0.7071067811865476
INV_SQRT_2PI = 0.3989422804014327
VMEM_LIMIT = 60 * 1024 * 1024


def mm(a, b):
    return lax.dot_general(a, b, (((1,), (0,)), ((), ())), preferred_element_type=F32)


def mm_nt(a, b):
    return lax.dot_general(a, b, (((1,), (1,)), ((), ())), preferred_element_type=F32)


def mm_tn(a, b):
    return lax.dot_general(a, b, (((0,), (0,)), ((), ())), preferred_element_type=F32)


def norm_stats(values):
    centered = values - jnp.mean(values, -1, keepdims=True)
    variance = jnp.mean(centered * centered, -1, keepdims=True)
    inverse = lax.rsqrt(variance + 1e-05)
    return centered * inverse, inverse


def layer_norm(values, gains, biases):
    unit, _ = norm_stats(values)
    return unit * gains + biases


def norm_back(values, gains, gradient):
    unit, inverse = norm_stats(values)
    scaled = gradient * gains
    mean_one = jnp.mean(scaled, -1, keepdims=True)
    mean_two = jnp.mean(scaled * unit, -1, keepdims=True)
    return inverse * (scaled - mean_one - unit * mean_two)


def whole(shape):
    return pl.BlockSpec(shape, lambda *_: (0,) * len(shape))


def params(count=1):
    return pltpu.CompilerParams(
        dimension_semantics=("arbitrary",) * count, vmem_limit_bytes=VMEM_LIMIT
    )


def cost(flops, moved, special=0):
    return pl.CostEstimate(flops=int(flops), bytes_accessed=int(moved), transcendentals=int(special))


def window(packed, start, width, rows=None, steps=1, step=0):
    block = width // steps
    rows = packed.shape[0] if rows is None else rows
    if start % block == 0 and block % LANES == 0:
        base = start // block
        return packed, pl.BlockSpec((rows, block), lambda *at: (0, base + (at[step] if steps > 1 else 0)))
    return packed[:, start : start + width], pl.BlockSpec(
        (rows, block), lambda *at: (0, at[step] if steps > 1 else 0)
    )


def qkv_kernel(x_ref, gain_ref, bias_ref, down_ref, up_ref, w_ref, normed_ref, lat_ref, out_ref):
    row_count = x_ref.shape[0]

    @pl.when(pl.program_id(0) == 0)
    def _():
        step = 128

        def some(at, carry):
            rows = pl.ds(pl.multiple_of(at * step, step), step)
            normed = layer_norm(x_ref[rows, :].astype(F32), gain_ref[...], bias_ref[...]).astype(BF)
            normed_ref[rows, :] = normed
            lat_ref[rows, :] = mm_nt(normed, down_ref[...]).astype(BF)
            return carry

        lax.fori_loop(0, row_count // step, some, 0)

    for at in range(0, row_count, 512):
        rows = pl.ds(at, min(512, row_count))
        out_ref[rows, :] = (
            mm(normed_ref[rows, :], w_ref[...]) + mm(lat_ref[rows, :], up_ref[...])
        ).astype(BF)


def qkv_project(x_all, gains, biases, down, up, packed, start, width):
    row_count, model = x_all.shape
    steps = 3 if (width // 3) % LANES == 0 else 1
    operand, spec = window(packed, start, width, steps=steps)
    block = width // steps
    if steps == 3:
        up_spec = pl.BlockSpec((None, up.shape[1], block), lambda at: (at, 0, 0))
    else:
        up = up.transpose(1, 0, 2).reshape(up.shape[1], width)
        up_spec = whole(up.shape)
    ranks = down.shape[0]
    return pl.pallas_call(
        qkv_kernel,
        grid=(steps,),
        in_specs=[whole(x_all.shape), whole(gains.shape), whole(biases.shape), whole(down.shape), up_spec, spec],
        out_specs=[
            whole(x_all.shape),
            whole((row_count, ranks)),
            pl.BlockSpec((row_count, block), lambda at: (0, at)),
        ],
        out_shape=[
            jax.ShapeDtypeStruct(x_all.shape, BF),
            jax.ShapeDtypeStruct((row_count, ranks), BF),
            jax.ShapeDtypeStruct((row_count, width), BF),
        ],
        compiler_params=params(),
        cost_estimate=cost(2 * row_count * model * width, 2 * (row_count + width) * model),
        name="qkv_project",
    )(x_all, gains, biases, down, up, operand)


def tri_start(at):
    return QB * at * (at + 1) // 2


def attend_kernel(q_ref, k_ref, v_ref, out_ref, prob_ref, val_t_ref, out_t_ref):
    frames = q_ref.shape[0]
    lane = lax.broadcasted_iota(jnp.int32, (1, LANES), 1) // HEAD
    val_t_ref[...] = v_ref[...].T
    for half in range(2):
        keep = lane == half
        for at in range(frames // QB):
            stop = (at + 1) * QB
            query = q_ref[at * QB : stop, :] * jnp.where(keep, SCALE, 0.0).astype(BF)
            score = mm_nt(k_ref[0:stop, :], query)
            row = lax.broadcasted_iota(jnp.int32, (stop, QB), 0)
            col = lax.broadcasted_iota(jnp.int32, (stop, QB), 1) + at * QB
            score = jnp.where(row <= col, score, -1e30)
            raised = jnp.exp(score - jnp.max(score, 0, keepdims=True))
            prob = (raised * (1.0 / jnp.sum(raised, 0, keepdims=True))).astype(BF)
            prob_ref[half, tri_start(at) : tri_start(at) + stop, :] = prob
            mixed = mm(val_t_ref[half * HEAD : (half + 1) * HEAD, 0:stop], prob)
            out_t_ref[half * HEAD : (half + 1) * HEAD, at * QB : stop] = mixed
    out_ref[...] = out_t_ref[...].T.astype(BF)


def pair_specs(frames, width):
    pairs = width // LANES
    return [pl.BlockSpec((frames, LANES), lambda at, part=part: (0, part * pairs + at)) for part in range(3)]


def attend(triple, width):
    frames = triple.shape[0]
    pairs = width // LANES
    tri = tri_start(frames // QB)
    return pl.pallas_call(
        attend_kernel,
        grid=(pairs,),
        in_specs=pair_specs(frames, width),
        out_specs=[
            pl.BlockSpec((frames, LANES), lambda at: (0, at)),
            pl.BlockSpec((2, tri, QB), lambda at: (at, 0, 0)),
        ],
        out_shape=[
            jax.ShapeDtypeStruct((frames, width), BF),
            jax.ShapeDtypeStruct((2 * pairs, tri, QB), BF),
        ],
        scratch_shapes=[pltpu.VMEM((LANES, frames), BF), pltpu.VMEM((LANES, frames), F32)],
        compiler_params=params(),
        cost_estimate=cost(
            8 * tri * QB * HEAD * pairs, 2 * (4 * frames * width + 2 * pairs * tri * QB), 2 * pairs * tri * QB
        ),
        name="attend",
    )(triple, triple, triple)


def attend_back_kernel(
    q_ref, k_ref, v_ref, out_ref, grad_ref, prob_ref, back_ref, key_t_ref, dq_t_ref, dk_acc, dv_acc
):
    frames = q_ref.shape[0]
    lane = lax.broadcasted_iota(jnp.int32, (1, LANES), 1) // HEAD
    key_t_ref[...] = k_ref[...].T
    dk_acc[...] = jnp.zeros_like(dk_acc)
    dv_acc[...] = jnp.zeros_like(dv_acc)
    for at in range(frames // QB):
        stop = (at + 1) * QB
        rows = slice(at * QB, stop)
        product = (out_ref[rows, :].astype(F32) * grad_ref[rows, :].astype(F32)).T
        for half in range(2):
            keep = lane == half
            mask = jnp.where(keep, 1.0, 0.0).astype(BF)
            query = q_ref[rows, :] * jnp.where(keep, SCALE, 0.0).astype(BF)
            grad = grad_ref[rows, :] * mask
            delta = jnp.sum(product[half * HEAD : (half + 1) * HEAD, :], 0, keepdims=True)
            prob = prob_ref[half, tri_start(at) : tri_start(at) + stop, :]
            prob_grad = mm_nt(v_ref[0:stop, :], grad)
            score_grad = (prob.astype(F32) * (prob_grad - delta)).astype(BF)
            dv_acc[0:stop, :] += mm(prob, grad)
            dk_acc[0:stop, :] += mm(score_grad, query)
            dq_t_ref[half * HEAD : (half + 1) * HEAD, rows] = mm(
                key_t_ref[half * HEAD : (half + 1) * HEAD, 0:stop], score_grad
            )
    back_ref[0] = (dq_t_ref[...].T * SCALE).astype(BF)
    back_ref[1] = dk_acc[...].astype(BF)
    back_ref[2] = dv_acc[...].astype(BF)


def attend_back(triple, attended, gradient, probs, width):
    frames = triple.shape[0]
    pairs = width // LANES
    tri = tri_start(frames // QB)
    column = pl.BlockSpec((frames, LANES), lambda at: (0, at))
    return pl.pallas_call(
        attend_back_kernel,
        grid=(pairs,),
        in_specs=pair_specs(frames, width) + [column, column, pl.BlockSpec((2, tri, QB), lambda at: (at, 0, 0))],
        out_specs=pl.BlockSpec((3, frames, LANES), lambda at: (0, 0, at)),
        out_shape=jax.ShapeDtypeStruct((3, frames, width), BF),
        scratch_shapes=[
            pltpu.VMEM((LANES, frames), BF),
            pltpu.VMEM((LANES, frames), F32),
            pltpu.VMEM((frames, LANES), F32),
            pltpu.VMEM((frames, LANES), F32),
        ],
        compiler_params=params(),
        cost_estimate=cost(16 * tri * QB * HEAD * pairs, 2 * (8 * frames * width + 2 * pairs * tri * QB)),
        name="attend_back",
    )(triple, triple, triple, attended, gradient, probs)


def feed_kernel(
    normed_ref, cot_ref, down_in_ref, up_in_ref, down_out_ref, up_out_ref, w_in_ref, w_out_ref,
    out_ref, gu_ref, gdown_in_ref, gup_in_ref, gdown_out_ref, gup_out_ref,
    out_acc, gu_acc, lat_in, glat_out, lat_acc, glat_acc, lat_t, glat_t,
):
    at = pl.program_id(0)

    @pl.when(at == 0)
    def _():
        latent = mm_nt(normed_ref[...], down_in_ref[...]).astype(BF)
        glat = mm_nt(cot_ref[...], up_out_ref[...]).astype(BF)
        lat_in[...] = latent
        glat_out[...] = glat
        lat_t[...] = latent.astype(F32).T.astype(BF)
        glat_t[...] = glat.astype(F32).T.astype(BF)
        out_acc[...] = jnp.zeros_like(out_acc)
        gu_acc[...] = jnp.zeros_like(gu_acc)
        lat_acc[...] = jnp.zeros_like(lat_acc)
        glat_acc[...] = jnp.zeros_like(glat_acc)

    w_in = w_in_ref[...]
    w_out = w_out_ref[...]
    pre = mm(normed_ref[...], w_in) + mm(lat_in[...], up_in_ref[...])
    act_grad = mm_nt(cot_ref[...], w_out) + mm(glat_out[...], down_out_ref[...])
    cdf = 0.5 * (1.0 + lax.erf(pre * SQRT_HALF))
    slope = cdf + pre * (jnp.exp(-0.5 * pre * pre) * INV_SQRT_2PI)
    act = (pre * cdf).astype(BF)
    pre_grad = (act_grad * slope).astype(BF)
    out_acc[...] += mm(act, w_out)
    gu_acc[...] += mm_nt(pre_grad, w_in)
    lat_acc[...] += mm_nt(act, down_out_ref[...])
    glat_acc[...] += mm_nt(pre_grad, up_in_ref[...])
    gup_in_ref[...] = mm(lat_t[...], pre_grad)
    gdown_out_ref[...] = mm(glat_t[...], act)

    @pl.when(at == pl.num_programs(0) - 1)
    def _():
        latent = lat_acc[...].astype(BF)
        glat = glat_acc[...].astype(BF)
        out_ref[...] = (out_acc[...] + mm(latent, up_out_ref[...])).astype(out_ref.dtype)
        gu_ref[...] = (gu_acc[...] + mm(glat, down_in_ref[...])).astype(gu_ref.dtype)
        gup_out_ref[...] = mm(latent.astype(F32).T.astype(BF), cot_ref[...])
        gdown_in_ref[...] = mm(glat.astype(F32).T.astype(BF), normed_ref[...])


def feed_forward(normed, cotangent, down_in, up_in, down_out, up_out, weights, hidden, kind):
    row_count, model = normed.shape
    rank = down_in.shape[0]
    block = 512 if hidden % 512 == 0 else (256 if hidden % 256 == 0 else hidden)
    w_in, in_spec, w_out, out_spec = weights(block)
    main = whole((row_count, model))
    slim = pl.BlockSpec((rank, block), lambda at: (0, at))
    small = whole((rank, model))
    return pl.pallas_call(
        feed_kernel,
        grid=(hidden // block,),
        in_specs=[main, main, small, slim, slim, small, in_spec, out_spec],
        out_specs=[main, main, small, slim, slim, small],
        out_shape=[
            jax.ShapeDtypeStruct((row_count, model), kind),
            jax.ShapeDtypeStruct((row_count, model), kind),
            jax.ShapeDtypeStruct((rank, model), F32),
            jax.ShapeDtypeStruct((rank, hidden), F32),
            jax.ShapeDtypeStruct((rank, hidden), F32),
            jax.ShapeDtypeStruct((rank, model), F32),
        ],
        scratch_shapes=[pltpu.VMEM((row_count, model), F32)] * 2
        + [pltpu.VMEM((row_count, rank), BF)] * 2
        + [pltpu.VMEM((row_count, rank), F32)] * 2
        + [pltpu.VMEM((rank, row_count), BF)] * 2,
        compiler_params=params(),
        cost_estimate=cost(8 * row_count * model * hidden, 4 * hidden * model, 2 * row_count * hidden),
        name="feed_forward",
    )(normed, cotangent, down_in, up_in, down_out, up_out, w_in, w_out)


def spread_heads(rows_ref, into_ref, model):
    keys = rows_ref.shape[0]
    wide = 4 * HEAD
    row = lax.broadcasted_iota(jnp.int32, (4 * keys, wide), 0) // keys
    col = lax.broadcasted_iota(jnp.int32, (4 * keys, wide), 1) // HEAD
    mask = jnp.where(row == col, 1.0, 0.0).astype(BF)
    for group in range(model // wide):
        part = rows_ref[:, group * wide : (group + 1) * wide]
        into_ref[group * 4 * keys : (group + 1) * 4 * keys, :] = jnp.concatenate([part] * 4, 0) * mask


def half_sums(values, reduce, fill):
    pieces = []
    for at in range(values.shape[1] // LANES):
        piece = values[:, at * LANES : (at + 1) * LANES]
        low = lax.broadcasted_iota(jnp.int32, piece.shape, 1) < HEAD
        first = reduce(jnp.where(low, piece, fill), -1, keepdims=True)
        second = reduce(jnp.where(low, fill, piece), -1, keepdims=True)
        pieces.append(jnp.where(low, first, second))
    return jnp.concatenate(pieces, 1)


def middle_kernel(
    attended_ref, inputs_ref, w_self_ref, w_query_ref, w_cross_ref, adapt_ref, gain_ref, bias_ref, keys_ref, values_ref,
    resid1_ref, normed2_ref, query_ref, probs_ref, crossed_ref, resid2_ref, normed3_ref, lat_ref,
    key_wide, value_wide,
):
    model = attended_ref.shape[1]
    wide = 4 * HEAD

    @pl.when(pl.program_id(0) == 0)
    def _():
        spread_heads(keys_ref, key_wide, model)
        spread_heads(values_ref, value_wide, model)

    def adapted(moving, weight, index):
        latent = mm_nt(moving, adapt_ref[32 * index : 32 * index + 16, :]).astype(BF)
        lat_ref[:, 16 * index : 16 * index + 16] = latent
        return mm(moving, weight[...]) + mm(latent, adapt_ref[32 * index + 16 : 32 * index + 32, :])

    resid1 = inputs_ref[...].astype(F32) + adapted(attended_ref[...], w_self_ref, 0)
    resid1_ref[...] = resid1
    normed2 = layer_norm(resid1, gain_ref[1:2, :], bias_ref[1:2, :]).astype(BF)
    normed2_ref[...] = normed2
    query = adapted(normed2, w_query_ref, 1).astype(BF)
    query_ref[...] = query
    for group in range(model // wide):
        lanes = slice(group * wide, (group + 1) * wide)
        score = mm_nt(query[:, lanes], key_wide[lanes, :]) * SCALE
        raised = jnp.exp(score - half_sums(score, jnp.max, -1e30))
        prob = (raised / half_sums(raised, jnp.sum, 0.0)).astype(BF)
        probs_ref[:, lanes] = prob
        crossed_ref[:, lanes] = mm(prob, value_wide[lanes, :]).astype(BF)
    resid2 = resid1 + adapted(crossed_ref[...], w_cross_ref, 2)
    resid2_ref[...] = resid2
    normed3_ref[...] = layer_norm(resid2, gain_ref[2:3, :], bias_ref[2:3, :]).astype(BF)


def once(shape, at=None):
    spot = (0,) * len(shape) if at is None else at
    return pl.BlockSpec(shape, lambda *_: spot, pipeline_mode=pl.Buffered(1))


def square(packed, start):
    model = packed.shape[0]
    return packed, once((model, model), (0, start // model))


def middle(attended, inputs, packed, starts, adapters, gains, biases, keys, values):
    row_count, model = attended.shape
    step = min(row_count, 256)
    (w_self, spec_self), (w_query, spec_query), (w_cross, spec_cross) = [square(packed, at) for at in starts]
    rows = pl.BlockSpec((step, model), lambda at: (at, 0))
    shape = lambda kind: jax.ShapeDtypeStruct((row_count, model), kind)
    return pl.pallas_call(
        middle_kernel,
        grid=(row_count // step,),
        in_specs=[rows, rows, spec_self, spec_query, spec_cross]
        + [once(item.shape) for item in (adapters, gains, biases, keys, values)],
        out_specs=[rows] * 7 + [pl.BlockSpec((step, 48), lambda at: (at, 0))],
        out_shape=[shape(kind) for kind in (F32, BF, BF, BF, BF, F32, BF)]
        + [jax.ShapeDtypeStruct((row_count, 48), BF)],
        scratch_shapes=[pltpu.VMEM((model // HEAD * keys.shape[0], 4 * HEAD), BF)] * 2,
        compiler_params=params(),
        cost_estimate=cost(6 * row_count * model * model, 6 * model * model + 24 * row_count * model),
        name="middle",
    )(attended, inputs, w_self, w_query, w_cross, adapters, gains, biases, keys, values)


def middle_back_kernel(
    gu_ref, more_ref, cot_ref, resid2_ref, resid1_ref, normed2_ref, query_ref, probs_ref, crossed_ref, attended_ref,
    lat_ref, w_self_ref, w_query_ref, w_cross_ref, adapt_ref, gain_ref, keys_ref, values_ref,
    resid1_grad_ref, attended_grad_ref, memory_ref, small_ref,
    key_wide, value_wide, key_acc, value_acc,
):
    model = gu_ref.shape[1]
    wide = 4 * HEAD
    keys = keys_ref.shape[0]
    at = pl.program_id(0)

    @pl.when(at == 0)
    def _():
        spread_heads(keys_ref, key_wide, model)
        spread_heads(values_ref, value_wide, model)
        key_acc[...] = jnp.zeros_like(key_acc)
        value_acc[...] = jnp.zeros_like(value_acc)
        small_ref[...] = jnp.zeros_like(small_ref)

    def back(gradient, moving, weight, index):
        down = adapt_ref[32 * index : 32 * index + 16, :]
        upper = adapt_ref[32 * index + 16 : 32 * index + 32, :]
        glat = mm_nt(gradient, upper).astype(BF)
        small_ref[32 * index : 32 * index + 16, :] += mm_tn(glat, moving)
        small_ref[32 * index + 16 : 32 * index + 32, :] += mm_tn(lat_ref[:, 16 * index : 16 * index + 16], gradient)
        return mm_nt(gradient, weight[...]) + mm(glat, down)

    gradient = gu_ref[...].astype(F32) + more_ref[...].astype(F32)
    resid2_grad = cot_ref[...].astype(F32) + norm_back(resid2_ref[...], gain_ref[2:3, :], gradient)
    cross_grad = back(resid2_grad.astype(BF), crossed_ref[...], w_cross_ref, 2).astype(BF)
    pieces = []
    for group in range(model // wide):
        lanes = slice(group * wide, (group + 1) * wide)
        part = cross_grad[:, lanes]
        prob = probs_ref[:, lanes]
        wide_prob = prob.astype(F32)
        weighted = wide_prob * mm_nt(part, value_wide[lanes, :])
        score_grad = (weighted - wide_prob * half_sums(weighted, jnp.sum, 0.0)).astype(BF)
        pieces.append((mm(score_grad, key_wide[lanes, :]) * SCALE).astype(BF))
        key_acc[lanes, :] += mm_tn(score_grad, query_ref[:, lanes])
        value_acc[lanes, :] += mm_tn(prob, part)
    query_grad = jnp.concatenate(pieces, 1)
    normed2_grad = back(query_grad, normed2_ref[...], w_query_ref, 1)
    resid1_grad = resid2_grad + norm_back(resid1_ref[...], gain_ref[1:2, :], normed2_grad)
    resid1_grad_ref[...] = resid1_grad
    attended_grad_ref[...] = back(resid1_grad.astype(BF), attended_ref[...], w_self_ref, 0).astype(BF)

    @pl.when(at == pl.num_programs(0) - 1)
    def _():
        col = lax.broadcasted_iota(jnp.int32, (keys, wide), 1) // HEAD
        for group in range(model // wide):
            lanes = slice(group * wide, (group + 1) * wide)
            key_sum = jnp.zeros((keys, wide), F32)
            value_sum = jnp.zeros((keys, wide), F32)
            for head in range(4):
                rows = slice(group * wide + head * keys, group * wide + (head + 1) * keys)
                key_sum = jnp.where(col == head, key_acc[rows, :], key_sum)
                value_sum = jnp.where(col == head, value_acc[rows, :], value_sum)
            memory_ref[0, :, lanes] = (key_sum * SCALE).astype(BF)
            memory_ref[1, :, lanes] = value_sum.astype(BF)


def middle_back(gu, more, cotangent, kept, packed, starts, adapters, gains, keys, values):
    row_count, model = gu.shape
    step = min(row_count, 128)
    attended, resid1, normed2, query, probs, crossed, resid2, latents = kept
    (w_self, spec_self), (w_query, spec_query), (w_cross, spec_cross) = [square(packed, at) for at in starts]
    rows = pl.BlockSpec((step, model), lambda at: (at, 0))
    scratch = pltpu.VMEM((model // HEAD * keys.shape[0], 4 * HEAD), BF)
    wider = pltpu.VMEM((model // HEAD * keys.shape[0], 4 * HEAD), F32)
    memory = (2,) + keys.shape
    return pl.pallas_call(
        middle_back_kernel,
        grid=(row_count // step,),
        in_specs=[rows] * 10
        + [pl.BlockSpec((step, 48), lambda at: (at, 0)), spec_self, spec_query, spec_cross]
        + [once(item.shape) for item in (adapters, gains, keys, values)],
        out_specs=[rows, rows, whole(memory), whole(adapters.shape)],
        out_shape=[
            jax.ShapeDtypeStruct((row_count, model), F32),
            jax.ShapeDtypeStruct((row_count, model), BF),
            jax.ShapeDtypeStruct(memory, BF),
            jax.ShapeDtypeStruct(adapters.shape, F32),
        ],
        scratch_shapes=[scratch, scratch, wider, wider],
        compiler_params=params(),
        cost_estimate=cost(6 * row_count * model * model, 6 * model * model + 36 * row_count * model),
        name="middle_back",
    )(
        gu, more, cotangent, resid2, resid1, normed2, query, probs, crossed, attended, latents,
        w_self, w_query, w_cross, adapters, gains, keys, values,
    )


def qkv_back_kernel(
    place_ref, grad_ref, normed_ref, lat_ref, down_ref, up_ref, w_ref, gu_ref, gdown_ref, gup_ref, gu_acc, glat_acc
):
    at = pl.program_id(0)
    gradient = grad_ref[...]
    direct = mm_nt(gradient, w_ref[...])
    glat = mm_nt(gradient, up_ref[...])
    gup_ref[...] = mm_tn(lat_ref[...], gradient)

    @pl.when(at == 0)
    def _():
        gu_acc[...] = direct
        glat_acc[...] = glat

    @pl.when(at > 0)
    def _():
        gu_acc[...] += direct
        glat_acc[...] += glat

    @pl.when(at == pl.num_programs(0) - 1)
    def _():
        low = glat_acc[...].astype(BF)
        gu_ref[...] = (gu_acc[...] + mm(low, down_ref[...])).astype(gu_ref.dtype)
        gdown_ref[...] = mm_tn(low, normed_ref[...])


def qkv_back(place, row_count, gradient, normed, latent, down, up, packed, start, kind):
    model = normed.shape[1]
    width = gradient.shape[2]
    ranks = down.shape[0]
    if start % width == 0 and width % LANES == 0:
        weight, spec = packed, pl.BlockSpec((model, width), lambda at, ref: (0, start // width + at))
    else:
        weight = packed[:, start : start + 3 * width].reshape(model, 3, width).transpose(1, 0, 2)
        spec = pl.BlockSpec((None, model, width), lambda at, ref: (at, 0, 0))
    part = pl.BlockSpec((None, ranks, width), lambda at, ref: (at, 0, 0))
    return pl.pallas_call(
        qkv_back_kernel,
        grid_spec=pltpu.PrefetchScalarGridSpec(
            num_scalar_prefetch=1,
            grid=(3,),
            in_specs=[
                pl.BlockSpec((None, row_count, width), lambda at, ref: (at, ref[0], 0)),
                pl.BlockSpec((row_count, model), lambda at, ref: (ref[0], 0)),
                pl.BlockSpec((row_count, ranks), lambda at, ref: (ref[0], 0)),
                whole(down.shape),
                part,
                spec,
            ],
            out_specs=[whole((row_count, model)), whole((ranks, model)), part],
            scratch_shapes=[pltpu.VMEM((row_count, model), F32), pltpu.VMEM((row_count, ranks), F32)],
        ),
        out_shape=[
            jax.ShapeDtypeStruct((row_count, model), kind),
            jax.ShapeDtypeStruct((ranks, model), F32),
            jax.ShapeDtypeStruct((3, ranks, width), F32),
        ],
        compiler_params=params(),
        cost_estimate=cost(6 * row_count * model * width, 6 * model * width + 8 * row_count * model),
        name="qkv_back",
    )(place, gradient, normed, latent, down, up, weight)


def body(
    inputs,
    text_states,
    adapter_index,
    norm_gains,
    norm_biases,
    self_in,
    self_out,
    cross_query,
    cross_text,
    cross_out,
    hidden_in,
    hidden_out,
    adapter_down,
    adapter_up,
    cotangent,
    *,
    sizes,
):
    seq, fsdp = sizes
    spot = lax.axis_index("seq")
    local = self_in.shape[0]
    model = inputs.shape[2]
    rows = inputs.shape[1]
    frames = rows * seq
    wide = model // seq
    hidden_all = hidden_in.shape[1]
    hidden = hidden_all // seq
    adapters, rank, piece = adapter_down.shape
    total = piece * fsdp

    def swap(value):
        return lax.ppermute(value, "seq", [(0, 1), (1, 0)])

    def pick(value, axis, extent):
        return lax.dynamic_slice_in_dim(value, spot * extent, extent, axis)

    def joined(mine, other, axis):
        return jnp.where(
            spot == 0, jnp.concatenate([mine, other], axis), jnp.concatenate([other, mine], axis)
        )

    def gather(value, axis):
        if seq == 2:
            return joined(value, swap(value), axis)
        return lax.all_gather(value, "seq", axis=axis, tiled=True)

    def after(value, *others):
        return lax.optimization_barrier((value,) + others)[0]

    index_all = lax.all_to_all(jnp.broadcast_to(adapter_index, (fsdp,)), "fsdp", 0, 0, tiled=True)
    table = jnp.concatenate([adapter_down, adapter_up], 1)
    picked = jnp.take(table, index_all, axis=0)
    arrived = lax.all_to_all(picked, "fsdp", 0, 0, tiled=True)
    chosen = arrived.transpose(1, 0, 2).reshape(2 * rank, total)
    down_all, upper_all = chosen[:rank], chosen[rank:]
    in_cuts = [0, 3 * model, 4 * model, 5 * model, 7 * model, 8 * model, 9 * model, 9 * model + hidden_all]
    out_cuts = [0, 3 * model, 4 * model, 5 * model, 7 * model, 8 * model, 8 * model + hidden_all, 9 * model + hidden_all]
    downs = [down_all[:, in_cuts[at] : in_cuts[at + 1]] for at in range(7)]
    uppers = [upper_all[:, out_cuts[at] : out_cuts[at + 1]] for at in range(7)]

    def own_parts(matrix, parts):
        return lax.dynamic_index_in_dim(matrix.reshape(-1, parts, seq, wide), spot, 2, False)

    def part_down(matrix, parts):
        return matrix.reshape(rank, parts, model).transpose(1, 0, 2).reshape(parts * rank, model)

    def part_upper(matrix, parts):
        own = own_parts(matrix, parts).transpose(1, 0, 2)
        eye = jnp.eye(parts, dtype=BF)[:, :, None, None]
        return (eye * own[:, None]).reshape(parts, parts * rank, wide)

    own_in = own_parts(self_in, 3).reshape(local, 3 * wide)
    own_text = own_parts(cross_text, 2).reshape(local, 2 * wide)
    first = jnp.concatenate([self_out, cross_query, cross_out, own_in, own_text], 1)
    starts = (0, model, 2 * model)
    start_in, start_text = 3 * model, 3 * model + 3 * wide
    packed = lax.all_gather(first, "fsdp", axis=0, tiled=True)
    depth = hidden_out.shape[0] // seq
    merged = depth % local == 0
    if merged:
        folds = depth // local
        unit_shape = (fsdp, seq, folds, local)

        def own_units(matrix):
            kept = lax.dynamic_index_in_dim(matrix.reshape((-1,) + unit_shape), spot, 2, False)
            return kept.transpose(0, 2, 1, 3).reshape(-1, hidden)

        def place_units(matrix):
            kept = matrix.reshape(-1, folds, fsdp, local).transpose(0, 2, 1, 3)[:, :, None]
            return put(kept, 2).reshape(-1, hidden_all)

        low = pick(hidden_out, 0, depth).reshape(folds, local, model).transpose(1, 0, 2)
        second = jnp.concatenate([own_units(hidden_in), low.reshape(local, folds * model)], 1)
        packed_feed = lax.all_gather(second, "fsdp", axis=0, tiled=True)

        def feed_weights(block):
            per = model // block
            return (
                packed_feed,
                pl.BlockSpec((model, block), lambda at: (0, at)),
                packed_feed,
                pl.BlockSpec((block, model), lambda at: (at % per, folds + at // per)),
            )
    else:

        def own_units(matrix):
            kept = lax.dynamic_index_in_dim(matrix.reshape(-1, fsdp, seq, depth), spot, 2, False)
            return kept.reshape(-1, hidden)

        def place_units(matrix):
            return put(matrix.reshape(-1, fsdp, 1, depth), 2).reshape(-1, hidden_all)

        whole_in = lax.all_gather(own_units(hidden_in), "fsdp", axis=0, tiled=True)
        whole_out = lax.all_gather(pick(hidden_out, 0, depth), "fsdp", axis=0, tiled=True)

        def feed_weights(block):
            return (
                whole_in,
                pl.BlockSpec((model, block), lambda at: (0, at)),
                whole_out,
                pl.BlockSpec((block, model), lambda at: (at, 0)),
            )

    def put(value, axis):
        shape = list(value.shape)
        shape[axis] = seq
        return lax.dynamic_update_slice_in_dim(jnp.zeros(shape, value.dtype), value, spot, axis)

    frames_in = inputs[0]
    cot = cotangent[0]
    down_qkv, upper_qkv = part_down(downs[0], 3), part_upper(uppers[0], 3)
    x_all = gather(frames_in, 0)
    normed1, lat_qkv, triple = qkv_project(
        x_all, norm_gains[0:1], norm_biases[0:1], down_qkv, upper_qkv, packed, start_in, 3 * wide
    )
    padded = -(-wide // LANES) * LANES
    if padded != wide:
        triple = jnp.pad(triple.reshape(frames, 3, wide), ((0, 0), (0, 0), (0, padded - wide)))
        triple = triple.reshape(frames, 3 * padded)
    head_out, probs = attend(triple, padded)
    if seq == 2:
        mine = pick(head_out, 0, rows)
        theirs = lax.dynamic_slice_in_dim(head_out, (1 - spot) * rows, rows, 0)
        attended = joined(mine, swap(theirs), 1)
    else:
        attended = lax.all_to_all(head_out[:, :wide], "seq", split_axis=0, concat_axis=1, tiled=True)

    text = text_states[0]
    down_text, upper_text = part_down(downs[3], 2), part_upper(uppers[3], 2)
    w_text = packed[:, start_text : start_text + 2 * wide]
    flat_text = upper_text.transpose(1, 0, 2).reshape(2 * rank, 2 * wide)
    lat_text = mm_nt(text, down_text).astype(BF)
    memory = (mm(text, w_text) + mm(lat_text, flat_text)).astype(BF).reshape(-1, 2, wide)
    memory_all = gather(memory, 2)
    keys, values = memory_all[:, 0], memory_all[:, 1]

    square_adapters = jnp.concatenate([downs[1], uppers[1], downs[2], uppers[2], downs[4], uppers[4]], 0)
    resid1, normed2, query, cross_probs, crossed, resid2, normed3, latents = middle(
        attended, frames_in, packed, starts, square_adapters, norm_gains, norm_biases, keys, values
    )

    feed_adapters = (downs[5], own_units(uppers[5]), own_units(downs[6]), uppers[6])
    if seq == 2:
        cot_other = swap(after(cot, x_all))
        normed3_other = swap(normed3)
        theirs = feed_forward(normed3_other, cot_other, *feed_adapters, feed_weights, hidden, BF)
        ours = feed_forward(after(normed3, theirs[1]), cot, *feed_adapters, feed_weights, hidden, F32)
        gu_more = swap(theirs[1])
        out_more = swap(after(theirs[0], gu_more))
        output = (resid2 + ours[0] + out_more.astype(F32)).astype(BF)
        gu = ours[1]
        feed_grads = [one + two for one, two in zip(ours[2:], theirs[2:])]
    else:
        all_out = feed_forward(gather(normed3, 0), gather(cot, 0), *feed_adapters, feed_weights, hidden, F32)
        summed = [
            lax.psum_scatter(item.astype(BF), "seq", scatter_dimension=0, tiled=True) for item in all_out[:2]
        ]
        output = (resid2 + summed[0].astype(F32)).astype(BF)
        gu, gu_more = summed[1], jnp.zeros_like(summed[1])
        feed_grads = all_out[2:]
    gdown_in, gup_in, gdown_out, gup_out = feed_grads

    kept = (attended, resid1, normed2, query, cross_probs, crossed, resid2, latents)
    resid1_grad, attended_grad, memory_part, square_grads = middle_back(
        gu, gu_more, cot, kept, packed, starts, square_adapters, norm_gains, keys, values
    )

    if seq == 2:
        other_part = lax.dynamic_slice_in_dim(memory_part, (1 - spot) * wide, wide, 2)
        memory_grad = (
            pick(memory_part, 2, wide).astype(F32) + swap(other_part).astype(F32)
        ).astype(BF)
    else:
        memory_grad = lax.psum_scatter(memory_part, "seq", scatter_dimension=2, tiled=True)
    memory_flat = memory_grad.transpose(1, 0, 2).reshape(-1, 2 * wide)
    glat_text = mm_nt(memory_flat, flat_text).astype(BF)
    gup_text = mm_tn(lat_text, memory_flat)
    gdown_text = mm_tn(glat_text, text)
    text_grad = mm_nt(memory_flat, w_text) + mm(glat_text, down_text)

    if seq == 2:
        grad_theirs = lax.dynamic_slice_in_dim(attended_grad, (1 - spot) * wide, wide, 1)
        head_grad = joined(pick(attended_grad, 1, wide), swap(grad_theirs), 0)
    else:
        head_grad = lax.all_to_all(attended_grad, "seq", split_axis=1, concat_axis=0, tiled=True)
        head_grad = jnp.pad(head_grad, ((0, 0), (0, padded - wide)))
    triple_grad = attend_back(triple, head_out, head_grad, probs, padded)[:, :, :wide]
    back = partial(
        qkv_back, gradient=triple_grad, normed=normed1, latent=lat_qkv, down=down_qkv, up=upper_qkv, packed=packed,
        start=start_in,
    )
    if seq == 2:
        there = back((1 - spot)[None], rows, kind=BF)
        here = back(after(spot, there[0])[None], rows, kind=F32)
        normed1_grad = here[0] + swap(there[0]).astype(F32)
        gdown_qkv, gup_qkv = there[1] + here[1], there[2] + here[2]
    else:
        full, gdown_qkv, gup_qkv = back(jnp.zeros((1,), jnp.int32), frames, kind=BF)
        normed1_grad = lax.psum_scatter(full, "seq", scatter_dimension=0, tiled=True).astype(F32)
    input_grad = resid1_grad + norm_back(frames_in.astype(F32), norm_gains[0:1], normed1_grad)

    def flat_down(grads, parts):
        return grads.reshape(parts, rank, model).transpose(1, 0, 2).reshape(rank, parts * model)

    def flat_upper(grads, parts):
        own = jnp.stack([grads[at, at * rank : (at + 1) * rank] for at in range(parts)], 1)
        return put(own[:, :, None], 2).reshape(rank, parts * model)

    gup_text = gup_text.reshape(2 * rank, 2, wide).transpose(1, 0, 2)
    squares = [square_grads[rank * at : rank * (at + 1)] for at in range(6)]
    down_grads = jnp.concatenate(
        [flat_down(gdown_qkv, 3), squares[0], squares[2], flat_down(gdown_text, 2), squares[4], gdown_in,
         place_units(gdown_out)], 1
    )
    upper_grads = jnp.concatenate(
        [flat_upper(gup_qkv, 3), squares[1], squares[3], flat_upper(gup_text, 2), squares[5], place_units(gup_in),
         gup_out], 1
    )
    sent = jnp.concatenate([down_grads, upper_grads], 0).astype(BF)
    sent = sent.reshape(2 * rank, fsdp, piece).transpose(1, 0, 2)
    received = lax.all_to_all(sent, "fsdp", 0, 0, tiled=True)
    selector = (index_all[None, :] == jnp.arange(adapters, dtype=jnp.int32)[:, None]).astype(BF)
    shares = jnp.einsum("ac,crw->arw", selector, received, preferred_element_type=F32)
    if seq == 2:
        shares = shares + swap(shares.astype(BF)).astype(F32)
        text_total = text_grad + swap(text_grad.astype(BF)).astype(F32)
    else:
        shares = lax.psum(shares.astype(BF), "seq").astype(F32)
        text_total = lax.psum(text_grad.astype(BF), "seq").astype(F32)
    return (output[None], input_grad[None], text_total[None], shares[:, :rank], shares[:, rank:])


def solution(mesh):
    return jax.shard_map(
        partial(body, sizes=(mesh.shape["seq"], mesh.shape["fsdp"])),
        mesh=mesh,
        in_specs=(
            P("fsdp", "seq", None),
            P("fsdp", None, None),
            P("fsdp"),
            P(),
            P(),
            P("fsdp", None),
            P("fsdp", None),
            P("fsdp", None),
            P("fsdp", None),
            P("fsdp", None),
            P("fsdp", None),
            P("fsdp", None),
            P(None, None, "fsdp"),
            P(None, None, "fsdp"),
            P("fsdp", "seq", None),
        ),
        out_specs=(
            P("fsdp", "seq", None),
            P("fsdp", "seq", None),
            P("fsdp", None, None),
            P(None, None, "fsdp"),
            P(None, None, "fsdp"),
        ),
        check_vma=False,
    )
```

```python
from functools import partial

import jax
import jax.numpy as jnp
from jax import lax
from jax.experimental import pallas as pl
from jax.experimental.pallas import tpu as pltpu
from jax.sharding import PartitionSpec as P

HEAD = 64
LANES = 128
QB = 256
BF = jnp.bfloat16
F32 = jnp.float32
SCALE = float(HEAD) ** (-0.5)
SQRT_HALF = 0.7071067811865476
INV_SQRT_2PI = 0.3989422804014327
VMEM_LIMIT = 60 * 1024 * 1024


def mm(a, b):
    return lax.dot_general(a, b, (((1,), (0,)), ((), ())), preferred_element_type=F32)


def mm_nt(a, b):
    return lax.dot_general(a, b, (((1,), (1,)), ((), ())), preferred_element_type=F32)


def mm_tn(a, b):
    return lax.dot_general(a, b, (((0,), (0,)), ((), ())), preferred_element_type=F32)


def norm_stats(values):
    centered = values - jnp.mean(values, -1, keepdims=True)
    variance = jnp.mean(centered * centered, -1, keepdims=True)
    inverse = lax.rsqrt(variance + 1e-05)
    return centered * inverse, inverse


def layer_norm(values, gains, biases):
    unit, _ = norm_stats(values)
    return unit * gains + biases


def norm_back(values, gains, gradient):
    unit, inverse = norm_stats(values)
    scaled = gradient * gains
    mean_one = jnp.mean(scaled, -1, keepdims=True)
    mean_two = jnp.mean(scaled * unit, -1, keepdims=True)
    return inverse * (scaled - mean_one - unit * mean_two)


def whole(shape):
    return pl.BlockSpec(shape, lambda *_: (0,) * len(shape))


def params(count=1):
    return pltpu.CompilerParams(
        dimension_semantics=("arbitrary",) * count if count else None, vmem_limit_bytes=VMEM_LIMIT
    )


def cost(flops, moved, special=0):
    return pl.CostEstimate(flops=int(flops), bytes_accessed=int(moved), transcendentals=int(special))


def window(packed, start, width, rows=None, steps=1, step=0):
    block = width // steps
    rows = packed.shape[0] if rows is None else rows
    if start % block == 0 and block % LANES == 0:
        base = start // block
        return packed, pl.BlockSpec((rows, block), lambda *at: (0, base + (at[step] if steps > 1 else 0)))
    return packed[:, start : start + width], pl.BlockSpec(
        (rows, block), lambda *at: (0, at[step] if steps > 1 else 0)
    )


def norm_kernel(place_ref, *refs):
    count = len(refs) - 5
    parts, (gain_ref, bias_ref, down_ref, normed_ref, lat_ref) = refs[:count], refs[count:]
    step = 128
    for index, part_ref in enumerate(parts):
        base = place_ref[index] * part_ref.shape[0]

        def some(at, carry):
            rows = pl.ds(pl.multiple_of(at * step, step), step)
            into = pl.ds(pl.multiple_of(base + at * step, step), step)
            normed = layer_norm(part_ref[rows, :].astype(F32), gain_ref[...], bias_ref[...]).astype(BF)
            normed_ref[into, :] = normed
            lat_ref[into, :] = mm_nt(normed, down_ref[...]).astype(BF)
            return carry

        lax.fori_loop(0, part_ref.shape[0] // step, some, 0)


def smem():
    return pl.BlockSpec(memory_space=pltpu.SMEM)


def norm_project(places, parts, gains, biases, down):
    model = parts[0].shape[1]
    frames = sum(part.shape[0] for part in parts)
    ranks = down.shape[0]
    return pl.pallas_call(
        norm_kernel,
        in_specs=[smem()] + [whole(item.shape) for item in parts + [gains, biases, down]],
        out_specs=[whole((frames, model)), whole((frames, ranks))],
        out_shape=[jax.ShapeDtypeStruct((frames, model), BF), jax.ShapeDtypeStruct((frames, ranks), BF)],
        grid=(1,),
        compiler_params=params(),
        cost_estimate=cost(2 * frames * model * ranks, 4 * frames * model),
        name="norm_project",
    )(places, *parts, gains, biases, down)


def qkv_kernel(normed_ref, lat_ref, up_ref, w_ref, out_ref):
    step = 256

    def some(at, carry):
        rows = pl.ds(pl.multiple_of(at * step, step), step)
        out_ref[rows, :] = (mm(normed_ref[rows, :], w_ref[...]) + mm(lat_ref[rows, :], up_ref[...])).astype(BF)
        return carry

    lax.fori_loop(0, normed_ref.shape[0] // step, some, 0)


def qkv_project(normed, latent, up, packed, start, width):
    row_count, model = normed.shape
    ranks = latent.shape[1]
    steps = 3 if (width // 3) % LANES == 0 else 1
    operand, spec = window(packed, start, width, steps=steps)
    block = width // steps
    if steps == 3:
        up_spec = pl.BlockSpec((None, ranks, block), lambda at: (at, 0, 0))
    else:
        up = up.transpose(1, 0, 2).reshape(ranks, width)
        up_spec = whole(up.shape)
    return pl.pallas_call(
        qkv_kernel,
        grid=(steps,),
        in_specs=[whole(normed.shape), whole(latent.shape), up_spec, spec],
        out_specs=pl.BlockSpec((row_count, block), lambda at: (0, at)),
        out_shape=jax.ShapeDtypeStruct((row_count, width), BF),
        compiler_params=params(),
        cost_estimate=cost(2 * row_count * model * width, 2 * (row_count + width) * model),
        name="qkv_project",
    )(normed, latent, up, operand)


def tri_start(at):
    return QB * at * (at + 1) // 2


def attend_kernel(q_ref, k_ref, v_ref, out_ref, prob_ref, val_t_ref, out_t_ref):
    frames = q_ref.shape[0]
    lane = lax.broadcasted_iota(jnp.int32, (1, LANES), 1) // HEAD
    val_t_ref[...] = v_ref[...].T
    square = (QB, QB)
    keep_tri = lax.broadcasted_iota(jnp.int32, square, 0) <= lax.broadcasted_iota(jnp.int32, square, 1)
    for half in range(2):
        keep = lane == half
        for at in range(frames // QB):
            stop = (at + 1) * QB
            query = q_ref[at * QB : stop, :] * jnp.where(keep, SCALE, 0.0).astype(BF)
            score = jnp.where(keep_tri, mm_nt(k_ref[stop - QB : stop, :], query), -1e30)
            if at:
                score = jnp.concatenate([mm_nt(k_ref[0 : stop - QB, :], query), score], 0)
            raised = jnp.exp(score - jnp.max(score, 0, keepdims=True))
            prob = (raised * (1.0 / jnp.sum(raised, 0, keepdims=True))).astype(BF)
            prob_ref[half, tri_start(at) : tri_start(at) + stop, :] = prob
            mixed = mm(val_t_ref[half * HEAD : (half + 1) * HEAD, 0:stop], prob)
            out_t_ref[half * HEAD : (half + 1) * HEAD, at * QB : stop] = mixed
    out_ref[...] = out_t_ref[...].T.astype(BF)


def pair_specs(frames, width):
    pairs = width // LANES
    return [pl.BlockSpec((frames, LANES), lambda at, part=part: (0, part * pairs + at)) for part in range(3)]


def attend(triple, width):
    frames = triple.shape[0]
    pairs = width // LANES
    tri = tri_start(frames // QB)
    return pl.pallas_call(
        attend_kernel,
        grid=(pairs,),
        in_specs=pair_specs(frames, width),
        out_specs=[
            pl.BlockSpec((frames, LANES), lambda at: (0, at)),
            pl.BlockSpec((2, tri, QB), lambda at: (at, 0, 0)),
        ],
        out_shape=[
            jax.ShapeDtypeStruct((frames, width), BF),
            jax.ShapeDtypeStruct((2 * pairs, tri, QB), BF),
        ],
        scratch_shapes=[pltpu.VMEM((LANES, frames), BF), pltpu.VMEM((LANES, frames), F32)],
        compiler_params=params(),
        cost_estimate=cost(
            8 * tri * QB * HEAD * pairs, 2 * (4 * frames * width + 2 * pairs * tri * QB), 2 * pairs * tri * QB
        ),
        name="attend",
    )(triple, triple, triple)


def attend_back_kernel(place_ref, q_ref, k_ref, v_ref, out_ref, prob_ref, *refs):
    pieces, (back_ref, grad_ref, key_t_ref, dq_t_ref, dk_acc, dv_acc) = refs[:-6], refs[-6:]
    frames = q_ref.shape[0]
    for index, piece_ref in enumerate(pieces):
        size = piece_ref.shape[0]
        grad_ref[pl.ds(pl.multiple_of(place_ref[index] * size, size), size), :] = piece_ref[...]
    lane = lax.broadcasted_iota(jnp.int32, (1, LANES), 1) // HEAD
    key_t_ref[...] = k_ref[...].T
    dk_acc[...] = jnp.zeros_like(dk_acc)
    dv_acc[...] = jnp.zeros_like(dv_acc)
    for at in range(frames // QB):
        stop = (at + 1) * QB
        rows = slice(at * QB, stop)
        product = (out_ref[rows, :].astype(F32) * grad_ref[rows, :].astype(F32)).T
        for half in range(2):
            keep = lane == half
            mask = jnp.where(keep, 1.0, 0.0).astype(BF)
            query = q_ref[rows, :] * jnp.where(keep, SCALE, 0.0).astype(BF)
            grad = grad_ref[rows, :] * mask
            delta = jnp.sum(product[half * HEAD : (half + 1) * HEAD, :], 0, keepdims=True)
            prob = prob_ref[half, tri_start(at) : tri_start(at) + stop, :]
            prob_grad = mm_nt(v_ref[0:stop, :], grad)
            score_grad = (prob.astype(F32) * (prob_grad - delta)).astype(BF)
            dv_acc[0:stop, :] += mm(prob, grad)
            dk_acc[0:stop, :] += mm(score_grad, query)
            dq_t_ref[half * HEAD : (half + 1) * HEAD, rows] = mm(
                key_t_ref[half * HEAD : (half + 1) * HEAD, 0:stop], score_grad
            )
    back_ref[0] = (dq_t_ref[...].T * SCALE).astype(BF)
    back_ref[1] = dk_acc[...].astype(BF)
    back_ref[2] = dv_acc[...].astype(BF)


def attend_back(places, triple, attended, pieces, probs, width):
    frames = triple.shape[0]
    pairs = width // LANES
    tri = tri_start(frames // QB)
    column = pl.BlockSpec((frames, LANES), lambda at: (0, at))
    return pl.pallas_call(
        attend_back_kernel,
        grid=(pairs,),
        in_specs=[smem()]
        + pair_specs(frames, width)
        + [column, pl.BlockSpec((2, tri, QB), lambda at: (at, 0, 0))]
        + [pl.BlockSpec((piece.shape[0], LANES), lambda at: (0, at)) for piece in pieces],
        out_specs=pl.BlockSpec((3, frames, LANES), lambda at: (0, 0, at)),
        out_shape=jax.ShapeDtypeStruct((3, frames, width), BF),
        scratch_shapes=[
            pltpu.VMEM((frames, LANES), BF),
            pltpu.VMEM((LANES, frames), BF),
            pltpu.VMEM((LANES, frames), F32),
            pltpu.VMEM((frames, LANES), F32),
            pltpu.VMEM((frames, LANES), F32),
        ],
        compiler_params=params(),
        cost_estimate=cost(16 * tri * QB * HEAD * pairs, 2 * (8 * frames * width + 2 * pairs * tri * QB)),
        name="attend_back",
    )(places, triple, triple, triple, attended, probs, *pieces)


def feed_kernel(
    normed_ref, cot_ref, down_in_ref, up_in_ref, down_out_ref, up_out_ref, w_in_ref, w_out_ref,
    out_ref, gu_ref, gdown_in_ref, gup_in_ref, gdown_out_ref, gup_out_ref,
    out_acc, gu_acc, lat_in, glat_out, lat_acc, glat_acc, lat_t, glat_t,
):
    at = pl.program_id(0)

    @pl.when(at == 0)
    def _():
        latent = mm_nt(normed_ref[...], down_in_ref[...]).astype(BF)
        glat = mm_nt(cot_ref[...], up_out_ref[...]).astype(BF)
        lat_in[...] = latent
        glat_out[...] = glat
        lat_t[...] = latent.astype(F32).T.astype(BF)
        glat_t[...] = glat.astype(F32).T.astype(BF)
        out_acc[...] = jnp.zeros_like(out_acc)
        gu_acc[...] = jnp.zeros_like(gu_acc)
        lat_acc[...] = jnp.zeros_like(lat_acc)
        glat_acc[...] = jnp.zeros_like(glat_acc)

    w_in = w_in_ref[...]
    w_out = w_out_ref[...]
    pre = mm(normed_ref[...], w_in) + mm(lat_in[...], up_in_ref[...])
    act_grad = mm_nt(cot_ref[...], w_out) + mm(glat_out[...], down_out_ref[...])
    cdf = 0.5 * (1.0 + lax.erf(pre * SQRT_HALF))
    slope = cdf + pre * (jnp.exp(-0.5 * pre * pre) * INV_SQRT_2PI)
    act = (pre * cdf).astype(BF)
    pre_grad = (act_grad * slope).astype(BF)
    out_acc[...] += mm(act, w_out)
    gu_acc[...] += mm_nt(pre_grad, w_in)
    lat_acc[...] += mm_nt(act, down_out_ref[...])
    glat_acc[...] += mm_nt(pre_grad, up_in_ref[...])
    gup_in_ref[...] = mm(lat_t[...], pre_grad)
    gdown_out_ref[...] = mm(glat_t[...], act)

    @pl.when(at == pl.num_programs(0) - 1)
    def _():
        latent = lat_acc[...].astype(BF)
        glat = glat_acc[...].astype(BF)
        out_ref[...] = (out_acc[...] + mm(latent, up_out_ref[...])).astype(out_ref.dtype)
        gu_ref[...] = (gu_acc[...] + mm(glat, down_in_ref[...])).astype(gu_ref.dtype)
        gup_out_ref[...] = mm(latent.astype(F32).T.astype(BF), cot_ref[...])
        gdown_in_ref[...] = mm(glat.astype(F32).T.astype(BF), normed_ref[...])


def feed_forward(normed, cotangent, down_in, up_in, down_out, up_out, weights, hidden, kind):
    row_count, model = normed.shape
    rank = down_in.shape[0]
    block = 512 if hidden % 512 == 0 else (256 if hidden % 256 == 0 else hidden)
    w_in, in_spec, w_out, out_spec = weights(block)
    main = whole((row_count, model))
    slim = pl.BlockSpec((rank, block), lambda at: (0, at))
    small = whole((rank, model))
    return pl.pallas_call(
        feed_kernel,
        grid=(hidden // block,),
        in_specs=[main, main, small, slim, slim, small, in_spec, out_spec],
        out_specs=[main, main, small, slim, slim, small],
        out_shape=[
            jax.ShapeDtypeStruct((row_count, model), kind),
            jax.ShapeDtypeStruct((row_count, model), kind),
            jax.ShapeDtypeStruct((rank, model), F32),
            jax.ShapeDtypeStruct((rank, hidden), F32),
            jax.ShapeDtypeStruct((rank, hidden), F32),
            jax.ShapeDtypeStruct((rank, model), F32),
        ],
        scratch_shapes=[pltpu.VMEM((row_count, model), F32)] * 2
        + [pltpu.VMEM((row_count, rank), BF)] * 2
        + [pltpu.VMEM((row_count, rank), F32)] * 2
        + [pltpu.VMEM((rank, row_count), BF)] * 2,
        compiler_params=params(),
        cost_estimate=cost(8 * row_count * model * hidden, 4 * hidden * model, 2 * row_count * hidden),
        name="feed_forward",
    )(normed, cotangent, down_in, up_in, down_out, up_out, w_in, w_out)


def spread_heads(rows_ref, into_ref, model):
    keys = rows_ref.shape[0]
    wide = 4 * HEAD
    row = lax.broadcasted_iota(jnp.int32, (4 * keys, wide), 0) // keys
    col = lax.broadcasted_iota(jnp.int32, (4 * keys, wide), 1) // HEAD
    mask = jnp.where(row == col, 1.0, 0.0).astype(BF)

    def some(group, carry):
        part = rows_ref[:, pl.ds(pl.multiple_of(group * wide, wide), wide)]
        into = pl.ds(pl.multiple_of(group * 4 * keys, 4 * keys), 4 * keys)
        into_ref[into, :] = jnp.concatenate([part] * 4, 0) * mask
        return carry

    lax.fori_loop(0, model // wide, some, 0)


def head_total(values, keys, reduce):
    split = values.reshape(4, keys, values.shape[1])
    return jnp.broadcast_to(reduce(split, 1, keepdims=True), split.shape).reshape(values.shape)


def each(count, step, work):
    def some(at, carry):
        work(pl.ds(pl.multiple_of(at * step, step), step))
        return carry

    lax.fori_loop(0, count // step, some, 0)


def weight_copies(packed_ref, starts, hold_ref, sem_ref):
    model = hold_ref.shape[1]
    return [
        pltpu.make_async_copy(packed_ref.at[:, pl.ds(start, model)], hold_ref.at[index], sem_ref.at[index])
        for index, start in enumerate(starts)
    ]


def middle_kernel(starts, place_ref, packed_ref, inputs_ref, adapt_ref, gain_ref, bias_ref, keys_ref, values_ref, *refs):
    pieces = refs[:-13]
    (
        attended_ref, resid1_ref, normed2_ref, query_ref, probs_ref, crossed_ref, resid2_ref, normed3_ref, lat_ref,
        hold_ref, key_wide, value_wide, sem_ref,
    ) = refs[-13:]
    model = inputs_ref.shape[1]
    keys = keys_ref.shape[0]
    rows = inputs_ref.shape[0]
    wide = 4 * HEAD
    copies = weight_copies(packed_ref, starts, hold_ref, sem_ref)
    for copy in copies:
        copy.start()
    for index, piece_ref in enumerate(pieces):
        size = piece_ref.shape[1]
        attended_ref[:, pl.ds(pl.multiple_of(place_ref[index] * size, size), size)] = piece_ref[...]
    spread_heads(keys_ref, key_wide, model)
    spread_heads(values_ref, value_wide, model)

    def adapted(moving_ref, index, store):
        latent = mm_nt(moving_ref[...], adapt_ref[32 * index : 32 * index + 16, :]).astype(BF)
        lat_ref[:, 16 * index : 16 * index + 16] = latent
        copies[index].wait()

        def some(cols):
            store(
                cols,
                mm(moving_ref[...], hold_ref[index, :, cols])
                + mm(latent, adapt_ref[32 * index + 16 : 32 * index + 32, cols]),
            )

        each(model, 512, some)

    def add_first(cols, value):
        resid1_ref[:, cols] = inputs_ref[:, cols].astype(F32) + value

    def add_second(cols, value):
        resid2_ref[:, cols] = resid1_ref[:, cols] + value

    def keep_query(cols, value):
        query_ref[:, cols] = value.astype(BF)

    def normed(values_at, into_ref, which):
        def some(part):
            into_ref[part, :] = layer_norm(
                values_at[part, :], gain_ref[which : which + 1, :], bias_ref[which : which + 1, :]
            ).astype(BF)

        each(rows, 64, some)

    def cross(lanes):
        score = mm_nt(key_wide[lanes, :], query_ref[:, lanes]) * SCALE
        raised = jnp.exp(score - head_total(score, keys, jnp.max))
        prob = (raised / head_total(raised, keys, jnp.sum)).astype(BF)
        probs_ref[lanes, :] = prob
        crossed_ref[:, lanes] = mm_tn(prob, value_wide[lanes, :]).astype(BF)

    adapted(attended_ref, 0, add_first)
    normed(resid1_ref, normed2_ref, 1)
    adapted(normed2_ref, 1, keep_query)
    each(model, wide, cross)
    adapted(crossed_ref, 2, add_second)
    normed(resid2_ref, normed3_ref, 2)


def middle(places, own, own_spec, others, inputs, at, packed, starts, adapters, gains, biases, keys, values):
    rows, model = own_spec[0], inputs.shape[1]
    spread = model // HEAD * keys.shape[0]
    shape = lambda kind, dims=(rows, model): jax.ShapeDtypeStruct(dims, kind)
    flat = lambda dims: pl.BlockSpec(dims, lambda _, ref: (0,) * len(dims))
    shapes = [shape(kind) for kind in (BF, F32, BF, BF)]
    shapes += [shape(BF, (spread, rows)), shape(BF), shape(F32), shape(BF), shape(BF, (rows, 48))]
    return pl.pallas_call(
        partial(middle_kernel, starts),
        grid_spec=pltpu.PrefetchScalarGridSpec(
            num_scalar_prefetch=1,
            grid=(1,),
            in_specs=[
                pl.BlockSpec(memory_space=pl.ANY),
                pl.BlockSpec((rows, model), lambda _, ref: (at, 0)),
            ]
            + [flat(item.shape) for item in (adapters, gains, biases, keys, values)]
            + [pl.BlockSpec(own_spec, lambda _, ref: (ref[2], 0))]
            + [flat(item.shape) for item in others],
            out_specs=[flat(item.shape) for item in shapes],
            scratch_shapes=[
                pltpu.VMEM((3, model, model), BF),
                pltpu.VMEM((spread, 4 * HEAD), BF),
                pltpu.VMEM((spread, 4 * HEAD), BF),
                pltpu.SemaphoreType.DMA((3,)),
            ],
        ),
        out_shape=shapes,
        compiler_params=params(),
        cost_estimate=cost(6 * rows * model * model, 6 * model * model + 24 * rows * model),
        name="middle",
    )(places, packed, inputs, adapters, gains, biases, keys, values, own, *others)


def middle_back_kernel(
    starts, split, place_ref, packed_ref, cot_ref, gu_ref, more_ref,
    attended_ref, resid1_ref, normed2_ref, query_ref, probs_ref, crossed_ref, resid2_ref, lat_ref,
    adapt_ref, gain_ref, keys_ref, values_ref, *refs,
):
    outs = refs[: 2 if split else 1]
    resid1_grad_ref, memory_ref, small_ref, hold_ref, key_wide, value_wide, work_ref, low_ref, sem_ref = refs[len(outs) :]
    rows, model = cot_ref.shape
    keys = keys_ref.shape[0]
    wide = 4 * HEAD
    copies = weight_copies(packed_ref, starts, hold_ref, sem_ref)
    for index in (2, 1, 0):
        copies[index].start()
    spread_heads(keys_ref, key_wide, model)
    spread_heads(values_ref, value_wide, model)

    def first(part):
        gradient = gu_ref[part, :].astype(F32) + more_ref[part, :].astype(F32)
        value = cot_ref[part, :].astype(F32) + norm_back(resid2_ref[part, :], gain_ref[2:3, :], gradient)
        resid1_grad_ref[part, :] = value
        low_ref[part, :] = value.astype(BF)

    def second(part):
        value = resid1_grad_ref[part, :] + norm_back(resid1_ref[part, :], gain_ref[1:2, :], work_ref[part, :])
        resid1_grad_ref[part, :] = value
        low_ref[part, :] = value.astype(BF)

    def back(moving_ref, index, store):
        down = slice(32 * index, 32 * index + 16)
        upper = slice(32 * index + 16, 32 * index + 32)
        glat = mm_nt(low_ref[...], adapt_ref[upper, :]).astype(BF)
        glat_t = glat.astype(F32).T.astype(BF)
        lat_t = lat_ref[:, 16 * index : 16 * index + 16].astype(F32).T.astype(BF)
        copies[index].wait()

        def some(cols):
            small_ref[down, cols] = mm(glat_t, moving_ref[:, cols])
            small_ref[upper, cols] = mm(lat_t, low_ref[:, cols])
            store(cols, mm_nt(low_ref[...], hold_ref[index, cols, :]) + mm(glat, adapt_ref[down, cols]))

        each(model, 512, some)

    def keep(cols, value):
        work_ref[:, cols] = value

    def cross(lanes):
        part = work_ref[:, lanes].astype(BF)
        prob = probs_ref[lanes, :]
        wide_prob = prob.astype(F32)
        weighted = wide_prob * mm_nt(value_wide[lanes, :], part)
        score_grad = (weighted - wide_prob * head_total(weighted, keys, jnp.sum)).astype(BF)
        low_ref[:, lanes] = (mm_tn(score_grad, key_wide[lanes, :]) * SCALE).astype(BF)
        key_full = mm(score_grad, query_ref[:, lanes])
        value_full = mm(prob, part)
        col = lax.broadcasted_iota(jnp.int32, (keys, wide), 1) // HEAD
        key_sum, value_sum = key_full[:keys], value_full[:keys]
        for head in range(1, 4):
            rows_at = slice(head * keys, (head + 1) * keys)
            key_sum = jnp.where(col == head, key_full[rows_at], key_sum)
            value_sum = jnp.where(col == head, value_full[rows_at], value_sum)
        memory_ref[0, :, lanes] = key_sum * SCALE
        memory_ref[1, :, lanes] = value_sum

    each(rows, 64, first)
    back(crossed_ref, 2, keep)
    each(model, wide, cross)
    back(normed2_ref, 1, keep)
    each(rows, 64, second)
    back(attended_ref, 0, keep)
    if split:
        size = outs[0].shape[1]
        for out_ref, index in zip(outs, range(2)):
            out_ref[...] = work_ref[:, pl.ds(pl.multiple_of(place_ref[index] * size, size), size)].astype(BF)
    else:
        outs[0][...] = work_ref[...].astype(BF)


def middle_back(places, parts, at, cotangent, gu, more, kept, packed, starts, adapters, gains, keys, values):
    model = cotangent.shape[1]
    rows = kept[0].shape[0]
    spread = model // HEAD * keys.shape[0]
    flat = lambda dims: pl.BlockSpec(dims, lambda _, ref: (0,) * len(dims))
    block = pl.BlockSpec((rows, model), lambda _, ref: (at, 0))
    more_spec = flat(more.shape) if more.shape[0] == rows else block
    shapes = [jax.ShapeDtypeStruct((rows, model // parts), BF)] * parts + [
        jax.ShapeDtypeStruct((rows, model), F32),
        jax.ShapeDtypeStruct((2,) + keys.shape, F32),
        jax.ShapeDtypeStruct(adapters.shape, F32),
    ]
    return pl.pallas_call(
        partial(middle_back_kernel, starts, parts == 2),
        grid_spec=pltpu.PrefetchScalarGridSpec(
            num_scalar_prefetch=1,
            grid=(1,),
            in_specs=[pl.BlockSpec(memory_space=pl.ANY), block, block, more_spec]
            + [flat(item.shape) for item in kept]
            + [flat(item.shape) for item in (adapters, gains, keys, values)],
            out_specs=[flat(item.shape) for item in shapes],
            scratch_shapes=[
                pltpu.VMEM((3, model, model), BF),
                pltpu.VMEM((spread, 4 * HEAD), BF),
                pltpu.VMEM((spread, 4 * HEAD), BF),
                pltpu.VMEM((rows, model), F32),
                pltpu.VMEM((rows, model), BF),
                pltpu.SemaphoreType.DMA((3,)),
            ],
        ),
        out_shape=shapes,
        compiler_params=params(),
        cost_estimate=cost(6 * rows * model * model, 6 * model * model + 36 * rows * model),
        name="middle_back",
    )(places, packed, cotangent, gu, more, *kept, adapters, gains, keys, values)


def qkv_grads_kernel(grad_ref, normed_ref, lat_ref, up_ref, glat_ref, gdown_ref, gup_ref, glat_acc, gup_acc):
    at = pl.program_id(0)
    gradient = grad_ref[...]
    rank = gup_ref.shape[0]
    gup_acc[...] = mm_tn(lat_ref[...], gradient)
    gup_ref[...] = gup_acc[pl.ds(pl.multiple_of(at * rank, rank), rank), :]

    @pl.when(at == 0)
    def _():
        glat_acc[...] = jnp.zeros_like(glat_acc)

    glat_acc[...] += mm_nt(gradient, up_ref[...])

    @pl.when(at == pl.num_programs(0) - 1)
    def _():
        low = glat_acc[...].astype(BF)
        glat_ref[...] = low
        gdown_ref[...] = mm_tn(low, normed_ref[...])


def qkv_grads(gradient, normed, latent, up):
    frames, model = normed.shape
    parts, ranks, width = up.shape
    rank = ranks // parts
    return pl.pallas_call(
        qkv_grads_kernel,
        grid=(parts,),
        in_specs=[
            pl.BlockSpec((None, frames, width), lambda at: (at, 0, 0)),
            whole(normed.shape),
            whole(latent.shape),
            pl.BlockSpec((None, ranks, width), lambda at: (at, 0, 0)),
        ],
        out_specs=[
            whole(latent.shape),
            whole((ranks, model)),
            pl.BlockSpec((None, rank, width), lambda at: (at, 0, 0)),
        ],
        out_shape=[
            jax.ShapeDtypeStruct(latent.shape, BF),
            jax.ShapeDtypeStruct((ranks, model), F32),
            jax.ShapeDtypeStruct((parts, rank, width), F32),
        ],
        scratch_shapes=[pltpu.VMEM(latent.shape, F32), pltpu.VMEM((ranks, width), F32)],
        compiler_params=params(),
        cost_estimate=cost(8 * frames * ranks * width * parts, 2 * frames * (model + parts * width)),
        name="qkv_grads",
    )(gradient, normed, latent, up)


def qkv_back_kernel(place_ref, grad_ref, glat_ref, down_ref, w_ref, gu_ref, gu_acc):
    at = pl.program_id(0)
    model = gu_ref.shape[1]
    last = pl.num_programs(0) - 1

    def some(cols):
        direct = mm_nt(grad_ref[...], w_ref[cols, :])

        @pl.when(at == 0)
        def _():
            gu_acc[:, cols] = direct + mm(glat_ref[...], down_ref[:, cols])

        @pl.when(jnp.logical_and(at > 0, at < last))
        def _():
            gu_acc[:, cols] += direct

        @pl.when(at == last)
        def _():
            gu_ref[:, cols] = (gu_acc[:, cols] + direct).astype(gu_ref.dtype)

    each(model, 512, some)


def qkv_back(place, row_count, gradient, glat, down, packed, start, kind):
    ranks, model = down.shape
    width = gradient.shape[2]
    if start % width == 0 and width % LANES == 0:
        weight, spec = packed, pl.BlockSpec((model, width), lambda at, ref: (0, start // width + at))
    else:
        weight = packed[:, start : start + 3 * width].reshape(model, 3, width).transpose(1, 0, 2)
        spec = pl.BlockSpec((None, model, width), lambda at, ref: (at, 0, 0))
    return pl.pallas_call(
        qkv_back_kernel,
        grid_spec=pltpu.PrefetchScalarGridSpec(
            num_scalar_prefetch=1,
            grid=(3,),
            in_specs=[
                pl.BlockSpec((None, row_count, width), lambda at, ref: (at, ref[0], 0)),
                pl.BlockSpec((row_count, ranks), lambda at, ref: (ref[0], 0)),
                pl.BlockSpec(down.shape, lambda at, ref: (0, 0)),
                spec,
            ],
            out_specs=pl.BlockSpec((row_count, model), lambda at, ref: (0, 0)),
            scratch_shapes=[pltpu.VMEM((row_count, model), F32)],
        ),
        out_shape=jax.ShapeDtypeStruct((row_count, model), kind),
        compiler_params=params(),
        cost_estimate=cost(6 * row_count * model * width, 6 * model * width + 8 * row_count * model),
        name="qkv_back",
    )(place, gradient, glat, down, weight)


def run_length(size):
    count = 1
    while count * size % LANES:
        count *= 2
    return count


def join_kernel(pieces_ref, flat_ref):
    count, _, size = pieces_ref.shape
    run = run_length(size)

    def some(at, carry):
        parts = [pieces_ref[at * run + index] for index in range(run)]
        into = pl.ds(pl.multiple_of(at * run * size, LANES), run * size)
        flat_ref[:, into] = jnp.concatenate(parts, 1)
        return carry

    lax.fori_loop(0, count // run, some, 0)


def join_pieces(pieces):
    count, rows, size = pieces.shape
    if count % run_length(size):
        return pieces.transpose(1, 0, 2).reshape(rows, count * size)
    return pl.pallas_call(
        join_kernel,
        out_shape=jax.ShapeDtypeStruct((rows, count * size), pieces.dtype),
        compiler_params=params(0),
        name="join_pieces",
    )(pieces)


def split_kernel(flat_ref, pieces_ref):
    count, _, size = pieces_ref.shape
    run = run_length(size)

    def some(at, carry):
        block = flat_ref[:, pl.ds(pl.multiple_of(at * run * size, LANES), run * size)]
        for index in range(run):
            pieces_ref[at * run + index] = block[:, index * size : (index + 1) * size]
        return carry

    lax.fori_loop(0, count // run, some, 0)


def split_pieces(flat, count):
    rows = flat.shape[0]
    size = flat.shape[1] // count
    if count % run_length(size):
        return flat.reshape(rows, count, size).transpose(1, 0, 2)
    return pl.pallas_call(
        split_kernel,
        out_shape=jax.ShapeDtypeStruct((count, rows, size), flat.dtype),
        compiler_params=params(0),
        name="split_pieces",
    )(flat)


def unit_loop(plan, work):
    fsdp, seq, folds, local = plan
    run = run_length(local)

    def some(at, carry):
        span = run * seq * folds * local
        block = pl.ds(pl.multiple_of(at * span, LANES), span)
        folded = [
            pl.ds(pl.multiple_of(fold * fsdp * local + at * run * local, LANES), run * local) for fold in range(folds)
        ]
        work(run, block, folded)
        return carry

    lax.fori_loop(0, fsdp // run, some, 0)


def take_units_kernel(plan, place_ref, all_ref, *refs):
    own_ref = refs[-1]
    _, seq, folds, local = plan
    spot = place_ref[0]

    def work(run, block, folded):
        values = all_ref[:, block]
        for fold, into in enumerate(folded):
            parts = []
            for index in range(run):
                base = (index * seq * folds + fold) * local
                part = values[:, base : base + local]
                for other in range(1, seq):
                    shift = base + other * folds * local
                    part = jnp.where(spot == other, values[:, shift : shift + local], part)
                parts.append(part)
            own_ref[:, into] = jnp.concatenate(parts, 1)

    unit_loop(plan, work)
    if len(refs) == 2:
        model = refs[0].shape[1]
        hidden = own_ref.shape[1] - folds * model
        for fold in range(folds):
            rows = pl.ds(pl.multiple_of((spot * folds + fold) * local, 16), local)
            own_ref[:, hidden + fold * model : hidden + (fold + 1) * model] = refs[0][rows, :]


def take_units(plan, places, matrix, low=None):
    _, seq, folds, local = plan
    rows, width = matrix.shape
    extra = [] if low is None else [low]
    out_width = width // seq + sum(folds * item.shape[1] for item in extra)
    return pl.pallas_call(
        partial(take_units_kernel, plan),
        in_specs=[smem()] + [pl.BlockSpec(memory_space=pltpu.VMEM)] * (1 + len(extra)),
        out_shape=jax.ShapeDtypeStruct((rows, out_width), matrix.dtype),
        compiler_params=params(0),
        name="take_units",
    )(places, matrix, *extra)


def place_units_kernel(plan, place_ref, own_ref, all_ref):
    _, seq, folds, local = plan
    spot = place_ref[0]

    def work(run, block, folded):
        values = [own_ref[:, into] for into in folded]
        parts = []
        for index in range(run):
            for other in range(seq):
                for fold in range(folds):
                    part = values[fold][:, index * local : (index + 1) * local]
                    parts.append(jnp.where(spot == other, part, 0.0))
        all_ref[:, block] = jnp.concatenate(parts, 1)

    unit_loop(plan, work)


def place_units(plan, places, matrix):
    rows, width = matrix.shape
    return pl.pallas_call(
        partial(place_units_kernel, plan),
        in_specs=[smem(), pl.BlockSpec(memory_space=pltpu.VMEM)],
        out_shape=jax.ShapeDtypeStruct((rows, width * plan[1]), matrix.dtype),
        compiler_params=params(0),
        name="place_units",
    )(places, matrix)


def body(
    inputs,
    text_states,
    adapter_index,
    norm_gains,
    norm_biases,
    self_in,
    self_out,
    cross_query,
    cross_text,
    cross_out,
    hidden_in,
    hidden_out,
    adapter_down,
    adapter_up,
    cotangent,
    *,
    sizes,
):
    seq, fsdp = sizes
    pair = seq == 2
    spot = lax.axis_index("seq")
    first_here = spot == 0
    there = (seq - 1) - spot
    local = self_in.shape[0]
    model = inputs.shape[2]
    rows = inputs.shape[1]
    frames = rows * seq
    wide = model // seq
    hidden_all = hidden_in.shape[1]
    hidden = hidden_all // seq
    adapters, rank, piece = adapter_down.shape
    total = piece * fsdp

    def swap(value):
        return lax.ppermute(value, "seq", [(0, 1), (1, 0)])

    def pick(value, axis, extent, which=None):
        return lax.dynamic_slice_in_dim(value, (spot if which is None else which) * extent, extent, axis)

    def ordered(mine, other):
        return jnp.where(first_here, mine, other), jnp.where(first_here, other, mine)

    def gather(value, axis):
        if pair:
            return jnp.concatenate(ordered(value, swap(value)), axis)
        return lax.all_gather(value, "seq", axis=axis, tiled=True)

    def after(value, *others):
        return lax.optimization_barrier((value,) + others)[0]

    def put(value, axis):
        shape = list(value.shape)
        shape[axis] = seq
        return lax.dynamic_update_slice_in_dim(jnp.zeros(shape, value.dtype), value, spot, axis)

    def own_columns(matrix, parts):
        return [pick(matrix[:, at * model : (at + 1) * model], 1, wide) for at in range(parts)]

    first = jnp.concatenate(
        [self_out, cross_query, cross_out] + own_columns(self_in, 3) + own_columns(cross_text, 2), 1
    )
    starts = (0, model, 2 * model)
    start_in, start_text = 3 * model, 3 * model + 3 * wide
    packed = lax.all_gather(first, "fsdp", axis=0, tiled=True)
    depth = hidden_out.shape[0] // seq
    merged = depth % local == 0 and fsdp % run_length(local) == 0
    where_here = jnp.stack([spot, there]).astype(jnp.int32)
    if merged:
        folds = depth // local
        plan = (fsdp, seq, folds, local)
        own_units = partial(take_units, plan, where_here)
        all_units = partial(place_units, plan, where_here)
        packed_feed = lax.all_gather(own_units(hidden_in, hidden_out), "fsdp", axis=0, tiled=True)

        def feed_weights(block):
            per = model // block
            return (
                packed_feed,
                pl.BlockSpec((model, block), lambda at: (0, at)),
                packed_feed,
                pl.BlockSpec((block, model), lambda at: (at % per, folds + at // per)),
            )
    else:

        def own_units(matrix):
            kept = lax.dynamic_index_in_dim(matrix.reshape(-1, fsdp, seq, depth), spot, 2, False)
            return kept.reshape(-1, hidden)

        def all_units(matrix):
            return put(matrix.reshape(-1, fsdp, 1, depth), 2).reshape(-1, hidden_all)

        whole_in = lax.all_gather(own_units(hidden_in), "fsdp", axis=0, tiled=True)
        whole_out = lax.all_gather(pick(hidden_out, 0, depth), "fsdp", axis=0, tiled=True)

        def feed_weights(block):
            return (
                whole_in,
                pl.BlockSpec((model, block), lambda at: (0, at)),
                whole_out,
                pl.BlockSpec((block, model), lambda at: (at, 0)),
            )

    index_all = lax.all_to_all(jnp.broadcast_to(adapter_index, (fsdp,)), "fsdp", 0, 0, tiled=True)
    if pair:
        table = jnp.where(first_here, adapter_down, adapter_up)
        mine = join_pieces(lax.all_to_all(jnp.take(table, index_all, axis=0), "fsdp", 0, 0, tiled=True))
        down_all, upper_all = ordered(mine, swap(mine))
    else:
        table = jnp.concatenate([adapter_down, adapter_up], 1)
        chosen = join_pieces(lax.all_to_all(jnp.take(table, index_all, axis=0), "fsdp", 0, 0, tiled=True))
        down_all, upper_all = chosen[:rank], chosen[rank:]
    in_cuts = [0, 3 * model, 4 * model, 5 * model, 7 * model, 8 * model, 9 * model, 9 * model + hidden_all]
    out_cuts = [0, 3 * model, 4 * model, 5 * model, 7 * model, 8 * model, 8 * model + hidden_all, 9 * model + hidden_all]
    downs = [down_all[:, in_cuts[at] : in_cuts[at + 1]] for at in range(7)]
    uppers = [upper_all[:, out_cuts[at] : out_cuts[at + 1]] for at in range(7)]

    def part_down(matrix, parts):
        return jnp.concatenate([matrix[:, at * model : (at + 1) * model] for at in range(parts)], 0)

    def part_upper(matrix, parts):
        own = own_columns(matrix, parts)
        return jnp.stack(
            [jnp.pad(item, ((at * rank, (parts - 1 - at) * rank), (0, 0))) for at, item in enumerate(own)], 0
        )

    units = own_units(jnp.concatenate([uppers[5], downs[6]], 0))
    feed_adapters = (downs[5], units[:rank], units[rank:], uppers[6])
    square_adapters = jnp.concatenate([downs[1], uppers[1], downs[2], uppers[2], downs[4], uppers[4]], 0)
    down_qkv, upper_qkv = part_down(downs[0], 3), part_upper(uppers[0], 3)
    down_text, upper_text = part_down(downs[3], 2), part_upper(uppers[3], 2)
    flat_text = jnp.concatenate([upper_text[0], upper_text[1]], 1)

    frames_in = inputs[0]
    cot = cotangent[0]
    if pair:
        frames_parts = [frames_in, swap(frames_in)]
        cot_other = swap(after(cot, frames_parts[1]))
    else:
        frames_parts = [lax.all_gather(frames_in, "seq", axis=0, tiled=True)]
    norm_places = where_here if pair else jnp.zeros((1,), jnp.int32)
    normed1, lat_qkv = norm_project(norm_places, frames_parts, norm_gains[0:1], norm_biases[0:1], down_qkv)
    triple = qkv_project(normed1, lat_qkv, upper_qkv, packed, start_in, 3 * wide)
    padded = -(-wide // LANES) * LANES
    if padded != wide:
        triple = jnp.pad(triple.reshape(frames, 3, wide), ((0, 0), (0, 0), (0, padded - wide)))
        triple = triple.reshape(frames, 3 * padded)
    head_out, probs = attend(triple, padded)

    text = text_states[0]
    w_text = packed[:, start_text : start_text + 2 * wide]
    lat_text = mm_nt(text, down_text).astype(BF)
    memory = (mm(text, w_text) + mm(lat_text, flat_text)).astype(BF)
    memory_all = gather(memory.reshape(-1, 2, wide), 2)
    keys, values = memory_all[:, 0], memory_all[:, 1]

    blocks = max(rows // 256, 1)
    size = rows // blocks
    constants = (packed, starts, square_adapters, norm_gains, norm_biases, keys, values)
    if pair:
        received = [swap(lax.dynamic_slice_in_dim(head_out, there * rows + at * size, size, 0)) for at in range(blocks)]
    else:
        natural = lax.all_to_all(head_out[:, :wide], "seq", split_axis=0, concat_axis=1, tiled=True)
    made = []
    for at in range(blocks):
        if pair:
            places = jnp.stack([spot, there, spot * blocks + at]).astype(jnp.int32)
            own, spec, others = head_out, (size, wide), [received[at]]
        else:
            places = jnp.array([0, 0, at], jnp.int32)
            own, spec, others = natural, (size, model), []
        made.append(middle(places, own, spec, others, frames_in, at, *constants))
    normed3 = jnp.concatenate([item[7] for item in made], 0)
    resid2 = jnp.concatenate([item[6] for item in made], 0)

    if pair:
        normed3_other = jnp.concatenate([swap(item[7]) for item in made], 0)
        theirs = feed_forward(normed3_other, cot_other, *feed_adapters, feed_weights, hidden, BF)
        ours = feed_forward(after(normed3, theirs[1]), cot, *feed_adapters, feed_weights, hidden, F32)
        gu_more = swap(theirs[1])
        out_more = swap(after(theirs[0], gu_more))
        output = (resid2 + ours[0] + out_more.astype(F32)).astype(BF)
        gu = ours[1]
        feed_grads = [one + two for one, two in zip(ours[2:], theirs[2:])]
    else:
        all_out = feed_forward(gather(normed3, 0), gather(cot, 0), *feed_adapters, feed_weights, hidden, F32)
        summed = [
            lax.psum_scatter(item.astype(BF), "seq", scatter_dimension=0, tiled=True) for item in all_out[:2]
        ]
        output = (resid2 + summed[0].astype(F32)).astype(BF)
        gu, gu_more = summed[1].astype(F32), jnp.zeros_like(summed[1])
        feed_grads = all_out[2:]
    gdown_in, gup_in, gdown_out, gup_out = feed_grads

    pieces, resid1_grads, memory_parts, square_parts = [], [], [], []
    gu_here = gu
    for at in range(blocks):
        kept = made[at][:7] + made[at][8:9]
        result = middle_back(
            where_here, 2 if pair else 1, at, cot, gu_here, gu_more, kept, packed, starts, square_adapters, norm_gains,
            keys, values,
        )
        gu_here = after(gu, result[-3])
        if pair:
            pieces.append((result[0], swap(result[1])))
        else:
            pieces.append(result[0])
        resid1_grads.append(result[-3])
        memory_parts.append(result[-2])
        square_parts.append(result[-1])
    resid1_grad = jnp.concatenate(resid1_grads, 0)
    memory_part = sum(memory_parts[1:], memory_parts[0]).astype(BF)
    square_grads = sum(square_parts[1:], square_parts[0])

    if pair:
        grad_pieces = [item[0] for item in pieces] + [item[1] for item in pieces]
        spots = [spot * blocks + at for at in range(blocks)] + [there * blocks + at for at in range(blocks)]
        grad_places = jnp.stack(spots).astype(jnp.int32)
    else:
        head_grad = lax.all_to_all(jnp.concatenate(pieces, 0), "seq", split_axis=1, concat_axis=0, tiled=True)
        grad_pieces = [jnp.pad(head_grad, ((0, 0), (0, padded - wide)))]
        grad_places = jnp.zeros((1,), jnp.int32)
    triple_grad = attend_back(grad_places, triple, head_out, grad_pieces, probs, padded)[:, :, :wide]
    glat_qkv, gdown_qkv, gup_qkv = qkv_grads(triple_grad, normed1, lat_qkv, upper_qkv)
    back = partial(
        qkv_back, gradient=triple_grad, glat=glat_qkv, down=down_qkv, packed=packed, start=start_in,
    )
    if pair:
        for_them = back(there[None], rows, kind=BF)
        for_us = back(after(spot, for_them)[None], rows, kind=F32)
        normed1_grad = for_us + swap(for_them).astype(F32)
    else:
        full = back(jnp.zeros((1,), jnp.int32), frames, kind=BF)
        normed1_grad = lax.psum_scatter(full, "seq", scatter_dimension=0, tiled=True).astype(F32)
    input_grad = resid1_grad + norm_back(frames_in.astype(F32), norm_gains[0:1], normed1_grad)

    if pair:
        other_part = pick(memory_part, 2, wide, there)
        memory_grad = (pick(memory_part, 2, wide).astype(F32) + swap(other_part).astype(F32)).astype(BF)
    else:
        memory_grad = lax.psum_scatter(memory_part, "seq", scatter_dimension=2, tiled=True)
    memory_flat = jnp.concatenate([memory_grad[0], memory_grad[1]], 1)
    glat_text = mm_nt(memory_flat, flat_text).astype(BF)
    gup_text = mm_tn(lat_text, memory_flat)
    gdown_text = mm_tn(glat_text, text)
    text_grad = mm_nt(memory_flat, w_text) + mm(glat_text, down_text)

    def flat_down(grads, parts):
        return jnp.concatenate([grads[at * rank : (at + 1) * rank] for at in range(parts)], 1)

    def flat_upper(own):
        return put(jnp.stack(own, 1)[:, :, None], 2).reshape(rank, len(own) * model)

    own_text = [gup_text[at * rank : (at + 1) * rank, at * wide : (at + 1) * wide] for at in range(2)]
    squares = [square_grads[rank * at : rank * (at + 1)] for at in range(6)]
    unit_grads = all_units(jnp.concatenate([gup_in, gdown_out], 0))
    down_early = jnp.concatenate(
        [squares[0], squares[2], flat_down(gdown_text, 2), squares[4], gdown_in, unit_grads[rank:]], 1
    ).astype(BF)
    upper_early = jnp.concatenate(
        [squares[1], squares[3], flat_upper(own_text), squares[5], unit_grads[:rank], gup_out], 1
    ).astype(BF)
    down_late = flat_down(gdown_qkv, 3).astype(BF)
    upper_late = flat_upper([gup_qkv[at] for at in range(3)]).astype(BF)
    selector = (index_all[None, :] == jnp.arange(adapters, dtype=jnp.int32)[:, None]).astype(BF)

    def by_adapter(sent):
        received = lax.all_to_all(split_pieces(sent, fsdp), "fsdp", 0, 0, tiled=True)
        return jnp.einsum("ac,crw->arw", selector, received, preferred_element_type=F32)

    text_low = text_grad.astype(BF)
    if pair:

        def halves(down, upper):
            mine, theirs = ordered(down, upper)
            return (mine.astype(F32) + swap(theirs).astype(F32)).astype(BF)

        early = halves(down_early, upper_early)
        late = halves(down_late, upper_late)
        shares = by_adapter(jnp.concatenate([late, early], 1)).astype(BF)
        grad_down, grad_up = ordered(shares, swap(shares))
        text_total = text_low.astype(F32) + swap(text_low).astype(F32)
    else:
        down_sent = jnp.concatenate([down_late, down_early], 1)
        upper_sent = jnp.concatenate([upper_late, upper_early], 1)
        shares = by_adapter(jnp.concatenate([down_sent, upper_sent], 0))
        shares = lax.psum(shares.astype(BF), "seq")
        grad_down, grad_up = shares[:, :rank], shares[:, rank:]
        text_total = lax.psum(text_low, "seq").astype(F32)
    return (output[None], input_grad[None], text_total[None], grad_down.astype(F32), grad_up.astype(F32))


def solution(mesh):
    return jax.shard_map(
        partial(body, sizes=(mesh.shape["seq"], mesh.shape["fsdp"])),
        mesh=mesh,
        in_specs=(
            P("fsdp", "seq", None),
            P("fsdp", None, None),
            P("fsdp"),
            P(),
            P(),
            P("fsdp", None),
            P("fsdp", None),
            P("fsdp", None),
            P("fsdp", None),
            P("fsdp", None),
            P("fsdp", None),
            P("fsdp", None),
            P(None, None, "fsdp"),
            P(None, None, "fsdp"),
            P("fsdp", "seq", None),
        ),
        out_specs=(
            P("fsdp", "seq", None),
            P("fsdp", "seq", None),
            P("fsdp", None, None),
            P(None, None, "fsdp"),
            P(None, None, "fsdp"),
        ),
        check_vma=False,
    )
```

```python
from functools import partial

import jax
import jax.numpy as jnp
from jax import lax
from jax.experimental import pallas as pl
from jax.experimental.pallas import tpu as pltpu
from jax.sharding import PartitionSpec as P

HEAD = 64
LANES = 128
QB = 256
BF = jnp.bfloat16
F32 = jnp.float32
SCALE = float(HEAD) ** (-0.5)
SQRT_HALF = 0.7071067811865476
INV_SQRT_2PI = 0.3989422804014327
VMEM_LIMIT = 60 * 1024 * 1024
COST = 1.0


def mm(a, b):
    return lax.dot_general(a, b, (((1,), (0,)), ((), ())), preferred_element_type=F32)


def mm_nt(a, b):
    return lax.dot_general(a, b, (((1,), (1,)), ((), ())), preferred_element_type=F32)


def mm_tn(a, b):
    return lax.dot_general(a, b, (((0,), (0,)), ((), ())), preferred_element_type=F32)


def norm_stats(values):
    centered = values - jnp.mean(values, -1, keepdims=True)
    variance = jnp.mean(centered * centered, -1, keepdims=True)
    inverse = lax.rsqrt(variance + 1e-05)
    return centered * inverse, inverse


def layer_norm(values, gains, biases):
    unit, _ = norm_stats(values)
    return unit * gains + biases


def norm_back(values, gains, gradient):
    unit, inverse = norm_stats(values)
    scaled = gradient * gains
    mean_one = jnp.mean(scaled, -1, keepdims=True)
    mean_two = jnp.mean(scaled * unit, -1, keepdims=True)
    return inverse * (scaled - mean_one - unit * mean_two)


def whole(shape):
    return pl.BlockSpec(shape, lambda *_: (0,) * len(shape))


def once(shape):
    return pl.BlockSpec(shape, lambda *_: (0,) * len(shape), pipeline_mode=pl.Buffered(1))


def params(count=1):
    return pltpu.CompilerParams(
        dimension_semantics=("arbitrary",) * count if count else None, vmem_limit_bytes=VMEM_LIMIT
    )


def cost(flops, moved, special=0):
    return pl.CostEstimate(
        flops=int(flops * COST), bytes_accessed=int(moved * COST), transcendentals=int(special * COST)
    )


def window(packed, start, width, rows=None, steps=1, step=0):
    block = width // steps
    rows = packed.shape[0] if rows is None else rows
    if start % block == 0 and block % LANES == 0:
        base = start // block
        return packed, pl.BlockSpec((rows, block), lambda *at: (0, base + (at[step] if steps > 1 else 0)))
    return packed[:, start : start + width], pl.BlockSpec(
        (rows, block), lambda *at: (0, at[step] if steps > 1 else 0)
    )


def norm_kernel(place_ref, *refs):
    count = len(refs) - 5
    parts, (gain_ref, bias_ref, down_ref, normed_ref, lat_ref) = refs[:count], refs[count:]
    step = 128
    for index, part_ref in enumerate(parts):
        base = place_ref[index] * part_ref.shape[0]

        def some(at, carry):
            rows = pl.ds(pl.multiple_of(at * step, step), step)
            into = pl.ds(pl.multiple_of(base + at * step, step), step)
            normed = layer_norm(part_ref[rows, :].astype(F32), gain_ref[...], bias_ref[...]).astype(BF)
            normed_ref[into, :] = normed
            lat_ref[into, :] = mm_nt(normed, down_ref[...]).astype(BF)
            return carry

        lax.fori_loop(0, part_ref.shape[0] // step, some, 0)


def smem():
    return pl.BlockSpec(memory_space=pltpu.SMEM)


def norm_project(places, parts, gains, biases, down):
    model = parts[0].shape[1]
    frames = sum(part.shape[0] for part in parts)
    ranks = down.shape[0]
    return pl.pallas_call(
        norm_kernel,
        in_specs=[smem()] + [whole(item.shape) for item in parts + [gains, biases, down]],
        out_specs=[whole((frames, model)), whole((frames, ranks))],
        out_shape=[jax.ShapeDtypeStruct((frames, model), BF), jax.ShapeDtypeStruct((frames, ranks), BF)],
        grid=(1,),
        compiler_params=params(),
        cost_estimate=cost(2 * frames * model * ranks, 4 * frames * model),
        name="norm_project",
    )(places, *parts, gains, biases, down)


def qkv_kernel(normed_ref, lat_ref, up_ref, w_ref, out_ref):
    step = 256

    def some(at, carry):
        rows = pl.ds(pl.multiple_of(at * step, step), step)
        out_ref[rows, :] = (mm(normed_ref[rows, :], w_ref[...]) + mm(lat_ref[rows, :], up_ref[...])).astype(BF)
        return carry

    lax.fori_loop(0, normed_ref.shape[0] // step, some, 0)


def qkv_project(normed, latent, up, packed, start, width):
    row_count, model = normed.shape
    ranks = latent.shape[1]
    steps = 3 if (width // 3) % LANES == 0 else 1
    operand, spec = window(packed, start, width, steps=steps)
    block = width // steps
    if steps == 3:
        up_spec = pl.BlockSpec((None, ranks, block), lambda at: (at, 0, 0))
    else:
        up = up.transpose(1, 0, 2).reshape(ranks, width)
        up_spec = whole(up.shape)
    return pl.pallas_call(
        qkv_kernel,
        grid=(steps,),
        in_specs=[whole(normed.shape), whole(latent.shape), up_spec, spec],
        out_specs=pl.BlockSpec((row_count, block), lambda at: (0, at)),
        out_shape=jax.ShapeDtypeStruct((row_count, width), BF),
        compiler_params=params(),
        cost_estimate=cost(2 * row_count * model * width, 2 * (row_count + width) * model),
        name="qkv_project",
    )(normed, latent, up, operand)


def tri_start(at):
    return QB * at * (at + 1) // 2


def attend_kernel(place_ref, q_ref, k_ref, v_ref, out_ref, prob_ref, *refs):
    sent, (val_t_ref, out_t_ref) = refs[:-2], refs[-2:]
    frames = q_ref.shape[0]
    lane = lax.broadcasted_iota(jnp.int32, (1, LANES), 1) // HEAD
    val_t_ref[...] = v_ref[...].T
    square = (QB, QB)
    keep_tri = lax.broadcasted_iota(jnp.int32, square, 0) <= lax.broadcasted_iota(jnp.int32, square, 1)
    for half in range(2):
        keep = lane == half
        for at in range(frames // QB):
            stop = (at + 1) * QB
            query = q_ref[at * QB : stop, :] * jnp.where(keep, SCALE, 0.0).astype(BF)
            score = jnp.where(keep_tri, mm_nt(k_ref[stop - QB : stop, :], query), -1e30)
            if at:
                score = jnp.concatenate([mm_nt(k_ref[0 : stop - QB, :], query), score], 0)
            raised = jnp.exp(score - jnp.max(score, 0, keepdims=True))
            prob = (raised * (1.0 / jnp.sum(raised, 0, keepdims=True))).astype(BF)
            prob_ref[half, tri_start(at) : tri_start(at) + stop, :] = prob
            mixed = mm(val_t_ref[half * HEAD : (half + 1) * HEAD, 0:stop], prob)
            out_t_ref[half * HEAD : (half + 1) * HEAD, at * QB : stop] = mixed
    out_ref[...] = out_t_ref[...].T.astype(BF)
    for index, sent_ref in enumerate(sent):
        size = sent_ref.shape[0]
        at = place_ref[1] * len(sent) + index
        sent_ref[...] = out_ref[pl.ds(pl.multiple_of(at * size, size), size), :]


def pair_specs(frames, width):
    pairs = width // LANES
    return [pl.BlockSpec((frames, LANES), lambda at, part=part: (0, part * pairs + at)) for part in range(3)]


def attend(places, sizes, triple, width):
    frames = triple.shape[0]
    pairs = width // LANES
    tri = tri_start(frames // QB)
    return pl.pallas_call(
        attend_kernel,
        grid=(pairs,),
        in_specs=[smem()] + pair_specs(frames, width),
        out_specs=[
            pl.BlockSpec((frames, LANES), lambda at: (0, at)),
            pl.BlockSpec((2, tri, QB), lambda at: (at, 0, 0)),
        ]
        + [pl.BlockSpec((size, LANES), lambda at: (0, at)) for size in sizes],
        out_shape=[
            jax.ShapeDtypeStruct((frames, width), BF),
            jax.ShapeDtypeStruct((2 * pairs, tri, QB), BF),
        ]
        + [jax.ShapeDtypeStruct((size, width), BF) for size in sizes],
        scratch_shapes=[pltpu.VMEM((LANES, frames), BF), pltpu.VMEM((LANES, frames), F32)],
        compiler_params=params(),
        cost_estimate=cost(
            8 * tri * QB * HEAD * pairs, 2 * (4 * frames * width + 2 * pairs * tri * QB), 2 * pairs * tri * QB
        ),
        name="attend",
    )(places, triple, triple, triple)


def attend_back_kernel(place_ref, q_ref, k_ref, v_ref, out_ref, prob_ref, *refs):
    pieces, (back_ref, grad_ref, key_t_ref, dq_t_ref, dk_acc, dv_acc) = refs[:-6], refs[-6:]
    frames = q_ref.shape[0]
    for index, piece_ref in enumerate(pieces):
        size = piece_ref.shape[0]
        count = max(len(pieces) // 2, 1)
        at = place_ref[index // count] * count + index % count if len(pieces) > 1 else 0
        grad_ref[pl.ds(pl.multiple_of(at * size, size), size), :] = piece_ref[...]
    lane = lax.broadcasted_iota(jnp.int32, (1, LANES), 1) // HEAD
    key_t_ref[...] = k_ref[...].T
    dk_acc[...] = jnp.zeros_like(dk_acc)
    dv_acc[...] = jnp.zeros_like(dv_acc)
    for at in range(frames // QB):
        stop = (at + 1) * QB
        rows = slice(at * QB, stop)
        product = (out_ref[rows, :].astype(F32) * grad_ref[rows, :].astype(F32)).T
        for half in range(2):
            keep = lane == half
            mask = jnp.where(keep, 1.0, 0.0).astype(BF)
            query = q_ref[rows, :] * jnp.where(keep, SCALE, 0.0).astype(BF)
            grad = grad_ref[rows, :] * mask
            delta = jnp.sum(product[half * HEAD : (half + 1) * HEAD, :], 0, keepdims=True)
            prob = prob_ref[half, tri_start(at) : tri_start(at) + stop, :]
            prob_grad = mm_nt(v_ref[0:stop, :], grad)
            score_grad = (prob.astype(F32) * (prob_grad - delta)).astype(BF)
            dv_acc[0:stop, :] += mm(prob, grad)
            dk_acc[0:stop, :] += mm(score_grad, query)
            dq_t_ref[half * HEAD : (half + 1) * HEAD, rows] = mm(
                key_t_ref[half * HEAD : (half + 1) * HEAD, 0:stop], score_grad
            )
    back_ref[0] = (dq_t_ref[...].T * SCALE).astype(BF)
    back_ref[1] = dk_acc[...].astype(BF)
    back_ref[2] = dv_acc[...].astype(BF)


def attend_back(places, triple, attended, pieces, probs, width):
    frames = triple.shape[0]
    pairs = width // LANES
    tri = tri_start(frames // QB)
    column = pl.BlockSpec((frames, LANES), lambda at: (0, at))
    return pl.pallas_call(
        attend_back_kernel,
        grid=(pairs,),
        in_specs=[smem()]
        + pair_specs(frames, width)
        + [column, pl.BlockSpec((2, tri, QB), lambda at: (at, 0, 0))]
        + [pl.BlockSpec((piece.shape[0], LANES), lambda at: (0, at)) for piece in pieces],
        out_specs=pl.BlockSpec((3, frames, LANES), lambda at: (0, 0, at)),
        out_shape=jax.ShapeDtypeStruct((3, frames, width), BF),
        scratch_shapes=[
            pltpu.VMEM((frames, LANES), BF),
            pltpu.VMEM((LANES, frames), BF),
            pltpu.VMEM((LANES, frames), F32),
            pltpu.VMEM((frames, LANES), F32),
            pltpu.VMEM((frames, LANES), F32),
        ],
        compiler_params=params(),
        cost_estimate=cost(16 * tri * QB * HEAD * pairs, 2 * (8 * frames * width + 2 * pairs * tri * QB)),
        name="attend_back",
    )(places, triple, triple, triple, attended, probs, *pieces)


def feed_kernel(count, based, *refs):
    pieces, refs = refs[:count], refs[count:]
    bases, refs = refs[:based], refs[based:]
    cot_ref, down_in_ref, up_in_ref, down_out_ref, up_out_ref, w_in_ref, w_out_ref = refs[:7]
    out_refs, gu_refs, refs = refs[7 : 7 + count], refs[7 + count : 7 + 2 * count], refs[7 + 2 * count :]
    (
        gdown_in_ref, gup_in_ref, gdown_out_ref, gup_out_ref, normed_ref,
        out_acc, gu_acc, lat_in, glat_out, lat_acc, glat_acc, lat_t, glat_t,
    ) = refs
    at = pl.program_id(0)

    @pl.when(at == 0)
    def _():
        start = 0
        for piece_ref in pieces:
            normed_ref[start : start + piece_ref.shape[0], :] = piece_ref[...]
            start += piece_ref.shape[0]
        latent = mm_nt(normed_ref[...], down_in_ref[...]).astype(BF)
        glat = mm_nt(cot_ref[...], up_out_ref[...]).astype(BF)
        lat_in[...] = latent
        glat_out[...] = glat
        lat_t[...] = latent.astype(F32).T.astype(BF)
        glat_t[...] = glat.astype(F32).T.astype(BF)
        start = 0
        for base_ref in bases:
            out_acc[start : start + base_ref.shape[0], :] = base_ref[...]
            start += base_ref.shape[0]
        if not bases:
            out_acc[...] = jnp.zeros_like(out_acc)
        gu_acc[...] = jnp.zeros_like(gu_acc)
        lat_acc[...] = jnp.zeros_like(lat_acc)
        glat_acc[...] = jnp.zeros_like(glat_acc)

    w_in = w_in_ref[...]
    w_out = w_out_ref[...]
    pre = mm(normed_ref[...], w_in) + mm(lat_in[...], up_in_ref[...])
    act_grad = mm_nt(cot_ref[...], w_out) + mm(glat_out[...], down_out_ref[...])
    cdf = 0.5 * (1.0 + lax.erf(pre * SQRT_HALF))
    slope = cdf + pre * (jnp.exp(-0.5 * pre * pre) * INV_SQRT_2PI)
    act = (pre * cdf).astype(BF)
    pre_grad = (act_grad * slope).astype(BF)
    out_acc[...] += mm(act, w_out)
    gu_acc[...] += mm_nt(pre_grad, w_in)
    lat_acc[...] += mm_nt(act, down_out_ref[...])
    glat_acc[...] += mm_nt(pre_grad, up_in_ref[...])
    gup_in_ref[...] = mm(lat_t[...], pre_grad)
    gdown_out_ref[...] = mm(glat_t[...], act)

    @pl.when(at == pl.num_programs(0) - 1)
    def _():
        latent = lat_acc[...].astype(BF)
        glat = glat_acc[...].astype(BF)
        start = 0
        for out_ref, gu_ref in zip(out_refs, gu_refs):
            rows = slice(start, start + out_ref.shape[0])
            out_ref[...] = (out_acc[rows, :] + mm(latent[rows], up_out_ref[...])).astype(out_ref.dtype)
            gu_ref[...] = (gu_acc[rows, :] + mm(glat[rows], down_in_ref[...])).astype(gu_ref.dtype)
            start += out_ref.shape[0]
        gup_out_ref[...] = mm(latent.astype(F32).T.astype(BF), cot_ref[...])
        gdown_in_ref[...] = mm(glat.astype(F32).T.astype(BF), normed_ref[...])


def feed_forward(pieces, bases, cotangent, block_at, down_in, up_in, down_out, up_out, weights, hidden, kind):
    model = cotangent.shape[1]
    row_count = sum(item.shape[0] for item in pieces)
    rank = down_in.shape[0]
    block = 512 if hidden % 512 == 0 else (256 if hidden % 256 == 0 else hidden)
    w_in, in_spec, w_out, out_spec = weights(block)
    main = pl.BlockSpec((row_count, model), lambda at: (block_at, 0))
    slim = pl.BlockSpec((rank, block), lambda at: (0, at))
    small = whole((rank, model))
    return pl.pallas_call(
        partial(feed_kernel, len(pieces), len(bases)),
        grid=(hidden // block,),
        in_specs=[once(item.shape) for item in pieces + bases]
        + [main, small, slim, slim, small, in_spec, out_spec],
        out_specs=[whole(item.shape) for item in pieces] * 2 + [small, slim, slim, small],
        out_shape=[jax.ShapeDtypeStruct(item.shape, kind) for item in pieces]
        + [jax.ShapeDtypeStruct(item.shape, BF) for item in pieces]
        + [
            jax.ShapeDtypeStruct((rank, model), F32),
            jax.ShapeDtypeStruct((rank, hidden), F32),
            jax.ShapeDtypeStruct((rank, hidden), F32),
            jax.ShapeDtypeStruct((rank, model), F32),
        ],
        scratch_shapes=[pltpu.VMEM((row_count, model), BF)]
        + [pltpu.VMEM((row_count, model), F32)] * 2
        + [pltpu.VMEM((row_count, rank), BF)] * 2
        + [pltpu.VMEM((row_count, rank), F32)] * 2
        + [pltpu.VMEM((rank, row_count), BF)] * 2,
        compiler_params=params(),
        cost_estimate=cost(8 * row_count * model * hidden, 4 * hidden * model, 2 * row_count * hidden),
        name="feed_forward",
    )(*pieces, *bases, cotangent, down_in, up_in, down_out, up_out, w_in, w_out)


def spread_heads(rows_ref, into_ref, model):
    keys = rows_ref.shape[0]
    wide = 4 * HEAD
    row = lax.broadcasted_iota(jnp.int32, (4 * keys, wide), 0) // keys
    col = lax.broadcasted_iota(jnp.int32, (4 * keys, wide), 1) // HEAD
    mask = jnp.where(row == col, 1.0, 0.0).astype(BF)

    def some(group, carry):
        part = rows_ref[:, pl.ds(pl.multiple_of(group * wide, wide), wide)]
        into = pl.ds(pl.multiple_of(group * 4 * keys, 4 * keys), 4 * keys)
        into_ref[into, :] = jnp.concatenate([part] * 4, 0) * mask
        return carry

    lax.fori_loop(0, model // wide, some, 0)


def head_total(values, keys, reduce):
    split = values.reshape(4, keys, values.shape[1])
    return jnp.broadcast_to(reduce(split, 1, keepdims=True), split.shape).reshape(values.shape)


def each(count, step, work):
    def some(at, carry):
        work(pl.ds(pl.multiple_of(at * step, step), step))
        return carry

    lax.fori_loop(0, count // step, some, 0)


def weight_copies(plan, place_ref, sources, hold_ref, sem_ref):
    model = hold_ref.shape[1]
    groups = []
    for index, (start, extra) in enumerate(plan):
        if extra is None:
            pairs = [(sources[0].at[:, pl.ds(start, model)], hold_ref.at[index])]
        else:
            half = model // 2
            here, there = [pl.ds(pl.multiple_of(place_ref[at] * half, half), half) for at in range(2)]
            pairs = [(sources[0].at[:, pl.ds(start, half)], hold_ref.at[index, :, here])]
            for at in range(2):
                rows = pl.ds(pl.multiple_of(place_ref[2 + at] * half, half), half)
                pairs.append((sources[extra + at], hold_ref.at[index, rows, there]))
        groups.append(
            [pltpu.make_async_copy(src, dst, sem_ref.at[index, at]) for at, (src, dst) in enumerate(pairs)]
        )
    return groups


def source_count(plan):
    return 1 + 2 * sum(extra is not None for _, extra in plan)


def start_all(copies):
    for copy in copies:
        copy.start()


def wait_all(copies):
    for copy in copies:
        copy.wait()


def middle_kernel(plan, place_ref, *refs):
    sources, refs = refs[: source_count(plan)], refs[source_count(plan) :]
    inputs_ref, adapt_ref, gain_ref, bias_ref, keys_ref, values_ref = refs[:6]
    pieces = refs[6:-13]
    (
        attended_ref, resid1_ref, normed2_ref, query_ref, probs_ref, crossed_ref, resid2_ref, normed3_ref, lat_ref,
        hold_ref, key_wide, value_wide, sem_ref,
    ) = refs[-13:]
    model = inputs_ref.shape[1]
    keys = keys_ref.shape[0]
    rows = inputs_ref.shape[0]
    wide = 4 * HEAD
    copies = weight_copies(plan, place_ref, sources, hold_ref, sem_ref)
    for group in copies:
        start_all(group)
    for index, piece_ref in enumerate(pieces):
        size = piece_ref.shape[1]
        attended_ref[:, pl.ds(pl.multiple_of(place_ref[index] * size, size), size)] = piece_ref[...]
    spread_heads(keys_ref, key_wide, model)
    spread_heads(values_ref, value_wide, model)

    def adapted(moving_ref, index, store):
        latent = mm_nt(moving_ref[...], adapt_ref[32 * index : 32 * index + 16, :]).astype(BF)
        lat_ref[:, 16 * index : 16 * index + 16] = latent
        wait_all(copies[index])

        def some(cols):
            store(
                cols,
                mm(moving_ref[...], hold_ref[index, :, cols])
                + mm(latent, adapt_ref[32 * index + 16 : 32 * index + 32, cols]),
            )

        each(model, 512, some)

    def add_first(cols, value):
        resid1_ref[:, cols] = inputs_ref[:, cols].astype(F32) + value

    def add_second(cols, value):
        resid2_ref[:, cols] = resid1_ref[:, cols] + value

    def keep_query(cols, value):
        query_ref[:, cols] = value.astype(BF)

    def normed(values_at, into_ref, which):
        def some(part):
            into_ref[part, :] = layer_norm(
                values_at[part, :], gain_ref[which : which + 1, :], bias_ref[which : which + 1, :]
            ).astype(BF)

        each(rows, 64, some)

    def cross(lanes):
        score = mm_nt(key_wide[lanes, :], query_ref[:, lanes]) * SCALE
        raised = jnp.exp(score - head_total(score, keys, jnp.max))
        prob = (raised / head_total(raised, keys, jnp.sum)).astype(BF)
        probs_ref[lanes, :] = prob
        crossed_ref[:, lanes] = mm_tn(prob, value_wide[lanes, :]).astype(BF)

    adapted(attended_ref, 0, add_first)
    normed(resid1_ref, normed2_ref, 1)
    adapted(normed2_ref, 1, keep_query)
    each(model, wide, cross)
    adapted(crossed_ref, 2, add_second)
    normed(resid2_ref, normed3_ref, 2)


def middle(places, own, own_spec, others, inputs, at, blocks, sources, plan, adapters, gains, biases, keys, values):
    rows, model = own_spec[0], inputs.shape[1]
    spread = model // HEAD * keys.shape[0]
    shape = lambda kind, dims=(rows, model): jax.ShapeDtypeStruct(dims, kind)
    flat = lambda dims: pl.BlockSpec(dims, lambda _, ref: (0,) * len(dims))
    shapes = [shape(kind) for kind in (BF, F32, BF, BF)]
    shapes += [shape(BF, (spread, rows)), shape(BF), shape(F32), shape(BF), shape(BF, (rows, 48))]
    return pl.pallas_call(
        partial(middle_kernel, plan),
        grid_spec=pltpu.PrefetchScalarGridSpec(
            num_scalar_prefetch=1,
            grid=(1,),
            in_specs=[pl.BlockSpec(memory_space=pl.ANY)] * len(sources)
            + [pl.BlockSpec((rows, model), lambda _, ref: (at, 0))]
            + [flat(item.shape) for item in (adapters, gains, biases, keys, values)]
            + [pl.BlockSpec(own_spec, lambda _, ref: (ref[0] * blocks + at, 0) if others else (at, 0))]
            + [flat(item.shape) for item in others],
            out_specs=[flat(item.shape) for item in shapes],
            scratch_shapes=[
                pltpu.VMEM((3, model, model), BF),
                pltpu.VMEM((spread, 4 * HEAD), BF),
                pltpu.VMEM((spread, 4 * HEAD), BF),
                pltpu.SemaphoreType.DMA((3, 3)),
            ],
        ),
        out_shape=shapes,
        compiler_params=params(),
        cost_estimate=cost(6 * rows * model * model, 6 * model * model + 24 * rows * model),
        name="middle",
    )(places, *sources, inputs, adapters, gains, biases, keys, values, own, *others)


def middle_back_kernel(plan, split, place_ref, *refs):
    sources, refs = refs[: source_count(plan)], refs[source_count(plan) :]
    (
        cot_ref, gu_ref, more_ref, attended_ref, resid1_ref, normed2_ref, query_ref, probs_ref, crossed_ref, resid2_ref,
        lat_ref, adapt_ref, gain_ref, keys_ref, values_ref,
    ) = refs[:15]
    refs = refs[15:]
    outs = refs[: 2 if split else 1]
    resid1_grad_ref, memory_ref, small_ref, hold_ref, key_wide, value_wide, work_ref, low_ref, sem_ref = refs[len(outs) :]
    rows, model = cot_ref.shape
    keys = keys_ref.shape[0]
    wide = 4 * HEAD
    copies = weight_copies(plan, place_ref, sources, hold_ref, sem_ref)
    for index in (2, 1, 0):
        start_all(copies[index])
    spread_heads(keys_ref, key_wide, model)
    spread_heads(values_ref, value_wide, model)

    def first(part):
        gradient = gu_ref[part, :].astype(F32) + more_ref[part, :].astype(F32)
        value = cot_ref[part, :].astype(F32) + norm_back(resid2_ref[part, :], gain_ref[2:3, :], gradient)
        resid1_grad_ref[part, :] = value
        low_ref[part, :] = value.astype(BF)

    def second(part):
        value = resid1_grad_ref[part, :] + norm_back(resid1_ref[part, :], gain_ref[1:2, :], work_ref[part, :])
        resid1_grad_ref[part, :] = value
        low_ref[part, :] = value.astype(BF)

    def back(moving_ref, index, store):
        down = slice(32 * index, 32 * index + 16)
        upper = slice(32 * index + 16, 32 * index + 32)
        glat = mm_nt(low_ref[...], adapt_ref[upper, :]).astype(BF)
        glat_t = glat.astype(F32).T.astype(BF)
        lat_t = lat_ref[:, 16 * index : 16 * index + 16].astype(F32).T.astype(BF)
        wait_all(copies[index])

        def some(cols):
            small_ref[down, cols] = mm(glat_t, moving_ref[:, cols])
            small_ref[upper, cols] = mm(lat_t, low_ref[:, cols])
            store(cols, mm_nt(low_ref[...], hold_ref[index, cols, :]) + mm(glat, adapt_ref[down, cols]))

        each(model, 512, some)

    def keep(cols, value):
        work_ref[:, cols] = value

    def cross(lanes):
        part = work_ref[:, lanes].astype(BF)
        prob = probs_ref[lanes, :]
        wide_prob = prob.astype(F32)
        weighted = wide_prob * mm_nt(value_wide[lanes, :], part)
        score_grad = (weighted - wide_prob * head_total(weighted, keys, jnp.sum)).astype(BF)
        low_ref[:, lanes] = (mm_tn(score_grad, key_wide[lanes, :]) * SCALE).astype(BF)
        key_full = mm(score_grad, query_ref[:, lanes])
        value_full = mm(prob, part)
        col = lax.broadcasted_iota(jnp.int32, (keys, wide), 1) // HEAD
        key_sum, value_sum = key_full[:keys], value_full[:keys]
        for head in range(1, 4):
            rows_at = slice(head * keys, (head + 1) * keys)
            key_sum = jnp.where(col == head, key_full[rows_at], key_sum)
            value_sum = jnp.where(col == head, value_full[rows_at], value_sum)
        memory_ref[0, :, lanes] = key_sum * SCALE
        memory_ref[1, :, lanes] = value_sum

    each(rows, 64, first)
    back(crossed_ref, 2, keep)
    each(model, wide, cross)
    back(normed2_ref, 1, keep)
    each(rows, 64, second)
    back(attended_ref, 0, keep)
    if split:
        size = outs[0].shape[1]
        for out_ref, index in zip(outs, range(2)):
            out_ref[...] = work_ref[:, pl.ds(pl.multiple_of(place_ref[index] * size, size), size)].astype(BF)
    else:
        outs[0][...] = work_ref[...].astype(BF)


def middle_back(places, parts, at, cotangent, gu, more, kept, sources, plan, adapters, gains, keys, values):
    model = cotangent.shape[1]
    rows = kept[0].shape[0]
    spread = model // HEAD * keys.shape[0]
    flat = lambda dims: pl.BlockSpec(dims, lambda _, ref: (0,) * len(dims))
    block = pl.BlockSpec((rows, model), lambda _, ref: (at, 0))
    shapes = [jax.ShapeDtypeStruct((rows, model // parts), BF)] * parts + [
        jax.ShapeDtypeStruct((rows, model), F32),
        jax.ShapeDtypeStruct((2,) + keys.shape, F32),
        jax.ShapeDtypeStruct(adapters.shape, F32),
    ]
    return pl.pallas_call(
        partial(middle_back_kernel, plan, parts == 2),
        grid_spec=pltpu.PrefetchScalarGridSpec(
            num_scalar_prefetch=1,
            grid=(1,),
            in_specs=[pl.BlockSpec(memory_space=pl.ANY)] * len(sources)
            + [block, flat(gu.shape), flat(more.shape)]
            + [flat(item.shape) for item in kept]
            + [flat(item.shape) for item in (adapters, gains, keys, values)],
            out_specs=[flat(item.shape) for item in shapes],
            scratch_shapes=[
                pltpu.VMEM((3, model, model), BF),
                pltpu.VMEM((spread, 4 * HEAD), BF),
                pltpu.VMEM((spread, 4 * HEAD), BF),
                pltpu.VMEM((rows, model), F32),
                pltpu.VMEM((rows, model), BF),
                pltpu.SemaphoreType.DMA((3, 3)),
            ],
        ),
        out_shape=shapes,
        compiler_params=params(),
        cost_estimate=cost(6 * rows * model * model, 6 * model * model + 36 * rows * model),
        name="middle_back",
    )(places, *sources, cotangent, gu, more, *kept, adapters, gains, keys, values)


def qkv_grads_kernel(
    place_ref, grad_ref, normed_ref, lat_ref, up_ref, glat_ref, mine_ref, theirs_ref, glat_acc, gup_acc, down_acc,
    down_all, upper_all,
):
    at = pl.program_id(0)
    gradient = grad_ref[...]
    rank = mine_ref.shape[0]
    model = normed_ref.shape[1]
    width = gradient.shape[1]
    gup_acc[...] = mm_tn(lat_ref[...], gradient)

    @pl.when(at == 0)
    def _():
        glat_acc[...] = jnp.zeros_like(glat_acc)
        upper_all[...] = jnp.zeros_like(upper_all)

    into = pl.ds(pl.multiple_of(at * model + place_ref[0] * width, LANES), width)
    upper_all[:, into] = gup_acc[pl.ds(pl.multiple_of(at * rank, rank), rank), :].astype(BF)
    glat_acc[...] += mm_nt(gradient, up_ref[...])

    @pl.when(at == pl.num_programs(0) - 1)
    def _():
        low = glat_acc[...].astype(BF)
        glat_ref[...] = low
        down_acc[...] = mm_tn(low, normed_ref[...])
        for part in range(3):
            down_all[:, part * model : (part + 1) * model] = down_acc[part * rank : (part + 1) * rank, :].astype(BF)
        share(place_ref, down_all, upper_all, mine_ref, theirs_ref)


def share(place_ref, down_all, upper_all, mine_ref, theirs_ref):
    @pl.when(place_ref[0] == 0)
    def _():
        mine_ref[...] = down_all[...]
        theirs_ref[...] = upper_all[...]

    @pl.when(place_ref[0] != 0)
    def _():
        mine_ref[...] = upper_all[...]
        theirs_ref[...] = down_all[...]


def qkv_grads(places, gradient, normed, latent, up):
    frames, model = normed.shape
    parts, ranks, width = up.shape
    rank = ranks // parts
    table = jax.ShapeDtypeStruct((rank, parts * model), BF)
    return pl.pallas_call(
        qkv_grads_kernel,
        grid=(parts,),
        in_specs=[
            smem(),
            pl.BlockSpec((None, frames, width), lambda at: (at, 0, 0)),
            whole(normed.shape),
            whole(latent.shape),
            pl.BlockSpec((None, ranks, width), lambda at: (at, 0, 0)),
        ],
        out_specs=[whole(latent.shape), whole(table.shape), whole(table.shape)],
        out_shape=[jax.ShapeDtypeStruct(latent.shape, BF), table, table],
        scratch_shapes=[
            pltpu.VMEM(latent.shape, F32),
            pltpu.VMEM((ranks, width), F32),
            pltpu.VMEM((ranks, model), F32),
            pltpu.VMEM(table.shape, BF),
            pltpu.VMEM(table.shape, BF),
        ],
        compiler_params=params(),
        cost_estimate=cost(8 * frames * ranks * width * parts, 2 * frames * (model + parts * width)),
        name="qkv_grads",
    )(places, gradient, normed, latent, up)


def qkv_back_kernel(place_ref, grad_ref, glat_ref, down_ref, w_ref, gu_ref, gu_acc):
    at = pl.program_id(0)
    model = gu_ref.shape[1]
    last = pl.num_programs(0) - 1

    def some(cols):
        direct = mm_nt(grad_ref[...], w_ref[cols, :])

        @pl.when(at == 0)
        def _():
            gu_acc[:, cols] = direct + mm(glat_ref[...], down_ref[:, cols])

        @pl.when(jnp.logical_and(at > 0, at < last))
        def _():
            gu_acc[:, cols] += direct

        @pl.when(at == last)
        def _():
            gu_ref[:, cols] = (gu_acc[:, cols] + direct).astype(gu_ref.dtype)

    each(model, 512, some)


def qkv_back(place, row_count, gradient, glat, down, packed, start, kind):
    ranks, model = down.shape
    width = gradient.shape[2]
    if start % width == 0 and width % LANES == 0:
        weight, spec = packed, pl.BlockSpec((model, width), lambda at, ref: (0, start // width + at))
    else:
        weight = packed[:, start : start + 3 * width].reshape(model, 3, width).transpose(1, 0, 2)
        spec = pl.BlockSpec((None, model, width), lambda at, ref: (at, 0, 0))
    return pl.pallas_call(
        qkv_back_kernel,
        grid_spec=pltpu.PrefetchScalarGridSpec(
            num_scalar_prefetch=1,
            grid=(3,),
            in_specs=[
                pl.BlockSpec((None, row_count, width), lambda at, ref: (at, ref[0], 0)),
                pl.BlockSpec((row_count, ranks), lambda at, ref: (ref[0], 0)),
                pl.BlockSpec(down.shape, lambda at, ref: (0, 0)),
                spec,
            ],
            out_specs=pl.BlockSpec((row_count, model), lambda at, ref: (0, 0)),
            scratch_shapes=[pltpu.VMEM((row_count, model), F32)],
        ),
        out_shape=jax.ShapeDtypeStruct((row_count, model), kind),
        compiler_params=params(),
        cost_estimate=cost(6 * row_count * model * width, 6 * model * width + 8 * row_count * model),
        name="qkv_back",
    )(place, gradient, glat, down, weight)


def run_length(size):
    count = 1
    while count * size % LANES:
        count *= 2
    return count


def join_kernel(pieces_ref, flat_ref):
    count, _, size = pieces_ref.shape
    run = run_length(size)

    def some(at, carry):
        parts = [pieces_ref[at * run + index] for index in range(run)]
        into = pl.ds(pl.multiple_of(at * run * size, LANES), run * size)
        flat_ref[:, into] = jnp.concatenate(parts, 1)
        return carry

    lax.fori_loop(0, count // run, some, 0)


def join_pieces(pieces):
    count, rows, size = pieces.shape
    if count % run_length(size):
        return pieces.transpose(1, 0, 2).reshape(rows, count * size)
    return pl.pallas_call(
        join_kernel,
        out_shape=jax.ShapeDtypeStruct((rows, count * size), pieces.dtype),
        compiler_params=params(0),
        name="join_pieces",
    )(pieces)


def split_kernel(*refs):
    sources, pieces_ref, flat_ref = refs[:-2], refs[-2], refs[-1]
    count, _, size = pieces_ref.shape
    run = run_length(size)
    start = 0
    for first_ref, second_ref in zip(sources[::2], sources[1::2]):
        width = first_ref.shape[1]
        both = first_ref[...].astype(F32) + second_ref[...].astype(F32)
        flat_ref[:, start : start + width] = both.astype(BF)
        start += width

    def some(at, carry):
        block = flat_ref[:, pl.ds(pl.multiple_of(at * run * size, LANES), run * size)]
        for index in range(run):
            pieces_ref[at * run + index] = block[:, index * size : (index + 1) * size]
        return carry

    lax.fori_loop(0, count // run, some, 0)


def split_sums(pairs, count):
    rows = pairs[0].shape[0]
    total = sum(item.shape[1] for item in pairs[::2])
    return pl.pallas_call(
        split_kernel,
        out_shape=jax.ShapeDtypeStruct((count, rows, total // count), BF),
        scratch_shapes=[pltpu.VMEM((rows, total), BF)],
        compiler_params=params(0),
        name="split_sums",
    )(*pairs)


def unit_loop(plan, work):
    fsdp, seq, folds, local = plan
    run = run_length(local)

    def some(at, carry):
        span = run * seq * folds * local
        block = pl.ds(pl.multiple_of(at * span, LANES), span)
        folded = [
            pl.ds(pl.multiple_of(fold * fsdp * local + at * run * local, LANES), run * local) for fold in range(folds)
        ]
        work(run, block, folded)
        return carry

    lax.fori_loop(0, fsdp // run, some, 0)


def take_units_kernel(plan, place_ref, all_ref, *refs):
    own_ref = refs[-1]
    _, seq, folds, local = plan
    spot = place_ref[0]

    def work(run, block, folded):
        values = all_ref[:, block]
        for fold, into in enumerate(folded):
            parts = []
            for index in range(run):
                base = (index * seq * folds + fold) * local
                part = values[:, base : base + local]
                for other in range(1, seq):
                    shift = base + other * folds * local
                    part = jnp.where(spot == other, values[:, shift : shift + local], part)
                parts.append(part)
            own_ref[:, into] = jnp.concatenate(parts, 1)

    unit_loop(plan, work)
    if len(refs) == 2:
        model = refs[0].shape[1]
        hidden = own_ref.shape[1] - folds * model
        for fold in range(folds):
            rows = pl.ds(pl.multiple_of((spot * folds + fold) * local, 16), local)
            own_ref[:, hidden + fold * model : hidden + (fold + 1) * model] = refs[0][rows, :]


def take_units(plan, places, matrix, low=None):
    _, seq, folds, local = plan
    rows, width = matrix.shape
    extra = [] if low is None else [low]
    out_width = width // seq + sum(folds * item.shape[1] for item in extra)
    return pl.pallas_call(
        partial(take_units_kernel, plan),
        in_specs=[smem()] + [pl.BlockSpec(memory_space=pltpu.VMEM)] * (1 + len(extra)),
        out_shape=jax.ShapeDtypeStruct((rows, out_width), matrix.dtype),
        compiler_params=params(0),
        name="take_units",
    )(places, matrix, *extra)


def collect_kernel(plan, blocks, place_ref, *refs):
    parts, squares, refs = refs[:blocks], refs[blocks : 2 * blocks], refs[2 * blocks :]
    feeds = [refs[at : at + 4] for at in range(0, len(refs) - 12, 4)]
    (
        other_ref, lat_ref, flat_ref, down_text_ref, text_ref, w_ref,
        mine_ref, theirs_ref, text_grad_ref, down_all, upper_all, unit_acc,
    ) = refs[-12:]
    _, seq, folds, local = plan
    rank = mine_ref.shape[0]
    model = text_ref.shape[1]
    wide = other_ref.shape[2]
    spot = place_ref[0]
    own = pl.ds(pl.multiple_of(spot * wide, wide), wide)

    def total(items, rows):
        value = items[0][rows, :]
        for item in items[1:]:
            value = value + item[rows, :]
        return value

    moved = []
    for part in range(2):
        value = parts[0][part, :, own]
        for item in parts[1:]:
            value = value + item[part, :, own]
        moved.append((value + other_ref[part].astype(F32)).astype(BF))
    moved = jnp.concatenate(moved, 1)
    glat = mm_nt(moved, flat_ref[...]).astype(BF)
    gup = mm_tn(lat_ref[...], moved)
    gdown = mm_tn(glat, text_ref[...])
    text_grad_ref[...] = (mm_nt(moved, w_ref[...]) + mm(glat, down_text_ref[...])).astype(BF)

    upper_all[:, 2 * model : 4 * model] = jnp.zeros((rank, 2 * model), BF)
    for part in range(2):
        rows = slice(part * rank, (part + 1) * rank)
        down_all[:, (2 + part) * model : (3 + part) * model] = gdown[rows].astype(BF)
        into = pl.ds(pl.multiple_of((2 + part) * model + spot * wide, LANES), wide)
        upper_all[:, into] = gup[rows, part * wide : (part + 1) * wide].astype(BF)
    for index, at in enumerate((0, 1, 4)):
        cols = slice(at * model, (at + 1) * model)
        down_all[:, cols] = total(squares, slice(2 * index * rank, (2 * index + 1) * rank)).astype(BF)
        upper_all[:, cols] = total(squares, slice((2 * index + 1) * rank, (2 * index + 2) * rank)).astype(BF)
    every = slice(0, rank)
    down_all[:, 5 * model : 6 * model] = total([item[0] for item in feeds], every).astype(BF)
    upper_all[:, upper_all.shape[1] - model :] = total([item[3] for item in feeds], every).astype(BF)
    for into_ref, start, which in ((upper_all, 5 * model, 1), (down_all, 6 * model, 2)):
        unit_acc[...] = total([item[which] for item in feeds], every)

        def work(run, block, folded):
            values = [unit_acc[:, cols] for cols in folded]
            spread = []
            for index in range(run):
                for other in range(seq):
                    for fold in range(folds):
                        part = values[fold][:, index * local : (index + 1) * local]
                        spread.append(jnp.where(spot == other, part, 0.0))
            at = pl.ds(pl.multiple_of(start + block.start, LANES), block.size)
            into_ref[:, at] = jnp.concatenate(spread, 1).astype(BF)

        unit_loop(plan, work)
    share(place_ref, down_all, upper_all, mine_ref, theirs_ref)


def collect(plan, places, parts, squares, feeds, other, lat_text, flat_text, down_text, text, packed, start):
    rank = squares[0].shape[0] // 6
    model = text.shape[1]
    hidden = feeds[0][1].shape[1]
    wide2 = flat_text.shape[1]
    width = 6 * model + hidden * plan[1]
    weight, spec = window(packed, start, wide2)
    feeds = [item for feed in feeds for item in feed]
    before = list(parts) + list(squares) + feeds + [other, lat_text, flat_text, down_text, text]
    table = jax.ShapeDtypeStruct((rank, width), BF)
    shapes = [table, table, jax.ShapeDtypeStruct(text.shape, BF)]
    return pl.pallas_call(
        partial(collect_kernel, plan, len(parts)),
        grid=(1,),
        in_specs=[smem()] + [whole(item.shape) for item in before] + [spec],
        out_specs=[whole(item.shape) for item in shapes],
        out_shape=shapes,
        scratch_shapes=[pltpu.VMEM(table.shape, BF)] * 2 + [pltpu.VMEM((rank, hidden), F32)],
        compiler_params=params(),
        cost_estimate=cost(4 * text.shape[0] * model * wide2, 2 * model * wide2),
        name="collect",
    )(places, *before, weight)


def body(
    inputs,
    text_states,
    adapter_index,
    norm_gains,
    norm_biases,
    self_in,
    self_out,
    cross_query,
    cross_text,
    cross_out,
    hidden_in,
    hidden_out,
    adapter_down,
    adapter_up,
    cotangent,
    *,
    sizes,
):
    seq, fsdp = sizes
    spot = lax.axis_index("seq")
    first_here = spot == 0
    there = (seq - 1) - spot
    local = self_in.shape[0]
    depth = hidden_out.shape[0] // seq
    pair = seq == 2 and depth % local == 0 and fsdp % run_length(local) == 0
    model = inputs.shape[2]
    rows = inputs.shape[1]
    frames = rows * seq
    wide = model // seq
    hidden_all = hidden_in.shape[1]
    hidden = hidden_all // seq
    adapters, rank, piece = adapter_down.shape
    total = piece * fsdp

    blocks = max(rows // 256, 1)
    size = rows // blocks

    def swap(value):
        return lax.ppermute(value, "seq", [(0, 1), (1, 0)])

    def pick(value, axis, extent, which=None):
        return lax.dynamic_slice_in_dim(value, (spot if which is None else which) * extent, extent, axis)

    def ordered(mine, other):
        return jnp.where(first_here, mine, other), jnp.where(first_here, other, mine)

    def gather(value, axis):
        if pair:
            return jnp.concatenate(ordered(value, swap(value)), axis)
        return lax.all_gather(value, "seq", axis=axis, tiled=True)

    def after(value, *others):
        return lax.optimization_barrier((value,) + others)[0]

    def put(value, axis):
        shape = list(value.shape)
        shape[axis] = seq
        return lax.dynamic_update_slice_in_dim(jnp.zeros(shape, value.dtype), value, spot, axis)

    def own_columns(matrix, parts):
        return [pick(matrix[:, at * model : (at + 1) * model], 1, wide) for at in range(parts)]

    def flat_down(grads, parts):
        return jnp.concatenate([grads[at * rank : (at + 1) * rank] for at in range(parts)], 1)

    def flat_upper(own):
        return put(jnp.stack(own, 1)[:, :, None], 2).reshape(rank, len(own) * model)

    squares_here = [cross_out, cross_query] + [pick(self_out, 1, wide) if pair else self_out]
    first = squares_here + own_columns(self_in, 3) + own_columns(cross_text, 2)
    edges = [0]
    for item in first:
        edges.append(edges[-1] + item.shape[1])
    start_in, start_text = edges[3], edges[6]
    packed = lax.all_gather(jnp.concatenate(first, 1), "fsdp", axis=0, tiled=True)
    squares_plan = ((edges[2], None), (edges[1], None), (edges[0], None))
    if pair:
        squares_plan = ((edges[2], 1),) + squares_plan[1:]
    core = lax.rem(lax.axis_index("fsdp"), 2)
    where_here = jnp.stack([spot, there, core, 1 - core]).astype(jnp.int32)
    if pair:
        folds = depth // local
        plan = (fsdp, seq, folds, local)
        own_units = partial(take_units, plan, where_here)
        packed_feed = lax.all_gather(own_units(hidden_in, hidden_out), "fsdp", axis=0, tiled=True)

        def feed_weights(block):
            per = model // block
            return (
                packed_feed,
                pl.BlockSpec((model, block), lambda at: (0, at)),
                packed_feed,
                pl.BlockSpec((block, model), lambda at: (at % per, folds + at // per)),
            )
    else:

        def own_units(matrix):
            kept = lax.dynamic_index_in_dim(matrix.reshape(-1, fsdp, seq, depth), spot, 2, False)
            return kept.reshape(-1, hidden)

        def all_units(matrix):
            return put(matrix.reshape(-1, fsdp, 1, depth), 2).reshape(-1, hidden_all)

        whole_in = lax.all_gather(own_units(hidden_in), "fsdp", axis=0, tiled=True)
        whole_out = lax.all_gather(pick(hidden_out, 0, depth), "fsdp", axis=0, tiled=True)

        def feed_weights(block):
            return (
                whole_in,
                pl.BlockSpec((model, block), lambda at: (0, at)),
                whole_out,
                pl.BlockSpec((block, model), lambda at: (at, 0)),
            )

    index_all = lax.all_to_all(jnp.broadcast_to(adapter_index, (fsdp,)), "fsdp", 0, 0, tiled=True)
    if pair:
        table = jnp.where(first_here, adapter_down, adapter_up)
        mine = join_pieces(lax.all_to_all(jnp.take(table, index_all, axis=0), "fsdp", 0, 0, tiled=True))
        down_all, upper_all = ordered(mine, swap(mine))
    else:
        table = jnp.concatenate([adapter_down, adapter_up], 1)
        chosen = join_pieces(lax.all_to_all(jnp.take(table, index_all, axis=0), "fsdp", 0, 0, tiled=True))
        down_all, upper_all = chosen[:rank], chosen[rank:]
    in_cuts = [0, 3 * model, 4 * model, 5 * model, 7 * model, 8 * model, 9 * model, 9 * model + hidden_all]
    out_cuts = [0, 3 * model, 4 * model, 5 * model, 7 * model, 8 * model, 8 * model + hidden_all, 9 * model + hidden_all]
    downs = [down_all[:, in_cuts[at] : in_cuts[at + 1]] for at in range(7)]
    uppers = [upper_all[:, out_cuts[at] : out_cuts[at + 1]] for at in range(7)]

    def part_down(matrix, parts):
        return jnp.concatenate([matrix[:, at * model : (at + 1) * model] for at in range(parts)], 0)

    def part_upper(matrix, parts):
        own = own_columns(matrix, parts)
        return jnp.stack(
            [jnp.pad(item, ((at * rank, (parts - 1 - at) * rank), (0, 0))) for at, item in enumerate(own)], 0
        )

    units = own_units(jnp.concatenate([uppers[5], downs[6]], 0))
    feed_adapters = (downs[5], units[:rank], units[rank:], uppers[6])
    square_adapters = jnp.concatenate([downs[1], uppers[1], downs[2], uppers[2], downs[4], uppers[4]], 0)
    down_qkv, upper_qkv = part_down(downs[0], 3), part_upper(uppers[0], 3)
    down_text, upper_text = part_down(downs[3], 2), part_upper(uppers[3], 2)
    flat_text = jnp.concatenate([upper_text[0], upper_text[1]], 1)

    frames_in = inputs[0]
    cot = cotangent[0]
    if pair:
        frames_parts = [frames_in, swap(frames_in)]
        cot_other = swap(after(cot, frames_parts[1]))
    else:
        frames_parts = [lax.all_gather(frames_in, "seq", axis=0, tiled=True)]
    norm_places = where_here if pair else jnp.zeros((4,), jnp.int32)
    if pair:
        frames_parts[1] = after(frames_parts[1], cot_other, units)
    normed1, lat_qkv = norm_project(norm_places, frames_parts, norm_gains[0:1], norm_biases[0:1], down_qkv)
    packed = after(packed, normed1)
    sources = [packed]
    if pair:
        half = model // 2
        straight = swap(lax.dynamic_slice(packed, (core * half, edges[2]), (half, wide)))
    triple = qkv_project(normed1, lat_qkv, upper_qkv, packed, start_in, 3 * wide)
    padded = -(-wide // LANES) * LANES
    if padded != wide:
        triple = jnp.pad(triple.reshape(frames, 3, wide), ((0, 0), (0, 0), (0, padded - wide)))
        triple = triple.reshape(frames, 3 * padded)
    text = after(text_states[0], triple)
    w_text = packed[:, start_text : start_text + 2 * wide]
    lat_text = mm_nt(text, down_text).astype(BF)
    memory = (mm(text, w_text) + mm(lat_text, flat_text)).astype(BF)
    head_out, probs, *leaving = attend(where_here, [size] * blocks if pair else [], after(triple, memory), padded)

    if pair:
        neighbours = [(at, at ^ 1) for at in range(fsdp)]
        sources += [straight, lax.ppermute(after(straight, head_out), "fsdp", neighbours)]

    memory_all = gather(memory.reshape(-1, 2, wide), 2)
    keys, values = memory_all[:, 0], memory_all[:, 1]

    constants = (sources, squares_plan, square_adapters, norm_gains, norm_biases, keys, values)
    if pair:
        received = [swap(leaving[0])]
        for item in leaving[1:]:
            received.append(swap(after(item, received[-1])))
    else:
        natural = lax.all_to_all(head_out[:, :wide], "seq", split_axis=0, concat_axis=1, tiled=True)
    made = []
    for at in range(blocks):
        if pair:
            own, spec, others = head_out, (size, wide), [received[at]]
        else:
            own, spec, others = natural, (size, model), []
        ready = after(frames_in, made[-1][7]) if made else frames_in
        made.append(middle(where_here if pair else jnp.zeros((4,), jnp.int32), own, spec, others, ready, at, blocks, *constants))
    normed3 = [item[7] for item in made]
    resid2 = [item[6] for item in made]

    feed_tail = feed_adapters + (feed_weights, hidden)
    if pair:
        others = [swap(item) for item in normed3]
        ours = [feed_forward(normed3[:1], resid2[:1], cot, 0, *feed_tail, F32)]
        theirs = feed_forward([others[0], after(others[1], ours[0][0])] if blocks > 1 else others, [], cot_other, 0, *feed_tail, BF)
        out_leaving, gu_leaving = theirs[:blocks], theirs[blocks : 2 * blocks]
        gu_more = [swap(gu_leaving[0])]
        for at in range(1, blocks):
            ours.append(feed_forward([after(normed3[at], gu_leaving[0])], [resid2[at]], cot, at, *feed_tail, F32))
            gu_more.append(swap(after(gu_leaving[at], gu_more[-1], ours[-1][0])))
        gu = [item[1] for item in ours]
        out_more = []
        feed_grads = [item[2:] for item in ours] + [theirs[2 * blocks :]]
    else:
        wide_in = gather(jnp.concatenate(normed3, 0), 0)
        all_out = feed_forward([wide_in], [], gather(cot, 0), 0, *feed_tail, F32)
        summed = [
            lax.psum_scatter(item.astype(BF), "seq", scatter_dimension=0, tiled=True) for item in all_out[:2]
        ]
        output = (jnp.concatenate(resid2, 0) + summed[0].astype(F32)).astype(BF)
        gu = [summed[1][at * size : (at + 1) * size] for at in range(blocks)]
        gu_more = [jnp.zeros_like(item) for item in gu]
        feed_grads = [all_out[2:]]

    pieces, resid1_grads, memory_parts, square_parts = [], [], [], []
    for at in range(blocks):
        gu_here = gu[at] if at == 0 else after(gu[at], result[-3])
        kept = made[at][:7] + made[at][8:9]
        result = middle_back(
            where_here, 2 if pair else 1, at, cot, gu_here, gu_more[at],
            kept, sources, squares_plan, square_adapters, norm_gains, keys, values,
        )
        if pair:
            waited = [pieces[-1][1]] if at else []
            if at == 0:
                out_more.append(swap(after(out_leaving[0], result[0])))
            if at == blocks - 1:
                memory_part = sum(memory_parts, result[-2]).astype(BF)
                memory_other = swap(after(pick(memory_part, 2, wide, there), *out_more))
                waited.append(memory_other)
            pieces.append((result[0], swap(after(result[1], *waited) if waited else result[1])))
        else:
            pieces.append(result[0])
        resid1_grads.append(result[-3])
        memory_parts.append(result[-2])
        square_parts.append(result[-1])
    resid1_grad = jnp.concatenate(resid1_grads, 0)
    square_grads = sum(square_parts[1:], square_parts[0])

    if pair:
        early, early_leaving, text_low = collect(
            plan, where_here, memory_parts, square_parts, feed_grads, memory_other, lat_text, flat_text, down_text,
            text_states[0], packed, start_text,
        )
        grad_pieces = [item[0] for item in pieces] + [item[1] for item in pieces]
    else:
        head_grad = lax.all_to_all(jnp.concatenate(pieces, 0), "seq", split_axis=1, concat_axis=0, tiled=True)
        grad_pieces = [jnp.pad(head_grad, ((0, 0), (0, padded - wide)))]
    triple_grad = attend_back(where_here, triple, head_out, grad_pieces, probs, padded)[:, :, :wide]
    if pair:
        early_other = swap(after(early_leaving, pieces[-1][1]))
        for at in range(1, blocks):
            out_more.append(swap(after(out_leaving[at], early_other, triple_grad)))
        glat_qkv, late, late_leaving = qkv_grads(
            where_here, after(triple_grad, early_other), normed1, lat_qkv, upper_qkv
        )
        late_other = swap(late_leaving)
    else:
        glat_qkv = sum(mm_nt(triple_grad[at], upper_qkv[at]) for at in range(3)).astype(BF)
        gdown_qkv = mm_tn(glat_qkv, normed1)
        gup_qkv = [mm_tn(lat_qkv[:, at * rank : (at + 1) * rank], triple_grad[at]) for at in range(3)]
    back = partial(qkv_back, gradient=triple_grad, glat=glat_qkv, down=down_qkv, packed=packed, start=start_in)
    if pair:
        for_them = back(there[None], rows, kind=BF)
        for_us = back(after(spot, for_them, *out_more)[None], rows, kind=F32)
        normed1_grad = for_us + swap(for_them).astype(F32)
        output = jnp.concatenate(
            [(item[0] + other.astype(F32)).astype(BF) for item, other in zip(ours, out_more)], 0
        )
    else:
        full = back(jnp.zeros((1,), jnp.int32), frames, kind=BF)
        normed1_grad = lax.psum_scatter(full, "seq", scatter_dimension=0, tiled=True).astype(F32)
    resid1_grad = jnp.concatenate(resid1_grads, 0)
    input_grad = resid1_grad + norm_back(frames_in.astype(F32), norm_gains[0:1], normed1_grad)

    selector = (index_all[None, :] == jnp.arange(adapters, dtype=jnp.int32)[:, None]).astype(BF)

    def by_adapter(sent):
        received = lax.all_to_all(sent, "fsdp", 0, 0, tiled=True)
        return jnp.einsum("ac,crw->arw", selector, received, preferred_element_type=F32)

    if pair:
        shares = by_adapter(split_sums([after(late, for_them), late_other, early, early_other], fsdp)).astype(BF)
        grad_down, grad_up = ordered(shares, swap(shares))
        text_total = text_low.astype(F32) + swap(text_low).astype(F32)
    else:
        memory_part = sum(memory_parts[1:], memory_parts[0]).astype(BF)
        memory_grad = lax.psum_scatter(memory_part, "seq", scatter_dimension=2, tiled=True)
        memory_flat = jnp.concatenate([memory_grad[0], memory_grad[1]], 1)
        glat_text = mm_nt(memory_flat, flat_text).astype(BF)
        gup_text = mm_tn(lat_text, memory_flat)
        gdown_text = mm_tn(glat_text, text)
        text_low = (mm_nt(memory_flat, w_text) + mm(glat_text, down_text)).astype(BF)
        own_text = [gup_text[at * rank : (at + 1) * rank, at * wide : (at + 1) * wide] for at in range(2)]
        gdown_in, gup_in, gdown_out, gup_out = feed_grads[0]
        square_grads = sum(square_parts[1:], square_parts[0])
        squares = [square_grads[rank * at : rank * (at + 1)] for at in range(6)]
        down_sent = [flat_down(gdown_qkv, 3), squares[0], squares[2], flat_down(gdown_text, 2), squares[4], gdown_in]
        upper_sent = [flat_upper(gup_qkv), squares[1], squares[3], flat_upper(own_text), squares[5]]
        down_sent = jnp.concatenate(down_sent + [all_units(gdown_out)], 1)
        upper_sent = jnp.concatenate(upper_sent + [all_units(gup_in), gup_out], 1)
        sent = jnp.concatenate([down_sent, upper_sent], 0).astype(BF).reshape(2 * rank, fsdp, piece).transpose(1, 0, 2)
        shares = lax.psum(by_adapter(sent).astype(BF), "seq")
        grad_down, grad_up = shares[:, :rank], shares[:, rank:]
        text_total = lax.psum(text_low, "seq").astype(F32)
    return (output[None], input_grad[None], text_total[None], grad_down.astype(F32), grad_up.astype(F32))


def solution(mesh):
    return jax.shard_map(
        partial(body, sizes=(mesh.shape["seq"], mesh.shape["fsdp"])),
        mesh=mesh,
        in_specs=(
            P("fsdp", "seq", None),
            P("fsdp", None, None),
            P("fsdp"),
            P(),
            P(),
            P("fsdp", None),
            P("fsdp", None),
            P("fsdp", None),
            P("fsdp", None),
            P("fsdp", None),
            P("fsdp", None),
            P("fsdp", None),
            P(None, None, "fsdp"),
            P(None, None, "fsdp"),
            P("fsdp", "seq", None),
        ),
        out_specs=(
            P("fsdp", "seq", None),
            P("fsdp", "seq", None),
            P("fsdp", None, None),
            P(None, None, "fsdp"),
            P(None, None, "fsdp"),
        ),
        check_vma=False,
    )
```

```python
from functools import partial

import jax
import jax.numpy as jnp
from jax import lax
from jax.experimental import pallas as pl
from jax.experimental.pallas import tpu as pltpu
from jax.sharding import PartitionSpec as P

HEAD = 64
LANES = 128
QB = 256
BF = jnp.bfloat16
F32 = jnp.float32
SCALE = float(HEAD) ** (-0.5)
SQRT_HALF = 0.7071067811865476
INV_SQRT_2PI = 0.3989422804014327
MIB = 1024 * 1024
VMEM_LIMIT = 60 * MIB
COST = 1.0
FEED_BLOCK = 512


def mm(a, b):
    return lax.dot_general(a, b, (((1,), (0,)), ((), ())), preferred_element_type=F32)


def mm_nt(a, b):
    return lax.dot_general(a, b, (((1,), (1,)), ((), ())), preferred_element_type=F32)


def mm_tn(a, b):
    return lax.dot_general(a, b, (((0,), (0,)), ((), ())), preferred_element_type=F32)


def norm_stats(values):
    centered = values - jnp.mean(values, -1, keepdims=True)
    variance = jnp.mean(centered * centered, -1, keepdims=True)
    inverse = lax.rsqrt(variance + 1e-05)
    return centered * inverse, inverse


def layer_norm(values, gains, biases):
    unit, _ = norm_stats(values)
    return unit * gains + biases


def norm_back(values, gains, gradient):
    unit, inverse = norm_stats(values)
    scaled = gradient * gains
    mean_one = jnp.mean(scaled, -1, keepdims=True)
    mean_two = jnp.mean(scaled * unit, -1, keepdims=True)
    return inverse * (scaled - mean_one - unit * mean_two)


def whole(shape):
    return pl.BlockSpec(shape, lambda *_: (0,) * len(shape))


def once(shape):
    return pl.BlockSpec(shape, lambda *_: (0,) * len(shape), pipeline_mode=pl.Buffered(1))


def params(count=1, limit=None):
    return pltpu.CompilerParams(
        dimension_semantics=("arbitrary",) * count if count else None, vmem_limit_bytes=limit or VMEM_LIMIT
    )


def cost(flops, moved, special=0):
    return pl.CostEstimate(
        flops=int(flops * COST), bytes_accessed=int(moved * COST), transcendentals=int(special * COST)
    )


def window(packed, start, width, rows=None, steps=1, step=0):
    block = width // steps
    rows = packed.shape[0] if rows is None else rows
    if start % block == 0 and block % LANES == 0:
        base = start // block
        return packed, pl.BlockSpec((rows, block), lambda *at: (0, base + (at[step] if steps > 1 else 0)))
    return packed[:, start : start + width], pl.BlockSpec(
        (rows, block), lambda *at: (0, at[step] if steps > 1 else 0)
    )


def norm_kernel(place_ref, *refs):
    count = len(refs) - 5
    parts, (gain_ref, bias_ref, down_ref, normed_ref, lat_ref) = refs[:count], refs[count:]
    step = 128
    for index, part_ref in enumerate(parts):
        base = place_ref[index] * part_ref.shape[0]

        def some(at, carry):
            rows = pl.ds(pl.multiple_of(at * step, step), step)
            into = pl.ds(pl.multiple_of(base + at * step, step), step)
            normed = layer_norm(part_ref[rows, :].astype(F32), gain_ref[...], bias_ref[...]).astype(BF)
            normed_ref[into, :] = normed
            lat_ref[into, :] = mm_nt(normed, down_ref[...]).astype(BF)
            return carry

        lax.fori_loop(0, part_ref.shape[0] // step, some, 0)


def smem():
    return pl.BlockSpec(memory_space=pltpu.SMEM)


def norm_project(places, parts, gains, biases, down):
    model = parts[0].shape[1]
    frames = sum(part.shape[0] for part in parts)
    ranks = down.shape[0]
    return pl.pallas_call(
        norm_kernel,
        in_specs=[smem()] + [whole(item.shape) for item in parts + [gains, biases, down]],
        out_specs=[whole((frames, model)), whole((frames, ranks))],
        out_shape=[jax.ShapeDtypeStruct((frames, model), BF), jax.ShapeDtypeStruct((frames, ranks), BF)],
        grid=(1,),
        compiler_params=params(1),
        cost_estimate=cost(2 * frames * model * ranks, 4 * frames * model),
        name="norm_project",
    )(places, *parts, gains, biases, down)


def qkv_kernel(normed_ref, lat_ref, up_ref, w_ref, out_ref):
    step = 256

    def some(at, carry):
        rows = pl.ds(pl.multiple_of(at * step, step), step)
        out_ref[rows, :] = (mm(normed_ref[rows, :], w_ref[...]) + mm(lat_ref[rows, :], up_ref[...])).astype(BF)
        return carry

    lax.fori_loop(0, normed_ref.shape[0] // step, some, 0)


def qkv_project(normed, latent, up, packed, start, width):
    row_count, model = normed.shape
    ranks = latent.shape[1]
    steps = 3 if (width // 3) % LANES == 0 else 1
    operand, spec = window(packed, start, width, steps=steps)
    block = width // steps
    if steps == 3:
        up_spec = pl.BlockSpec((None, ranks, block), lambda at: (at, 0, 0))
    else:
        up = up.transpose(1, 0, 2).reshape(ranks, width)
        up_spec = whole(up.shape)
    return pl.pallas_call(
        qkv_kernel,
        grid=(steps,),
        in_specs=[whole(normed.shape), whole(latent.shape), up_spec, spec],
        out_specs=pl.BlockSpec((row_count, block), lambda at: (0, at)),
        out_shape=jax.ShapeDtypeStruct((row_count, width), BF),
        compiler_params=params(1, 42 * MIB),
        cost_estimate=cost(2 * row_count * model * width, 2 * (row_count + width) * model),
        name="qkv_project",
    )(normed, latent, up, operand)


def tri_start(at):
    return QB * at * (at + 1) // 2


def attend_kernel(place_ref, q_ref, k_ref, v_ref, out_ref, prob_ref, *refs):
    sent, (val_t_ref, out_t_ref) = refs[:-2], refs[-2:]
    frames = q_ref.shape[0]
    lane = lax.broadcasted_iota(jnp.int32, (1, LANES), 1) // HEAD
    val_t_ref[...] = v_ref[...].T
    square = (QB, QB)
    keep_tri = lax.broadcasted_iota(jnp.int32, square, 0) <= lax.broadcasted_iota(jnp.int32, square, 1)

    def scores(half, at):
        stop = (at + 1) * QB
        query = q_ref[at * QB : stop, :] * jnp.where(lane == half, SCALE, 0.0).astype(BF)
        last = jnp.where(keep_tri, mm_nt(k_ref[stop - QB : stop, :], query), -1e30)
        if at == 0:
            return last
        return jnp.concatenate([mm_nt(k_ref[0 : stop - QB, :], query), last], 0)

    turns = [(half, at) for at in range(frames // QB) for half in range(2)]
    score = scores(*turns[0])
    for index, (half, at) in enumerate(turns):
        stop = (at + 1) * QB
        own = slice(half * HEAD, (half + 1) * HEAD)
        later = scores(*turns[index + 1]) if index + 1 < len(turns) else None
        raised = jnp.exp(score - jnp.max(score, 0, keepdims=True))
        prob = (raised * (1.0 / jnp.sum(raised, 0, keepdims=True))).astype(BF)
        prob_ref[half, tri_start(at) : tri_start(at) + stop, :] = prob
        out_t_ref[own, at * QB : stop] = mm(val_t_ref[own, 0:stop], prob)
        score = later
    out_ref[...] = out_t_ref[...].T.astype(BF)
    for index, sent_ref in enumerate(sent):
        size = sent_ref.shape[0]
        at = place_ref[1] * len(sent) + index
        sent_ref[...] = out_ref[pl.ds(pl.multiple_of(at * size, size), size), :]


def pair_specs(frames, width):
    pairs = width // LANES
    return [pl.BlockSpec((frames, LANES), lambda at, part=part: (0, part * pairs + at)) for part in range(3)]


def attend(places, sizes, triple, width):
    frames = triple.shape[0]
    pairs = width // LANES
    tri = tri_start(frames // QB)
    return pl.pallas_call(
        attend_kernel,
        grid=(pairs,),
        in_specs=[smem()] + pair_specs(frames, width),
        out_specs=[
            pl.BlockSpec((frames, LANES), lambda at: (0, at)),
            pl.BlockSpec((2, tri, QB), lambda at: (at, 0, 0)),
        ]
        + [pl.BlockSpec((size, LANES), lambda at: (0, at)) for size in sizes],
        out_shape=[
            jax.ShapeDtypeStruct((frames, width), BF),
            jax.ShapeDtypeStruct((2 * pairs, tri, QB), BF),
        ]
        + [jax.ShapeDtypeStruct((size, width), BF) for size in sizes],
        scratch_shapes=[pltpu.VMEM((LANES, frames), BF), pltpu.VMEM((LANES, frames), F32)],
        compiler_params=params(1),
        cost_estimate=cost(
            8 * tri * QB * HEAD * pairs, 2 * (4 * frames * width + 2 * pairs * tri * QB), 2 * pairs * tri * QB
        ),
        name="attend",
    )(places, triple, triple, triple)


def attend_back_kernel(place_ref, q_ref, k_ref, v_ref, out_ref, prob_ref, *refs):
    pieces, (back_ref, grad_ref, key_t_ref, dq_t_ref, dk_acc, dv_acc) = refs[:-6], refs[-6:]
    frames = q_ref.shape[0]
    for index, piece_ref in enumerate(pieces):
        size = piece_ref.shape[0]
        count = max(len(pieces) // 2, 1)
        at = place_ref[index // count] * count + index % count if len(pieces) > 1 else 0
        grad_ref[pl.ds(pl.multiple_of(at * size, size), size), :] = piece_ref[...]
    lane = lax.broadcasted_iota(jnp.int32, (1, LANES), 1) // HEAD
    key_t_ref[...] = k_ref[...].T
    dk_acc[...] = jnp.zeros_like(dk_acc)
    dv_acc[...] = jnp.zeros_like(dv_acc)
    turns = [(half, at) for at in range(frames // QB) for half in range(2)]

    def start(half, at):
        rows = slice(at * QB, (at + 1) * QB)
        grad = grad_ref[rows, :] * jnp.where(lane == half, 1.0, 0.0).astype(BF)
        return grad, mm_nt(v_ref[0 : (at + 1) * QB, :], grad)

    ready = start(*turns[0])
    for index, (half, at) in enumerate(turns):
        stop = (at + 1) * QB
        rows = slice(at * QB, stop)
        own = slice(half * HEAD, (half + 1) * HEAD)
        grad, prob_grad = ready
        if half == 0:
            product = (out_ref[rows, :].astype(F32) * grad_ref[rows, :].astype(F32)).T
        if index + 1 < len(turns):
            ready = start(*turns[index + 1])
        query = q_ref[rows, :] * jnp.where(lane == half, SCALE, 0.0).astype(BF)
        delta = jnp.sum(product[own, :], 0, keepdims=True)
        prob = prob_ref[half, tri_start(at) : tri_start(at) + stop, :]
        dv_acc[0:stop, :] += mm(prob, grad)
        score_grad = (prob.astype(F32) * (prob_grad - delta)).astype(BF)
        dk_acc[0:stop, :] += mm(score_grad, query)
        dq_t_ref[own, rows] = mm(key_t_ref[own, 0:stop], score_grad)
    back_ref[0] = (dq_t_ref[...].T * SCALE).astype(BF)
    back_ref[1] = dk_acc[...].astype(BF)
    back_ref[2] = dv_acc[...].astype(BF)


def attend_back(places, triple, attended, pieces, probs, width):
    frames = triple.shape[0]
    pairs = width // LANES
    tri = tri_start(frames // QB)
    column = pl.BlockSpec((frames, LANES), lambda at: (0, at))
    return pl.pallas_call(
        attend_back_kernel,
        grid=(pairs,),
        in_specs=[smem()]
        + pair_specs(frames, width)
        + [column, pl.BlockSpec((2, tri, QB), lambda at: (at, 0, 0))]
        + [pl.BlockSpec((piece.shape[0], LANES), lambda at: (0, at)) for piece in pieces],
        out_specs=pl.BlockSpec((3, frames, LANES), lambda at: (0, 0, at)),
        out_shape=jax.ShapeDtypeStruct((3, frames, width), BF),
        scratch_shapes=[
            pltpu.VMEM((frames, LANES), BF),
            pltpu.VMEM((LANES, frames), BF),
            pltpu.VMEM((LANES, frames), F32),
            pltpu.VMEM((frames, LANES), F32),
            pltpu.VMEM((frames, LANES), F32),
        ],
        compiler_params=params(1, 42 * MIB),
        cost_estimate=cost(16 * tri * QB * HEAD * pairs, 2 * (8 * frames * width + 2 * pairs * tri * QB)),
        name="attend_back",
    )(places, triple, triple, triple, attended, probs, *pieces)


def feed_kernel(count, based, *refs):
    pieces, refs = refs[:count], refs[count:]
    bases, refs = refs[:based], refs[based:]
    cot_ref, down_in_ref, up_in_ref, down_out_ref, up_out_ref, w_in_ref, w_out_ref = refs[:7]
    out_refs, gu_refs, refs = refs[7 : 7 + count], refs[7 + count : 7 + 2 * count], refs[7 + 2 * count :]
    (
        gdown_in_ref, gup_in_ref, gdown_out_ref, gup_out_ref, normed_ref,
        out_acc, gu_acc, lat_in, glat_out, lat_acc, glat_acc, lat_t, glat_t,
    ) = refs
    at = pl.program_id(0)

    @pl.when(at == 0)
    def _():
        start = 0
        for piece_ref in pieces:
            normed_ref[start : start + piece_ref.shape[0], :] = piece_ref[...]
            start += piece_ref.shape[0]
        latent = mm_nt(normed_ref[...], down_in_ref[...]).astype(BF)
        glat = mm_nt(cot_ref[...], up_out_ref[...]).astype(BF)
        lat_in[...] = latent
        glat_out[...] = glat
        lat_t[...] = latent.astype(F32).T.astype(BF)
        glat_t[...] = glat.astype(F32).T.astype(BF)
        start = 0
        for base_ref in bases:
            out_acc[start : start + base_ref.shape[0], :] = base_ref[...]
            start += base_ref.shape[0]
        if not bases:
            out_acc[...] = jnp.zeros_like(out_acc)
        gu_acc[...] = jnp.zeros_like(gu_acc)
        lat_acc[...] = jnp.zeros_like(lat_acc)
        glat_acc[...] = jnp.zeros_like(glat_acc)

    w_in = w_in_ref[...]
    w_out = w_out_ref[...]
    pre = mm(normed_ref[...], w_in) + mm(lat_in[...], up_in_ref[...])
    act_grad = mm_nt(cot_ref[...], w_out) + mm(glat_out[...], down_out_ref[...])
    cdf = 0.5 * (1.0 + lax.erf(pre * SQRT_HALF))
    slope = cdf + pre * (jnp.exp(-0.5 * pre * pre) * INV_SQRT_2PI)
    act = (pre * cdf).astype(BF)
    pre_grad = (act_grad * slope).astype(BF)
    out_acc[...] += mm(act, w_out)
    gu_acc[...] += mm_nt(pre_grad, w_in)
    lat_acc[...] += mm_nt(act, down_out_ref[...])
    glat_acc[...] += mm_nt(pre_grad, up_in_ref[...])
    gup_in_ref[...] = mm(lat_t[...], pre_grad)
    gdown_out_ref[...] = mm(glat_t[...], act)

    @pl.when(at == pl.num_programs(0) - 1)
    def _():
        latent = lat_acc[...].astype(BF)
        glat = glat_acc[...].astype(BF)
        start = 0
        for out_ref, gu_ref in zip(out_refs, gu_refs):
            rows = slice(start, start + out_ref.shape[0])
            out_ref[...] = (out_acc[rows, :] + mm(latent[rows], up_out_ref[...])).astype(out_ref.dtype)
            gu_ref[...] = (gu_acc[rows, :] + mm(glat[rows], down_in_ref[...])).astype(gu_ref.dtype)
            start += out_ref.shape[0]
        gup_out_ref[...] = mm(latent.astype(F32).T.astype(BF), cot_ref[...])
        gdown_in_ref[...] = mm(glat.astype(F32).T.astype(BF), normed_ref[...])


def feed_forward(pieces, bases, cotangent, block_at, down_in, up_in, down_out, up_out, weights, hidden, kind):
    model = cotangent.shape[1]
    row_count = sum(item.shape[0] for item in pieces)
    rank = down_in.shape[0]
    block = FEED_BLOCK if hidden % FEED_BLOCK == 0 else hidden
    w_in, in_spec, w_out, out_spec = weights(block)
    main = pl.BlockSpec((row_count, model), lambda at: (block_at, 0))
    slim = pl.BlockSpec((rank, block), lambda at: (0, at))
    small = whole((rank, model))
    return pl.pallas_call(
        partial(feed_kernel, len(pieces), len(bases)),
        grid=(hidden // block,),
        in_specs=[once(item.shape) for item in pieces + bases]
        + [main, small, slim, slim, small, in_spec, out_spec],
        out_specs=[whole(item.shape) for item in pieces] * 2 + [small, slim, slim, small],
        out_shape=[jax.ShapeDtypeStruct(item.shape, kind) for item in pieces]
        + [jax.ShapeDtypeStruct(item.shape, BF) for item in pieces]
        + [
            jax.ShapeDtypeStruct((rank, model), F32),
            jax.ShapeDtypeStruct((rank, hidden), F32),
            jax.ShapeDtypeStruct((rank, hidden), F32),
            jax.ShapeDtypeStruct((rank, model), F32),
        ],
        scratch_shapes=[pltpu.VMEM((row_count, model), BF)]
        + [pltpu.VMEM((row_count, model), F32)] * 2
        + [pltpu.VMEM((row_count, rank), BF)] * 2
        + [pltpu.VMEM((row_count, rank), F32)] * 2
        + [pltpu.VMEM((rank, row_count), BF)] * 2,
        compiler_params=params(1),
        cost_estimate=cost(8 * row_count * model * hidden, 4 * hidden * model, 2 * row_count * hidden),
        name="feed_forward",
    )(*pieces, *bases, cotangent, down_in, up_in, down_out, up_out, w_in, w_out)


def spread_heads(rows_ref, into_ref, model):
    keys = rows_ref.shape[0]
    wide = 4 * HEAD
    row = lax.broadcasted_iota(jnp.int32, (4 * keys, wide), 0) // keys
    col = lax.broadcasted_iota(jnp.int32, (4 * keys, wide), 1) // HEAD
    mask = jnp.where(row == col, 1.0, 0.0).astype(BF)

    def some(group, carry):
        part = rows_ref[:, pl.ds(pl.multiple_of(group * wide, wide), wide)]
        into = pl.ds(pl.multiple_of(group * 4 * keys, 4 * keys), 4 * keys)
        into_ref[into, :] = jnp.concatenate([part] * 4, 0) * mask
        return carry

    lax.fori_loop(0, model // wide, some, 0)


def head_total(values, keys, reduce):
    split = values.reshape(4, keys, values.shape[1])
    return jnp.broadcast_to(reduce(split, 1, keepdims=True), split.shape).reshape(values.shape)


def each(count, step, work):
    def some(at, carry):
        work(pl.ds(pl.multiple_of(at * step, step), step))
        return carry

    lax.fori_loop(0, count // step, some, 0)


def weight_copies(plan, place_ref, sources, hold_ref, sem_ref):
    model = hold_ref.shape[1]
    groups = []
    for index, (start, extra) in enumerate(plan):
        if extra is None:
            pairs = [(sources[0].at[:, pl.ds(start, model)], hold_ref.at[index])]
        else:
            half = model // 2
            here, there = [pl.ds(pl.multiple_of(place_ref[at] * half, half), half) for at in range(2)]
            pairs = [(sources[0].at[:, pl.ds(start, half)], hold_ref.at[index, :, here])]
            for at in range(2):
                rows = pl.ds(pl.multiple_of(place_ref[2 + at] * half, half), half)
                pairs.append((sources[extra + at], hold_ref.at[index, rows, there]))
        groups.append(
            [pltpu.make_async_copy(src, dst, sem_ref.at[index, at]) for at, (src, dst) in enumerate(pairs)]
        )
    return groups


def source_count(plan):
    return 1 + 2 * sum(extra is not None for _, extra in plan)


def start_all(copies):
    for copy in copies:
        copy.start()


def wait_all(copies):
    for copy in copies:
        copy.wait()


def middle_kernel(plan, place_ref, *refs):
    sources, refs = refs[: source_count(plan)], refs[source_count(plan) :]
    inputs_ref, adapt_ref, gain_ref, bias_ref, keys_ref, values_ref = refs[:6]
    pieces = refs[6:-13]
    (
        attended_ref, resid1_ref, normed2_ref, query_ref, probs_ref, crossed_ref, resid2_ref, normed3_ref, lat_ref,
        hold_ref, key_wide, value_wide, sem_ref,
    ) = refs[-13:]
    model = inputs_ref.shape[1]
    keys = keys_ref.shape[0]
    rows = inputs_ref.shape[0]
    wide = 4 * HEAD
    copies = weight_copies(plan, place_ref, sources, hold_ref, sem_ref)
    start_all(copies[0])
    for index, piece_ref in enumerate(pieces):
        size = piece_ref.shape[1]
        attended_ref[:, pl.ds(pl.multiple_of(place_ref[index] * size, size), size)] = piece_ref[...]
    spread_heads(keys_ref, key_wide, model)
    spread_heads(values_ref, value_wide, model)

    def adapted(moving_ref, index, store):
        latent = mm_nt(moving_ref[...], adapt_ref[32 * index : 32 * index + 16, :]).astype(BF)
        lat_ref[:, 16 * index : 16 * index + 16] = latent
        wait_all(copies[index])
        if index < 2:
            start_all(copies[index + 1])

        def some(cols):
            store(
                cols,
                mm(moving_ref[...], hold_ref[index, :, cols])
                + mm(latent, adapt_ref[32 * index + 16 : 32 * index + 32, cols]),
            )

        each(model, 512, some)

    def add_first(cols, value):
        resid1_ref[:, cols] = inputs_ref[:, cols].astype(F32) + value

    def add_second(cols, value):
        resid2_ref[:, cols] = resid1_ref[:, cols] + value

    def keep_query(cols, value):
        query_ref[:, cols] = value.astype(BF)

    def normed(values_at, into_ref, which):
        def some(part):
            into_ref[part, :] = layer_norm(
                values_at[part, :], gain_ref[which : which + 1, :], bias_ref[which : which + 1, :]
            ).astype(BF)

        each(rows, 64, some)

    def cross(lanes):
        score = mm_nt(key_wide[lanes, :], query_ref[:, lanes]) * SCALE
        raised = jnp.exp(score - head_total(score, keys, jnp.max))
        prob = (raised / head_total(raised, keys, jnp.sum)).astype(BF)
        probs_ref[lanes, :] = prob
        crossed_ref[:, lanes] = mm_tn(prob, value_wide[lanes, :]).astype(BF)

    adapted(attended_ref, 0, add_first)
    normed(resid1_ref, normed2_ref, 1)
    adapted(normed2_ref, 1, keep_query)
    each(model, wide, cross)
    adapted(crossed_ref, 2, add_second)
    normed(resid2_ref, normed3_ref, 2)


def middle(places, own, own_spec, others, inputs, at, blocks, sources, plan, adapters, gains, biases, keys, values):
    rows, model = own_spec[0], inputs.shape[1]
    spread = model // HEAD * keys.shape[0]
    shape = lambda kind, dims=(rows, model): jax.ShapeDtypeStruct(dims, kind)
    flat = lambda dims: pl.BlockSpec(dims, lambda _, ref: (0,) * len(dims))
    shapes = [shape(kind) for kind in (BF, F32, BF, BF)]
    shapes += [shape(BF, (spread, rows)), shape(BF), shape(F32), shape(BF), shape(BF, (rows, 48))]
    return pl.pallas_call(
        partial(middle_kernel, plan),
        grid_spec=pltpu.PrefetchScalarGridSpec(
            num_scalar_prefetch=1,
            grid=(1,),
            in_specs=[pl.BlockSpec(memory_space=pl.ANY)] * len(sources)
            + [pl.BlockSpec((rows, model), lambda _, ref: (at, 0))]
            + [flat(item.shape) for item in (adapters, gains, biases, keys, values)]
            + [pl.BlockSpec(own_spec, lambda _, ref: (ref[0] * blocks + at, 0) if others else (at, 0))]
            + [flat(item.shape) for item in others],
            out_specs=[flat(item.shape) for item in shapes],
            scratch_shapes=[
                pltpu.VMEM((3, model, model), BF),
                pltpu.VMEM((spread, 4 * HEAD), BF),
                pltpu.VMEM((spread, 4 * HEAD), BF),
                pltpu.SemaphoreType.DMA((3, 3)),
            ],
        ),
        out_shape=shapes,
        compiler_params=params(),
        cost_estimate=cost(6 * rows * model * model, 6 * model * model + 24 * rows * model),
        name="middle",
    )(places, *sources, inputs, adapters, gains, biases, keys, values, own, *others)


def middle_back_kernel(plan, split, place_ref, *refs):
    sources, refs = refs[: source_count(plan)], refs[source_count(plan) :]
    (
        cot_ref, gu_ref, more_ref, attended_ref, resid1_ref, normed2_ref, query_ref, probs_ref, crossed_ref, resid2_ref,
        lat_ref, adapt_ref, gain_ref, keys_ref, values_ref,
    ) = refs[:15]
    refs = refs[15:]
    outs = refs[: 2 if split else 1]
    resid1_grad_ref, memory_ref, small_ref, hold_ref, key_wide, value_wide, work_ref, low_ref, sem_ref = refs[len(outs) :]
    rows, model = cot_ref.shape
    keys = keys_ref.shape[0]
    wide = 4 * HEAD
    copies = weight_copies(plan, place_ref, sources, hold_ref, sem_ref)
    start_all(copies[2])
    spread_heads(keys_ref, key_wide, model)
    spread_heads(values_ref, value_wide, model)

    def first(part):
        gradient = gu_ref[part, :].astype(F32) + more_ref[part, :].astype(F32)
        value = cot_ref[part, :].astype(F32) + norm_back(resid2_ref[part, :], gain_ref[2:3, :], gradient)
        resid1_grad_ref[part, :] = value
        low_ref[part, :] = value.astype(BF)

    def second(part):
        value = resid1_grad_ref[part, :] + norm_back(resid1_ref[part, :], gain_ref[1:2, :], work_ref[part, :])
        resid1_grad_ref[part, :] = value
        low_ref[part, :] = value.astype(BF)

    def back(moving_ref, index, store):
        down = slice(32 * index, 32 * index + 16)
        upper = slice(32 * index + 16, 32 * index + 32)
        glat = mm_nt(low_ref[...], adapt_ref[upper, :]).astype(BF)
        glat_t = glat.astype(F32).T.astype(BF)
        lat_t = lat_ref[:, 16 * index : 16 * index + 16].astype(F32).T.astype(BF)
        wait_all(copies[index])
        if index:
            start_all(copies[index - 1])

        def some(cols):
            small_ref[down, cols] = mm(glat_t, moving_ref[:, cols])
            small_ref[upper, cols] = mm(lat_t, low_ref[:, cols])
            store(cols, mm_nt(low_ref[...], hold_ref[index, cols, :]) + mm(glat, adapt_ref[down, cols]))

        each(model, 512, some)

    def keep(cols, value):
        work_ref[:, cols] = value

    def cross(lanes):
        part = work_ref[:, lanes].astype(BF)
        prob = probs_ref[lanes, :]
        wide_prob = prob.astype(F32)
        weighted = wide_prob * mm_nt(value_wide[lanes, :], part)
        score_grad = (weighted - wide_prob * head_total(weighted, keys, jnp.sum)).astype(BF)
        low_ref[:, lanes] = (mm_tn(score_grad, key_wide[lanes, :]) * SCALE).astype(BF)
        key_full = mm(score_grad, query_ref[:, lanes])
        value_full = mm(prob, part)
        col = lax.broadcasted_iota(jnp.int32, (keys, wide), 1) // HEAD
        key_sum, value_sum = key_full[:keys], value_full[:keys]
        for head in range(1, 4):
            rows_at = slice(head * keys, (head + 1) * keys)
            key_sum = jnp.where(col == head, key_full[rows_at], key_sum)
            value_sum = jnp.where(col == head, value_full[rows_at], value_sum)
        memory_ref[0, :, lanes] = key_sum * SCALE
        memory_ref[1, :, lanes] = value_sum

    each(rows, 64, first)
    back(crossed_ref, 2, keep)
    each(model, wide, cross)
    back(normed2_ref, 1, keep)
    each(rows, 64, second)
    back(attended_ref, 0, keep)
    if split:
        size = outs[0].shape[1]
        for out_ref, index in zip(outs, range(2)):
            out_ref[...] = work_ref[:, pl.ds(pl.multiple_of(place_ref[index] * size, size), size)].astype(BF)
    else:
        outs[0][...] = work_ref[...].astype(BF)


def middle_back(places, parts, at, cotangent, gu, more, kept, sources, plan, adapters, gains, keys, values):
    model = cotangent.shape[1]
    rows = kept[0].shape[0]
    spread = model // HEAD * keys.shape[0]
    flat = lambda dims: pl.BlockSpec(dims, lambda _, ref: (0,) * len(dims))
    block = pl.BlockSpec((rows, model), lambda _, ref: (at, 0))
    shapes = [jax.ShapeDtypeStruct((rows, model // parts), BF)] * parts + [
        jax.ShapeDtypeStruct((rows, model), F32),
        jax.ShapeDtypeStruct((2,) + keys.shape, F32),
        jax.ShapeDtypeStruct(adapters.shape, F32),
    ]
    return pl.pallas_call(
        partial(middle_back_kernel, plan, parts == 2),
        grid_spec=pltpu.PrefetchScalarGridSpec(
            num_scalar_prefetch=1,
            grid=(1,),
            in_specs=[pl.BlockSpec(memory_space=pl.ANY)] * len(sources)
            + [block, flat(gu.shape), flat(more.shape)]
            + [flat(item.shape) for item in kept]
            + [flat(item.shape) for item in (adapters, gains, keys, values)],
            out_specs=[flat(item.shape) for item in shapes],
            scratch_shapes=[
                pltpu.VMEM((3, model, model), BF),
                pltpu.VMEM((spread, 4 * HEAD), BF),
                pltpu.VMEM((spread, 4 * HEAD), BF),
                pltpu.VMEM((rows, model), F32),
                pltpu.VMEM((rows, model), BF),
                pltpu.SemaphoreType.DMA((3, 3)),
            ],
        ),
        out_shape=shapes,
        compiler_params=params(),
        cost_estimate=cost(6 * rows * model * model, 6 * model * model + 36 * rows * model),
        name="middle_back",
    )(places, *sources, cotangent, gu, more, *kept, adapters, gains, keys, values)


def qkv_grads_kernel(
    place_ref, grad_ref, normed_ref, lat_ref, up_ref, glat_ref, mine_ref, theirs_ref, glat_acc, gup_acc, down_acc,
    down_all, upper_all,
):
    at = pl.program_id(0)
    gradient = grad_ref[...]
    rank = mine_ref.shape[0]
    model = normed_ref.shape[1]
    width = gradient.shape[1]
    gup_acc[...] = mm_tn(lat_ref[...], gradient)

    @pl.when(at == 0)
    def _():
        glat_acc[...] = jnp.zeros_like(glat_acc)
        upper_all[...] = jnp.zeros_like(upper_all)

    into = pl.ds(pl.multiple_of(at * model + place_ref[0] * width, LANES), width)
    upper_all[:, into] = gup_acc[pl.ds(pl.multiple_of(at * rank, rank), rank), :].astype(BF)
    glat_acc[...] += mm_nt(gradient, up_ref[...])

    @pl.when(at == pl.num_programs(0) - 1)
    def _():
        low = glat_acc[...].astype(BF)
        glat_ref[...] = low
        down_acc[...] = mm_tn(low, normed_ref[...])
        for part in range(3):
            down_all[:, part * model : (part + 1) * model] = down_acc[part * rank : (part + 1) * rank, :].astype(BF)
        share(place_ref, down_all, upper_all, mine_ref, theirs_ref)


def share(place_ref, down_all, upper_all, mine_ref, theirs_ref):
    @pl.when(place_ref[0] == 0)
    def _():
        mine_ref[...] = down_all[...]
        theirs_ref[...] = upper_all[...]

    @pl.when(place_ref[0] != 0)
    def _():
        mine_ref[...] = upper_all[...]
        theirs_ref[...] = down_all[...]


def qkv_grads(places, gradient, normed, latent, up):
    frames, model = normed.shape
    parts, ranks, width = up.shape
    rank = ranks // parts
    table = jax.ShapeDtypeStruct((rank, parts * model), BF)
    return pl.pallas_call(
        qkv_grads_kernel,
        grid=(parts,),
        in_specs=[
            smem(),
            pl.BlockSpec((None, frames, width), lambda at: (at, 0, 0)),
            whole(normed.shape),
            whole(latent.shape),
            pl.BlockSpec((None, ranks, width), lambda at: (at, 0, 0)),
        ],
        out_specs=[whole(latent.shape), whole(table.shape), whole(table.shape)],
        out_shape=[jax.ShapeDtypeStruct(latent.shape, BF), table, table],
        scratch_shapes=[
            pltpu.VMEM(latent.shape, F32),
            pltpu.VMEM((ranks, width), F32),
            pltpu.VMEM((ranks, model), F32),
            pltpu.VMEM(table.shape, BF),
            pltpu.VMEM(table.shape, BF),
        ],
        compiler_params=params(1, 42 * MIB),
        cost_estimate=cost(8 * frames * ranks * width * parts, 2 * frames * (model + parts * width)),
        name="qkv_grads",
    )(places, gradient, normed, latent, up)


def qkv_back_kernel(place_ref, grad_ref, glat_ref, down_ref, w_ref, gu_ref, gu_acc):
    at = pl.program_id(0)
    model = gu_ref.shape[1]
    last = pl.num_programs(0) - 1

    def some(cols):
        direct = mm_nt(grad_ref[...], w_ref[cols, :])

        @pl.when(at == 0)
        def _():
            gu_acc[:, cols] = direct + mm(glat_ref[...], down_ref[:, cols])

        @pl.when(jnp.logical_and(at > 0, at < last))
        def _():
            gu_acc[:, cols] += direct

        @pl.when(at == last)
        def _():
            gu_ref[:, cols] = (gu_acc[:, cols] + direct).astype(gu_ref.dtype)

    each(model, 512, some)


def qkv_back(place, row_count, gradient, glat, down, packed, start, kind):
    ranks, model = down.shape
    width = gradient.shape[2]
    if start % width == 0 and width % LANES == 0:
        weight, spec = packed, pl.BlockSpec((model, width), lambda at, ref: (0, start // width + at))
    else:
        weight = packed[:, start : start + 3 * width].reshape(model, 3, width).transpose(1, 0, 2)
        spec = pl.BlockSpec((None, model, width), lambda at, ref: (at, 0, 0))
    return pl.pallas_call(
        qkv_back_kernel,
        grid_spec=pltpu.PrefetchScalarGridSpec(
            num_scalar_prefetch=1,
            grid=(3,),
            in_specs=[
                pl.BlockSpec((None, row_count, width), lambda at, ref: (at, ref[0], 0)),
                pl.BlockSpec((row_count, ranks), lambda at, ref: (ref[0], 0)),
                pl.BlockSpec(down.shape, lambda at, ref: (0, 0)),
                spec,
            ],
            out_specs=pl.BlockSpec((row_count, model), lambda at, ref: (0, 0)),
            scratch_shapes=[pltpu.VMEM((row_count, model), F32)],
        ),
        out_shape=jax.ShapeDtypeStruct((row_count, model), kind),
        compiler_params=params(1, 42 * MIB),
        cost_estimate=cost(6 * row_count * model * width, 6 * model * width + 8 * row_count * model),
        name="qkv_back",
    )(place, gradient, glat, down, weight)


def last_norm_kernel(blocks, frames_ref, ours_ref, theirs_ref, gain_ref, *refs):
    pieces, grad_ref = refs[:-1], refs[-1]
    at = pl.program_id(0)
    gradient = ours_ref[...] + theirs_ref[...].astype(F32)
    back = norm_back(frames_ref[...].astype(F32), gain_ref[...], gradient)
    for index, piece_ref in enumerate(pieces):

        @pl.when(at // blocks == index)
        def _(piece_ref=piece_ref):
            grad_ref[...] = back + piece_ref[...]


def last_norm(frames, ours, theirs, gains, pieces):
    rows, model = frames.shape
    step = min(128, rows)
    blocks = pieces[0].shape[0] // step
    block = pl.BlockSpec((step, model), lambda at: (at, 0))

    def piece_spec(index):
        return pl.BlockSpec((step, model), lambda at: (jnp.clip(at - index * blocks, 0, blocks - 1), 0))

    return pl.pallas_call(
        partial(last_norm_kernel, blocks),
        grid=(rows // step,),
        in_specs=[block, block, block, whole(gains.shape)] + [piece_spec(index) for index in range(len(pieces))],
        out_specs=block,
        out_shape=jax.ShapeDtypeStruct((rows, model), F32),
        compiler_params=params(1, 42 * MIB),
        cost_estimate=cost(20 * rows * model, 16 * rows * model),
        name="last_norm",
    )(frames, ours, theirs, gains, *pieces)


def run_length(size):
    count = 1
    while count * size % LANES:
        count *= 2
    return count


def join_kernel(pieces_ref, flat_ref):
    count, _, size = pieces_ref.shape
    run = run_length(size)

    def some(at, carry):
        parts = [pieces_ref[at * run + index] for index in range(run)]
        into = pl.ds(pl.multiple_of(at * run * size, LANES), run * size)
        flat_ref[:, into] = jnp.concatenate(parts, 1)
        return carry

    lax.fori_loop(0, count // run, some, 0)


def join_pieces(pieces):
    count, rows, size = pieces.shape
    if count % run_length(size):
        return pieces.transpose(1, 0, 2).reshape(rows, count * size)
    return pl.pallas_call(
        join_kernel,
        out_shape=jax.ShapeDtypeStruct((rows, count * size), pieces.dtype),
        compiler_params=params(0),
        name="join_pieces",
    )(pieces)


def split_kernel(*refs):
    sources, pieces_ref, flat_ref = refs[:-2], refs[-2], refs[-1]
    count, _, size = pieces_ref.shape
    run = run_length(size)
    start = 0
    for first_ref, second_ref in zip(sources[::2], sources[1::2]):
        width = first_ref.shape[1]
        both = first_ref[...].astype(F32) + second_ref[...].astype(F32)
        flat_ref[:, start : start + width] = both.astype(BF)
        start += width

    def some(at, carry):
        block = flat_ref[:, pl.ds(pl.multiple_of(at * run * size, LANES), run * size)]
        for index in range(run):
            pieces_ref[at * run + index] = block[:, index * size : (index + 1) * size]
        return carry

    lax.fori_loop(0, count // run, some, 0)


def split_sums(pairs, count):
    rows = pairs[0].shape[0]
    total = sum(item.shape[1] for item in pairs[::2])
    return pl.pallas_call(
        split_kernel,
        out_shape=jax.ShapeDtypeStruct((count, rows, total // count), BF),
        scratch_shapes=[pltpu.VMEM((rows, total), BF)],
        compiler_params=params(0, 42 * MIB),
        name="split_sums",
    )(*pairs)


def unit_loop(plan, work):
    fsdp, seq, folds, local = plan
    run = run_length(local)

    def some(at, carry):
        span = run * seq * folds * local
        block = pl.ds(pl.multiple_of(at * span, LANES), span)
        folded = [
            pl.ds(pl.multiple_of(fold * fsdp * local + at * run * local, LANES), run * local) for fold in range(folds)
        ]
        work(run, block, folded)
        return carry

    lax.fori_loop(0, fsdp // run, some, 0)


def take_units_kernel(plan, place_ref, all_ref, *refs):
    own_ref = refs[-1]
    _, seq, folds, local = plan
    spot = place_ref[0]

    def work(run, block, folded):
        values = all_ref[:, block]
        for fold, into in enumerate(folded):
            parts = []
            for index in range(run):
                base = (index * seq * folds + fold) * local
                part = values[:, base : base + local]
                for other in range(1, seq):
                    shift = base + other * folds * local
                    part = jnp.where(spot == other, values[:, shift : shift + local], part)
                parts.append(part)
            own_ref[:, into] = jnp.concatenate(parts, 1)

    unit_loop(plan, work)
    if len(refs) == 2:
        model = refs[0].shape[1]
        hidden = own_ref.shape[1] - folds * model
        for fold in range(folds):
            rows = pl.ds(pl.multiple_of((spot * folds + fold) * local, 16), local)
            own_ref[:, hidden + fold * model : hidden + (fold + 1) * model] = refs[0][rows, :]


def take_units(plan, places, matrix, low=None):
    _, seq, folds, local = plan
    rows, width = matrix.shape
    extra = [] if low is None else [low]
    out_width = width // seq + sum(folds * item.shape[1] for item in extra)
    return pl.pallas_call(
        partial(take_units_kernel, plan),
        in_specs=[smem()] + [pl.BlockSpec(memory_space=pltpu.VMEM)] * (1 + len(extra)),
        out_shape=jax.ShapeDtypeStruct((rows, out_width), matrix.dtype),
        compiler_params=params(0),
        name="take_units",
    )(places, matrix, *extra)


def collect_kernel(plan, blocks, place_ref, *refs):
    parts, squares, refs = refs[:blocks], refs[blocks : 2 * blocks], refs[2 * blocks :]
    feeds = [refs[at : at + 4] for at in range(0, len(refs) - 12, 4)]
    (
        other_ref, lat_ref, flat_ref, down_text_ref, text_ref, w_ref,
        mine_ref, theirs_ref, text_grad_ref, down_all, upper_all, unit_acc,
    ) = refs[-12:]
    _, seq, folds, local = plan
    rank = mine_ref.shape[0]
    model = text_ref.shape[1]
    wide = other_ref.shape[2]
    spot = place_ref[0]
    own = pl.ds(pl.multiple_of(spot * wide, wide), wide)

    def total(items, rows):
        value = items[0][rows, :]
        for item in items[1:]:
            value = value + item[rows, :]
        return value

    moved = []
    for part in range(2):
        value = parts[0][part, :, own]
        for item in parts[1:]:
            value = value + item[part, :, own]
        moved.append((value + other_ref[part].astype(F32)).astype(BF))
    moved = jnp.concatenate(moved, 1)
    glat = mm_nt(moved, flat_ref[...]).astype(BF)
    gup = mm_tn(lat_ref[...], moved)
    gdown = mm_tn(glat, text_ref[...])
    text_grad_ref[...] = (mm_nt(moved, w_ref[...]) + mm(glat, down_text_ref[...])).astype(BF)

    upper_all[:, 2 * model : 4 * model] = jnp.zeros((rank, 2 * model), BF)
    for part in range(2):
        rows = slice(part * rank, (part + 1) * rank)
        down_all[:, (2 + part) * model : (3 + part) * model] = gdown[rows].astype(BF)
        into = pl.ds(pl.multiple_of((2 + part) * model + spot * wide, LANES), wide)
        upper_all[:, into] = gup[rows, part * wide : (part + 1) * wide].astype(BF)
    for index, at in enumerate((0, 1, 4)):
        cols = slice(at * model, (at + 1) * model)
        down_all[:, cols] = total(squares, slice(2 * index * rank, (2 * index + 1) * rank)).astype(BF)
        upper_all[:, cols] = total(squares, slice((2 * index + 1) * rank, (2 * index + 2) * rank)).astype(BF)
    every = slice(0, rank)
    down_all[:, 5 * model : 6 * model] = total([item[0] for item in feeds], every).astype(BF)
    upper_all[:, upper_all.shape[1] - model :] = total([item[3] for item in feeds], every).astype(BF)
    for into_ref, start, which in ((upper_all, 5 * model, 1), (down_all, 6 * model, 2)):
        unit_acc[...] = total([item[which] for item in feeds], every)

        def work(run, block, folded):
            values = [unit_acc[:, cols] for cols in folded]
            spread = []
            for index in range(run):
                for other in range(seq):
                    for fold in range(folds):
                        part = values[fold][:, index * local : (index + 1) * local]
                        spread.append(jnp.where(spot == other, part, 0.0))
            at = pl.ds(pl.multiple_of(start + block.start, LANES), block.size)
            into_ref[:, at] = jnp.concatenate(spread, 1).astype(BF)

        unit_loop(plan, work)
    share(place_ref, down_all, upper_all, mine_ref, theirs_ref)


def collect(plan, places, parts, squares, feeds, other, lat_text, flat_text, down_text, text, packed, start):
    rank = squares[0].shape[0] // 6
    model = text.shape[1]
    hidden = feeds[0][1].shape[1]
    wide2 = flat_text.shape[1]
    width = 6 * model + hidden * plan[1]
    weight, spec = window(packed, start, wide2)
    feeds = [item for feed in feeds for item in feed]
    before = list(parts) + list(squares) + feeds + [other, lat_text, flat_text, down_text, text]
    table = jax.ShapeDtypeStruct((rank, width), BF)
    shapes = [table, table, jax.ShapeDtypeStruct(text.shape, BF)]
    return pl.pallas_call(
        partial(collect_kernel, plan, len(parts)),
        grid=(1,),
        in_specs=[smem()] + [whole(item.shape) for item in before] + [spec],
        out_specs=[whole(item.shape) for item in shapes],
        out_shape=shapes,
        scratch_shapes=[pltpu.VMEM(table.shape, BF)] * 2 + [pltpu.VMEM((rank, hidden), F32)],
        compiler_params=params(1),
        cost_estimate=cost(4 * text.shape[0] * model * wide2, 2 * model * wide2),
        name="collect",
    )(places, *before, weight)


def both_kernel(place_ref, mine_ref, other_ref, down_ref, upper_ref):
    first = place_ref[0] == 0
    for at in range(mine_ref.shape[0]):
        mine, other = mine_ref[at].astype(F32), other_ref[at].astype(F32)
        down_ref[at] = jnp.where(first, mine, other)
        upper_ref[at] = jnp.where(first, other, mine)


def both_tables(places, mine, other):
    return pl.pallas_call(
        both_kernel,
        in_specs=[smem()] + [pl.BlockSpec(memory_space=pltpu.VMEM)] * 2,
        out_shape=[jax.ShapeDtypeStruct(mine.shape, F32)] * 2,
        compiler_params=params(0, 42 * MIB),
        name="both_tables",
    )(places, mine, other)


def body(
    inputs,
    text_states,
    adapter_index,
    norm_gains,
    norm_biases,
    self_in,
    self_out,
    cross_query,
    cross_text,
    cross_out,
    hidden_in,
    hidden_out,
    adapter_down,
    adapter_up,
    cotangent,
    *,
    sizes,
):
    seq, fsdp = sizes
    spot = lax.axis_index("seq")
    first_here = spot == 0
    there = (seq - 1) - spot
    local = self_in.shape[0]
    depth = hidden_out.shape[0] // seq
    pair = seq == 2 and depth % local == 0 and fsdp % run_length(local) == 0
    model = inputs.shape[2]
    rows = inputs.shape[1]
    frames = rows * seq
    wide = model // seq
    hidden_all = hidden_in.shape[1]
    hidden = hidden_all // seq
    adapters, rank, piece = adapter_down.shape
    total = piece * fsdp

    blocks = max(rows // 256, 1)
    size = rows // blocks

    def swap(value):
        return lax.ppermute(value, "seq", [(0, 1), (1, 0)])

    def pick(value, axis, extent, which=None):
        return lax.dynamic_slice_in_dim(value, (spot if which is None else which) * extent, extent, axis)

    def ordered(mine, other):
        return jnp.where(first_here, mine, other), jnp.where(first_here, other, mine)

    def gather(value, axis):
        if pair:
            return jnp.concatenate(ordered(value, swap(value)), axis)
        return lax.all_gather(value, "seq", axis=axis, tiled=True)

    def after(value, *others):
        return lax.optimization_barrier((value,) + others)[0]

    def put(value, axis):
        shape = list(value.shape)
        shape[axis] = seq
        return lax.dynamic_update_slice_in_dim(jnp.zeros(shape, value.dtype), value, spot, axis)

    def own_columns(matrix, parts):
        return [pick(matrix[:, at * model : (at + 1) * model], 1, wide) for at in range(parts)]

    def flat_down(grads, parts):
        return jnp.concatenate([grads[at * rank : (at + 1) * rank] for at in range(parts)], 1)

    def flat_upper(own):
        return put(jnp.stack(own, 1)[:, :, None], 2).reshape(rank, len(own) * model)

    squares_here = [cross_out, cross_query] + [pick(self_out, 1, wide) if pair else self_out]
    first = squares_here + own_columns(self_in, 3) + own_columns(cross_text, 2)
    edges = [0]
    for item in first:
        edges.append(edges[-1] + item.shape[1])
    start_in, start_text = edges[3], edges[6]
    packed = lax.all_gather(jnp.concatenate(first, 1), "fsdp", axis=0, tiled=True)
    squares_plan = ((edges[2], None), (edges[1], None), (edges[0], None))
    if pair:
        squares_plan = ((edges[2], 1),) + squares_plan[1:]
    core = lax.rem(lax.axis_index("fsdp"), 2)
    where_here = jnp.stack([spot, there, core, 1 - core]).astype(jnp.int32)
    if pair:
        folds = depth // local
        plan = (fsdp, seq, folds, local)
        own_units = partial(take_units, plan, where_here)
        packed_feed = lax.all_gather(own_units(hidden_in, hidden_out), "fsdp", axis=0, tiled=True)

        def feed_weights(block):
            per = model // block
            return (
                packed_feed,
                pl.BlockSpec((model, block), lambda at: (0, at)),
                packed_feed,
                pl.BlockSpec((block, model), lambda at: (at % per, folds + at // per)),
            )
    else:

        def own_units(matrix):
            kept = lax.dynamic_index_in_dim(matrix.reshape(-1, fsdp, seq, depth), spot, 2, False)
            return kept.reshape(-1, hidden)

        def all_units(matrix):
            return put(matrix.reshape(-1, fsdp, 1, depth), 2).reshape(-1, hidden_all)

        whole_in = lax.all_gather(own_units(hidden_in), "fsdp", axis=0, tiled=True)
        whole_out = lax.all_gather(pick(hidden_out, 0, depth), "fsdp", axis=0, tiled=True)

        def feed_weights(block):
            return (
                whole_in,
                pl.BlockSpec((model, block), lambda at: (0, at)),
                whole_out,
                pl.BlockSpec((block, model), lambda at: (at, 0)),
            )

    index_all = lax.all_to_all(jnp.broadcast_to(adapter_index, (fsdp,)), "fsdp", 0, 0, tiled=True)
    if pair:
        table = jnp.where(first_here, adapter_down, adapter_up)
        mine = join_pieces(lax.all_to_all(jnp.take(table, index_all, axis=0), "fsdp", 0, 0, tiled=True))
        down_all, upper_all = ordered(mine, swap(mine))
    else:
        table = jnp.concatenate([adapter_down, adapter_up], 1)
        chosen = join_pieces(lax.all_to_all(jnp.take(table, index_all, axis=0), "fsdp", 0, 0, tiled=True))
        down_all, upper_all = chosen[:rank], chosen[rank:]
    in_cuts = [0, 3 * model, 4 * model, 5 * model, 7 * model, 8 * model, 9 * model, 9 * model + hidden_all]
    out_cuts = [0, 3 * model, 4 * model, 5 * model, 7 * model, 8 * model, 8 * model + hidden_all, 9 * model + hidden_all]
    downs = [down_all[:, in_cuts[at] : in_cuts[at + 1]] for at in range(7)]
    uppers = [upper_all[:, out_cuts[at] : out_cuts[at + 1]] for at in range(7)]

    def part_down(matrix, parts):
        return jnp.concatenate([matrix[:, at * model : (at + 1) * model] for at in range(parts)], 0)

    def part_upper(matrix, parts):
        own = own_columns(matrix, parts)
        return jnp.stack(
            [jnp.pad(item, ((at * rank, (parts - 1 - at) * rank), (0, 0))) for at, item in enumerate(own)], 0
        )

    units = own_units(jnp.concatenate([uppers[5], downs[6]], 0))
    feed_adapters = (downs[5], units[:rank], units[rank:], uppers[6])
    square_adapters = jnp.concatenate([downs[1], uppers[1], downs[2], uppers[2], downs[4], uppers[4]], 0)
    down_qkv, upper_qkv = part_down(downs[0], 3), part_upper(uppers[0], 3)
    down_text, upper_text = part_down(downs[3], 2), part_upper(uppers[3], 2)
    flat_text = jnp.concatenate([upper_text[0], upper_text[1]], 1)

    frames_in = inputs[0]
    cot = cotangent[0]
    if pair:
        frames_parts = [frames_in, swap(frames_in)]
        cot_other = swap(after(cot, frames_parts[1]))
    else:
        frames_parts = [lax.all_gather(frames_in, "seq", axis=0, tiled=True)]
    norm_places = where_here if pair else jnp.zeros((4,), jnp.int32)
    if pair:
        frames_parts[1] = after(frames_parts[1], cot_other, units)
    normed1, lat_qkv = norm_project(norm_places, frames_parts, norm_gains[0:1], norm_biases[0:1], down_qkv)
    packed = after(packed, normed1)
    sources = [packed]
    if pair:
        half = model // 2
        straight = swap(lax.dynamic_slice(packed, (core * half, edges[2]), (half, wide)))
    triple = qkv_project(normed1, lat_qkv, upper_qkv, packed, start_in, 3 * wide)
    padded = -(-wide // LANES) * LANES
    if padded != wide:
        triple = jnp.pad(triple.reshape(frames, 3, wide), ((0, 0), (0, 0), (0, padded - wide)))
        triple = triple.reshape(frames, 3 * padded)
    text = after(text_states[0], triple)
    w_text = packed[:, start_text : start_text + 2 * wide]
    lat_text = mm_nt(text, down_text).astype(BF)
    memory = (mm(text, w_text) + mm(lat_text, flat_text)).astype(BF)
    head_out, probs, *leaving = attend(where_here, [size] * blocks if pair else [], after(triple, memory), padded)

    if pair:
        neighbours = [(at, at ^ 1) for at in range(fsdp)]
        sources += [straight, lax.ppermute(after(straight, head_out), "fsdp", neighbours)]

    memory_all = gather(memory.reshape(-1, 2, wide), 2)
    keys, values = memory_all[:, 0], memory_all[:, 1]

    constants = (sources, squares_plan, square_adapters, norm_gains, norm_biases, keys, values)
    if pair:
        received = [swap(leaving[0])]
        for item in leaving[1:]:
            received.append(swap(after(item, received[-1])))
    else:
        natural = lax.all_to_all(head_out[:, :wide], "seq", split_axis=0, concat_axis=1, tiled=True)
    made = []
    for at in range(blocks):
        if pair:
            own, spec, others = head_out, (size, wide), [received[at]]
        else:
            own, spec, others = natural, (size, model), []
        ready = after(frames_in, made[-1][7]) if made else frames_in
        made.append(middle(where_here if pair else jnp.zeros((4,), jnp.int32), own, spec, others, ready, at, blocks, *constants))
    normed3 = [item[7] for item in made]
    resid2 = [item[6] for item in made]

    feed_tail = feed_adapters + (feed_weights, hidden)
    if pair:
        others = [swap(item) for item in normed3]
        ours = [feed_forward(normed3[:1], resid2[:1], cot, 0, *feed_tail, F32)]
        theirs = feed_forward([others[0], after(others[1], ours[0][0])] if blocks > 1 else others, [], cot_other, 0, *feed_tail, BF)
        out_leaving, gu_leaving = theirs[:blocks], theirs[blocks : 2 * blocks]
        gu_more = [swap(gu_leaving[0])]
        for at in range(1, blocks):
            ours.append(feed_forward([after(normed3[at], gu_leaving[0])], [resid2[at]], cot, at, *feed_tail, F32))
            gu_more.append(swap(after(gu_leaving[at], gu_more[-1], ours[-1][0])))
        gu = [item[1] for item in ours]
        out_more = []
        feed_grads = [item[2:] for item in ours] + [theirs[2 * blocks :]]
    else:
        wide_in = gather(jnp.concatenate(normed3, 0), 0)
        all_out = feed_forward([wide_in], [], gather(cot, 0), 0, *feed_tail, F32)
        summed = [
            lax.psum_scatter(item.astype(BF), "seq", scatter_dimension=0, tiled=True) for item in all_out[:2]
        ]
        output = (jnp.concatenate(resid2, 0) + summed[0].astype(F32)).astype(BF)
        gu = [summed[1][at * size : (at + 1) * size] for at in range(blocks)]
        gu_more = [jnp.zeros_like(item) for item in gu]
        feed_grads = [all_out[2:]]

    pieces, resid1_grads, memory_parts, square_parts = [], [], [], []
    for at in range(blocks):
        gu_here = gu[at] if at == 0 else after(gu[at], result[-3])
        kept = made[at][:7] + made[at][8:9]
        result = middle_back(
            where_here, 2 if pair else 1, at, cot, gu_here, gu_more[at],
            kept, sources, squares_plan, square_adapters, norm_gains, keys, values,
        )
        if pair:
            waited = [pieces[-1][1]] if at else []
            if at == 0:
                out_more.append(swap(after(out_leaving[0], result[0])))
            if at == blocks - 1:
                memory_part = sum(memory_parts, result[-2]).astype(BF)
                memory_other = swap(after(pick(memory_part, 2, wide, there), *out_more))
                waited.append(memory_other)
            pieces.append((result[0], swap(after(result[1], *waited) if waited else result[1])))
        else:
            pieces.append(result[0])
        resid1_grads.append(result[-3])
        memory_parts.append(result[-2])
        square_parts.append(result[-1])
    resid1_grad = jnp.concatenate(resid1_grads, 0)
    square_grads = sum(square_parts[1:], square_parts[0])

    if pair:
        early, early_leaving, text_low = collect(
            plan, where_here, memory_parts, square_parts, feed_grads, memory_other, lat_text, flat_text, down_text,
            text_states[0], packed, start_text,
        )
        grad_pieces = [item[0] for item in pieces] + [item[1] for item in pieces]
    else:
        head_grad = lax.all_to_all(jnp.concatenate(pieces, 0), "seq", split_axis=1, concat_axis=0, tiled=True)
        grad_pieces = [jnp.pad(head_grad, ((0, 0), (0, padded - wide)))]
    triple_grad = attend_back(where_here, triple, head_out, grad_pieces, probs, padded)[:, :, :wide]
    if pair:
        early_other = swap(after(early_leaving, pieces[-1][1]))
        for at in range(1, blocks):
            out_more.append(swap(after(out_leaving[at], early_other, triple_grad)))
        glat_qkv, late, late_leaving = qkv_grads(
            where_here, after(triple_grad, early_other), normed1, lat_qkv, upper_qkv
        )
        late_other = swap(late_leaving)
    else:
        glat_qkv = sum(mm_nt(triple_grad[at], upper_qkv[at]) for at in range(3)).astype(BF)
        gdown_qkv = mm_tn(glat_qkv, normed1)
        gup_qkv = [mm_tn(lat_qkv[:, at * rank : (at + 1) * rank], triple_grad[at]) for at in range(3)]
    back = partial(qkv_back, gradient=triple_grad, glat=glat_qkv, down=down_qkv, packed=packed, start=start_in)
    if pair:
        for_them = back(there[None], rows, kind=BF)
        for_us = back(after(spot, for_them, *out_more)[None], rows, kind=F32)
        input_grad = last_norm(frames_in, for_us, swap(for_them), norm_gains[0:1], resid1_grads)
        output = jnp.concatenate(
            [(item[0] + other.astype(F32)).astype(BF) for item, other in zip(ours, out_more)], 0
        )
    else:
        full = back(jnp.zeros((1,), jnp.int32), frames, kind=BF)
        normed1_grad = lax.psum_scatter(full, "seq", scatter_dimension=0, tiled=True).astype(F32)
        resid1_grad = jnp.concatenate(resid1_grads, 0)
        input_grad = resid1_grad + norm_back(frames_in.astype(F32), norm_gains[0:1], normed1_grad)

    selector = (index_all[None, :] == jnp.arange(adapters, dtype=jnp.int32)[:, None]).astype(BF)

    def by_adapter(sent, *others):
        received = lax.all_to_all(sent, "fsdp", 0, 0, tiled=True)
        chooser = after(selector, *others) if others else selector
        return jnp.einsum("ac,crw->arw", chooser, received, preferred_element_type=F32)

    if pair:
        shares = by_adapter(split_sums([after(late, for_them), late_other, early, early_other], fsdp), for_us).astype(BF)
        grad_down, grad_up = both_tables(where_here, shares, swap(shares))
        text_total = text_low.astype(F32) + swap(text_low).astype(F32)
    else:
        memory_part = sum(memory_parts[1:], memory_parts[0]).astype(BF)
        memory_grad = lax.psum_scatter(memory_part, "seq", scatter_dimension=2, tiled=True)
        memory_flat = jnp.concatenate([memory_grad[0], memory_grad[1]], 1)
        glat_text = mm_nt(memory_flat, flat_text).astype(BF)
        gup_text = mm_tn(lat_text, memory_flat)
        gdown_text = mm_tn(glat_text, text)
        text_low = (mm_nt(memory_flat, w_text) + mm(glat_text, down_text)).astype(BF)
        own_text = [gup_text[at * rank : (at + 1) * rank, at * wide : (at + 1) * wide] for at in range(2)]
        gdown_in, gup_in, gdown_out, gup_out = feed_grads[0]
        square_grads = sum(square_parts[1:], square_parts[0])
        squares = [square_grads[rank * at : rank * (at + 1)] for at in range(6)]
        down_sent = [flat_down(gdown_qkv, 3), squares[0], squares[2], flat_down(gdown_text, 2), squares[4], gdown_in]
        upper_sent = [flat_upper(gup_qkv), squares[1], squares[3], flat_upper(own_text), squares[5]]
        down_sent = jnp.concatenate(down_sent + [all_units(gdown_out)], 1)
        upper_sent = jnp.concatenate(upper_sent + [all_units(gup_in), gup_out], 1)
        sent = jnp.concatenate([down_sent, upper_sent], 0).astype(BF).reshape(2 * rank, fsdp, piece).transpose(1, 0, 2)
        shares = lax.psum(by_adapter(sent).astype(BF), "seq")
        grad_down, grad_up = shares[:, :rank], shares[:, rank:]
        text_total = lax.psum(text_low, "seq").astype(F32)
    return (output[None], input_grad[None], text_total[None], grad_down.astype(F32), grad_up.astype(F32))


def solution(mesh):
    return jax.shard_map(
        partial(body, sizes=(mesh.shape["seq"], mesh.shape["fsdp"])),
        mesh=mesh,
        in_specs=(
            P("fsdp", "seq", None),
            P("fsdp", None, None),
            P("fsdp"),
            P(),
            P(),
            P("fsdp", None),
            P("fsdp", None),
            P("fsdp", None),
            P("fsdp", None),
            P("fsdp", None),
            P("fsdp", None),
            P("fsdp", None),
            P(None, None, "fsdp"),
            P(None, None, "fsdp"),
            P("fsdp", "seq", None),
        ),
        out_specs=(
            P("fsdp", "seq", None),
            P("fsdp", "seq", None),
            P("fsdp", None, None),
            P(None, None, "fsdp"),
            P(None, None, "fsdp"),
        ),
        check_vma=False,
    )
```

```python
from functools import partial

import jax
import jax.numpy as jnp
from jax import lax
from jax.experimental import pallas as pl
from jax.experimental.pallas import tpu as pltpu
from jax.sharding import PartitionSpec as P

HEAD = 64
LANES = 128
QB = 256
BF = jnp.bfloat16
F32 = jnp.float32
SCALE = float(HEAD) ** (-0.5)
SQRT_HALF = 0.7071067811865476
INV_SQRT_2PI = 0.3989422804014327
MIB = 1024 * 1024
VMEM_LIMIT = 60 * MIB
COST = 1.0
FEED_BLOCK = 512


def mm(a, b):
    return lax.dot_general(a, b, (((1,), (0,)), ((), ())), preferred_element_type=F32)


def mm_nt(a, b):
    return lax.dot_general(a, b, (((1,), (1,)), ((), ())), preferred_element_type=F32)


def mm_tn(a, b):
    return lax.dot_general(a, b, (((0,), (0,)), ((), ())), preferred_element_type=F32)


def norm_stats(values):
    centered = values - jnp.mean(values, -1, keepdims=True)
    variance = jnp.mean(centered * centered, -1, keepdims=True)
    inverse = lax.rsqrt(variance + 1e-05)
    return centered * inverse, inverse


def layer_norm(values, gains, biases):
    unit, _ = norm_stats(values)
    return unit * gains + biases


def norm_back(values, gains, gradient):
    unit, inverse = norm_stats(values)
    scaled = gradient * gains
    mean_one = jnp.mean(scaled, -1, keepdims=True)
    mean_two = jnp.mean(scaled * unit, -1, keepdims=True)
    return inverse * (scaled - mean_one - unit * mean_two)


def whole(shape):
    return pl.BlockSpec(shape, lambda *_: (0,) * len(shape))


def once(shape):
    return pl.BlockSpec(shape, lambda *_: (0,) * len(shape), pipeline_mode=pl.Buffered(1))


def params(count=1, limit=None):
    return pltpu.CompilerParams(
        dimension_semantics=("arbitrary",) * count if count else None, vmem_limit_bytes=limit or VMEM_LIMIT
    )


def cost(flops, moved, special=0):
    return pl.CostEstimate(
        flops=int(flops * COST), bytes_accessed=int(moved * COST), transcendentals=int(special * COST)
    )


def window(packed, start, width, rows=None, steps=1, step=0):
    block = width // steps
    rows = packed.shape[0] if rows is None else rows
    if start % block == 0 and block % LANES == 0:
        base = start // block
        return packed, pl.BlockSpec((rows, block), lambda *at: (0, base + (at[step] if steps > 1 else 0)))
    return packed[:, start : start + width], pl.BlockSpec(
        (rows, block), lambda *at: (0, at[step] if steps > 1 else 0)
    )


def norm_kernel(place_ref, *refs):
    count = len(refs) - 5
    parts, (gain_ref, bias_ref, down_ref, normed_ref, lat_ref) = refs[:count], refs[count:]
    step = 128
    for index, part_ref in enumerate(parts):
        base = place_ref[index] * part_ref.shape[0]

        def some(at, carry):
            rows = pl.ds(pl.multiple_of(at * step, step), step)
            into = pl.ds(pl.multiple_of(base + at * step, step), step)
            normed = layer_norm(part_ref[rows, :].astype(F32), gain_ref[...], bias_ref[...]).astype(BF)
            normed_ref[into, :] = normed
            lat_ref[into, :] = mm_nt(normed, down_ref[...]).astype(BF)
            return carry

        lax.fori_loop(0, part_ref.shape[0] // step, some, 0)


def smem():
    return pl.BlockSpec(memory_space=pltpu.SMEM)


def norm_project(places, parts, gains, biases, down):
    model = parts[0].shape[1]
    frames = sum(part.shape[0] for part in parts)
    ranks = down.shape[0]
    return pl.pallas_call(
        norm_kernel,
        in_specs=[smem()] + [whole(item.shape) for item in parts + [gains, biases, down]],
        out_specs=[whole((frames, model)), whole((frames, ranks))],
        out_shape=[jax.ShapeDtypeStruct((frames, model), BF), jax.ShapeDtypeStruct((frames, ranks), BF)],
        grid=(1,),
        compiler_params=params(1),
        cost_estimate=cost(2 * frames * model * ranks, 4 * frames * model),
        name="norm_project",
    )(places, *parts, gains, biases, down)


def qkv_kernel(normed_ref, lat_ref, up_ref, w_ref, out_ref):
    step = 256

    def some(at, carry):
        rows = pl.ds(pl.multiple_of(at * step, step), step)
        out_ref[rows, :] = (mm(normed_ref[rows, :], w_ref[...]) + mm(lat_ref[rows, :], up_ref[...])).astype(BF)
        return carry

    lax.fori_loop(0, normed_ref.shape[0] // step, some, 0)


def qkv_project(normed, latent, up, packed, start, width):
    row_count, model = normed.shape
    ranks = latent.shape[1]
    steps = 3 if (width // 3) % LANES == 0 else 1
    operand, spec = window(packed, start, width, steps=steps)
    block = width // steps
    if steps == 3:
        up_spec = pl.BlockSpec((None, ranks, block), lambda at: (at, 0, 0))
    else:
        up = up.transpose(1, 0, 2).reshape(ranks, width)
        up_spec = whole(up.shape)
    return pl.pallas_call(
        qkv_kernel,
        grid=(steps,),
        in_specs=[whole(normed.shape), whole(latent.shape), up_spec, spec],
        out_specs=pl.BlockSpec((row_count, block), lambda at: (0, at)),
        out_shape=jax.ShapeDtypeStruct((row_count, width), BF),
        compiler_params=params(1, 42 * MIB),
        cost_estimate=cost(2 * row_count * model * width, 2 * (row_count + width) * model),
        name="qkv_project",
    )(normed, latent, up, operand)


def tri_start(at):
    return QB * at * (at + 1) // 2


def attend_kernel(place_ref, q_ref, k_ref, v_ref, out_ref, prob_ref, *refs):
    sent, (val_t_ref, out_t_ref) = refs[:-2], refs[-2:]
    frames = q_ref.shape[0]
    lane = lax.broadcasted_iota(jnp.int32, (1, LANES), 1) // HEAD
    val_t_ref[...] = v_ref[...].T
    square = (QB, QB)
    keep_tri = lax.broadcasted_iota(jnp.int32, square, 0) <= lax.broadcasted_iota(jnp.int32, square, 1)

    def scores(half, at):
        stop = (at + 1) * QB
        query = q_ref[at * QB : stop, :] * jnp.where(lane == half, SCALE, 0.0).astype(BF)
        last = jnp.where(keep_tri, mm_nt(k_ref[stop - QB : stop, :], query), -1e30)
        if at == 0:
            return last
        return jnp.concatenate([mm_nt(k_ref[0 : stop - QB, :], query), last], 0)

    turns = [(half, at) for at in range(frames // QB) for half in range(2)]
    score = scores(*turns[0])
    for index, (half, at) in enumerate(turns):
        stop = (at + 1) * QB
        own = slice(half * HEAD, (half + 1) * HEAD)
        later = scores(*turns[index + 1]) if index + 1 < len(turns) else None
        raised = jnp.exp(score - jnp.max(score, 0, keepdims=True))
        prob = (raised * (1.0 / jnp.sum(raised, 0, keepdims=True))).astype(BF)
        prob_ref[half, tri_start(at) : tri_start(at) + stop, :] = prob
        out_t_ref[own, at * QB : stop] = mm(val_t_ref[own, 0:stop], prob)
        score = later
    out_ref[...] = out_t_ref[...].T.astype(BF)
    for index, sent_ref in enumerate(sent):
        size = sent_ref.shape[0]
        at = place_ref[1] * len(sent) + index
        sent_ref[...] = out_ref[pl.ds(pl.multiple_of(at * size, size), size), :]


def pair_specs(frames, width):
    pairs = width // LANES
    return [pl.BlockSpec((frames, LANES), lambda at, part=part: (0, part * pairs + at)) for part in range(3)]


def attend(places, sizes, triple, width):
    frames = triple.shape[0]
    pairs = width // LANES
    tri = tri_start(frames // QB)
    return pl.pallas_call(
        attend_kernel,
        grid=(pairs,),
        in_specs=[smem()] + pair_specs(frames, width),
        out_specs=[
            pl.BlockSpec((frames, LANES), lambda at: (0, at)),
            pl.BlockSpec((2, tri, QB), lambda at: (at, 0, 0)),
        ]
        + [pl.BlockSpec((size, LANES), lambda at: (0, at)) for size in sizes],
        out_shape=[
            jax.ShapeDtypeStruct((frames, width), BF),
            jax.ShapeDtypeStruct((2 * pairs, tri, QB), BF),
        ]
        + [jax.ShapeDtypeStruct((size, width), BF) for size in sizes],
        scratch_shapes=[pltpu.VMEM((LANES, frames), BF), pltpu.VMEM((LANES, frames), F32)],
        compiler_params=params(1),
        cost_estimate=cost(
            8 * tri * QB * HEAD * pairs, 2 * (4 * frames * width + 2 * pairs * tri * QB), 2 * pairs * tri * QB
        ),
        name="attend",
    )(places, triple, triple, triple)


def attend_back_kernel(place_ref, q_ref, k_ref, v_ref, out_ref, prob_ref, *refs):
    pieces, (back_ref, grad_ref, key_t_ref, dq_t_ref, dk_acc, dv_acc) = refs[:-6], refs[-6:]
    frames = q_ref.shape[0]
    for index, piece_ref in enumerate(pieces):
        size = piece_ref.shape[0]
        count = max(len(pieces) // 2, 1)
        at = place_ref[index // count] * count + index % count if len(pieces) > 1 else 0
        grad_ref[pl.ds(pl.multiple_of(at * size, size), size), :] = piece_ref[...]
    lane = lax.broadcasted_iota(jnp.int32, (1, LANES), 1) // HEAD
    key_t_ref[...] = k_ref[...].T
    dk_acc[...] = jnp.zeros_like(dk_acc)
    dv_acc[...] = jnp.zeros_like(dv_acc)
    turns = [(half, at) for at in range(frames // QB) for half in range(2)]

    def start(half, at):
        rows = slice(at * QB, (at + 1) * QB)
        grad = grad_ref[rows, :] * jnp.where(lane == half, 1.0, 0.0).astype(BF)
        return grad, mm_nt(v_ref[0 : (at + 1) * QB, :], grad)

    ready = start(*turns[0])
    for index, (half, at) in enumerate(turns):
        stop = (at + 1) * QB
        rows = slice(at * QB, stop)
        own = slice(half * HEAD, (half + 1) * HEAD)
        grad, prob_grad = ready
        if half == 0:
            product = (out_ref[rows, :].astype(F32) * grad_ref[rows, :].astype(F32)).T
        if index + 1 < len(turns):
            ready = start(*turns[index + 1])
        query = q_ref[rows, :] * jnp.where(lane == half, SCALE, 0.0).astype(BF)
        delta = jnp.sum(product[own, :], 0, keepdims=True)
        prob = prob_ref[half, tri_start(at) : tri_start(at) + stop, :]
        dv_acc[0:stop, :] += mm(prob, grad)
        score_grad = (prob.astype(F32) * (prob_grad - delta)).astype(BF)
        dk_acc[0:stop, :] += mm(score_grad, query)
        dq_t_ref[own, rows] = mm(key_t_ref[own, 0:stop], score_grad)
    back_ref[0] = (dq_t_ref[...].T * SCALE).astype(BF)
    back_ref[1] = dk_acc[...].astype(BF)
    back_ref[2] = dv_acc[...].astype(BF)


def attend_back(places, triple, attended, pieces, probs, width):
    frames = triple.shape[0]
    pairs = width // LANES
    tri = tri_start(frames // QB)
    column = pl.BlockSpec((frames, LANES), lambda at: (0, at))
    return pl.pallas_call(
        attend_back_kernel,
        grid=(pairs,),
        in_specs=[smem()]
        + pair_specs(frames, width)
        + [column, pl.BlockSpec((2, tri, QB), lambda at: (at, 0, 0))]
        + [pl.BlockSpec((piece.shape[0], LANES), lambda at: (0, at)) for piece in pieces],
        out_specs=pl.BlockSpec((3, frames, LANES), lambda at: (0, 0, at)),
        out_shape=jax.ShapeDtypeStruct((3, frames, width), BF),
        scratch_shapes=[
            pltpu.VMEM((frames, LANES), BF),
            pltpu.VMEM((LANES, frames), BF),
            pltpu.VMEM((LANES, frames), F32),
            pltpu.VMEM((frames, LANES), F32),
            pltpu.VMEM((frames, LANES), F32),
        ],
        compiler_params=params(1, 42 * MIB),
        cost_estimate=cost(16 * tri * QB * HEAD * pairs, 2 * (8 * frames * width + 2 * pairs * tri * QB)),
        name="attend_back",
    )(places, triple, triple, triple, attended, probs, *pieces)


def feed_kernel(count, based, *refs):
    pieces, refs = refs[:count], refs[count:]
    bases, refs = refs[:based], refs[based:]
    cot_ref, down_in_ref, up_in_ref, down_out_ref, up_out_ref, w_in_ref, w_out_ref = refs[:7]
    out_refs, gu_refs, refs = refs[7 : 7 + count], refs[7 + count : 7 + 2 * count], refs[7 + 2 * count :]
    (
        gdown_in_ref, gup_in_ref, gdown_out_ref, gup_out_ref, normed_ref,
        out_acc, gu_acc, lat_in, glat_out, lat_acc, glat_acc, lat_t, glat_t,
    ) = refs
    at = pl.program_id(0)

    @pl.when(at == 0)
    def _():
        start = 0
        for piece_ref in pieces:
            normed_ref[start : start + piece_ref.shape[0], :] = piece_ref[...]
            start += piece_ref.shape[0]
        latent = mm_nt(normed_ref[...], down_in_ref[...]).astype(BF)
        glat = mm_nt(cot_ref[...], up_out_ref[...]).astype(BF)
        lat_in[...] = latent
        glat_out[...] = glat
        lat_t[...] = latent.astype(F32).T.astype(BF)
        glat_t[...] = glat.astype(F32).T.astype(BF)
        start = 0
        for base_ref in bases:
            out_acc[start : start + base_ref.shape[0], :] = base_ref[...]
            start += base_ref.shape[0]
        if not bases:
            out_acc[...] = jnp.zeros_like(out_acc)
        gu_acc[...] = jnp.zeros_like(gu_acc)
        lat_acc[...] = jnp.zeros_like(lat_acc)
        glat_acc[...] = jnp.zeros_like(glat_acc)

    w_in = w_in_ref[...]
    w_out = w_out_ref[...]
    pre = mm(normed_ref[...], w_in) + mm(lat_in[...], up_in_ref[...])
    act_grad = mm_nt(cot_ref[...], w_out) + mm(glat_out[...], down_out_ref[...])
    cdf = 0.5 * (1.0 + lax.erf(pre * SQRT_HALF))
    slope = cdf + pre * (jnp.exp(-0.5 * pre * pre) * INV_SQRT_2PI)
    act = (pre * cdf).astype(BF)
    pre_grad = (act_grad * slope).astype(BF)
    out_acc[...] += mm(act, w_out)
    gu_acc[...] += mm_nt(pre_grad, w_in)
    lat_acc[...] += mm_nt(act, down_out_ref[...])
    glat_acc[...] += mm_nt(pre_grad, up_in_ref[...])
    gup_in_ref[...] = mm(lat_t[...], pre_grad)
    gdown_out_ref[...] = mm(glat_t[...], act)

    @pl.when(at == pl.num_programs(0) - 1)
    def _():
        latent = lat_acc[...].astype(BF)
        glat = glat_acc[...].astype(BF)
        start = 0
        for out_ref, gu_ref in zip(out_refs, gu_refs):
            rows = slice(start, start + out_ref.shape[0])
            out_ref[...] = (out_acc[rows, :] + mm(latent[rows], up_out_ref[...])).astype(out_ref.dtype)
            gu_ref[...] = (gu_acc[rows, :] + mm(glat[rows], down_in_ref[...])).astype(gu_ref.dtype)
            start += out_ref.shape[0]
        gup_out_ref[...] = mm(latent.astype(F32).T.astype(BF), cot_ref[...])
        gdown_in_ref[...] = mm(glat.astype(F32).T.astype(BF), normed_ref[...])


def feed_forward(pieces, bases, cotangent, block_at, down_in, up_in, down_out, up_out, weights, hidden, kind):
    model = cotangent.shape[1]
    row_count = sum(item.shape[0] for item in pieces)
    rank = down_in.shape[0]
    block = FEED_BLOCK if hidden % FEED_BLOCK == 0 else hidden
    w_in, in_spec, w_out, out_spec = weights(block)
    main = pl.BlockSpec((row_count, model), lambda at: (block_at, 0))
    slim = pl.BlockSpec((rank, block), lambda at: (0, at))
    small = whole((rank, model))
    return pl.pallas_call(
        partial(feed_kernel, len(pieces), len(bases)),
        grid=(hidden // block,),
        in_specs=[once(item.shape) for item in pieces + bases]
        + [main, small, slim, slim, small, in_spec, out_spec],
        out_specs=[whole(item.shape) for item in pieces] * 2 + [small, slim, slim, small],
        out_shape=[jax.ShapeDtypeStruct(item.shape, kind) for item in pieces]
        + [jax.ShapeDtypeStruct(item.shape, BF) for item in pieces]
        + [
            jax.ShapeDtypeStruct((rank, model), F32),
            jax.ShapeDtypeStruct((rank, hidden), F32),
            jax.ShapeDtypeStruct((rank, hidden), F32),
            jax.ShapeDtypeStruct((rank, model), F32),
        ],
        scratch_shapes=[pltpu.VMEM((row_count, model), BF)]
        + [pltpu.VMEM((row_count, model), F32)] * 2
        + [pltpu.VMEM((row_count, rank), BF)] * 2
        + [pltpu.VMEM((row_count, rank), F32)] * 2
        + [pltpu.VMEM((rank, row_count), BF)] * 2,
        compiler_params=params(1),
        cost_estimate=cost(8 * row_count * model * hidden, 4 * hidden * model, 2 * row_count * hidden),
        name="feed_forward",
    )(*pieces, *bases, cotangent, down_in, up_in, down_out, up_out, w_in, w_out)


def spread_heads(rows_ref, into_ref, model):
    keys = rows_ref.shape[0]
    wide = 4 * HEAD
    row = lax.broadcasted_iota(jnp.int32, (4 * keys, wide), 0) // keys
    col = lax.broadcasted_iota(jnp.int32, (4 * keys, wide), 1) // HEAD
    mask = jnp.where(row == col, 1.0, 0.0).astype(BF)

    def some(group, carry):
        part = rows_ref[:, pl.ds(pl.multiple_of(group * wide, wide), wide)]
        into = pl.ds(pl.multiple_of(group * 4 * keys, 4 * keys), 4 * keys)
        into_ref[into, :] = jnp.concatenate([part] * 4, 0) * mask
        return carry

    lax.fori_loop(0, model // wide, some, 0)


def head_total(values, keys, reduce):
    split = values.reshape(4, keys, values.shape[1])
    return jnp.broadcast_to(reduce(split, 1, keepdims=True), split.shape).reshape(values.shape)


def each(count, step, work):
    def some(at, carry):
        work(pl.ds(pl.multiple_of(at * step, step), step))
        return carry

    lax.fori_loop(0, count // step, some, 0)


def weight_copies(plan, place_ref, sources, hold_ref, sem_ref):
    model = hold_ref.shape[1]
    groups = []
    for index, (start, extra) in enumerate(plan):
        if extra is None:
            pairs = [(sources[0].at[:, pl.ds(start, model)], hold_ref.at[index])]
        else:
            half = model // 2
            here, there = [pl.ds(pl.multiple_of(place_ref[at] * half, half), half) for at in range(2)]
            pairs = [(sources[0].at[:, pl.ds(start, half)], hold_ref.at[index, :, here])]
            for at in range(2):
                rows = pl.ds(pl.multiple_of(place_ref[2 + at] * half, half), half)
                pairs.append((sources[extra + at], hold_ref.at[index, rows, there]))
        groups.append(
            [pltpu.make_async_copy(src, dst, sem_ref.at[index, at]) for at, (src, dst) in enumerate(pairs)]
        )
    return groups


def source_count(plan):
    return 1 + 2 * sum(extra is not None for _, extra in plan)


def start_all(copies):
    for copy in copies:
        copy.start()


def wait_all(copies):
    for copy in copies:
        copy.wait()


def middle_kernel(plan, place_ref, *refs):
    sources, refs = refs[: source_count(plan)], refs[source_count(plan) :]
    inputs_ref, adapt_ref, gain_ref, bias_ref, keys_ref, values_ref = refs[:6]
    pieces = refs[6:-13]
    (
        attended_ref, resid1_ref, normed2_ref, query_ref, probs_ref, crossed_ref, resid2_ref, normed3_ref, lat_ref,
        hold_ref, key_wide, value_wide, sem_ref,
    ) = refs[-13:]
    model = inputs_ref.shape[1]
    keys = keys_ref.shape[0]
    rows = inputs_ref.shape[0]
    wide = 4 * HEAD
    copies = weight_copies(plan, place_ref, sources, hold_ref, sem_ref)
    start_all(copies[0])
    for index, piece_ref in enumerate(pieces):
        size = piece_ref.shape[1]
        attended_ref[:, pl.ds(pl.multiple_of(place_ref[index] * size, size), size)] = piece_ref[...]
    spread_heads(keys_ref, key_wide, model)
    spread_heads(values_ref, value_wide, model)

    def adapted(moving_ref, index, store):
        latent = mm_nt(moving_ref[...], adapt_ref[32 * index : 32 * index + 16, :]).astype(BF)
        lat_ref[:, 16 * index : 16 * index + 16] = latent
        wait_all(copies[index])
        if index < 2:
            start_all(copies[index + 1])

        def some(cols):
            store(
                cols,
                mm(moving_ref[...], hold_ref[index, :, cols])
                + mm(latent, adapt_ref[32 * index + 16 : 32 * index + 32, cols]),
            )

        each(model, 512, some)

    def add_first(cols, value):
        resid1_ref[:, cols] = inputs_ref[:, cols].astype(F32) + value

    def add_second(cols, value):
        resid2_ref[:, cols] = resid1_ref[:, cols] + value

    def keep_query(cols, value):
        query_ref[:, cols] = value.astype(BF)

    def normed(values_at, into_ref, which):
        def some(part):
            into_ref[part, :] = layer_norm(
                values_at[part, :], gain_ref[which : which + 1, :], bias_ref[which : which + 1, :]
            ).astype(BF)

        each(rows, 64, some)

    def cross(lanes):
        score = mm_nt(key_wide[lanes, :], query_ref[:, lanes]) * SCALE
        raised = jnp.exp(score - head_total(score, keys, jnp.max))
        prob = (raised / head_total(raised, keys, jnp.sum)).astype(BF)
        probs_ref[lanes, :] = prob
        crossed_ref[:, lanes] = mm_tn(prob, value_wide[lanes, :]).astype(BF)

    adapted(attended_ref, 0, add_first)
    normed(resid1_ref, normed2_ref, 1)
    adapted(normed2_ref, 1, keep_query)
    each(model, wide, cross)
    adapted(crossed_ref, 2, add_second)
    normed(resid2_ref, normed3_ref, 2)


def middle(places, own, own_spec, others, inputs, at, blocks, sources, plan, adapters, gains, biases, keys, values):
    rows, model = own_spec[0], inputs.shape[1]
    spread = model // HEAD * keys.shape[0]
    shape = lambda kind, dims=(rows, model): jax.ShapeDtypeStruct(dims, kind)
    flat = lambda dims: pl.BlockSpec(dims, lambda _, ref: (0,) * len(dims))
    shapes = [shape(kind) for kind in (BF, F32, BF, BF)]
    shapes += [shape(BF, (spread, rows)), shape(BF), shape(F32), shape(BF), shape(BF, (rows, 48))]
    return pl.pallas_call(
        partial(middle_kernel, plan),
        grid_spec=pltpu.PrefetchScalarGridSpec(
            num_scalar_prefetch=1,
            grid=(1,),
            in_specs=[pl.BlockSpec(memory_space=pl.ANY)] * len(sources)
            + [pl.BlockSpec((rows, model), lambda _, ref: (at, 0))]
            + [flat(item.shape) for item in (adapters, gains, biases, keys, values)]
            + [pl.BlockSpec(own_spec, lambda _, ref: (ref[0] * blocks + at, 0) if others else (at, 0))]
            + [flat(item.shape) for item in others],
            out_specs=[flat(item.shape) for item in shapes],
            scratch_shapes=[
                pltpu.VMEM((3, model, model), BF),
                pltpu.VMEM((spread, 4 * HEAD), BF),
                pltpu.VMEM((spread, 4 * HEAD), BF),
                pltpu.SemaphoreType.DMA((3, 3)),
            ],
        ),
        out_shape=shapes,
        compiler_params=params(),
        cost_estimate=cost(6 * rows * model * model, 6 * model * model + 24 * rows * model),
        name="middle",
    )(places, *sources, inputs, adapters, gains, biases, keys, values, own, *others)


def middle_back_kernel(plan, split, place_ref, *refs):
    sources, refs = refs[: source_count(plan)], refs[source_count(plan) :]
    (
        cot_ref, gu_ref, more_ref, attended_ref, resid1_ref, normed2_ref, query_ref, probs_ref, crossed_ref, resid2_ref,
        lat_ref, adapt_ref, gain_ref, keys_ref, values_ref,
    ) = refs[:15]
    refs = refs[15:]
    outs = refs[: 2 if split else 1]
    resid1_grad_ref, memory_ref, small_ref, hold_ref, key_wide, value_wide, work_ref, low_ref, sem_ref = refs[len(outs) :]
    rows, model = cot_ref.shape
    keys = keys_ref.shape[0]
    wide = 4 * HEAD
    copies = weight_copies(plan, place_ref, sources, hold_ref, sem_ref)
    start_all(copies[2])
    spread_heads(keys_ref, key_wide, model)
    spread_heads(values_ref, value_wide, model)

    def first(part):
        gradient = gu_ref[part, :].astype(F32) + more_ref[part, :].astype(F32)
        value = cot_ref[part, :].astype(F32) + norm_back(resid2_ref[part, :], gain_ref[2:3, :], gradient)
        resid1_grad_ref[part, :] = value
        low_ref[part, :] = value.astype(BF)

    def second(part):
        value = resid1_grad_ref[part, :] + norm_back(resid1_ref[part, :], gain_ref[1:2, :], work_ref[part, :])
        resid1_grad_ref[part, :] = value
        low_ref[part, :] = value.astype(BF)

    def back(moving_ref, index, store):
        down = slice(32 * index, 32 * index + 16)
        upper = slice(32 * index + 16, 32 * index + 32)
        glat = mm_nt(low_ref[...], adapt_ref[upper, :]).astype(BF)
        glat_t = glat.astype(F32).T.astype(BF)
        lat_t = lat_ref[:, 16 * index : 16 * index + 16].astype(F32).T.astype(BF)
        wait_all(copies[index])
        if index:
            start_all(copies[index - 1])

        def some(cols):
            small_ref[down, cols] = mm(glat_t, moving_ref[:, cols])
            small_ref[upper, cols] = mm(lat_t, low_ref[:, cols])
            store(cols, mm_nt(low_ref[...], hold_ref[index, cols, :]) + mm(glat, adapt_ref[down, cols]))

        each(model, 512, some)

    def keep(cols, value):
        work_ref[:, cols] = value

    def cross(lanes):
        part = work_ref[:, lanes].astype(BF)
        prob = probs_ref[lanes, :]
        wide_prob = prob.astype(F32)
        weighted = wide_prob * mm_nt(value_wide[lanes, :], part)
        score_grad = (weighted - wide_prob * head_total(weighted, keys, jnp.sum)).astype(BF)
        low_ref[:, lanes] = (mm_tn(score_grad, key_wide[lanes, :]) * SCALE).astype(BF)
        key_full = mm(score_grad, query_ref[:, lanes])
        value_full = mm(prob, part)
        col = lax.broadcasted_iota(jnp.int32, (keys, wide), 1) // HEAD
        key_sum, value_sum = key_full[:keys], value_full[:keys]
        for head in range(1, 4):
            rows_at = slice(head * keys, (head + 1) * keys)
            key_sum = jnp.where(col == head, key_full[rows_at], key_sum)
            value_sum = jnp.where(col == head, value_full[rows_at], value_sum)
        memory_ref[0, :, lanes] = key_sum * SCALE
        memory_ref[1, :, lanes] = value_sum

    each(rows, 64, first)
    back(crossed_ref, 2, keep)
    each(model, wide, cross)
    back(normed2_ref, 1, keep)
    each(rows, 64, second)
    back(attended_ref, 0, keep)
    if split:
        size = outs[0].shape[1]
        for out_ref, index in zip(outs, range(2)):
            out_ref[...] = work_ref[:, pl.ds(pl.multiple_of(place_ref[index] * size, size), size)].astype(BF)
    else:
        outs[0][...] = work_ref[...].astype(BF)


def middle_back(places, parts, at, cotangent, gu, more, kept, sources, plan, adapters, gains, keys, values):
    model = cotangent.shape[1]
    rows = kept[0].shape[0]
    spread = model // HEAD * keys.shape[0]
    flat = lambda dims: pl.BlockSpec(dims, lambda _, ref: (0,) * len(dims))
    block = pl.BlockSpec((rows, model), lambda _, ref: (at, 0))
    shapes = [jax.ShapeDtypeStruct((rows, model // parts), BF)] * parts + [
        jax.ShapeDtypeStruct((rows, model), F32),
        jax.ShapeDtypeStruct((2,) + keys.shape, F32),
        jax.ShapeDtypeStruct(adapters.shape, F32),
    ]
    return pl.pallas_call(
        partial(middle_back_kernel, plan, parts == 2),
        grid_spec=pltpu.PrefetchScalarGridSpec(
            num_scalar_prefetch=1,
            grid=(1,),
            in_specs=[pl.BlockSpec(memory_space=pl.ANY)] * len(sources)
            + [block, flat(gu.shape), flat(more.shape)]
            + [flat(item.shape) for item in kept]
            + [flat(item.shape) for item in (adapters, gains, keys, values)],
            out_specs=[flat(item.shape) for item in shapes],
            scratch_shapes=[
                pltpu.VMEM((3, model, model), BF),
                pltpu.VMEM((spread, 4 * HEAD), BF),
                pltpu.VMEM((spread, 4 * HEAD), BF),
                pltpu.VMEM((rows, model), F32),
                pltpu.VMEM((rows, model), BF),
                pltpu.SemaphoreType.DMA((3, 3)),
            ],
        ),
        out_shape=shapes,
        compiler_params=params(),
        cost_estimate=cost(6 * rows * model * model, 6 * model * model + 36 * rows * model),
        name="middle_back",
    )(places, *sources, cotangent, gu, more, *kept, adapters, gains, keys, values)


def qkv_grads_kernel(
    place_ref, grad_ref, normed_ref, lat_ref, up_ref, glat_ref, mine_ref, theirs_ref, glat_acc, gup_acc, down_acc,
    down_all, upper_all,
):
    at = pl.program_id(0)
    gradient = grad_ref[...]
    rank = mine_ref.shape[0]
    model = normed_ref.shape[1]
    width = gradient.shape[1]
    gup_acc[...] = mm_tn(lat_ref[...], gradient)

    @pl.when(at == 0)
    def _():
        glat_acc[...] = jnp.zeros_like(glat_acc)
        upper_all[...] = jnp.zeros_like(upper_all)

    into = pl.ds(pl.multiple_of(at * model + place_ref[0] * width, LANES), width)
    upper_all[:, into] = gup_acc[pl.ds(pl.multiple_of(at * rank, rank), rank), :].astype(BF)
    glat_acc[...] += mm_nt(gradient, up_ref[...])

    @pl.when(at == pl.num_programs(0) - 1)
    def _():
        low = glat_acc[...].astype(BF)
        glat_ref[...] = low
        down_acc[...] = mm_tn(low, normed_ref[...])
        for part in range(3):
            down_all[:, part * model : (part + 1) * model] = down_acc[part * rank : (part + 1) * rank, :].astype(BF)
        share(place_ref, down_all, upper_all, mine_ref, theirs_ref)


def share(place_ref, down_all, upper_all, mine_ref, theirs_ref):
    @pl.when(place_ref[0] == 0)
    def _():
        mine_ref[...] = down_all[...]
        theirs_ref[...] = upper_all[...]

    @pl.when(place_ref[0] != 0)
    def _():
        mine_ref[...] = upper_all[...]
        theirs_ref[...] = down_all[...]


def qkv_grads(places, gradient, normed, latent, up):
    frames, model = normed.shape
    parts, ranks, width = up.shape
    rank = ranks // parts
    table = jax.ShapeDtypeStruct((rank, parts * model), BF)
    return pl.pallas_call(
        qkv_grads_kernel,
        grid=(parts,),
        in_specs=[
            smem(),
            pl.BlockSpec((None, frames, width), lambda at: (at, 0, 0)),
            whole(normed.shape),
            whole(latent.shape),
            pl.BlockSpec((None, ranks, width), lambda at: (at, 0, 0)),
        ],
        out_specs=[whole(latent.shape), whole(table.shape), whole(table.shape)],
        out_shape=[jax.ShapeDtypeStruct(latent.shape, BF), table, table],
        scratch_shapes=[
            pltpu.VMEM(latent.shape, F32),
            pltpu.VMEM((ranks, width), F32),
            pltpu.VMEM((ranks, model), F32),
            pltpu.VMEM(table.shape, BF),
            pltpu.VMEM(table.shape, BF),
        ],
        compiler_params=params(1, 42 * MIB),
        cost_estimate=cost(8 * frames * ranks * width * parts, 2 * frames * (model + parts * width)),
        name="qkv_grads",
    )(places, gradient, normed, latent, up)


def qkv_back_kernel(place_ref, grad_ref, glat_ref, down_ref, w_ref, gu_ref, gu_acc):
    at = pl.program_id(0)
    model = gu_ref.shape[1]
    last = pl.num_programs(0) - 1

    def some(cols):
        direct = mm_nt(grad_ref[...], w_ref[cols, :])

        @pl.when(at == 0)
        def _():
            gu_acc[:, cols] = direct + mm(glat_ref[...], down_ref[:, cols])

        @pl.when(jnp.logical_and(at > 0, at < last))
        def _():
            gu_acc[:, cols] += direct

        @pl.when(at == last)
        def _():
            gu_ref[:, cols] = (gu_acc[:, cols] + direct).astype(gu_ref.dtype)

    each(model, 512, some)


def qkv_back(place, row_count, gradient, glat, down, packed, start, kind):
    ranks, model = down.shape
    width = gradient.shape[2]
    if start % width == 0 and width % LANES == 0:
        weight, spec = packed, pl.BlockSpec((model, width), lambda at, ref: (0, start // width + at))
    else:
        weight = packed[:, start : start + 3 * width].reshape(model, 3, width).transpose(1, 0, 2)
        spec = pl.BlockSpec((None, model, width), lambda at, ref: (at, 0, 0))
    return pl.pallas_call(
        qkv_back_kernel,
        grid_spec=pltpu.PrefetchScalarGridSpec(
            num_scalar_prefetch=1,
            grid=(3,),
            in_specs=[
                pl.BlockSpec((None, row_count, width), lambda at, ref: (at, ref[0], 0)),
                pl.BlockSpec((row_count, ranks), lambda at, ref: (ref[0], 0)),
                pl.BlockSpec(down.shape, lambda at, ref: (0, 0)),
                spec,
            ],
            out_specs=pl.BlockSpec((row_count, model), lambda at, ref: (0, 0)),
            scratch_shapes=[pltpu.VMEM((row_count, model), F32)],
        ),
        out_shape=jax.ShapeDtypeStruct((row_count, model), kind),
        compiler_params=params(1, 42 * MIB),
        cost_estimate=cost(6 * row_count * model * width, 6 * model * width + 8 * row_count * model),
        name="qkv_back",
    )(place, gradient, glat, down, weight)


def last_norm_kernel(blocks, frames_ref, gradient_ref, gain_ref, *refs):
    pieces, grad_ref = refs[:-1], refs[-1]
    at = pl.program_id(0)
    back = norm_back(frames_ref[...].astype(F32), gain_ref[...], gradient_ref[...])
    for index, piece_ref in enumerate(pieces):

        @pl.when(at // blocks == index)
        def _(piece_ref=piece_ref):
            grad_ref[...] = back + piece_ref[...]


def last_norm(frames, gradient, gains, pieces):
    rows, model = frames.shape
    step = min(128, rows)
    blocks = pieces[0].shape[0] // step
    block = pl.BlockSpec((step, model), lambda at: (at, 0))

    def piece_spec(index):
        return pl.BlockSpec((step, model), lambda at: (jnp.clip(at - index * blocks, 0, blocks - 1), 0))

    return pl.pallas_call(
        partial(last_norm_kernel, blocks),
        grid=(rows // step,),
        in_specs=[block, block, whole(gains.shape)] + [piece_spec(index) for index in range(len(pieces))],
        out_specs=block,
        out_shape=jax.ShapeDtypeStruct((rows, model), F32),
        compiler_params=params(1, 42 * MIB),
        cost_estimate=cost(20 * rows * model, 16 * rows * model),
        name="last_norm",
    )(frames, gradient, gains, *pieces)


def run_length(size):
    count = 1
    while count * size % LANES:
        count *= 2
    return count


def join_kernel(pieces_ref, flat_ref):
    count, _, size = pieces_ref.shape
    run = run_length(size)

    def some(at, carry):
        parts = [pieces_ref[at * run + index] for index in range(run)]
        into = pl.ds(pl.multiple_of(at * run * size, LANES), run * size)
        flat_ref[:, into] = jnp.concatenate(parts, 1)
        return carry

    lax.fori_loop(0, count // run, some, 0)


def join_pieces(pieces):
    count, rows, size = pieces.shape
    if count % run_length(size):
        return pieces.transpose(1, 0, 2).reshape(rows, count * size)
    return pl.pallas_call(
        join_kernel,
        out_shape=jax.ShapeDtypeStruct((rows, count * size), pieces.dtype),
        compiler_params=params(0),
        name="join_pieces",
    )(pieces)


def split_kernel(*refs):
    sources, pieces_ref, flat_ref = refs[:-2], refs[-2], refs[-1]
    count, _, size = pieces_ref.shape
    run = run_length(size)
    start = 0
    for first_ref, second_ref in zip(sources[::2], sources[1::2]):
        width = first_ref.shape[1]
        both = first_ref[...].astype(F32) + second_ref[...].astype(F32)
        flat_ref[:, start : start + width] = both.astype(BF)
        start += width

    def some(at, carry):
        block = flat_ref[:, pl.ds(pl.multiple_of(at * run * size, LANES), run * size)]
        for index in range(run):
            pieces_ref[at * run + index] = block[:, index * size : (index + 1) * size]
        return carry

    lax.fori_loop(0, count // run, some, 0)


def split_sums(pairs, count):
    rows = pairs[0].shape[0]
    total = sum(item.shape[1] for item in pairs[::2])
    return pl.pallas_call(
        split_kernel,
        out_shape=jax.ShapeDtypeStruct((count, rows, total // count), BF),
        scratch_shapes=[pltpu.VMEM((rows, total), BF)],
        compiler_params=params(0, 42 * MIB),
        name="split_sums",
    )(*pairs)


def unit_loop(plan, work):
    fsdp, seq, folds, local = plan
    run = run_length(local)

    def some(at, carry):
        span = run * seq * folds * local
        block = pl.ds(pl.multiple_of(at * span, LANES), span)
        folded = [
            pl.ds(pl.multiple_of(fold * fsdp * local + at * run * local, LANES), run * local) for fold in range(folds)
        ]
        work(run, block, folded)
        return carry

    lax.fori_loop(0, fsdp // run, some, 0)


def take_units_kernel(plan, place_ref, all_ref, *refs):
    own_ref = refs[-1]
    _, seq, folds, local = plan
    spot = place_ref[0]

    def work(run, block, folded):
        values = all_ref[:, block]
        for fold, into in enumerate(folded):
            parts = []
            for index in range(run):
                base = (index * seq * folds + fold) * local
                part = values[:, base : base + local]
                for other in range(1, seq):
                    shift = base + other * folds * local
                    part = jnp.where(spot == other, values[:, shift : shift + local], part)
                parts.append(part)
            own_ref[:, into] = jnp.concatenate(parts, 1)

    unit_loop(plan, work)
    if len(refs) == 2:
        model = refs[0].shape[1]
        hidden = own_ref.shape[1] - folds * model
        for fold in range(folds):
            rows = pl.ds(pl.multiple_of((spot * folds + fold) * local, 16), local)
            own_ref[:, hidden + fold * model : hidden + (fold + 1) * model] = refs[0][rows, :]


def take_units(plan, places, matrix, low=None):
    _, seq, folds, local = plan
    rows, width = matrix.shape
    extra = [] if low is None else [low]
    out_width = width // seq + sum(folds * item.shape[1] for item in extra)
    return pl.pallas_call(
        partial(take_units_kernel, plan),
        in_specs=[smem()] + [pl.BlockSpec(memory_space=pltpu.VMEM)] * (1 + len(extra)),
        out_shape=jax.ShapeDtypeStruct((rows, out_width), matrix.dtype),
        compiler_params=params(0),
        name="take_units",
    )(places, matrix, *extra)


def collect_kernel(plan, blocks, place_ref, *refs):
    parts, squares, refs = refs[:blocks], refs[blocks : 2 * blocks], refs[2 * blocks :]
    feeds = [refs[at : at + 4] for at in range(0, len(refs) - 12, 4)]
    (
        other_ref, lat_ref, flat_ref, down_text_ref, text_ref, w_ref,
        mine_ref, theirs_ref, text_grad_ref, down_all, upper_all, unit_acc,
    ) = refs[-12:]
    _, seq, folds, local = plan
    rank = mine_ref.shape[0]
    model = text_ref.shape[1]
    wide = other_ref.shape[2]
    spot = place_ref[0]
    own = pl.ds(pl.multiple_of(spot * wide, wide), wide)

    def total(items, rows):
        value = items[0][rows, :]
        for item in items[1:]:
            value = value + item[rows, :]
        return value

    moved = []
    for part in range(2):
        value = parts[0][part, :, own]
        for item in parts[1:]:
            value = value + item[part, :, own]
        moved.append((value + other_ref[part].astype(F32)).astype(BF))
    moved = jnp.concatenate(moved, 1)
    glat = mm_nt(moved, flat_ref[...]).astype(BF)
    gup = mm_tn(lat_ref[...], moved)
    gdown = mm_tn(glat, text_ref[...])
    text_grad_ref[...] = (mm_nt(moved, w_ref[...]) + mm(glat, down_text_ref[...])).astype(BF)

    upper_all[:, 2 * model : 4 * model] = jnp.zeros((rank, 2 * model), BF)
    for part in range(2):
        rows = slice(part * rank, (part + 1) * rank)
        down_all[:, (2 + part) * model : (3 + part) * model] = gdown[rows].astype(BF)
        into = pl.ds(pl.multiple_of((2 + part) * model + spot * wide, LANES), wide)
        upper_all[:, into] = gup[rows, part * wide : (part + 1) * wide].astype(BF)
    for index, at in enumerate((0, 1, 4)):
        cols = slice(at * model, (at + 1) * model)
        down_all[:, cols] = total(squares, slice(2 * index * rank, (2 * index + 1) * rank)).astype(BF)
        upper_all[:, cols] = total(squares, slice((2 * index + 1) * rank, (2 * index + 2) * rank)).astype(BF)
    every = slice(0, rank)
    down_all[:, 5 * model : 6 * model] = total([item[0] for item in feeds], every).astype(BF)
    upper_all[:, upper_all.shape[1] - model :] = total([item[3] for item in feeds], every).astype(BF)
    for into_ref, start, which in ((upper_all, 5 * model, 1), (down_all, 6 * model, 2)):
        unit_acc[...] = total([item[which] for item in feeds], every)

        def work(run, block, folded):
            values = [unit_acc[:, cols] for cols in folded]
            spread = []
            for index in range(run):
                for other in range(seq):
                    for fold in range(folds):
                        part = values[fold][:, index * local : (index + 1) * local]
                        spread.append(jnp.where(spot == other, part, 0.0))
            at = pl.ds(pl.multiple_of(start + block.start, LANES), block.size)
            into_ref[:, at] = jnp.concatenate(spread, 1).astype(BF)

        unit_loop(plan, work)
    share(place_ref, down_all, upper_all, mine_ref, theirs_ref)


def collect(plan, places, parts, squares, feeds, other, lat_text, flat_text, down_text, text, packed, start):
    rank = squares[0].shape[0] // 6
    model = text.shape[1]
    hidden = feeds[0][1].shape[1]
    wide2 = flat_text.shape[1]
    width = 6 * model + hidden * plan[1]
    weight, spec = window(packed, start, wide2)
    feeds = [item for feed in feeds for item in feed]
    before = list(parts) + list(squares) + feeds + [other, lat_text, flat_text, down_text, text]
    table = jax.ShapeDtypeStruct((rank, width), BF)
    shapes = [table, table, jax.ShapeDtypeStruct(text.shape, BF)]
    return pl.pallas_call(
        partial(collect_kernel, plan, len(parts)),
        grid=(1,),
        in_specs=[smem()] + [whole(item.shape) for item in before] + [spec],
        out_specs=[whole(item.shape) for item in shapes],
        out_shape=shapes,
        scratch_shapes=[pltpu.VMEM(table.shape, BF)] * 2 + [pltpu.VMEM((rank, hidden), F32)],
        compiler_params=params(1),
        cost_estimate=cost(4 * text.shape[0] * model * wide2, 2 * model * wide2),
        name="collect",
    )(places, *before, weight)


def both_kernel(place_ref, mine_ref, other_ref, down_ref, upper_ref):
    first = place_ref[0] == 0
    for at in range(mine_ref.shape[0]):
        mine, other = mine_ref[at].astype(F32), other_ref[at].astype(F32)
        down_ref[at] = jnp.where(first, mine, other)
        upper_ref[at] = jnp.where(first, other, mine)


def both_tables(places, mine, other):
    return pl.pallas_call(
        both_kernel,
        in_specs=[smem()] + [pl.BlockSpec(memory_space=pltpu.VMEM)] * 2,
        out_shape=[jax.ShapeDtypeStruct(mine.shape, F32)] * 2,
        compiler_params=params(0, 42 * MIB),
        name="both_tables",
    )(places, mine, other)


def body(
    inputs,
    text_states,
    adapter_index,
    norm_gains,
    norm_biases,
    self_in,
    self_out,
    cross_query,
    cross_text,
    cross_out,
    hidden_in,
    hidden_out,
    adapter_down,
    adapter_up,
    cotangent,
    *,
    sizes,
):
    seq, fsdp = sizes
    spot = lax.axis_index("seq")
    first_here = spot == 0
    there = (seq - 1) - spot
    local = self_in.shape[0]
    depth = hidden_out.shape[0] // seq
    pair = seq == 2 and depth % local == 0 and fsdp % run_length(local) == 0
    model = inputs.shape[2]
    rows = inputs.shape[1]
    frames = rows * seq
    wide = model // seq
    hidden_all = hidden_in.shape[1]
    hidden = hidden_all // seq
    adapters, rank, piece = adapter_down.shape
    total = piece * fsdp

    blocks = max(rows // 256, 1)
    size = rows // blocks

    def swap(value):
        return lax.ppermute(value, "seq", [(0, 1), (1, 0)])

    def pick(value, axis, extent, which=None):
        return lax.dynamic_slice_in_dim(value, (spot if which is None else which) * extent, extent, axis)

    def ordered(mine, other):
        return jnp.where(first_here, mine, other), jnp.where(first_here, other, mine)

    def gather(value, axis):
        if pair:
            return jnp.concatenate(ordered(value, swap(value)), axis)
        return lax.all_gather(value, "seq", axis=axis, tiled=True)

    def after(value, *others):
        return lax.optimization_barrier((value,) + others)[0]

    def put(value, axis):
        shape = list(value.shape)
        shape[axis] = seq
        return lax.dynamic_update_slice_in_dim(jnp.zeros(shape, value.dtype), value, spot, axis)

    def own_columns(matrix, parts):
        return [pick(matrix[:, at * model : (at + 1) * model], 1, wide) for at in range(parts)]

    def flat_down(grads, parts):
        return jnp.concatenate([grads[at * rank : (at + 1) * rank] for at in range(parts)], 1)

    def flat_upper(own):
        return put(jnp.stack(own, 1)[:, :, None], 2).reshape(rank, len(own) * model)

    squares_here = [cross_out, cross_query] + [pick(self_out, 1, wide) if pair else self_out]
    first = squares_here + own_columns(self_in, 3) + own_columns(cross_text, 2)
    edges = [0]
    for item in first:
        edges.append(edges[-1] + item.shape[1])
    start_in, start_text = edges[3], edges[6]
    packed = lax.all_gather(jnp.concatenate(first, 1), "fsdp", axis=0, tiled=True)
    squares_plan = ((edges[2], None), (edges[1], None), (edges[0], None))
    if pair:
        squares_plan = ((edges[2], 1),) + squares_plan[1:]
    core = lax.rem(lax.axis_index("fsdp"), 2)
    where_here = jnp.stack([spot, there, core, 1 - core]).astype(jnp.int32)
    if pair:
        folds = depth // local
        plan = (fsdp, seq, folds, local)
        own_units = partial(take_units, plan, where_here)
        packed_feed = lax.all_gather(own_units(hidden_in, hidden_out), "fsdp", axis=0, tiled=True)

        def feed_weights(block):
            per = model // block
            return (
                packed_feed,
                pl.BlockSpec((model, block), lambda at: (0, at)),
                packed_feed,
                pl.BlockSpec((block, model), lambda at: (at % per, folds + at // per)),
            )
    else:

        def own_units(matrix):
            kept = lax.dynamic_index_in_dim(matrix.reshape(-1, fsdp, seq, depth), spot, 2, False)
            return kept.reshape(-1, hidden)

        def all_units(matrix):
            return put(matrix.reshape(-1, fsdp, 1, depth), 2).reshape(-1, hidden_all)

        whole_in = lax.all_gather(own_units(hidden_in), "fsdp", axis=0, tiled=True)
        whole_out = lax.all_gather(pick(hidden_out, 0, depth), "fsdp", axis=0, tiled=True)

        def feed_weights(block):
            return (
                whole_in,
                pl.BlockSpec((model, block), lambda at: (0, at)),
                whole_out,
                pl.BlockSpec((block, model), lambda at: (at, 0)),
            )

    index_all = lax.all_to_all(jnp.broadcast_to(adapter_index, (fsdp,)), "fsdp", 0, 0, tiled=True)
    if pair:
        table = jnp.where(first_here, adapter_down, adapter_up)
        mine = join_pieces(lax.all_to_all(jnp.take(table, index_all, axis=0), "fsdp", 0, 0, tiled=True))
        down_all, upper_all = ordered(mine, swap(mine))
    else:
        table = jnp.concatenate([adapter_down, adapter_up], 1)
        chosen = join_pieces(lax.all_to_all(jnp.take(table, index_all, axis=0), "fsdp", 0, 0, tiled=True))
        down_all, upper_all = chosen[:rank], chosen[rank:]
    in_cuts = [0, 3 * model, 4 * model, 5 * model, 7 * model, 8 * model, 9 * model, 9 * model + hidden_all]
    out_cuts = [0, 3 * model, 4 * model, 5 * model, 7 * model, 8 * model, 8 * model + hidden_all, 9 * model + hidden_all]
    downs = [down_all[:, in_cuts[at] : in_cuts[at + 1]] for at in range(7)]
    uppers = [upper_all[:, out_cuts[at] : out_cuts[at + 1]] for at in range(7)]

    def part_down(matrix, parts):
        return jnp.concatenate([matrix[:, at * model : (at + 1) * model] for at in range(parts)], 0)

    def part_upper(matrix, parts):
        own = own_columns(matrix, parts)
        return jnp.stack(
            [jnp.pad(item, ((at * rank, (parts - 1 - at) * rank), (0, 0))) for at, item in enumerate(own)], 0
        )

    units = own_units(jnp.concatenate([uppers[5], downs[6]], 0))
    feed_adapters = (downs[5], units[:rank], units[rank:], uppers[6])
    square_adapters = jnp.concatenate([downs[1], uppers[1], downs[2], uppers[2], downs[4], uppers[4]], 0)
    down_qkv, upper_qkv = part_down(downs[0], 3), part_upper(uppers[0], 3)
    down_text, upper_text = part_down(downs[3], 2), part_upper(uppers[3], 2)
    flat_text = jnp.concatenate([upper_text[0], upper_text[1]], 1)

    frames_in = inputs[0]
    cot = cotangent[0]
    if pair:
        frames_parts = [frames_in, swap(frames_in)]
        cot_other = swap(after(cot, frames_parts[1]))
    else:
        frames_parts = [lax.all_gather(frames_in, "seq", axis=0, tiled=True)]
    norm_places = where_here if pair else jnp.zeros((4,), jnp.int32)
    if pair:
        frames_parts[1] = after(frames_parts[1], cot_other, units)
    normed1, lat_qkv = norm_project(norm_places, frames_parts, norm_gains[0:1], norm_biases[0:1], down_qkv)
    packed = after(packed, normed1)
    sources = [packed]
    if pair:
        half = model // 2
        straight = swap(lax.dynamic_slice(packed, (core * half, edges[2]), (half, wide)))
    triple = qkv_project(normed1, lat_qkv, upper_qkv, packed, start_in, 3 * wide)
    padded = -(-wide // LANES) * LANES
    if padded != wide:
        triple = jnp.pad(triple.reshape(frames, 3, wide), ((0, 0), (0, 0), (0, padded - wide)))
        triple = triple.reshape(frames, 3 * padded)
    text = after(text_states[0], triple)
    w_text = packed[:, start_text : start_text + 2 * wide]
    lat_text = mm_nt(text, down_text).astype(BF)
    memory = (mm(text, w_text) + mm(lat_text, flat_text)).astype(BF)
    head_out, probs, *leaving = attend(where_here, [size] * blocks if pair else [], after(triple, memory), padded)

    if pair:
        neighbours = [(at, at ^ 1) for at in range(fsdp)]
        sources += [straight, lax.ppermute(after(straight, head_out), "fsdp", neighbours)]

    memory_all = gather(memory.reshape(-1, 2, wide), 2)
    keys, values = memory_all[:, 0], memory_all[:, 1]

    constants = (sources, squares_plan, square_adapters, norm_gains, norm_biases, keys, values)
    if pair:
        received = [swap(leaving[0])]
        for item in leaving[1:]:
            received.append(swap(after(item, received[-1])))
    else:
        natural = lax.all_to_all(head_out[:, :wide], "seq", split_axis=0, concat_axis=1, tiled=True)
    made = []
    for at in range(blocks):
        if pair:
            own, spec, others = head_out, (size, wide), [received[at]]
        else:
            own, spec, others = natural, (size, model), []
        ready = after(frames_in, made[-1][7]) if made else frames_in
        made.append(middle(where_here if pair else jnp.zeros((4,), jnp.int32), own, spec, others, ready, at, blocks, *constants))
    normed3 = [item[7] for item in made]
    resid2 = [item[6] for item in made]

    feed_tail = feed_adapters + (feed_weights, hidden)
    if pair:
        others = [swap(item) for item in normed3]
        ours = [feed_forward(normed3[:1], resid2[:1], cot, 0, *feed_tail, F32)]
        theirs = feed_forward([others[0], after(others[1], ours[0][0])] if blocks > 1 else others, [], cot_other, 0, *feed_tail, BF)
        out_leaving, gu_leaving = theirs[:blocks], theirs[blocks : 2 * blocks]
        gu_more = [swap(gu_leaving[0])]
        for at in range(1, blocks):
            ours.append(feed_forward([after(normed3[at], gu_leaving[0])], [resid2[at]], cot, at, *feed_tail, F32))
            gu_more.append(swap(after(gu_leaving[at], gu_more[-1], ours[-1][0])))
        gu = [item[1] for item in ours]
        out_more = []
        feed_grads = [item[2:] for item in ours] + [theirs[2 * blocks :]]
    else:
        wide_in = gather(jnp.concatenate(normed3, 0), 0)
        all_out = feed_forward([wide_in], [], gather(cot, 0), 0, *feed_tail, F32)
        summed = [
            lax.psum_scatter(item.astype(BF), "seq", scatter_dimension=0, tiled=True) for item in all_out[:2]
        ]
        output = (jnp.concatenate(resid2, 0) + summed[0].astype(F32)).astype(BF)
        gu = [summed[1][at * size : (at + 1) * size] for at in range(blocks)]
        gu_more = [jnp.zeros_like(item) for item in gu]
        feed_grads = [all_out[2:]]

    pieces, resid1_grads, memory_parts, square_parts = [], [], [], []
    for at in range(blocks):
        gu_here = gu[at] if at == 0 else after(gu[at], result[-3])
        kept = made[at][:7] + made[at][8:9]
        result = middle_back(
            where_here, 2 if pair else 1, at, cot, gu_here, gu_more[at],
            kept, sources, squares_plan, square_adapters, norm_gains, keys, values,
        )
        if pair:
            waited = [pieces[-1][1]] if at else []
            if at == 0:
                out_more.append(swap(after(out_leaving[0], result[0])))
            if at == blocks - 1:
                memory_part = sum(memory_parts, result[-2]).astype(BF)
                memory_other = swap(after(pick(memory_part, 2, wide, there), *out_more))
                waited.append(memory_other)
            pieces.append((result[0], swap(after(result[1], *waited) if waited else result[1])))
        else:
            pieces.append(result[0])
        resid1_grads.append(result[-3])
        memory_parts.append(result[-2])
        square_parts.append(result[-1])
    resid1_grad = jnp.concatenate(resid1_grads, 0)
    square_grads = sum(square_parts[1:], square_parts[0])

    if pair:
        early, early_leaving, text_low = collect(
            plan, where_here, memory_parts, square_parts, feed_grads, memory_other, lat_text, flat_text, down_text,
            text_states[0], packed, start_text,
        )
        grad_pieces = [item[0] for item in pieces] + [item[1] for item in pieces]
    else:
        head_grad = lax.all_to_all(jnp.concatenate(pieces, 0), "seq", split_axis=1, concat_axis=0, tiled=True)
        grad_pieces = [jnp.pad(head_grad, ((0, 0), (0, padded - wide)))]
    triple_grad = attend_back(where_here, triple, head_out, grad_pieces, probs, padded)[:, :, :wide]
    if pair:
        early_other = swap(after(early_leaving, pieces[-1][1]))
        for at in range(1, blocks):
            out_more.append(swap(after(out_leaving[at], early_other, triple_grad)))
        glat_qkv, late, late_leaving = qkv_grads(
            where_here, after(triple_grad, early_other), normed1, lat_qkv, upper_qkv
        )
        late_other = swap(late_leaving)
    else:
        glat_qkv = sum(mm_nt(triple_grad[at], upper_qkv[at]) for at in range(3)).astype(BF)
        gdown_qkv = mm_tn(glat_qkv, normed1)
        gup_qkv = [mm_tn(lat_qkv[:, at * rank : (at + 1) * rank], triple_grad[at]) for at in range(3)]
    back = partial(qkv_back, gradient=triple_grad, glat=glat_qkv, down=down_qkv, packed=packed, start=start_in)
    if pair:
        for_them = back(there[None], rows, kind=BF)
        for_us = back(after(spot, for_them, *out_more)[None], rows, kind=F32)
        input_grad = last_norm(frames_in, for_us + swap(for_them).astype(F32), norm_gains[0:1], resid1_grads)
        output = jnp.concatenate(
            [(item[0] + other.astype(F32)).astype(BF) for item, other in zip(ours, out_more)], 0
        )
    else:
        full = back(jnp.zeros((1,), jnp.int32), frames, kind=BF)
        normed1_grad = lax.psum_scatter(full, "seq", scatter_dimension=0, tiled=True).astype(F32)
        resid1_grad = jnp.concatenate(resid1_grads, 0)
        input_grad = resid1_grad + norm_back(frames_in.astype(F32), norm_gains[0:1], normed1_grad)

    selector = (index_all[None, :] == jnp.arange(adapters, dtype=jnp.int32)[:, None]).astype(BF)

    def by_adapter(sent, *others):
        received = lax.all_to_all(sent, "fsdp", 0, 0, tiled=True)
        chooser = after(selector, *others) if others else selector
        return jnp.einsum("ac,crw->arw", chooser, received, preferred_element_type=F32)

    if pair:
        shares = by_adapter(split_sums([after(late, for_them), late_other, early, early_other], fsdp)).astype(BF)
        grad_down, grad_up = both_tables(where_here, shares, swap(after(shares, for_us)))
        text_total = text_low.astype(F32) + swap(text_low).astype(F32)
    else:
        memory_part = sum(memory_parts[1:], memory_parts[0]).astype(BF)
        memory_grad = lax.psum_scatter(memory_part, "seq", scatter_dimension=2, tiled=True)
        memory_flat = jnp.concatenate([memory_grad[0], memory_grad[1]], 1)
        glat_text = mm_nt(memory_flat, flat_text).astype(BF)
        gup_text = mm_tn(lat_text, memory_flat)
        gdown_text = mm_tn(glat_text, text)
        text_low = (mm_nt(memory_flat, w_text) + mm(glat_text, down_text)).astype(BF)
        own_text = [gup_text[at * rank : (at + 1) * rank, at * wide : (at + 1) * wide] for at in range(2)]
        gdown_in, gup_in, gdown_out, gup_out = feed_grads[0]
        square_grads = sum(square_parts[1:], square_parts[0])
        squares = [square_grads[rank * at : rank * (at + 1)] for at in range(6)]
        down_sent = [flat_down(gdown_qkv, 3), squares[0], squares[2], flat_down(gdown_text, 2), squares[4], gdown_in]
        upper_sent = [flat_upper(gup_qkv), squares[1], squares[3], flat_upper(own_text), squares[5]]
        down_sent = jnp.concatenate(down_sent + [all_units(gdown_out)], 1)
        upper_sent = jnp.concatenate(upper_sent + [all_units(gup_in), gup_out], 1)
        sent = jnp.concatenate([down_sent, upper_sent], 0).astype(BF).reshape(2 * rank, fsdp, piece).transpose(1, 0, 2)
        shares = lax.psum(by_adapter(sent).astype(BF), "seq")
        grad_down, grad_up = shares[:, :rank], shares[:, rank:]
        text_total = lax.psum(text_low, "seq").astype(F32)
    return (output[None], input_grad[None], text_total[None], grad_down.astype(F32), grad_up.astype(F32))


def solution(mesh):
    return jax.shard_map(
        partial(body, sizes=(mesh.shape["seq"], mesh.shape["fsdp"])),
        mesh=mesh,
        in_specs=(
            P("fsdp", "seq", None),
            P("fsdp", None, None),
            P("fsdp"),
            P(),
            P(),
            P("fsdp", None),
            P("fsdp", None),
            P("fsdp", None),
            P("fsdp", None),
            P("fsdp", None),
            P("fsdp", None),
            P("fsdp", None),
            P(None, None, "fsdp"),
            P(None, None, "fsdp"),
            P("fsdp", "seq", None),
        ),
        out_specs=(
            P("fsdp", "seq", None),
            P("fsdp", "seq", None),
            P("fsdp", None, None),
            P(None, None, "fsdp"),
            P(None, None, "fsdp"),
        ),
        check_vma=False,
    )
```

```python
from functools import partial

import jax
import jax.numpy as jnp
from jax import lax
from jax.experimental import pallas as pl
from jax.experimental.pallas import tpu as pltpu
from jax.sharding import PartitionSpec as P

HEAD = 64
LANES = 128
QB = 256
BF = jnp.bfloat16
F32 = jnp.float32
SCALE = float(HEAD) ** (-0.5)
SQRT_HALF = 0.7071067811865476
INV_SQRT_2PI = 0.3989422804014327
MIB = 1024 * 1024
VMEM_LIMIT = 60 * MIB
COST = 1.0
FEED_BLOCK = 512


def mm(a, b):
    return lax.dot_general(a, b, (((1,), (0,)), ((), ())), preferred_element_type=F32)


def mm_nt(a, b):
    return lax.dot_general(a, b, (((1,), (1,)), ((), ())), preferred_element_type=F32)


def mm_tn(a, b):
    return lax.dot_general(a, b, (((0,), (0,)), ((), ())), preferred_element_type=F32)


def norm_stats(values):
    centered = values - jnp.mean(values, -1, keepdims=True)
    variance = jnp.mean(centered * centered, -1, keepdims=True)
    inverse = lax.rsqrt(variance + 1e-05)
    return centered * inverse, inverse


def layer_norm(values, gains, biases):
    unit, _ = norm_stats(values)
    return unit * gains + biases


def norm_back(values, gains, gradient):
    unit, inverse = norm_stats(values)
    scaled = gradient * gains
    mean_one = jnp.mean(scaled, -1, keepdims=True)
    mean_two = jnp.mean(scaled * unit, -1, keepdims=True)
    return inverse * (scaled - mean_one - unit * mean_two)


def whole(shape):
    return pl.BlockSpec(shape, lambda *_: (0,) * len(shape))


def once(shape):
    return pl.BlockSpec(shape, lambda *_: (0,) * len(shape), pipeline_mode=pl.Buffered(1))


def params(count=1, limit=None):
    return pltpu.CompilerParams(
        dimension_semantics=("arbitrary",) * count if count else None, vmem_limit_bytes=limit or VMEM_LIMIT
    )


def cost(flops, moved, special=0):
    return pl.CostEstimate(
        flops=int(flops * COST), bytes_accessed=int(moved * COST), transcendentals=int(special * COST)
    )


def window(packed, start, width, rows=None, steps=1, step=0):
    block = width // steps
    rows = packed.shape[0] if rows is None else rows
    if start % block == 0 and block % LANES == 0:
        base = start // block
        return packed, pl.BlockSpec((rows, block), lambda *at: (0, base + (at[step] if steps > 1 else 0)))
    return packed[:, start : start + width], pl.BlockSpec(
        (rows, block), lambda *at: (0, at[step] if steps > 1 else 0)
    )


def norm_kernel(place_ref, *refs):
    count = len(refs) - 5
    parts, (gain_ref, bias_ref, down_ref, normed_ref, lat_ref) = refs[:count], refs[count:]
    step = 128
    for index, part_ref in enumerate(parts):
        base = place_ref[index] * part_ref.shape[0]

        def some(at, carry):
            rows = pl.ds(pl.multiple_of(at * step, step), step)
            into = pl.ds(pl.multiple_of(base + at * step, step), step)
            normed = layer_norm(part_ref[rows, :].astype(F32), gain_ref[...], bias_ref[...]).astype(BF)
            normed_ref[into, :] = normed
            lat_ref[into, :] = mm_nt(normed, down_ref[...]).astype(BF)
            return carry

        lax.fori_loop(0, part_ref.shape[0] // step, some, 0)


def smem():
    return pl.BlockSpec(memory_space=pltpu.SMEM)


def norm_project(places, parts, gains, biases, down):
    model = parts[0].shape[1]
    frames = sum(part.shape[0] for part in parts)
    ranks = down.shape[0]
    return pl.pallas_call(
        norm_kernel,
        in_specs=[smem()] + [whole(item.shape) for item in parts + [gains, biases, down]],
        out_specs=[whole((frames, model)), whole((frames, ranks))],
        out_shape=[jax.ShapeDtypeStruct((frames, model), BF), jax.ShapeDtypeStruct((frames, ranks), BF)],
        grid=(1,),
        compiler_params=params(1),
        cost_estimate=cost(2 * frames * model * ranks, 4 * frames * model),
        name="norm_project",
    )(places, *parts, gains, biases, down)


def qkv_kernel(normed_ref, lat_ref, up_ref, w_ref, out_ref):
    step = 256

    def some(at, carry):
        rows = pl.ds(pl.multiple_of(at * step, step), step)
        out_ref[rows, :] = (mm(normed_ref[rows, :], w_ref[...]) + mm(lat_ref[rows, :], up_ref[...])).astype(BF)
        return carry

    lax.fori_loop(0, normed_ref.shape[0] // step, some, 0)


def qkv_project(normed, latent, up, packed, start, width):
    row_count, model = normed.shape
    ranks = latent.shape[1]
    steps = 3 if (width // 3) % LANES == 0 else 1
    operand, spec = window(packed, start, width, steps=steps)
    block = width // steps
    if steps == 3:
        up_spec = pl.BlockSpec((None, ranks, block), lambda at: (at, 0, 0))
    else:
        up = up.transpose(1, 0, 2).reshape(ranks, width)
        up_spec = whole(up.shape)
    return pl.pallas_call(
        qkv_kernel,
        grid=(steps,),
        in_specs=[whole(normed.shape), whole(latent.shape), up_spec, spec],
        out_specs=pl.BlockSpec((row_count, block), lambda at: (0, at)),
        out_shape=jax.ShapeDtypeStruct((row_count, width), BF),
        compiler_params=params(1, 42 * MIB),
        cost_estimate=cost(2 * row_count * model * width, 2 * (row_count + width) * model),
        name="qkv_project",
    )(normed, latent, up, operand)


def tri_start(at):
    return QB * at * (at + 1) // 2


def attend_kernel(place_ref, q_ref, k_ref, v_ref, out_ref, prob_ref, *refs):
    sent, (val_t_ref, out_t_ref) = refs[:-2], refs[-2:]
    frames = q_ref.shape[0]
    lane = lax.broadcasted_iota(jnp.int32, (1, LANES), 1) // HEAD
    val_t_ref[...] = v_ref[...].T
    square = (QB, QB)
    keep_tri = lax.broadcasted_iota(jnp.int32, square, 0) <= lax.broadcasted_iota(jnp.int32, square, 1)

    def scores(half, at):
        stop = (at + 1) * QB
        query = q_ref[at * QB : stop, :] * jnp.where(lane == half, SCALE, 0.0).astype(BF)
        last = jnp.where(keep_tri, mm_nt(k_ref[stop - QB : stop, :], query), -1e30)
        if at == 0:
            return last
        return jnp.concatenate([mm_nt(k_ref[0 : stop - QB, :], query), last], 0)

    turns = [(half, at) for at in range(frames // QB) for half in range(2)]
    score = scores(*turns[0])
    for index, (half, at) in enumerate(turns):
        stop = (at + 1) * QB
        own = slice(half * HEAD, (half + 1) * HEAD)
        later = scores(*turns[index + 1]) if index + 1 < len(turns) else None
        raised = jnp.exp(score - jnp.max(score, 0, keepdims=True))
        prob = (raised * (1.0 / jnp.sum(raised, 0, keepdims=True))).astype(BF)
        prob_ref[half, tri_start(at) : tri_start(at) + stop, :] = prob
        out_t_ref[own, at * QB : stop] = mm(val_t_ref[own, 0:stop], prob)
        score = later
    out_ref[...] = out_t_ref[...].T.astype(BF)
    for index, sent_ref in enumerate(sent):
        size = sent_ref.shape[0]
        at = place_ref[1] * len(sent) + index
        sent_ref[...] = out_ref[pl.ds(pl.multiple_of(at * size, size), size), :]


def pair_specs(frames, width):
    pairs = width // LANES
    return [pl.BlockSpec((frames, LANES), lambda at, part=part: (0, part * pairs + at)) for part in range(3)]


def attend(places, sizes, triple, width):
    frames = triple.shape[0]
    pairs = width // LANES
    tri = tri_start(frames // QB)
    return pl.pallas_call(
        attend_kernel,
        grid=(pairs,),
        in_specs=[smem()] + pair_specs(frames, width),
        out_specs=[
            pl.BlockSpec((frames, LANES), lambda at: (0, at)),
            pl.BlockSpec((2, tri, QB), lambda at: (at, 0, 0)),
        ]
        + [pl.BlockSpec((size, LANES), lambda at: (0, at)) for size in sizes],
        out_shape=[
            jax.ShapeDtypeStruct((frames, width), BF),
            jax.ShapeDtypeStruct((2 * pairs, tri, QB), BF),
        ]
        + [jax.ShapeDtypeStruct((size, width), BF) for size in sizes],
        scratch_shapes=[pltpu.VMEM((LANES, frames), BF), pltpu.VMEM((LANES, frames), F32)],
        compiler_params=params(1),
        cost_estimate=cost(
            8 * tri * QB * HEAD * pairs, 2 * (4 * frames * width + 2 * pairs * tri * QB), 2 * pairs * tri * QB
        ),
        name="attend",
    )(places, triple, triple, triple)


def attend_back_kernel(place_ref, q_ref, k_ref, v_ref, out_ref, prob_ref, *refs):
    pieces, (back_ref, grad_ref, key_t_ref, dq_t_ref, dk_acc, dv_acc) = refs[:-6], refs[-6:]
    frames = q_ref.shape[0]
    for index, piece_ref in enumerate(pieces):
        size = piece_ref.shape[0]
        count = max(len(pieces) // 2, 1)
        at = place_ref[index // count] * count + index % count if len(pieces) > 1 else 0
        grad_ref[pl.ds(pl.multiple_of(at * size, size), size), :] = piece_ref[...]
    lane = lax.broadcasted_iota(jnp.int32, (1, LANES), 1) // HEAD
    key_t_ref[...] = k_ref[...].T
    dk_acc[...] = jnp.zeros_like(dk_acc)
    dv_acc[...] = jnp.zeros_like(dv_acc)
    turns = [(half, at) for at in range(frames // QB) for half in range(2)]

    def start(half, at):
        rows = slice(at * QB, (at + 1) * QB)
        grad = grad_ref[rows, :] * jnp.where(lane == half, 1.0, 0.0).astype(BF)
        return grad, mm_nt(v_ref[0 : (at + 1) * QB, :], grad)

    ready = start(*turns[0])
    for index, (half, at) in enumerate(turns):
        stop = (at + 1) * QB
        rows = slice(at * QB, stop)
        own = slice(half * HEAD, (half + 1) * HEAD)
        grad, prob_grad = ready
        if half == 0:
            product = (out_ref[rows, :].astype(F32) * grad_ref[rows, :].astype(F32)).T
        if index + 1 < len(turns):
            ready = start(*turns[index + 1])
        query = q_ref[rows, :] * jnp.where(lane == half, SCALE, 0.0).astype(BF)
        delta = jnp.sum(product[own, :], 0, keepdims=True)
        prob = prob_ref[half, tri_start(at) : tri_start(at) + stop, :]
        dv_acc[0:stop, :] += mm(prob, grad)
        score_grad = (prob.astype(F32) * (prob_grad - delta)).astype(BF)
        dk_acc[0:stop, :] += mm(score_grad, query)
        dq_t_ref[own, rows] = mm(key_t_ref[own, 0:stop], score_grad)
    back_ref[0] = (dq_t_ref[...].T * SCALE).astype(BF)
    back_ref[1] = dk_acc[...].astype(BF)
    back_ref[2] = dv_acc[...].astype(BF)


def attend_back(places, triple, attended, pieces, probs, width):
    frames = triple.shape[0]
    pairs = width // LANES
    tri = tri_start(frames // QB)
    column = pl.BlockSpec((frames, LANES), lambda at: (0, at))
    return pl.pallas_call(
        attend_back_kernel,
        grid=(pairs,),
        in_specs=[smem()]
        + pair_specs(frames, width)
        + [column, pl.BlockSpec((2, tri, QB), lambda at: (at, 0, 0))]
        + [pl.BlockSpec((piece.shape[0], LANES), lambda at: (0, at)) for piece in pieces],
        out_specs=pl.BlockSpec((3, frames, LANES), lambda at: (0, 0, at)),
        out_shape=jax.ShapeDtypeStruct((3, frames, width), BF),
        scratch_shapes=[
            pltpu.VMEM((frames, LANES), BF),
            pltpu.VMEM((LANES, frames), BF),
            pltpu.VMEM((LANES, frames), F32),
            pltpu.VMEM((frames, LANES), F32),
            pltpu.VMEM((frames, LANES), F32),
        ],
        compiler_params=params(1, 42 * MIB),
        cost_estimate=cost(16 * tri * QB * HEAD * pairs, 2 * (8 * frames * width + 2 * pairs * tri * QB)),
        name="attend_back",
    )(places, triple, triple, triple, attended, probs, *pieces)


def feed_kernel(count, based, *refs):
    pieces, refs = refs[:count], refs[count:]
    bases, refs = refs[:based], refs[based:]
    cot_ref, down_in_ref, up_in_ref, down_out_ref, up_out_ref, w_in_ref, w_out_ref = refs[:7]
    out_refs, gu_refs, refs = refs[7 : 7 + count], refs[7 + count : 7 + 2 * count], refs[7 + 2 * count :]
    (
        gdown_in_ref, gup_in_ref, gdown_out_ref, gup_out_ref, normed_ref,
        out_acc, gu_acc, lat_in, glat_out, lat_acc, glat_acc, lat_t, glat_t,
    ) = refs
    at = pl.program_id(0)

    @pl.when(at == 0)
    def _():
        start = 0
        for piece_ref in pieces:
            normed_ref[start : start + piece_ref.shape[0], :] = piece_ref[...]
            start += piece_ref.shape[0]
        latent = mm_nt(normed_ref[...], down_in_ref[...]).astype(BF)
        glat = mm_nt(cot_ref[...], up_out_ref[...]).astype(BF)
        lat_in[...] = latent
        glat_out[...] = glat
        lat_t[...] = latent.astype(F32).T.astype(BF)
        glat_t[...] = glat.astype(F32).T.astype(BF)
        start = 0
        for base_ref in bases:
            out_acc[start : start + base_ref.shape[0], :] = base_ref[...]
            start += base_ref.shape[0]
        if not bases:
            out_acc[...] = jnp.zeros_like(out_acc)
        gu_acc[...] = jnp.zeros_like(gu_acc)
        lat_acc[...] = jnp.zeros_like(lat_acc)
        glat_acc[...] = jnp.zeros_like(glat_acc)

    w_in = w_in_ref[...]
    w_out = w_out_ref[...]
    pre = mm(normed_ref[...], w_in) + mm(lat_in[...], up_in_ref[...])
    act_grad = mm_nt(cot_ref[...], w_out) + mm(glat_out[...], down_out_ref[...])
    cdf = 0.5 * (1.0 + lax.erf(pre * SQRT_HALF))
    slope = cdf + pre * (jnp.exp(-0.5 * pre * pre) * INV_SQRT_2PI)
    act = (pre * cdf).astype(BF)
    pre_grad = (act_grad * slope).astype(BF)
    out_acc[...] += mm(act, w_out)
    gu_acc[...] += mm_nt(pre_grad, w_in)
    lat_acc[...] += mm_nt(act, down_out_ref[...])
    glat_acc[...] += mm_nt(pre_grad, up_in_ref[...])
    gup_in_ref[...] = mm(lat_t[...], pre_grad)
    gdown_out_ref[...] = mm(glat_t[...], act)

    @pl.when(at == pl.num_programs(0) - 1)
    def _():
        latent = lat_acc[...].astype(BF)
        glat = glat_acc[...].astype(BF)
        start = 0
        for out_ref, gu_ref in zip(out_refs, gu_refs):
            rows = slice(start, start + out_ref.shape[0])
            out_ref[...] = (out_acc[rows, :] + mm(latent[rows], up_out_ref[...])).astype(out_ref.dtype)
            gu_ref[...] = (gu_acc[rows, :] + mm(glat[rows], down_in_ref[...])).astype(gu_ref.dtype)
            start += out_ref.shape[0]
        gup_out_ref[...] = mm(latent.astype(F32).T.astype(BF), cot_ref[...])
        gdown_in_ref[...] = mm(glat.astype(F32).T.astype(BF), normed_ref[...])


def feed_forward(pieces, bases, cotangent, block_at, down_in, up_in, down_out, up_out, weights, hidden, kind):
    model = cotangent.shape[1]
    row_count = sum(item.shape[0] for item in pieces)
    rank = down_in.shape[0]
    block = FEED_BLOCK if hidden % FEED_BLOCK == 0 else hidden
    w_in, in_spec, w_out, out_spec = weights(block)
    main = pl.BlockSpec((row_count, model), lambda at: (block_at, 0))
    slim = pl.BlockSpec((rank, block), lambda at: (0, at))
    small = whole((rank, model))
    return pl.pallas_call(
        partial(feed_kernel, len(pieces), len(bases)),
        grid=(hidden // block,),
        in_specs=[once(item.shape) for item in pieces + bases]
        + [main, small, slim, slim, small, in_spec, out_spec],
        out_specs=[whole(item.shape) for item in pieces] * 2 + [small, slim, slim, small],
        out_shape=[jax.ShapeDtypeStruct(item.shape, kind) for item in pieces]
        + [jax.ShapeDtypeStruct(item.shape, BF) for item in pieces]
        + [
            jax.ShapeDtypeStruct((rank, model), F32),
            jax.ShapeDtypeStruct((rank, hidden), F32),
            jax.ShapeDtypeStruct((rank, hidden), F32),
            jax.ShapeDtypeStruct((rank, model), F32),
        ],
        scratch_shapes=[pltpu.VMEM((row_count, model), BF)]
        + [pltpu.VMEM((row_count, model), F32)] * 2
        + [pltpu.VMEM((row_count, rank), BF)] * 2
        + [pltpu.VMEM((row_count, rank), F32)] * 2
        + [pltpu.VMEM((rank, row_count), BF)] * 2,
        compiler_params=params(1),
        cost_estimate=cost(8 * row_count * model * hidden, 4 * hidden * model, 2 * row_count * hidden),
        name="feed_forward",
    )(*pieces, *bases, cotangent, down_in, up_in, down_out, up_out, w_in, w_out)


def spread_heads(rows_ref, into_ref, model):
    keys = rows_ref.shape[0]
    wide = 4 * HEAD
    row = lax.broadcasted_iota(jnp.int32, (4 * keys, wide), 0) // keys
    col = lax.broadcasted_iota(jnp.int32, (4 * keys, wide), 1) // HEAD
    mask = jnp.where(row == col, 1.0, 0.0).astype(BF)

    def some(group, carry):
        part = rows_ref[:, pl.ds(pl.multiple_of(group * wide, wide), wide)]
        into = pl.ds(pl.multiple_of(group * 4 * keys, 4 * keys), 4 * keys)
        into_ref[into, :] = jnp.concatenate([part] * 4, 0) * mask
        return carry

    lax.fori_loop(0, model // wide, some, 0)


def head_total(values, keys, reduce):
    split = values.reshape(4, keys, values.shape[1])
    return jnp.broadcast_to(reduce(split, 1, keepdims=True), split.shape).reshape(values.shape)


def each(count, step, work):
    def some(at, carry):
        work(pl.ds(pl.multiple_of(at * step, step), step))
        return carry

    lax.fori_loop(0, count // step, some, 0)


def weight_copies(plan, place_ref, sources, hold_ref, sem_ref):
    model = hold_ref.shape[1]
    groups = []
    for index, (start, extra) in enumerate(plan):
        if extra is None:
            pairs = [(sources[0].at[:, pl.ds(start, model)], hold_ref.at[index])]
        else:
            half = model // 2
            here, there = [pl.ds(pl.multiple_of(place_ref[at] * half, half), half) for at in range(2)]
            pairs = [(sources[0].at[:, pl.ds(start, half)], hold_ref.at[index, :, here])]
            for at in range(2):
                rows = pl.ds(pl.multiple_of(place_ref[2 + at] * half, half), half)
                pairs.append((sources[extra + at], hold_ref.at[index, rows, there]))
        groups.append(
            [pltpu.make_async_copy(src, dst, sem_ref.at[index, at]) for at, (src, dst) in enumerate(pairs)]
        )
    return groups


def source_count(plan):
    return 1 + 2 * sum(extra is not None for _, extra in plan)


def start_all(copies):
    for copy in copies:
        copy.start()


def wait_all(copies):
    for copy in copies:
        copy.wait()


def middle_kernel(plan, place_ref, *refs):
    sources, refs = refs[: source_count(plan)], refs[source_count(plan) :]
    inputs_ref, adapt_ref, gain_ref, bias_ref, keys_ref, values_ref = refs[:6]
    pieces = refs[6:-13]
    (
        attended_ref, resid1_ref, normed2_ref, query_ref, probs_ref, crossed_ref, resid2_ref, normed3_ref, lat_ref,
        hold_ref, key_wide, value_wide, sem_ref,
    ) = refs[-13:]
    model = inputs_ref.shape[1]
    keys = keys_ref.shape[0]
    rows = inputs_ref.shape[0]
    wide = 4 * HEAD
    copies = weight_copies(plan, place_ref, sources, hold_ref, sem_ref)
    start_all(copies[0])
    for index, piece_ref in enumerate(pieces):
        size = piece_ref.shape[1]
        attended_ref[:, pl.ds(pl.multiple_of(place_ref[index] * size, size), size)] = piece_ref[...]
    spread_heads(keys_ref, key_wide, model)
    spread_heads(values_ref, value_wide, model)

    def adapted(moving_ref, index, store):
        latent = mm_nt(moving_ref[...], adapt_ref[32 * index : 32 * index + 16, :]).astype(BF)
        lat_ref[:, 16 * index : 16 * index + 16] = latent
        wait_all(copies[index])
        if index < 2:
            start_all(copies[index + 1])

        def some(cols):
            store(
                cols,
                mm(moving_ref[...], hold_ref[index, :, cols])
                + mm(latent, adapt_ref[32 * index + 16 : 32 * index + 32, cols]),
            )

        each(model, 512, some)

    def add_first(cols, value):
        resid1_ref[:, cols] = inputs_ref[:, cols].astype(F32) + value

    def add_second(cols, value):
        resid2_ref[:, cols] = resid1_ref[:, cols] + value

    def keep_query(cols, value):
        query_ref[:, cols] = value.astype(BF)

    def normed(values_at, into_ref, which):
        def some(part):
            into_ref[part, :] = layer_norm(
                values_at[part, :], gain_ref[which : which + 1, :], bias_ref[which : which + 1, :]
            ).astype(BF)

        each(rows, 64, some)

    def cross(lanes):
        score = mm_nt(key_wide[lanes, :], query_ref[:, lanes]) * SCALE
        raised = jnp.exp(score - head_total(score, keys, jnp.max))
        prob = (raised / head_total(raised, keys, jnp.sum)).astype(BF)
        probs_ref[lanes, :] = prob
        crossed_ref[:, lanes] = mm_tn(prob, value_wide[lanes, :]).astype(BF)

    adapted(attended_ref, 0, add_first)
    normed(resid1_ref, normed2_ref, 1)
    adapted(normed2_ref, 1, keep_query)
    each(model, wide, cross)
    adapted(crossed_ref, 2, add_second)
    normed(resid2_ref, normed3_ref, 2)


def middle(places, own, own_spec, others, inputs, at, blocks, sources, plan, adapters, gains, biases, keys, values):
    rows, model = own_spec[0], inputs.shape[1]
    spread = model // HEAD * keys.shape[0]
    shape = lambda kind, dims=(rows, model): jax.ShapeDtypeStruct(dims, kind)
    flat = lambda dims: pl.BlockSpec(dims, lambda _, ref: (0,) * len(dims))
    shapes = [shape(kind) for kind in (BF, F32, BF, BF)]
    shapes += [shape(BF, (spread, rows)), shape(BF), shape(F32), shape(BF), shape(BF, (rows, 48))]
    return pl.pallas_call(
        partial(middle_kernel, plan),
        grid_spec=pltpu.PrefetchScalarGridSpec(
            num_scalar_prefetch=1,
            grid=(1,),
            in_specs=[pl.BlockSpec(memory_space=pl.ANY)] * len(sources)
            + [pl.BlockSpec((rows, model), lambda _, ref: (at, 0))]
            + [flat(item.shape) for item in (adapters, gains, biases, keys, values)]
            + [pl.BlockSpec(own_spec, lambda _, ref: (ref[0] * blocks + at, 0) if others else (at, 0))]
            + [flat(item.shape) for item in others],
            out_specs=[flat(item.shape) for item in shapes],
            scratch_shapes=[
                pltpu.VMEM((3, model, model), BF),
                pltpu.VMEM((spread, 4 * HEAD), BF),
                pltpu.VMEM((spread, 4 * HEAD), BF),
                pltpu.SemaphoreType.DMA((3, 3)),
            ],
        ),
        out_shape=shapes,
        compiler_params=params(),
        cost_estimate=cost(6 * rows * model * model, 6 * model * model + 24 * rows * model),
        name="middle",
    )(places, *sources, inputs, adapters, gains, biases, keys, values, own, *others)


def middle_back_kernel(plan, split, place_ref, *refs):
    sources, refs = refs[: source_count(plan)], refs[source_count(plan) :]
    (
        cot_ref, gu_ref, more_ref, attended_ref, resid1_ref, normed2_ref, query_ref, probs_ref, crossed_ref, resid2_ref,
        lat_ref, adapt_ref, gain_ref, keys_ref, values_ref,
    ) = refs[:15]
    refs = refs[15:]
    outs = refs[: 2 if split else 1]
    resid1_grad_ref, memory_ref, small_ref, hold_ref, key_wide, value_wide, work_ref, low_ref, sem_ref = refs[len(outs) :]
    rows, model = cot_ref.shape
    keys = keys_ref.shape[0]
    wide = 4 * HEAD
    copies = weight_copies(plan, place_ref, sources, hold_ref, sem_ref)
    start_all(copies[2])
    spread_heads(keys_ref, key_wide, model)
    spread_heads(values_ref, value_wide, model)

    def first(part):
        gradient = gu_ref[part, :].astype(F32) + more_ref[part, :].astype(F32)
        value = cot_ref[part, :].astype(F32) + norm_back(resid2_ref[part, :], gain_ref[2:3, :], gradient)
        resid1_grad_ref[part, :] = value
        low_ref[part, :] = value.astype(BF)

    def second(part):
        value = resid1_grad_ref[part, :] + norm_back(resid1_ref[part, :], gain_ref[1:2, :], work_ref[part, :])
        resid1_grad_ref[part, :] = value
        low_ref[part, :] = value.astype(BF)

    def back(moving_ref, index, store):
        down = slice(32 * index, 32 * index + 16)
        upper = slice(32 * index + 16, 32 * index + 32)
        glat = mm_nt(low_ref[...], adapt_ref[upper, :]).astype(BF)
        glat_t = glat.astype(F32).T.astype(BF)
        lat_t = lat_ref[:, 16 * index : 16 * index + 16].astype(F32).T.astype(BF)
        wait_all(copies[index])
        if index:
            start_all(copies[index - 1])

        def some(cols):
            small_ref[down, cols] = mm(glat_t, moving_ref[:, cols])
            small_ref[upper, cols] = mm(lat_t, low_ref[:, cols])
            store(cols, mm_nt(low_ref[...], hold_ref[index, cols, :]) + mm(glat, adapt_ref[down, cols]))

        each(model, 512, some)

    def keep(cols, value):
        work_ref[:, cols] = value

    def cross(lanes):
        part = work_ref[:, lanes].astype(BF)
        prob = probs_ref[lanes, :]
        wide_prob = prob.astype(F32)
        weighted = wide_prob * mm_nt(value_wide[lanes, :], part)
        score_grad = (weighted - wide_prob * head_total(weighted, keys, jnp.sum)).astype(BF)
        low_ref[:, lanes] = (mm_tn(score_grad, key_wide[lanes, :]) * SCALE).astype(BF)
        key_full = mm(score_grad, query_ref[:, lanes])
        value_full = mm(prob, part)
        col = lax.broadcasted_iota(jnp.int32, (keys, wide), 1) // HEAD
        key_sum, value_sum = key_full[:keys], value_full[:keys]
        for head in range(1, 4):
            rows_at = slice(head * keys, (head + 1) * keys)
            key_sum = jnp.where(col == head, key_full[rows_at], key_sum)
            value_sum = jnp.where(col == head, value_full[rows_at], value_sum)
        memory_ref[0, :, lanes] = key_sum * SCALE
        memory_ref[1, :, lanes] = value_sum

    each(rows, 64, first)
    back(crossed_ref, 2, keep)
    each(model, wide, cross)
    back(normed2_ref, 1, keep)
    each(rows, 64, second)
    back(attended_ref, 0, keep)
    if split:
        size = outs[0].shape[1]
        for out_ref, index in zip(outs, range(2)):
            out_ref[...] = work_ref[:, pl.ds(pl.multiple_of(place_ref[index] * size, size), size)].astype(BF)
    else:
        outs[0][...] = work_ref[...].astype(BF)


def middle_back(places, parts, at, cotangent, gu, more, kept, sources, plan, adapters, gains, keys, values):
    model = cotangent.shape[1]
    rows = kept[0].shape[0]
    spread = model // HEAD * keys.shape[0]
    flat = lambda dims: pl.BlockSpec(dims, lambda _, ref: (0,) * len(dims))
    block = pl.BlockSpec((rows, model), lambda _, ref: (at, 0))
    shapes = [jax.ShapeDtypeStruct((rows, model // parts), BF)] * parts + [
        jax.ShapeDtypeStruct((rows, model), F32),
        jax.ShapeDtypeStruct((2,) + keys.shape, F32),
        jax.ShapeDtypeStruct(adapters.shape, F32),
    ]
    return pl.pallas_call(
        partial(middle_back_kernel, plan, parts == 2),
        grid_spec=pltpu.PrefetchScalarGridSpec(
            num_scalar_prefetch=1,
            grid=(1,),
            in_specs=[pl.BlockSpec(memory_space=pl.ANY)] * len(sources)
            + [block, flat(gu.shape), flat(more.shape)]
            + [flat(item.shape) for item in kept]
            + [flat(item.shape) for item in (adapters, gains, keys, values)],
            out_specs=[flat(item.shape) for item in shapes],
            scratch_shapes=[
                pltpu.VMEM((3, model, model), BF),
                pltpu.VMEM((spread, 4 * HEAD), BF),
                pltpu.VMEM((spread, 4 * HEAD), BF),
                pltpu.VMEM((rows, model), F32),
                pltpu.VMEM((rows, model), BF),
                pltpu.SemaphoreType.DMA((3, 3)),
            ],
        ),
        out_shape=shapes,
        compiler_params=params(),
        cost_estimate=cost(6 * rows * model * model, 6 * model * model + 36 * rows * model),
        name="middle_back",
    )(places, *sources, cotangent, gu, more, *kept, adapters, gains, keys, values)


def qkv_grads_kernel(
    place_ref, grad_ref, normed_ref, lat_ref, up_ref, glat_ref, mine_ref, theirs_ref, glat_acc, gup_acc, down_acc,
    down_all, upper_all,
):
    at = pl.program_id(0)
    gradient = grad_ref[...]
    rank = mine_ref.shape[0]
    model = normed_ref.shape[1]
    width = gradient.shape[1]
    gup_acc[...] = mm_tn(lat_ref[...], gradient)

    @pl.when(at == 0)
    def _():
        glat_acc[...] = jnp.zeros_like(glat_acc)
        upper_all[...] = jnp.zeros_like(upper_all)

    into = pl.ds(pl.multiple_of(at * model + place_ref[0] * width, LANES), width)
    upper_all[:, into] = gup_acc[pl.ds(pl.multiple_of(at * rank, rank), rank), :].astype(BF)
    glat_acc[...] += mm_nt(gradient, up_ref[...])

    @pl.when(at == pl.num_programs(0) - 1)
    def _():
        low = glat_acc[...].astype(BF)
        glat_ref[...] = low
        down_acc[...] = mm_tn(low, normed_ref[...])
        for part in range(3):
            down_all[:, part * model : (part + 1) * model] = down_acc[part * rank : (part + 1) * rank, :].astype(BF)
        share(place_ref, down_all, upper_all, mine_ref, theirs_ref)


def share(place_ref, down_all, upper_all, mine_ref, theirs_ref):
    @pl.when(place_ref[0] == 0)
    def _():
        mine_ref[...] = down_all[...]
        theirs_ref[...] = upper_all[...]

    @pl.when(place_ref[0] != 0)
    def _():
        mine_ref[...] = upper_all[...]
        theirs_ref[...] = down_all[...]


def qkv_grads(places, gradient, normed, latent, up):
    frames, model = normed.shape
    parts, ranks, width = up.shape
    rank = ranks // parts
    table = jax.ShapeDtypeStruct((rank, parts * model), BF)
    return pl.pallas_call(
        qkv_grads_kernel,
        grid=(parts,),
        in_specs=[
            smem(),
            pl.BlockSpec((None, frames, width), lambda at: (at, 0, 0)),
            whole(normed.shape),
            whole(latent.shape),
            pl.BlockSpec((None, ranks, width), lambda at: (at, 0, 0)),
        ],
        out_specs=[whole(latent.shape), whole(table.shape), whole(table.shape)],
        out_shape=[jax.ShapeDtypeStruct(latent.shape, BF), table, table],
        scratch_shapes=[
            pltpu.VMEM(latent.shape, F32),
            pltpu.VMEM((ranks, width), F32),
            pltpu.VMEM((ranks, model), F32),
            pltpu.VMEM(table.shape, BF),
            pltpu.VMEM(table.shape, BF),
        ],
        compiler_params=params(1, 42 * MIB),
        cost_estimate=cost(8 * frames * ranks * width * parts, 2 * frames * (model + parts * width)),
        name="qkv_grads",
    )(places, gradient, normed, latent, up)


def qkv_back_kernel(place_ref, grad_ref, glat_ref, down_ref, w_ref, gu_ref, gu_acc):
    at = pl.program_id(0)
    model = gu_ref.shape[1]
    last = pl.num_programs(0) - 1

    def some(cols):
        direct = mm_nt(grad_ref[...], w_ref[cols, :])

        @pl.when(at == 0)
        def _():
            gu_acc[:, cols] = direct + mm(glat_ref[...], down_ref[:, cols])

        @pl.when(jnp.logical_and(at > 0, at < last))
        def _():
            gu_acc[:, cols] += direct

        @pl.when(at == last)
        def _():
            gu_ref[:, cols] = (gu_acc[:, cols] + direct).astype(gu_ref.dtype)

    each(model, 512, some)


def qkv_back(place, row_count, gradient, glat, down, packed, start, kind):
    ranks, model = down.shape
    width = gradient.shape[2]
    if start % width == 0 and width % LANES == 0:
        weight, spec = packed, pl.BlockSpec((model, width), lambda at, ref: (0, start // width + at))
    else:
        weight = packed[:, start : start + 3 * width].reshape(model, 3, width).transpose(1, 0, 2)
        spec = pl.BlockSpec((None, model, width), lambda at, ref: (at, 0, 0))
    return pl.pallas_call(
        qkv_back_kernel,
        grid_spec=pltpu.PrefetchScalarGridSpec(
            num_scalar_prefetch=1,
            grid=(3,),
            in_specs=[
                pl.BlockSpec((None, row_count, width), lambda at, ref: (at, ref[0], 0)),
                pl.BlockSpec((row_count, ranks), lambda at, ref: (ref[0], 0)),
                pl.BlockSpec(down.shape, lambda at, ref: (0, 0)),
                spec,
            ],
            out_specs=pl.BlockSpec((row_count, model), lambda at, ref: (0, 0)),
            scratch_shapes=[pltpu.VMEM((row_count, model), F32)],
        ),
        out_shape=jax.ShapeDtypeStruct((row_count, model), kind),
        compiler_params=params(1, 42 * MIB),
        cost_estimate=cost(6 * row_count * model * width, 6 * model * width + 8 * row_count * model),
        name="qkv_back",
    )(place, gradient, glat, down, weight)


def last_norm_kernel(blocks, frames_ref, gradient_ref, gain_ref, *refs):
    pieces, grad_ref = refs[:-1], refs[-1]
    at = pl.program_id(0)
    back = norm_back(frames_ref[...].astype(F32), gain_ref[...], gradient_ref[...])
    for index, piece_ref in enumerate(pieces):

        @pl.when(at // blocks == index)
        def _(piece_ref=piece_ref):
            grad_ref[...] = back + piece_ref[...]


def last_norm(frames, gradient, gains, pieces):
    rows, model = frames.shape
    step = min(128, rows)
    blocks = pieces[0].shape[0] // step
    block = pl.BlockSpec((step, model), lambda at: (at, 0))

    def piece_spec(index):
        return pl.BlockSpec((step, model), lambda at: (jnp.clip(at - index * blocks, 0, blocks - 1), 0))

    return pl.pallas_call(
        partial(last_norm_kernel, blocks),
        grid=(rows // step,),
        in_specs=[block, block, whole(gains.shape)] + [piece_spec(index) for index in range(len(pieces))],
        out_specs=block,
        out_shape=jax.ShapeDtypeStruct((rows, model), F32),
        compiler_params=params(1, 42 * MIB),
        cost_estimate=cost(20 * rows * model, 16 * rows * model),
        name="last_norm",
    )(frames, gradient, gains, *pieces)


def run_length(size):
    count = 1
    while count * size % LANES:
        count *= 2
    return count


def join_kernel(pieces_ref, flat_ref):
    count, _, size = pieces_ref.shape
    run = run_length(size)

    def some(at, carry):
        parts = [pieces_ref[at * run + index] for index in range(run)]
        into = pl.ds(pl.multiple_of(at * run * size, LANES), run * size)
        flat_ref[:, into] = jnp.concatenate(parts, 1)
        return carry

    lax.fori_loop(0, count // run, some, 0)


def join_pieces(pieces):
    count, rows, size = pieces.shape
    if count % run_length(size):
        return pieces.transpose(1, 0, 2).reshape(rows, count * size)
    return pl.pallas_call(
        join_kernel,
        out_shape=jax.ShapeDtypeStruct((rows, count * size), pieces.dtype),
        compiler_params=params(0),
        name="join_pieces",
    )(pieces)


def split_kernel(*refs):
    sources, pieces_ref, flat_ref = refs[:-2], refs[-2], refs[-1]
    count, _, size = pieces_ref.shape
    run = run_length(size)
    start = 0
    for first_ref, second_ref in zip(sources[::2], sources[1::2]):
        width = first_ref.shape[1]
        both = first_ref[...].astype(F32) + second_ref[...].astype(F32)
        flat_ref[:, start : start + width] = both.astype(BF)
        start += width

    def some(at, carry):
        block = flat_ref[:, pl.ds(pl.multiple_of(at * run * size, LANES), run * size)]
        for index in range(run):
            pieces_ref[at * run + index] = block[:, index * size : (index + 1) * size]
        return carry

    lax.fori_loop(0, count // run, some, 0)


def split_sums(pairs, count):
    rows = pairs[0].shape[0]
    total = sum(item.shape[1] for item in pairs[::2])
    return pl.pallas_call(
        split_kernel,
        out_shape=jax.ShapeDtypeStruct((count, rows, total // count), BF),
        scratch_shapes=[pltpu.VMEM((rows, total), BF)],
        compiler_params=params(0, 42 * MIB),
        name="split_sums",
    )(*pairs)


def unit_loop(plan, work):
    fsdp, seq, folds, local = plan
    run = run_length(local)

    def some(at, carry):
        span = run * seq * folds * local
        block = pl.ds(pl.multiple_of(at * span, LANES), span)
        folded = [
            pl.ds(pl.multiple_of(fold * fsdp * local + at * run * local, LANES), run * local) for fold in range(folds)
        ]
        work(run, block, folded)
        return carry

    lax.fori_loop(0, fsdp // run, some, 0)


def take_units_kernel(plan, place_ref, all_ref, *refs):
    own_ref = refs[-1]
    _, seq, folds, local = plan
    spot = place_ref[0]

    def work(run, block, folded):
        values = all_ref[:, block]
        for fold, into in enumerate(folded):
            parts = []
            for index in range(run):
                base = (index * seq * folds + fold) * local
                part = values[:, base : base + local]
                for other in range(1, seq):
                    shift = base + other * folds * local
                    part = jnp.where(spot == other, values[:, shift : shift + local], part)
                parts.append(part)
            own_ref[:, into] = jnp.concatenate(parts, 1)

    unit_loop(plan, work)
    if len(refs) == 2:
        model = refs[0].shape[1]
        hidden = own_ref.shape[1] - folds * model
        for fold in range(folds):
            rows = pl.ds(pl.multiple_of((spot * folds + fold) * local, 16), local)
            own_ref[:, hidden + fold * model : hidden + (fold + 1) * model] = refs[0][rows, :]


def take_units(plan, places, matrix, low=None):
    _, seq, folds, local = plan
    rows, width = matrix.shape
    extra = [] if low is None else [low]
    out_width = width // seq + sum(folds * item.shape[1] for item in extra)
    return pl.pallas_call(
        partial(take_units_kernel, plan),
        in_specs=[smem()] + [pl.BlockSpec(memory_space=pltpu.VMEM)] * (1 + len(extra)),
        out_shape=jax.ShapeDtypeStruct((rows, out_width), matrix.dtype),
        compiler_params=params(0),
        name="take_units",
    )(places, matrix, *extra)


def collect_kernel(plan, blocks, start_at, place_ref, *refs):
    parts, squares, refs = refs[:blocks], refs[blocks : 2 * blocks], refs[2 * blocks :]
    feeds = [refs[at : at + 4] for at in range(0, len(refs) - 14, 4)]
    (
        other_ref, lat_ref, flat_ref, down_text_ref, text_ref, w_ref,
        mine_ref, theirs_ref, text_grad_ref, down_all, upper_all, unit_acc, hold_ref, sem_ref,
    ) = refs[-14:]
    _, seq, folds, local = plan
    rank = mine_ref.shape[0]
    model = text_ref.shape[1]
    wide = other_ref.shape[2]
    spot = place_ref[0]
    own = pl.ds(pl.multiple_of(spot * wide, wide), wide)
    copy = pltpu.make_async_copy(w_ref.at[:, pl.ds(start_at, hold_ref.shape[1])], hold_ref, sem_ref)
    copy.start()

    def total(items, rows):
        value = items[0][rows, :]
        for item in items[1:]:
            value = value + item[rows, :]
        return value

    moved = []
    for part in range(2):
        value = parts[0][part, :, own]
        for item in parts[1:]:
            value = value + item[part, :, own]
        moved.append((value + other_ref[part].astype(F32)).astype(BF))
    moved = jnp.concatenate(moved, 1)
    glat = mm_nt(moved, flat_ref[...]).astype(BF)
    gup = mm_tn(lat_ref[...], moved)
    gdown = mm_tn(glat, text_ref[...])

    upper_all[:, 2 * model : 4 * model] = jnp.zeros((rank, 2 * model), BF)
    for part in range(2):
        rows = slice(part * rank, (part + 1) * rank)
        down_all[:, (2 + part) * model : (3 + part) * model] = gdown[rows].astype(BF)
        into = pl.ds(pl.multiple_of((2 + part) * model + spot * wide, LANES), wide)
        upper_all[:, into] = gup[rows, part * wide : (part + 1) * wide].astype(BF)
    for index, at in enumerate((0, 1, 4)):
        cols = slice(at * model, (at + 1) * model)
        down_all[:, cols] = total(squares, slice(2 * index * rank, (2 * index + 1) * rank)).astype(BF)
        upper_all[:, cols] = total(squares, slice((2 * index + 1) * rank, (2 * index + 2) * rank)).astype(BF)
    every = slice(0, rank)
    down_all[:, 5 * model : 6 * model] = total([item[0] for item in feeds], every).astype(BF)
    upper_all[:, upper_all.shape[1] - model :] = total([item[3] for item in feeds], every).astype(BF)
    for into_ref, start, which in ((upper_all, 5 * model, 1), (down_all, 6 * model, 2)):
        unit_acc[...] = total([item[which] for item in feeds], every)

        def work(run, block, folded):
            values = [unit_acc[:, cols] for cols in folded]
            spread = []
            for index in range(run):
                for other in range(seq):
                    for fold in range(folds):
                        part = values[fold][:, index * local : (index + 1) * local]
                        spread.append(jnp.where(spot == other, part, 0.0))
            at = pl.ds(pl.multiple_of(start + block.start, LANES), block.size)
            into_ref[:, at] = jnp.concatenate(spread, 1).astype(BF)

        unit_loop(plan, work)
    share(place_ref, down_all, upper_all, mine_ref, theirs_ref)
    copy.wait()
    text_grad_ref[...] = (mm_nt(moved, hold_ref[...]) + mm(glat, down_text_ref[...])).astype(BF)


def collect(plan, places, parts, squares, feeds, other, lat_text, flat_text, down_text, text, packed, start):
    rank = squares[0].shape[0] // 6
    model = text.shape[1]
    hidden = feeds[0][1].shape[1]
    wide2 = flat_text.shape[1]
    width = 6 * model + hidden * plan[1]
    feeds = [item for feed in feeds for item in feed]
    before = list(parts) + list(squares) + feeds + [other, lat_text, flat_text, down_text, text]
    table = jax.ShapeDtypeStruct((rank, width), BF)
    shapes = [table, table, jax.ShapeDtypeStruct(text.shape, BF)]
    return pl.pallas_call(
        partial(collect_kernel, plan, len(parts), start),
        grid=(1,),
        in_specs=[smem()] + [whole(item.shape) for item in before] + [pl.BlockSpec(memory_space=pl.ANY)],
        out_specs=[whole(item.shape) for item in shapes],
        out_shape=shapes,
        scratch_shapes=[pltpu.VMEM(table.shape, BF)] * 2
        + [pltpu.VMEM((rank, hidden), F32), pltpu.VMEM((model, wide2), BF), pltpu.SemaphoreType.DMA],
        compiler_params=params(1),
        cost_estimate=cost(4 * text.shape[0] * model * wide2, 2 * model * wide2),
        name="collect",
    )(places, *before, packed)


def both_kernel(place_ref, mine_ref, other_ref, down_ref, upper_ref):
    first = place_ref[0] == 0
    for at in range(mine_ref.shape[0]):
        mine, other = mine_ref[at].astype(F32), other_ref[at].astype(F32)
        down_ref[at] = jnp.where(first, mine, other)
        upper_ref[at] = jnp.where(first, other, mine)


def both_tables(places, mine, other):
    return pl.pallas_call(
        both_kernel,
        in_specs=[smem()] + [pl.BlockSpec(memory_space=pltpu.VMEM)] * 2,
        out_shape=[jax.ShapeDtypeStruct(mine.shape, F32)] * 2,
        compiler_params=params(0, 42 * MIB),
        name="both_tables",
    )(places, mine, other)


def body(
    inputs,
    text_states,
    adapter_index,
    norm_gains,
    norm_biases,
    self_in,
    self_out,
    cross_query,
    cross_text,
    cross_out,
    hidden_in,
    hidden_out,
    adapter_down,
    adapter_up,
    cotangent,
    *,
    sizes,
):
    seq, fsdp = sizes
    spot = lax.axis_index("seq")
    first_here = spot == 0
    there = (seq - 1) - spot
    local = self_in.shape[0]
    depth = hidden_out.shape[0] // seq
    pair = seq == 2 and depth % local == 0 and fsdp % run_length(local) == 0
    model = inputs.shape[2]
    rows = inputs.shape[1]
    frames = rows * seq
    wide = model // seq
    hidden_all = hidden_in.shape[1]
    hidden = hidden_all // seq
    adapters, rank, piece = adapter_down.shape
    total = piece * fsdp

    blocks = max(rows // 256, 1)
    size = rows // blocks

    def swap(value):
        return lax.ppermute(value, "seq", [(0, 1), (1, 0)])

    def pick(value, axis, extent, which=None):
        return lax.dynamic_slice_in_dim(value, (spot if which is None else which) * extent, extent, axis)

    def ordered(mine, other):
        return jnp.where(first_here, mine, other), jnp.where(first_here, other, mine)

    def gather(value, axis):
        if pair:
            return jnp.concatenate(ordered(value, swap(value)), axis)
        return lax.all_gather(value, "seq", axis=axis, tiled=True)

    def after(value, *others):
        return lax.optimization_barrier((value,) + others)[0]

    def put(value, axis):
        shape = list(value.shape)
        shape[axis] = seq
        return lax.dynamic_update_slice_in_dim(jnp.zeros(shape, value.dtype), value, spot, axis)

    def own_columns(matrix, parts):
        return [pick(matrix[:, at * model : (at + 1) * model], 1, wide) for at in range(parts)]

    def flat_down(grads, parts):
        return jnp.concatenate([grads[at * rank : (at + 1) * rank] for at in range(parts)], 1)

    def flat_upper(own):
        return put(jnp.stack(own, 1)[:, :, None], 2).reshape(rank, len(own) * model)

    halved = [pick(item, 1, wide) if pair else item for item in (self_out, cross_query)]
    first = [cross_out] + own_columns(cross_text, 2) + halved + own_columns(self_in, 3)
    edges = [0]
    for item in first:
        edges.append(edges[-1] + item.shape[1])
    start_in, start_text = edges[5], edges[1]
    packed = lax.all_gather(jnp.concatenate(first, 1), "fsdp", axis=0, tiled=True)
    squares_plan = ((edges[3], None), (edges[4], None), (edges[0], None))
    if pair:
        squares_plan = ((edges[3], 1), (edges[4], 3)) + squares_plan[2:]
    core = lax.rem(lax.axis_index("fsdp"), 2)
    where_here = jnp.stack([spot, there, core, 1 - core]).astype(jnp.int32)
    if pair:
        folds = depth // local
        plan = (fsdp, seq, folds, local)
        own_units = partial(take_units, plan, where_here)
        packed_feed = lax.all_gather(own_units(hidden_in, hidden_out), "fsdp", axis=0, tiled=True)

        def feed_weights(block):
            per = model // block
            return (
                packed_feed,
                pl.BlockSpec((model, block), lambda at: (0, at)),
                packed_feed,
                pl.BlockSpec((block, model), lambda at: (at % per, folds + at // per)),
            )
    else:

        def own_units(matrix):
            kept = lax.dynamic_index_in_dim(matrix.reshape(-1, fsdp, seq, depth), spot, 2, False)
            return kept.reshape(-1, hidden)

        def all_units(matrix):
            return put(matrix.reshape(-1, fsdp, 1, depth), 2).reshape(-1, hidden_all)

        whole_in = lax.all_gather(own_units(hidden_in), "fsdp", axis=0, tiled=True)
        whole_out = lax.all_gather(pick(hidden_out, 0, depth), "fsdp", axis=0, tiled=True)

        def feed_weights(block):
            return (
                whole_in,
                pl.BlockSpec((model, block), lambda at: (0, at)),
                whole_out,
                pl.BlockSpec((block, model), lambda at: (at, 0)),
            )

    index_all = lax.all_to_all(jnp.broadcast_to(adapter_index, (fsdp,)), "fsdp", 0, 0, tiled=True)
    if pair:
        table = jnp.where(first_here, adapter_down, adapter_up)
        mine = join_pieces(lax.all_to_all(jnp.take(table, index_all, axis=0), "fsdp", 0, 0, tiled=True))
        down_all, upper_all = ordered(mine, swap(mine))
    else:
        table = jnp.concatenate([adapter_down, adapter_up], 1)
        chosen = join_pieces(lax.all_to_all(jnp.take(table, index_all, axis=0), "fsdp", 0, 0, tiled=True))
        down_all, upper_all = chosen[:rank], chosen[rank:]
    in_cuts = [0, 3 * model, 4 * model, 5 * model, 7 * model, 8 * model, 9 * model, 9 * model + hidden_all]
    out_cuts = [0, 3 * model, 4 * model, 5 * model, 7 * model, 8 * model, 8 * model + hidden_all, 9 * model + hidden_all]
    downs = [down_all[:, in_cuts[at] : in_cuts[at + 1]] for at in range(7)]
    uppers = [upper_all[:, out_cuts[at] : out_cuts[at + 1]] for at in range(7)]

    def part_down(matrix, parts):
        return jnp.concatenate([matrix[:, at * model : (at + 1) * model] for at in range(parts)], 0)

    def part_upper(matrix, parts):
        own = own_columns(matrix, parts)
        return jnp.stack(
            [jnp.pad(item, ((at * rank, (parts - 1 - at) * rank), (0, 0))) for at, item in enumerate(own)], 0
        )

    units = own_units(jnp.concatenate([uppers[5], downs[6]], 0))
    feed_adapters = (downs[5], units[:rank], units[rank:], uppers[6])
    square_adapters = jnp.concatenate([downs[1], uppers[1], downs[2], uppers[2], downs[4], uppers[4]], 0)
    down_qkv, upper_qkv = part_down(downs[0], 3), part_upper(uppers[0], 3)
    down_text, upper_text = part_down(downs[3], 2), part_upper(uppers[3], 2)
    flat_text = jnp.concatenate([upper_text[0], upper_text[1]], 1)

    frames_in = inputs[0]
    cot = cotangent[0]
    if pair:
        frames_parts = [frames_in, swap(frames_in)]
        cot_other = swap(after(cot, frames_parts[1]))
    else:
        frames_parts = [lax.all_gather(frames_in, "seq", axis=0, tiled=True)]
    norm_places = where_here if pair else jnp.zeros((4,), jnp.int32)
    if pair:
        frames_parts[1] = after(frames_parts[1], cot_other, units)
    normed1, lat_qkv = norm_project(norm_places, frames_parts, norm_gains[0:1], norm_biases[0:1], down_qkv)
    packed = after(packed, normed1)
    sources = [packed]
    if pair:
        half = model // 2
        straight = [swap(lax.dynamic_slice(packed, (core * half, at), (half, wide))) for at in edges[3:5]]
    triple = qkv_project(normed1, lat_qkv, upper_qkv, packed, start_in, 3 * wide)
    padded = -(-wide // LANES) * LANES
    if padded != wide:
        triple = jnp.pad(triple.reshape(frames, 3, wide), ((0, 0), (0, 0), (0, padded - wide)))
        triple = triple.reshape(frames, 3 * padded)
    text = after(text_states[0], triple)
    w_text = packed[:, start_text : start_text + 2 * wide]
    lat_text = mm_nt(text, down_text).astype(BF)
    memory = (mm(text, w_text) + mm(lat_text, flat_text)).astype(BF)
    head_out, probs, *leaving = attend(where_here, [size] * blocks if pair else [], after(triple, memory), padded)

    memory_all = gather(memory.reshape(-1, 2, wide), 2)
    keys, values = memory_all[:, 0], memory_all[:, 1]

    constants = (sources, squares_plan, square_adapters, norm_gains, norm_biases, keys, values)
    if pair:
        received = [swap(leaving[0])]
        for item in leaving[1:]:
            received.append(swap(after(item, received[-1])))
        neighbours = [(at, at ^ 1) for at in range(fsdp)]
        for item in straight:
            sources += [item, lax.ppermute(after(item, received[0], memory_all), "fsdp", neighbours)]
    else:
        natural = lax.all_to_all(head_out[:, :wide], "seq", split_axis=0, concat_axis=1, tiled=True)
    made = []
    for at in range(blocks):
        if pair:
            own, spec, others = head_out, (size, wide), [received[at]]
        else:
            own, spec, others = natural, (size, model), []
        ready = after(frames_in, made[-1][7]) if made else frames_in
        made.append(middle(where_here if pair else jnp.zeros((4,), jnp.int32), own, spec, others, ready, at, blocks, *constants))
    normed3 = [item[7] for item in made]
    resid2 = [item[6] for item in made]

    feed_tail = feed_adapters + (feed_weights, hidden)
    if pair:
        others = [swap(item) for item in normed3]
        ours = [feed_forward(normed3[:1], resid2[:1], cot, 0, *feed_tail, F32)]
        theirs = feed_forward([others[0], after(others[1], ours[0][0])] if blocks > 1 else others, [], cot_other, 0, *feed_tail, BF)
        out_leaving, gu_leaving = theirs[:blocks], theirs[blocks : 2 * blocks]
        gu_more = [swap(gu_leaving[0])]
        for at in range(1, blocks):
            ours.append(feed_forward([after(normed3[at], gu_leaving[0])], [resid2[at]], cot, at, *feed_tail, F32))
            gu_more.append(swap(after(gu_leaving[at], gu_more[-1], ours[-1][0])))
        gu = [item[1] for item in ours]
        out_more = []
        feed_grads = [item[2:] for item in ours] + [theirs[2 * blocks :]]
    else:
        wide_in = gather(jnp.concatenate(normed3, 0), 0)
        all_out = feed_forward([wide_in], [], gather(cot, 0), 0, *feed_tail, F32)
        summed = [
            lax.psum_scatter(item.astype(BF), "seq", scatter_dimension=0, tiled=True) for item in all_out[:2]
        ]
        output = (jnp.concatenate(resid2, 0) + summed[0].astype(F32)).astype(BF)
        gu = [summed[1][at * size : (at + 1) * size] for at in range(blocks)]
        gu_more = [jnp.zeros_like(item) for item in gu]
        feed_grads = [all_out[2:]]

    pieces, resid1_grads, memory_parts, square_parts = [], [], [], []
    for at in range(blocks):
        gu_here = gu[at] if at == 0 else after(gu[at], result[-3])
        kept = made[at][:7] + made[at][8:9]
        result = middle_back(
            where_here, 2 if pair else 1, at, cot, gu_here, gu_more[at],
            kept, sources, squares_plan, square_adapters, norm_gains, keys, values,
        )
        if pair:
            waited = [pieces[-1][1]] if at else []
            if at == 0:
                out_more.append(swap(after(out_leaving[0], result[0])))
            if at == blocks - 1:
                memory_part = sum(memory_parts, result[-2]).astype(BF)
                memory_other = swap(after(pick(memory_part, 2, wide, there), *out_more))
                waited.append(memory_other)
            pieces.append((result[0], swap(after(result[1], *waited) if waited else result[1])))
        else:
            pieces.append(result[0])
        resid1_grads.append(result[-3])
        memory_parts.append(result[-2])
        square_parts.append(result[-1])
    resid1_grad = jnp.concatenate(resid1_grads, 0)
    square_grads = sum(square_parts[1:], square_parts[0])

    if pair:
        early, early_leaving, text_low = collect(
            plan, where_here, memory_parts, square_parts, feed_grads, memory_other, lat_text, flat_text, down_text,
            text_states[0], packed, start_text,
        )
        grad_pieces = [item[0] for item in pieces] + [item[1] for item in pieces]
    else:
        head_grad = lax.all_to_all(jnp.concatenate(pieces, 0), "seq", split_axis=1, concat_axis=0, tiled=True)
        grad_pieces = [jnp.pad(head_grad, ((0, 0), (0, padded - wide)))]
    triple_grad = attend_back(where_here, triple, head_out, grad_pieces, probs, padded)[:, :, :wide]
    if pair:
        early_other = swap(after(early_leaving, pieces[-1][1]))
        for at in range(1, blocks):
            out_more.append(swap(after(out_leaving[at], pieces[-1][1])))
        glat_qkv, late, late_leaving = qkv_grads(
            where_here, triple_grad, normed1, lat_qkv, upper_qkv
        )
        late_other = swap(late_leaving)
    else:
        glat_qkv = sum(mm_nt(triple_grad[at], upper_qkv[at]) for at in range(3)).astype(BF)
        gdown_qkv = mm_tn(glat_qkv, normed1)
        gup_qkv = [mm_tn(lat_qkv[:, at * rank : (at + 1) * rank], triple_grad[at]) for at in range(3)]
    back = partial(qkv_back, gradient=triple_grad, glat=glat_qkv, down=down_qkv, packed=packed, start=start_in)
    if pair:
        for_them = back(after(there, early_other, *out_more)[None], rows, kind=BF)
        for_us = back(after(spot, for_them, *out_more)[None], rows, kind=F32)
        input_grad = last_norm(frames_in, for_us + swap(for_them).astype(F32), norm_gains[0:1], resid1_grads)
        output = jnp.concatenate(
            [(item[0] + other.astype(F32)).astype(BF) for item, other in zip(ours, out_more)], 0
        )
    else:
        full = back(jnp.zeros((1,), jnp.int32), frames, kind=BF)
        normed1_grad = lax.psum_scatter(full, "seq", scatter_dimension=0, tiled=True).astype(F32)
        resid1_grad = jnp.concatenate(resid1_grads, 0)
        input_grad = resid1_grad + norm_back(frames_in.astype(F32), norm_gains[0:1], normed1_grad)

    selector = (index_all[None, :] == jnp.arange(adapters, dtype=jnp.int32)[:, None]).astype(BF)

    def by_adapter(sent, *others):
        received = lax.all_to_all(sent, "fsdp", 0, 0, tiled=True)
        chooser = after(selector, *others) if others else selector
        return jnp.einsum("ac,crw->arw", chooser, received, preferred_element_type=F32)

    if pair:
        shares = by_adapter(split_sums([after(late, for_them), late_other, early, early_other], fsdp)).astype(BF)
        grad_down, grad_up = both_tables(where_here, after(shares, input_grad), swap(after(shares, for_us)))
        text_total = text_low.astype(F32) + swap(text_low).astype(F32)
    else:
        memory_part = sum(memory_parts[1:], memory_parts[0]).astype(BF)
        memory_grad = lax.psum_scatter(memory_part, "seq", scatter_dimension=2, tiled=True)
        memory_flat = jnp.concatenate([memory_grad[0], memory_grad[1]], 1)
        glat_text = mm_nt(memory_flat, flat_text).astype(BF)
        gup_text = mm_tn(lat_text, memory_flat)
        gdown_text = mm_tn(glat_text, text)
        text_low = (mm_nt(memory_flat, w_text) + mm(glat_text, down_text)).astype(BF)
        own_text = [gup_text[at * rank : (at + 1) * rank, at * wide : (at + 1) * wide] for at in range(2)]
        gdown_in, gup_in, gdown_out, gup_out = feed_grads[0]
        square_grads = sum(square_parts[1:], square_parts[0])
        squares = [square_grads[rank * at : rank * (at + 1)] for at in range(6)]
        down_sent = [flat_down(gdown_qkv, 3), squares[0], squares[2], flat_down(gdown_text, 2), squares[4], gdown_in]
        upper_sent = [flat_upper(gup_qkv), squares[1], squares[3], flat_upper(own_text), squares[5]]
        down_sent = jnp.concatenate(down_sent + [all_units(gdown_out)], 1)
        upper_sent = jnp.concatenate(upper_sent + [all_units(gup_in), gup_out], 1)
        sent = jnp.concatenate([down_sent, upper_sent], 0).astype(BF).reshape(2 * rank, fsdp, piece).transpose(1, 0, 2)
        shares = lax.psum(by_adapter(sent).astype(BF), "seq")
        grad_down, grad_up = shares[:, :rank], shares[:, rank:]
        text_total = lax.psum(text_low, "seq").astype(F32)
    return (output[None], input_grad[None], text_total[None], grad_down.astype(F32), grad_up.astype(F32))


def solution(mesh):
    return jax.shard_map(
        partial(body, sizes=(mesh.shape["seq"], mesh.shape["fsdp"])),
        mesh=mesh,
        in_specs=(
            P("fsdp", "seq", None),
            P("fsdp", None, None),
            P("fsdp"),
            P(),
            P(),
            P("fsdp", None),
            P("fsdp", None),
            P("fsdp", None),
            P("fsdp", None),
            P("fsdp", None),
            P("fsdp", None),
            P("fsdp", None),
            P(None, None, "fsdp"),
            P(None, None, "fsdp"),
            P("fsdp", "seq", None),
        ),
        out_specs=(
            P("fsdp", "seq", None),
            P("fsdp", "seq", None),
            P("fsdp", None, None),
            P(None, None, "fsdp"),
            P(None, None, "fsdp"),
        ),
        check_vma=False,
    )
```

```python
from functools import partial

import jax
import jax.numpy as jnp
from jax import lax
from jax.experimental import pallas as pl
from jax.experimental.pallas import tpu as pltpu
from jax.sharding import PartitionSpec as P

HEAD = 64
LANES = 128
QB = 256
BF = jnp.bfloat16
F32 = jnp.float32
SCALE = float(HEAD) ** (-0.5)
SQRT_HALF = 0.7071067811865476
INV_SQRT_2PI = 0.3989422804014327
MIB = 1024 * 1024
VMEM_LIMIT = 60 * MIB
COST = 1.0
FEED_BLOCK = 512


def mm(a, b):
    return lax.dot_general(a, b, (((1,), (0,)), ((), ())), preferred_element_type=F32)


def mm_nt(a, b):
    return lax.dot_general(a, b, (((1,), (1,)), ((), ())), preferred_element_type=F32)


def mm_tn(a, b):
    return lax.dot_general(a, b, (((0,), (0,)), ((), ())), preferred_element_type=F32)


def norm_stats(values):
    centered = values - jnp.mean(values, -1, keepdims=True)
    variance = jnp.mean(centered * centered, -1, keepdims=True)
    inverse = lax.rsqrt(variance + 1e-05)
    return centered * inverse, inverse


def layer_norm(values, gains, biases):
    unit, _ = norm_stats(values)
    return unit * gains + biases


def norm_back(values, gains, gradient):
    unit, inverse = norm_stats(values)
    scaled = gradient * gains
    mean_one = jnp.mean(scaled, -1, keepdims=True)
    mean_two = jnp.mean(scaled * unit, -1, keepdims=True)
    return inverse * (scaled - mean_one - unit * mean_two)


def whole(shape):
    return pl.BlockSpec(shape, lambda *_: (0,) * len(shape))


def once(shape):
    return pl.BlockSpec(shape, lambda *_: (0,) * len(shape), pipeline_mode=pl.Buffered(1))


def params(count=1, limit=None):
    return pltpu.CompilerParams(
        dimension_semantics=("arbitrary",) * count if count else None, vmem_limit_bytes=limit or VMEM_LIMIT
    )


def cost(flops, moved, special=0):
    return pl.CostEstimate(
        flops=int(flops * COST), bytes_accessed=int(moved * COST), transcendentals=int(special * COST)
    )


def window(packed, start, width, rows=None, steps=1, step=0):
    block = width // steps
    rows = packed.shape[0] if rows is None else rows
    if start % block == 0 and block % LANES == 0:
        base = start // block
        return packed, pl.BlockSpec((rows, block), lambda *at: (0, base + (at[step] if steps > 1 else 0)))
    return packed[:, start : start + width], pl.BlockSpec(
        (rows, block), lambda *at: (0, at[step] if steps > 1 else 0)
    )


def norm_kernel(place_ref, *refs):
    count = len(refs) - 5
    parts, (gain_ref, bias_ref, down_ref, normed_ref, lat_ref) = refs[:count], refs[count:]
    step = 128
    for index, part_ref in enumerate(parts):
        base = place_ref[index] * part_ref.shape[0]

        def some(at, carry):
            rows = pl.ds(pl.multiple_of(at * step, step), step)
            into = pl.ds(pl.multiple_of(base + at * step, step), step)
            normed = layer_norm(part_ref[rows, :].astype(F32), gain_ref[...], bias_ref[...]).astype(BF)
            normed_ref[into, :] = normed
            lat_ref[into, :] = mm_nt(normed, down_ref[...]).astype(BF)
            return carry

        lax.fori_loop(0, part_ref.shape[0] // step, some, 0)


def smem():
    return pl.BlockSpec(memory_space=pltpu.SMEM)


def norm_project(places, parts, gains, biases, down):
    model = parts[0].shape[1]
    frames = sum(part.shape[0] for part in parts)
    ranks = down.shape[0]
    return pl.pallas_call(
        norm_kernel,
        in_specs=[smem()] + [whole(item.shape) for item in parts + [gains, biases, down]],
        out_specs=[whole((frames, model)), whole((frames, ranks))],
        out_shape=[jax.ShapeDtypeStruct((frames, model), BF), jax.ShapeDtypeStruct((frames, ranks), BF)],
        grid=(1,),
        compiler_params=params(1),
        cost_estimate=cost(2 * frames * model * ranks, 4 * frames * model),
        name="norm_project",
    )(places, *parts, gains, biases, down)


def qkv_kernel(normed_ref, lat_ref, up_ref, w_ref, out_ref):
    step = 256

    def some(at, carry):
        rows = pl.ds(pl.multiple_of(at * step, step), step)
        out_ref[rows, :] = (mm(normed_ref[rows, :], w_ref[...]) + mm(lat_ref[rows, :], up_ref[...])).astype(BF)
        return carry

    lax.fori_loop(0, normed_ref.shape[0] // step, some, 0)


def qkv_project(normed, latent, up, packed, start, width):
    row_count, model = normed.shape
    ranks = latent.shape[1]
    steps = 3 if (width // 3) % LANES == 0 else 1
    operand, spec = window(packed, start, width, steps=steps)
    block = width // steps
    if steps == 3:
        up_spec = pl.BlockSpec((None, ranks, block), lambda at: (at, 0, 0))
    else:
        up = up.transpose(1, 0, 2).reshape(ranks, width)
        up_spec = whole(up.shape)
    return pl.pallas_call(
        qkv_kernel,
        grid=(steps,),
        in_specs=[whole(normed.shape), whole(latent.shape), up_spec, spec],
        out_specs=pl.BlockSpec((row_count, block), lambda at: (0, at)),
        out_shape=jax.ShapeDtypeStruct((row_count, width), BF),
        compiler_params=params(1, 42 * MIB),
        cost_estimate=cost(2 * row_count * model * width, 2 * (row_count + width) * model),
        name="qkv_project",
    )(normed, latent, up, operand)


def tri_start(at):
    return QB * at * (at + 1) // 2


def attend_kernel(place_ref, q_ref, k_ref, v_ref, out_ref, prob_ref, *refs):
    sent, (val_t_ref, out_t_ref) = refs[:-2], refs[-2:]
    frames = q_ref.shape[0]
    lane = lax.broadcasted_iota(jnp.int32, (1, LANES), 1) // HEAD
    val_t_ref[...] = v_ref[...].T
    square = (QB, QB)
    keep_tri = lax.broadcasted_iota(jnp.int32, square, 0) <= lax.broadcasted_iota(jnp.int32, square, 1)

    def scores(half, at):
        stop = (at + 1) * QB
        query = q_ref[at * QB : stop, :] * jnp.where(lane == half, SCALE, 0.0).astype(BF)
        last = jnp.where(keep_tri, mm_nt(k_ref[stop - QB : stop, :], query), -1e30)
        if at == 0:
            return last
        return jnp.concatenate([mm_nt(k_ref[0 : stop - QB, :], query), last], 0)

    turns = [(half, at) for at in range(frames // QB) for half in range(2)]
    score = scores(*turns[0])
    for index, (half, at) in enumerate(turns):
        stop = (at + 1) * QB
        own = slice(half * HEAD, (half + 1) * HEAD)
        later = scores(*turns[index + 1]) if index + 1 < len(turns) else None
        raised = jnp.exp(score - jnp.max(score, 0, keepdims=True))
        prob = (raised * (1.0 / jnp.sum(raised, 0, keepdims=True))).astype(BF)
        prob_ref[half, tri_start(at) : tri_start(at) + stop, :] = prob
        out_t_ref[own, at * QB : stop] = mm(val_t_ref[own, 0:stop], prob)
        score = later
    out_ref[...] = out_t_ref[...].T.astype(BF)
    for index, sent_ref in enumerate(sent):
        size = sent_ref.shape[0]
        at = place_ref[1] * len(sent) + index
        sent_ref[...] = out_ref[pl.ds(pl.multiple_of(at * size, size), size), :]


def pair_specs(frames, width):
    pairs = width // LANES
    return [pl.BlockSpec((frames, LANES), lambda at, part=part: (0, part * pairs + at)) for part in range(3)]


def attend(places, sizes, triple, width):
    frames = triple.shape[0]
    pairs = width // LANES
    tri = tri_start(frames // QB)
    return pl.pallas_call(
        attend_kernel,
        grid=(pairs,),
        in_specs=[smem()] + pair_specs(frames, width),
        out_specs=[
            pl.BlockSpec((frames, LANES), lambda at: (0, at)),
            pl.BlockSpec((2, tri, QB), lambda at: (at, 0, 0)),
        ]
        + [pl.BlockSpec((size, LANES), lambda at: (0, at)) for size in sizes],
        out_shape=[
            jax.ShapeDtypeStruct((frames, width), BF),
            jax.ShapeDtypeStruct((2 * pairs, tri, QB), BF),
        ]
        + [jax.ShapeDtypeStruct((size, width), BF) for size in sizes],
        scratch_shapes=[pltpu.VMEM((LANES, frames), BF), pltpu.VMEM((LANES, frames), F32)],
        compiler_params=params(1),
        cost_estimate=cost(
            8 * tri * QB * HEAD * pairs, 2 * (4 * frames * width + 2 * pairs * tri * QB), 2 * pairs * tri * QB
        ),
        name="attend",
    )(places, triple, triple, triple)


def attend_back_kernel(place_ref, q_ref, k_ref, v_ref, out_ref, prob_ref, *refs):
    pieces, (back_ref, grad_ref, key_t_ref, dq_t_ref, dk_acc, dv_acc) = refs[:-6], refs[-6:]
    frames = q_ref.shape[0]
    for index, piece_ref in enumerate(pieces):
        size = piece_ref.shape[0]
        count = max(len(pieces) // 2, 1)
        at = place_ref[index // count] * count + index % count if len(pieces) > 1 else 0
        grad_ref[pl.ds(pl.multiple_of(at * size, size), size), :] = piece_ref[...]
    lane = lax.broadcasted_iota(jnp.int32, (1, LANES), 1) // HEAD
    key_t_ref[...] = k_ref[...].T
    dk_acc[...] = jnp.zeros_like(dk_acc)
    dv_acc[...] = jnp.zeros_like(dv_acc)
    turns = [(half, at) for at in range(frames // QB) for half in range(2)]

    def start(half, at):
        rows = slice(at * QB, (at + 1) * QB)
        grad = grad_ref[rows, :] * jnp.where(lane == half, 1.0, 0.0).astype(BF)
        return grad, mm_nt(v_ref[0 : (at + 1) * QB, :], grad)

    ready = start(*turns[0])
    for index, (half, at) in enumerate(turns):
        stop = (at + 1) * QB
        rows = slice(at * QB, stop)
        own = slice(half * HEAD, (half + 1) * HEAD)
        grad, prob_grad = ready
        if half == 0:
            product = (out_ref[rows, :].astype(F32) * grad_ref[rows, :].astype(F32)).T
        if index + 1 < len(turns):
            ready = start(*turns[index + 1])
        query = q_ref[rows, :] * jnp.where(lane == half, SCALE, 0.0).astype(BF)
        delta = jnp.sum(product[own, :], 0, keepdims=True)
        prob = prob_ref[half, tri_start(at) : tri_start(at) + stop, :]
        dv_acc[0:stop, :] += mm(prob, grad)
        score_grad = (prob.astype(F32) * (prob_grad - delta)).astype(BF)
        dk_acc[0:stop, :] += mm(score_grad, query)
        dq_t_ref[own, rows] = mm(key_t_ref[own, 0:stop], score_grad)
    back_ref[0] = (dq_t_ref[...].T * SCALE).astype(BF)
    back_ref[1] = dk_acc[...].astype(BF)
    back_ref[2] = dv_acc[...].astype(BF)


def attend_back(places, triple, attended, pieces, probs, width):
    frames = triple.shape[0]
    pairs = width // LANES
    tri = tri_start(frames // QB)
    column = pl.BlockSpec((frames, LANES), lambda at: (0, at))
    return pl.pallas_call(
        attend_back_kernel,
        grid=(pairs,),
        in_specs=[smem()]
        + pair_specs(frames, width)
        + [column, pl.BlockSpec((2, tri, QB), lambda at: (at, 0, 0))]
        + [pl.BlockSpec((piece.shape[0], LANES), lambda at: (0, at)) for piece in pieces],
        out_specs=pl.BlockSpec((3, frames, LANES), lambda at: (0, 0, at)),
        out_shape=jax.ShapeDtypeStruct((3, frames, width), BF),
        scratch_shapes=[
            pltpu.VMEM((frames, LANES), BF),
            pltpu.VMEM((LANES, frames), BF),
            pltpu.VMEM((LANES, frames), F32),
            pltpu.VMEM((frames, LANES), F32),
            pltpu.VMEM((frames, LANES), F32),
        ],
        compiler_params=params(1, 42 * MIB),
        cost_estimate=cost(16 * tri * QB * HEAD * pairs, 2 * (8 * frames * width + 2 * pairs * tri * QB)),
        name="attend_back",
    )(places, triple, triple, triple, attended, probs, *pieces)


def feed_kernel(count, based, *refs):
    pieces, refs = refs[:count], refs[count:]
    bases, refs = refs[:based], refs[based:]
    cot_ref, down_in_ref, up_in_ref, down_out_ref, up_out_ref, w_in_ref, w_out_ref = refs[:7]
    out_refs, gu_refs, refs = refs[7 : 7 + count], refs[7 + count : 7 + 2 * count], refs[7 + 2 * count :]
    (
        gdown_in_ref, gup_in_ref, gdown_out_ref, gup_out_ref, normed_ref,
        out_acc, gu_acc, lat_in, glat_out, lat_acc, glat_acc, lat_t, glat_t,
    ) = refs
    at = pl.program_id(0)

    @pl.when(at == 0)
    def _():
        start = 0
        for piece_ref in pieces:
            normed_ref[start : start + piece_ref.shape[0], :] = piece_ref[...]
            start += piece_ref.shape[0]
        latent = mm_nt(normed_ref[...], down_in_ref[...]).astype(BF)
        glat = mm_nt(cot_ref[...], up_out_ref[...]).astype(BF)
        lat_in[...] = latent
        glat_out[...] = glat
        lat_t[...] = latent.astype(F32).T.astype(BF)
        glat_t[...] = glat.astype(F32).T.astype(BF)
        start = 0
        for base_ref in bases:
            out_acc[start : start + base_ref.shape[0], :] = base_ref[...]
            start += base_ref.shape[0]
        if not bases:
            out_acc[...] = jnp.zeros_like(out_acc)
        gu_acc[...] = jnp.zeros_like(gu_acc)
        lat_acc[...] = jnp.zeros_like(lat_acc)
        glat_acc[...] = jnp.zeros_like(glat_acc)

    w_in = w_in_ref[...]
    w_out = w_out_ref[...]
    pre = mm(normed_ref[...], w_in) + mm(lat_in[...], up_in_ref[...])
    act_grad = mm_nt(cot_ref[...], w_out) + mm(glat_out[...], down_out_ref[...])
    cdf = 0.5 * (1.0 + lax.erf(pre * SQRT_HALF))
    slope = cdf + pre * (jnp.exp(-0.5 * pre * pre) * INV_SQRT_2PI)
    act = (pre * cdf).astype(BF)
    pre_grad = (act_grad * slope).astype(BF)
    out_acc[...] += mm(act, w_out)
    gu_acc[...] += mm_nt(pre_grad, w_in)
    lat_acc[...] += mm_nt(act, down_out_ref[...])
    glat_acc[...] += mm_nt(pre_grad, up_in_ref[...])
    gup_in_ref[...] = mm(lat_t[...], pre_grad)
    gdown_out_ref[...] = mm(glat_t[...], act)

    @pl.when(at == pl.num_programs(0) - 1)
    def _():
        latent = lat_acc[...].astype(BF)
        glat = glat_acc[...].astype(BF)
        start = 0
        for out_ref, gu_ref in zip(out_refs, gu_refs):
            rows = slice(start, start + out_ref.shape[0])
            out_ref[...] = (out_acc[rows, :] + mm(latent[rows], up_out_ref[...])).astype(out_ref.dtype)
            gu_ref[...] = (gu_acc[rows, :] + mm(glat[rows], down_in_ref[...])).astype(gu_ref.dtype)
            start += out_ref.shape[0]
        gup_out_ref[...] = mm(latent.astype(F32).T.astype(BF), cot_ref[...])
        gdown_in_ref[...] = mm(glat.astype(F32).T.astype(BF), normed_ref[...])


def feed_forward(pieces, bases, cotangent, block_at, down_in, up_in, down_out, up_out, weights, hidden, kind):
    model = cotangent.shape[1]
    row_count = sum(item.shape[0] for item in pieces)
    rank = down_in.shape[0]
    block = FEED_BLOCK if hidden % FEED_BLOCK == 0 else hidden
    w_in, in_spec, w_out, out_spec = weights(block)
    main = pl.BlockSpec((row_count, model), lambda at: (block_at, 0))
    slim = pl.BlockSpec((rank, block), lambda at: (0, at))
    small = whole((rank, model))
    return pl.pallas_call(
        partial(feed_kernel, len(pieces), len(bases)),
        grid=(hidden // block,),
        in_specs=[once(item.shape) for item in pieces + bases]
        + [main, small, slim, slim, small, in_spec, out_spec],
        out_specs=[whole(item.shape) for item in pieces] * 2 + [small, slim, slim, small],
        out_shape=[jax.ShapeDtypeStruct(item.shape, kind) for item in pieces]
        + [jax.ShapeDtypeStruct(item.shape, BF) for item in pieces]
        + [
            jax.ShapeDtypeStruct((rank, model), F32),
            jax.ShapeDtypeStruct((rank, hidden), F32),
            jax.ShapeDtypeStruct((rank, hidden), F32),
            jax.ShapeDtypeStruct((rank, model), F32),
        ],
        scratch_shapes=[pltpu.VMEM((row_count, model), BF)]
        + [pltpu.VMEM((row_count, model), F32)] * 2
        + [pltpu.VMEM((row_count, rank), BF)] * 2
        + [pltpu.VMEM((row_count, rank), F32)] * 2
        + [pltpu.VMEM((rank, row_count), BF)] * 2,
        compiler_params=params(1),
        cost_estimate=cost(8 * row_count * model * hidden, 4 * hidden * model, 2 * row_count * hidden),
        name="feed_forward",
    )(*pieces, *bases, cotangent, down_in, up_in, down_out, up_out, w_in, w_out)


def spread_heads(rows_ref, into_ref, model):
    keys = rows_ref.shape[0]
    wide = 4 * HEAD
    row = lax.broadcasted_iota(jnp.int32, (4 * keys, wide), 0) // keys
    col = lax.broadcasted_iota(jnp.int32, (4 * keys, wide), 1) // HEAD
    mask = jnp.where(row == col, 1.0, 0.0).astype(BF)

    def some(group, carry):
        part = rows_ref[:, pl.ds(pl.multiple_of(group * wide, wide), wide)]
        into = pl.ds(pl.multiple_of(group * 4 * keys, 4 * keys), 4 * keys)
        into_ref[into, :] = jnp.concatenate([part] * 4, 0) * mask
        return carry

    lax.fori_loop(0, model // wide, some, 0)


def head_total(values, keys, reduce):
    split = values.reshape(4, keys, values.shape[1])
    return jnp.broadcast_to(reduce(split, 1, keepdims=True), split.shape).reshape(values.shape)


def each(count, step, work):
    def some(at, carry):
        work(pl.ds(pl.multiple_of(at * step, step), step))
        return carry

    lax.fori_loop(0, count // step, some, 0)


def pair_of(both, size):
    return [pl.ds(pl.multiple_of(both.start + at * size, size), size) for at in range(both.size // size)]


def weight_copies(plan, place_ref, sources, hold_ref, sem_ref):
    model = hold_ref.shape[1]
    groups = []
    for index, (start, extra) in enumerate(plan):
        if extra is None:
            parts = [slice(at * model // 2, (at + 1) * model // 2) for at in range(2)]
            pairs = [(sources[0].at[rows, pl.ds(start, model)], hold_ref.at[index, rows, :]) for rows in parts]
        else:
            half = model // 2
            here, there = [pl.ds(pl.multiple_of(place_ref[at] * half, half), half) for at in range(2)]
            pairs = [(sources[0].at[:, pl.ds(start, half)], hold_ref.at[index, :, here])]
            for at in range(2):
                rows = pl.ds(pl.multiple_of(place_ref[2 + at] * half, half), half)
                pairs.append((sources[extra + at], hold_ref.at[index, rows, there]))
        groups.append(
            [pltpu.make_async_copy(src, dst, sem_ref.at[index, at]) for at, (src, dst) in enumerate(pairs)]
        )
    return groups


def source_count(plan):
    return 1 + 2 * sum(extra is not None for _, extra in plan)


def start_all(copies):
    for copy in copies:
        copy.start()


def wait_all(copies):
    for copy in copies:
        copy.wait()


def middle_kernel(plan, place_ref, *refs):
    sources, refs = refs[: source_count(plan)], refs[source_count(plan) :]
    inputs_ref, adapt_ref, gain_ref, bias_ref, keys_ref, values_ref = refs[:6]
    pieces = refs[6:-20]
    away = refs[-20:-14]
    resid2_ref, normed3_ref, lat_ref, hold_ref, key_wide, value_wide, sem_ref = refs[-14:-7]
    kept, out_sem = refs[-7:-1], refs[-1]
    attended_ref, resid1_ref, normed2_ref, query_ref, probs_ref, crossed_ref = kept
    leaving = [pltpu.make_async_copy(kept[at], away[at], out_sem.at[at]) for at in range(6)]
    model = inputs_ref.shape[1]
    keys = keys_ref.shape[0]
    rows = inputs_ref.shape[0]
    wide = 4 * HEAD
    copies = weight_copies(plan, place_ref, sources, hold_ref, sem_ref)
    start_all(copies[0])
    for index, piece_ref in enumerate(pieces):
        size = piece_ref.shape[1]
        attended_ref[:, pl.ds(pl.multiple_of(place_ref[index] * size, size), size)] = piece_ref[...]
    spread_heads(keys_ref, key_wide, model)
    spread_heads(values_ref, value_wide, model)

    def adapted(moving_ref, index, store):
        latent = mm_nt(moving_ref[...], adapt_ref[32 * index : 32 * index + 16, :]).astype(BF)
        lat_ref[:, 16 * index : 16 * index + 16] = latent
        wait_all(copies[index])
        if index < 2:
            start_all(copies[index + 1])

        def some(cols):
            store(
                cols,
                mm(moving_ref[...], hold_ref[index, :, cols])
                + mm(latent, adapt_ref[32 * index + 16 : 32 * index + 32, cols]),
            )

        each(model, 512, some)

    def add_first(cols, value):
        resid1_ref[:, cols] = inputs_ref[:, cols].astype(F32) + value

    def add_second(cols, value):
        resid2_ref[:, cols] = resid1_ref[:, cols] + value

    def keep_query(cols, value):
        query_ref[:, cols] = value.astype(BF)

    def normed(values_at, into_ref, which):
        def some(part):
            into_ref[part, :] = layer_norm(
                values_at[part, :], gain_ref[which : which + 1, :], bias_ref[which : which + 1, :]
            ).astype(BF)

        each(rows, 128, some)

    def cross(both):
        groups = pair_of(both, wide)
        scores = [mm_nt(key_wide[lanes, :], query_ref[:, lanes]) * SCALE for lanes in groups]
        for lanes, score in zip(groups, scores):
            raised = jnp.exp(score - head_total(score, keys, jnp.max))
            prob = (raised / head_total(raised, keys, jnp.sum)).astype(BF)
            probs_ref[lanes, :] = prob
            crossed_ref[:, lanes] = mm_tn(prob, value_wide[lanes, :]).astype(BF)

    leaving[0].start()
    adapted(attended_ref, 0, add_first)
    leaving[1].start()
    normed(resid1_ref, normed2_ref, 1)
    leaving[2].start()
    adapted(normed2_ref, 1, keep_query)
    leaving[3].start()
    each(model, 3 * wide, cross)
    leaving[4].start()
    leaving[5].start()
    adapted(crossed_ref, 2, add_second)
    normed(resid2_ref, normed3_ref, 2)
    wait_all(leaving)


def middle(places, own, own_spec, others, inputs, at, blocks, sources, plan, adapters, gains, biases, keys, values):
    rows, model = own_spec[0], inputs.shape[1]
    spread = model // HEAD * keys.shape[0]
    shape = lambda kind, dims=(rows, model): jax.ShapeDtypeStruct(dims, kind)
    flat = lambda dims: pl.BlockSpec(dims, lambda _, ref: (0,) * len(dims))
    shapes = [shape(kind) for kind in (BF, F32, BF, BF)]
    shapes += [shape(BF, (spread, rows)), shape(BF), shape(F32), shape(BF), shape(BF, (rows, 48))]
    return pl.pallas_call(
        partial(middle_kernel, plan),
        grid_spec=pltpu.PrefetchScalarGridSpec(
            num_scalar_prefetch=1,
            grid=(1,),
            in_specs=[pl.BlockSpec(memory_space=pl.ANY)] * len(sources)
            + [pl.BlockSpec((rows, model), lambda _, ref: (at, 0))]
            + [flat(item.shape) for item in (adapters, gains, biases, keys, values)]
            + [pl.BlockSpec(own_spec, lambda _, ref: (ref[0] * blocks + at, 0) if others else (at, 0))]
            + [flat(item.shape) for item in others],
            out_specs=[pl.BlockSpec(memory_space=pl.ANY)] * 6 + [flat(item.shape) for item in shapes[6:]],
            scratch_shapes=[
                pltpu.VMEM((3, model, model), BF),
                pltpu.VMEM((spread, 4 * HEAD), BF),
                pltpu.VMEM((spread, 4 * HEAD), BF),
                pltpu.SemaphoreType.DMA((3, 3)),
            ]
            + [pltpu.VMEM(item.shape, item.dtype) for item in shapes[:6]]
            + [pltpu.SemaphoreType.DMA((6,))],
        ),
        out_shape=shapes,
        compiler_params=params(),
        cost_estimate=cost(6 * rows * model * model, 6 * model * model + 24 * rows * model),
        name="middle",
    )(places, *sources, inputs, adapters, gains, biases, keys, values, own, *others)


def middle_back_kernel(plan, split, place_ref, *refs):
    sources, refs = refs[: source_count(plan)], refs[source_count(plan) :]
    cot_ref, gu_ref, more_ref = refs[:3]
    far = refs[3:9]
    resid2_ref, lat_ref, adapt_ref, gain_ref, keys_ref, values_ref = refs[9:15]
    kept, in_sem = refs[-7:-1], refs[-1]
    attended_ref, resid1_ref, normed2_ref, query_ref, probs_ref, crossed_ref = kept
    coming = [pltpu.make_async_copy(far[at], kept[at], in_sem.at[at]) for at in range(6)]
    refs = refs[15:-7]
    outs = refs[: 2 if split else 1]
    resid1_grad_ref, memory_ref, small_ref, hold_ref, key_wide, value_wide, work_ref, low_ref, sem_ref = refs[len(outs) :]
    rows, model = cot_ref.shape
    keys = keys_ref.shape[0]
    wide = 4 * HEAD
    copies = weight_copies(plan, place_ref, sources, hold_ref, sem_ref)
    start_all(copies[2])
    coming[5].start()
    spread_heads(keys_ref, key_wide, model)
    spread_heads(values_ref, value_wide, model)

    def first(part):
        gradient = gu_ref[part, :].astype(F32) + more_ref[part, :].astype(F32)
        value = cot_ref[part, :].astype(F32) + norm_back(resid2_ref[part, :], gain_ref[2:3, :], gradient)
        resid1_grad_ref[part, :] = value
        low_ref[part, :] = value.astype(BF)

    def second(part):
        value = resid1_grad_ref[part, :] + norm_back(resid1_ref[part, :], gain_ref[1:2, :], work_ref[part, :])
        resid1_grad_ref[part, :] = value
        low_ref[part, :] = value.astype(BF)

    def back(moving_ref, index, store):
        down = slice(32 * index, 32 * index + 16)
        upper = slice(32 * index + 16, 32 * index + 32)
        glat = mm_nt(low_ref[...], adapt_ref[upper, :]).astype(BF)
        glat_t = glat.astype(F32).T.astype(BF)
        lat_t = lat_ref[:, 16 * index : 16 * index + 16].astype(F32).T.astype(BF)
        wait_all(copies[index])
        if index == 2:
            wait_all(coming[5:])
            start_all(coming[2:5])
        if index == 1:
            wait_all(coming[2:3])
            start_all(coming[:2])
        if index == 0:
            wait_all(coming[:1])
        if index:
            start_all(copies[index - 1])

        def some(cols):
            small_ref[down, cols] = mm(glat_t, moving_ref[:, cols])
            small_ref[upper, cols] = mm(lat_t, low_ref[:, cols])
            store(cols, mm_nt(low_ref[...], hold_ref[index, cols, :]) + mm(glat, adapt_ref[down, cols]))

        each(model, 512, some)

    def keep(cols, value):
        work_ref[:, cols] = value

    def cross(both):
        groups = pair_of(both, wide)
        parts = [work_ref[:, lanes].astype(BF) for lanes in groups]
        prob_grads = [mm_nt(value_wide[lanes, :], part) for lanes, part in zip(groups, parts)]
        for lanes, part, prob_grad in zip(groups, parts, prob_grads):
            cross_one(lanes, part, prob_grad)

    def cross_one(lanes, part, prob_grad):
        prob = probs_ref[lanes, :]
        wide_prob = prob.astype(F32)
        weighted = wide_prob * prob_grad
        score_grad = (weighted - wide_prob * head_total(weighted, keys, jnp.sum)).astype(BF)
        low_ref[:, lanes] = (mm_tn(score_grad, key_wide[lanes, :]) * SCALE).astype(BF)
        key_full = mm(score_grad, query_ref[:, lanes])
        value_full = mm(prob, part)
        col = lax.broadcasted_iota(jnp.int32, (keys, wide), 1) // HEAD
        key_sum, value_sum = key_full[:keys], value_full[:keys]
        for head in range(1, 4):
            rows_at = slice(head * keys, (head + 1) * keys)
            key_sum = jnp.where(col == head, key_full[rows_at], key_sum)
            value_sum = jnp.where(col == head, value_full[rows_at], value_sum)
        memory_ref[0, :, lanes] = key_sum * SCALE
        memory_ref[1, :, lanes] = value_sum

    each(rows, 128, first)
    back(crossed_ref, 2, keep)
    wait_all(coming[3:5])
    each(model, 3 * wide, cross)
    back(normed2_ref, 1, keep)
    wait_all(coming[1:2])
    each(rows, 128, second)
    back(attended_ref, 0, keep)
    if split:
        size = outs[0].shape[1]
        for out_ref, index in zip(outs, range(2)):
            out_ref[...] = work_ref[:, pl.ds(pl.multiple_of(place_ref[index] * size, size), size)].astype(BF)
    else:
        outs[0][...] = work_ref[...].astype(BF)


def middle_back(places, parts, at, cotangent, gu, more, kept, sources, plan, adapters, gains, keys, values):
    model = cotangent.shape[1]
    rows = kept[0].shape[0]
    spread = model // HEAD * keys.shape[0]
    flat = lambda dims: pl.BlockSpec(dims, lambda _, ref: (0,) * len(dims))
    block = pl.BlockSpec((rows, model), lambda _, ref: (at, 0))
    shapes = [jax.ShapeDtypeStruct((rows, model // parts), BF)] * parts + [
        jax.ShapeDtypeStruct((rows, model), F32),
        jax.ShapeDtypeStruct((2,) + keys.shape, F32),
        jax.ShapeDtypeStruct(adapters.shape, F32),
    ]
    return pl.pallas_call(
        partial(middle_back_kernel, plan, parts == 2),
        grid_spec=pltpu.PrefetchScalarGridSpec(
            num_scalar_prefetch=1,
            grid=(1,),
            in_specs=[pl.BlockSpec(memory_space=pl.ANY)] * len(sources)
            + [block, flat(gu.shape), flat(more.shape)]
            + [pl.BlockSpec(memory_space=pl.ANY)] * 6
            + [flat(item.shape) for item in kept[6:]]
            + [flat(item.shape) for item in (adapters, gains, keys, values)],
            out_specs=[flat(item.shape) for item in shapes],
            scratch_shapes=[
                pltpu.VMEM((3, model, model), BF),
                pltpu.VMEM((spread, 4 * HEAD), BF),
                pltpu.VMEM((spread, 4 * HEAD), BF),
                pltpu.VMEM((rows, model), F32),
                pltpu.VMEM((rows, model), BF),
                pltpu.SemaphoreType.DMA((3, 3)),
            ]
            + [pltpu.VMEM(item.shape, item.dtype) for item in kept[:6]]
            + [pltpu.SemaphoreType.DMA((6,))],
        ),
        out_shape=shapes,
        compiler_params=params(),
        cost_estimate=cost(6 * rows * model * model, 6 * model * model + 36 * rows * model),
        name="middle_back",
    )(places, *sources, cotangent, gu, more, *kept, adapters, gains, keys, values)


def qkv_grads_kernel(
    place_ref, grad_ref, normed_ref, lat_ref, up_ref, glat_ref, mine_ref, theirs_ref, glat_acc, gup_acc, down_acc,
    down_all, upper_all,
):
    at = pl.program_id(0)
    gradient = grad_ref[...]
    rank = mine_ref.shape[0]
    model = normed_ref.shape[1]
    width = gradient.shape[1]
    gup_acc[...] = mm_tn(lat_ref[...], gradient)

    @pl.when(at == 0)
    def _():
        glat_acc[...] = jnp.zeros_like(glat_acc)
        upper_all[...] = jnp.zeros_like(upper_all)

    into = pl.ds(pl.multiple_of(at * model + place_ref[0] * width, LANES), width)
    upper_all[:, into] = gup_acc[pl.ds(pl.multiple_of(at * rank, rank), rank), :].astype(BF)
    glat_acc[...] += mm_nt(gradient, up_ref[...])

    @pl.when(at == pl.num_programs(0) - 1)
    def _():
        low = glat_acc[...].astype(BF)
        glat_ref[...] = low
        down_acc[...] = mm_tn(low, normed_ref[...])
        for part in range(3):
            down_all[:, part * model : (part + 1) * model] = down_acc[part * rank : (part + 1) * rank, :].astype(BF)
        share(place_ref, down_all, upper_all, mine_ref, theirs_ref)


def share(place_ref, down_all, upper_all, mine_ref, theirs_ref):
    @pl.when(place_ref[0] == 0)
    def _():
        mine_ref[...] = down_all[...]
        theirs_ref[...] = upper_all[...]

    @pl.when(place_ref[0] != 0)
    def _():
        mine_ref[...] = upper_all[...]
        theirs_ref[...] = down_all[...]


def qkv_grads(places, gradient, normed, latent, up):
    frames, model = normed.shape
    parts, ranks, width = up.shape
    rank = ranks // parts
    table = jax.ShapeDtypeStruct((rank, parts * model), BF)
    return pl.pallas_call(
        qkv_grads_kernel,
        grid=(parts,),
        in_specs=[
            smem(),
            pl.BlockSpec((None, frames, width), lambda at: (at, 0, 0)),
            whole(normed.shape),
            whole(latent.shape),
            pl.BlockSpec((None, ranks, width), lambda at: (at, 0, 0)),
        ],
        out_specs=[whole(latent.shape), whole(table.shape), whole(table.shape)],
        out_shape=[jax.ShapeDtypeStruct(latent.shape, BF), table, table],
        scratch_shapes=[
            pltpu.VMEM(latent.shape, F32),
            pltpu.VMEM((ranks, width), F32),
            pltpu.VMEM((ranks, model), F32),
            pltpu.VMEM(table.shape, BF),
            pltpu.VMEM(table.shape, BF),
        ],
        compiler_params=params(1, 42 * MIB),
        cost_estimate=cost(8 * frames * ranks * width * parts, 2 * frames * (model + parts * width)),
        name="qkv_grads",
    )(places, gradient, normed, latent, up)


def qkv_back_kernel(place_ref, grad_ref, glat_ref, down_ref, w_ref, gu_ref, gu_acc):
    at = pl.program_id(0)
    model = gu_ref.shape[1]
    last = pl.num_programs(0) - 1

    def some(cols):
        direct = mm_nt(grad_ref[...], w_ref[cols, :])

        @pl.when(at == 0)
        def _():
            gu_acc[:, cols] = direct + mm(glat_ref[...], down_ref[:, cols])

        @pl.when(jnp.logical_and(at > 0, at < last))
        def _():
            gu_acc[:, cols] += direct

        @pl.when(at == last)
        def _():
            gu_ref[:, cols] = (gu_acc[:, cols] + direct).astype(gu_ref.dtype)

    each(model, 512, some)


def qkv_back(place, row_count, gradient, glat, down, packed, start, kind):
    ranks, model = down.shape
    width = gradient.shape[2]
    if start % width == 0 and width % LANES == 0:
        weight, spec = packed, pl.BlockSpec((model, width), lambda at, ref: (0, start // width + at))
    else:
        weight = packed[:, start : start + 3 * width].reshape(model, 3, width).transpose(1, 0, 2)
        spec = pl.BlockSpec((None, model, width), lambda at, ref: (at, 0, 0))
    return pl.pallas_call(
        qkv_back_kernel,
        grid_spec=pltpu.PrefetchScalarGridSpec(
            num_scalar_prefetch=1,
            grid=(3,),
            in_specs=[
                pl.BlockSpec((None, row_count, width), lambda at, ref: (at, ref[0], 0)),
                pl.BlockSpec((row_count, ranks), lambda at, ref: (ref[0], 0)),
                pl.BlockSpec(down.shape, lambda at, ref: (0, 0)),
                spec,
            ],
            out_specs=pl.BlockSpec((row_count, model), lambda at, ref: (0, 0)),
            scratch_shapes=[pltpu.VMEM((row_count, model), F32)],
        ),
        out_shape=jax.ShapeDtypeStruct((row_count, model), kind),
        compiler_params=params(1, 42 * MIB),
        cost_estimate=cost(6 * row_count * model * width, 6 * model * width + 8 * row_count * model),
        name="qkv_back",
    )(place, gradient, glat, down, weight)


def last_norm_kernel(blocks, frames_ref, gradient_ref, gain_ref, *refs):
    pieces, grad_ref = refs[:-1], refs[-1]
    at = pl.program_id(0)
    back = norm_back(frames_ref[...].astype(F32), gain_ref[...], gradient_ref[...])
    for index, piece_ref in enumerate(pieces):

        @pl.when(at // blocks == index)
        def _(piece_ref=piece_ref):
            grad_ref[...] = back + piece_ref[...]


def last_norm(frames, gradient, gains, pieces):
    rows, model = frames.shape
    step = min(128, rows)
    blocks = pieces[0].shape[0] // step
    block = pl.BlockSpec((step, model), lambda at: (at, 0))

    def piece_spec(index):
        return pl.BlockSpec((step, model), lambda at: (jnp.clip(at - index * blocks, 0, blocks - 1), 0))

    return pl.pallas_call(
        partial(last_norm_kernel, blocks),
        grid=(rows // step,),
        in_specs=[block, block, whole(gains.shape)] + [piece_spec(index) for index in range(len(pieces))],
        out_specs=block,
        out_shape=jax.ShapeDtypeStruct((rows, model), F32),
        compiler_params=params(1, 42 * MIB),
        cost_estimate=cost(20 * rows * model, 16 * rows * model),
        name="last_norm",
    )(frames, gradient, gains, *pieces)


def run_length(size):
    count = 1
    while count * size % LANES:
        count *= 2
    return count


def join_kernel(pieces_ref, flat_ref):
    count, _, size = pieces_ref.shape
    run = run_length(size)

    def some(at, carry):
        parts = [pieces_ref[at * run + index] for index in range(run)]
        into = pl.ds(pl.multiple_of(at * run * size, LANES), run * size)
        flat_ref[:, into] = jnp.concatenate(parts, 1)
        return carry

    lax.fori_loop(0, count // run, some, 0)


def join_pieces(pieces):
    count, rows, size = pieces.shape
    if count % run_length(size):
        return pieces.transpose(1, 0, 2).reshape(rows, count * size)
    return pl.pallas_call(
        join_kernel,
        out_shape=jax.ShapeDtypeStruct((rows, count * size), pieces.dtype),
        compiler_params=params(0),
        name="join_pieces",
    )(pieces)


def split_kernel(*refs):
    sources, pieces_ref, flat_ref = refs[:-2], refs[-2], refs[-1]
    count, _, size = pieces_ref.shape
    run = run_length(size)
    start = 0
    for first_ref, second_ref in zip(sources[::2], sources[1::2]):
        width = first_ref.shape[1]
        both = first_ref[...].astype(F32) + second_ref[...].astype(F32)
        flat_ref[:, start : start + width] = both.astype(BF)
        start += width

    def some(at, carry):
        block = flat_ref[:, pl.ds(pl.multiple_of(at * run * size, LANES), run * size)]
        for index in range(run):
            pieces_ref[at * run + index] = block[:, index * size : (index + 1) * size]
        return carry

    lax.fori_loop(0, count // run, some, 0)


def split_sums(pairs, count):
    rows = pairs[0].shape[0]
    total = sum(item.shape[1] for item in pairs[::2])
    return pl.pallas_call(
        split_kernel,
        out_shape=jax.ShapeDtypeStruct((count, rows, total // count), BF),
        scratch_shapes=[pltpu.VMEM((rows, total), BF)],
        compiler_params=params(0, 42 * MIB),
        name="split_sums",
    )(*pairs)


def unit_loop(plan, work):
    fsdp, seq, folds, local = plan
    run = run_length(local)

    def some(at, carry):
        span = run * seq * folds * local
        block = pl.ds(pl.multiple_of(at * span, LANES), span)
        folded = [
            pl.ds(pl.multiple_of(fold * fsdp * local + at * run * local, LANES), run * local) for fold in range(folds)
        ]
        work(run, block, folded)
        return carry

    lax.fori_loop(0, fsdp // run, some, 0)


def take_units_kernel(plan, place_ref, all_ref, *refs):
    own_ref = refs[-1]
    _, seq, folds, local = plan
    spot = place_ref[0]

    def work(run, block, folded):
        values = all_ref[:, block]
        for fold, into in enumerate(folded):
            parts = []
            for index in range(run):
                base = (index * seq * folds + fold) * local
                part = values[:, base : base + local]
                for other in range(1, seq):
                    shift = base + other * folds * local
                    part = jnp.where(spot == other, values[:, shift : shift + local], part)
                parts.append(part)
            own_ref[:, into] = jnp.concatenate(parts, 1)

    unit_loop(plan, work)
    if len(refs) == 2:
        model = refs[0].shape[1]
        hidden = own_ref.shape[1] - folds * model
        for fold in range(folds):
            rows = pl.ds(pl.multiple_of((spot * folds + fold) * local, 16), local)
            own_ref[:, hidden + fold * model : hidden + (fold + 1) * model] = refs[0][rows, :]


def take_units(plan, places, matrix, low=None):
    _, seq, folds, local = plan
    rows, width = matrix.shape
    extra = [] if low is None else [low]
    out_width = width // seq + sum(folds * item.shape[1] for item in extra)
    return pl.pallas_call(
        partial(take_units_kernel, plan),
        in_specs=[smem()] + [pl.BlockSpec(memory_space=pltpu.VMEM)] * (1 + len(extra)),
        out_shape=jax.ShapeDtypeStruct((rows, out_width), matrix.dtype),
        compiler_params=params(0),
        name="take_units",
    )(places, matrix, *extra)


def collect_kernel(plan, blocks, start_at, place_ref, *refs):
    parts, squares, refs = refs[:blocks], refs[blocks : 2 * blocks], refs[2 * blocks :]
    feeds = [refs[at : at + 4] for at in range(0, len(refs) - 14, 4)]
    (
        other_ref, lat_ref, flat_ref, down_text_ref, text_ref, w_ref,
        mine_ref, theirs_ref, text_grad_ref, down_all, upper_all, unit_acc, hold_ref, sem_ref,
    ) = refs[-14:]
    _, seq, folds, local = plan
    rank = mine_ref.shape[0]
    model = text_ref.shape[1]
    wide = other_ref.shape[2]
    spot = place_ref[0]
    own = pl.ds(pl.multiple_of(spot * wide, wide), wide)
    copy = pltpu.make_async_copy(w_ref.at[:, pl.ds(start_at, hold_ref.shape[1])], hold_ref, sem_ref)
    copy.start()

    def total(items, rows):
        value = items[0][rows, :]
        for item in items[1:]:
            value = value + item[rows, :]
        return value

    moved = []
    for part in range(2):
        value = parts[0][part, :, own]
        for item in parts[1:]:
            value = value + item[part, :, own]
        moved.append((value + other_ref[part].astype(F32)).astype(BF))
    moved = jnp.concatenate(moved, 1)
    glat = mm_nt(moved, flat_ref[...]).astype(BF)
    gup = mm_tn(lat_ref[...], moved)
    gdown = mm_tn(glat, text_ref[...])

    upper_all[:, 2 * model : 4 * model] = jnp.zeros((rank, 2 * model), BF)
    for part in range(2):
        rows = slice(part * rank, (part + 1) * rank)
        down_all[:, (2 + part) * model : (3 + part) * model] = gdown[rows].astype(BF)
        into = pl.ds(pl.multiple_of((2 + part) * model + spot * wide, LANES), wide)
        upper_all[:, into] = gup[rows, part * wide : (part + 1) * wide].astype(BF)
    for index, at in enumerate((0, 1, 4)):
        cols = slice(at * model, (at + 1) * model)
        down_all[:, cols] = total(squares, slice(2 * index * rank, (2 * index + 1) * rank)).astype(BF)
        upper_all[:, cols] = total(squares, slice((2 * index + 1) * rank, (2 * index + 2) * rank)).astype(BF)
    every = slice(0, rank)
    down_all[:, 5 * model : 6 * model] = total([item[0] for item in feeds], every).astype(BF)
    upper_all[:, upper_all.shape[1] - model :] = total([item[3] for item in feeds], every).astype(BF)
    for into_ref, start, which in ((upper_all, 5 * model, 1), (down_all, 6 * model, 2)):
        unit_acc[...] = total([item[which] for item in feeds], every)

        def work(run, block, folded):
            values = [unit_acc[:, cols] for cols in folded]
            spread = []
            for index in range(run):
                for other in range(seq):
                    for fold in range(folds):
                        part = values[fold][:, index * local : (index + 1) * local]
                        spread.append(jnp.where(spot == other, part, 0.0))
            at = pl.ds(pl.multiple_of(start + block.start, LANES), block.size)
            into_ref[:, at] = jnp.concatenate(spread, 1).astype(BF)

        unit_loop(plan, work)
    share(place_ref, down_all, upper_all, mine_ref, theirs_ref)
    copy.wait()
    text_grad_ref[...] = (mm_nt(moved, hold_ref[...]) + mm(glat, down_text_ref[...])).astype(BF)


def collect(plan, places, parts, squares, feeds, other, lat_text, flat_text, down_text, text, packed, start):
    rank = squares[0].shape[0] // 6
    model = text.shape[1]
    hidden = feeds[0][1].shape[1]
    wide2 = flat_text.shape[1]
    width = 6 * model + hidden * plan[1]
    feeds = [item for feed in feeds for item in feed]
    before = list(parts) + list(squares) + feeds + [other, lat_text, flat_text, down_text, text]
    table = jax.ShapeDtypeStruct((rank, width), BF)
    shapes = [table, table, jax.ShapeDtypeStruct(text.shape, BF)]
    return pl.pallas_call(
        partial(collect_kernel, plan, len(parts), start),
        grid=(1,),
        in_specs=[smem()] + [whole(item.shape) for item in before] + [pl.BlockSpec(memory_space=pl.ANY)],
        out_specs=[whole(item.shape) for item in shapes],
        out_shape=shapes,
        scratch_shapes=[pltpu.VMEM(table.shape, BF)] * 2
        + [pltpu.VMEM((rank, hidden), F32), pltpu.VMEM((model, wide2), BF), pltpu.SemaphoreType.DMA],
        compiler_params=params(1),
        cost_estimate=cost(4 * text.shape[0] * model * wide2, 2 * model * wide2),
        name="collect",
    )(places, *before, packed)


def both_kernel(place_ref, mine_ref, other_ref, down_ref, upper_ref):
    first = place_ref[0] == 0
    for at in range(mine_ref.shape[0]):
        mine, other = mine_ref[at].astype(F32), other_ref[at].astype(F32)
        down_ref[at] = jnp.where(first, mine, other)
        upper_ref[at] = jnp.where(first, other, mine)


def both_tables(places, mine, other):
    return pl.pallas_call(
        both_kernel,
        in_specs=[smem()] + [pl.BlockSpec(memory_space=pltpu.VMEM)] * 2,
        out_shape=[jax.ShapeDtypeStruct(mine.shape, F32)] * 2,
        compiler_params=params(0, 42 * MIB),
        name="both_tables",
    )(places, mine, other)


def body(
    inputs,
    text_states,
    adapter_index,
    norm_gains,
    norm_biases,
    self_in,
    self_out,
    cross_query,
    cross_text,
    cross_out,
    hidden_in,
    hidden_out,
    adapter_down,
    adapter_up,
    cotangent,
    *,
    sizes,
):
    seq, fsdp = sizes
    spot = lax.axis_index("seq")
    first_here = spot == 0
    there = (seq - 1) - spot
    local = self_in.shape[0]
    depth = hidden_out.shape[0] // seq
    pair = seq == 2 and depth % local == 0 and fsdp % run_length(local) == 0
    model = inputs.shape[2]
    rows = inputs.shape[1]
    frames = rows * seq
    wide = model // seq
    hidden_all = hidden_in.shape[1]
    hidden = hidden_all // seq
    adapters, rank, piece = adapter_down.shape
    total = piece * fsdp

    blocks = max(rows // 256, 1)
    size = rows // blocks

    def swap(value):
        return lax.ppermute(value, "seq", [(0, 1), (1, 0)])

    def pick(value, axis, extent, which=None):
        return lax.dynamic_slice_in_dim(value, (spot if which is None else which) * extent, extent, axis)

    def ordered(mine, other):
        return jnp.where(first_here, mine, other), jnp.where(first_here, other, mine)

    def gather(value, axis):
        if pair:
            return jnp.concatenate(ordered(value, swap(value)), axis)
        return lax.all_gather(value, "seq", axis=axis, tiled=True)

    def after(value, *others):
        return lax.optimization_barrier((value,) + others)[0]

    def put(value, axis):
        shape = list(value.shape)
        shape[axis] = seq
        return lax.dynamic_update_slice_in_dim(jnp.zeros(shape, value.dtype), value, spot, axis)

    def own_columns(matrix, parts):
        return [pick(matrix[:, at * model : (at + 1) * model], 1, wide) for at in range(parts)]

    def flat_down(grads, parts):
        return jnp.concatenate([grads[at * rank : (at + 1) * rank] for at in range(parts)], 1)

    def flat_upper(own):
        return put(jnp.stack(own, 1)[:, :, None], 2).reshape(rank, len(own) * model)

    halved = [pick(item, 1, wide) if pair else item for item in (self_out, cross_query)]
    first = [cross_out] + own_columns(cross_text, 2) + halved + own_columns(self_in, 3)
    edges = [0]
    for item in first:
        edges.append(edges[-1] + item.shape[1])
    start_in, start_text = edges[5], edges[1]
    packed = lax.all_gather(jnp.concatenate(first, 1), "fsdp", axis=0, tiled=True)
    squares_plan = ((edges[3], None), (edges[4], None), (edges[0], None))
    if pair:
        squares_plan = ((edges[3], 1), (edges[4], 3)) + squares_plan[2:]
    core = lax.rem(lax.axis_index("fsdp"), 2)
    where_here = jnp.stack([spot, there, core, 1 - core]).astype(jnp.int32)
    if pair:
        folds = depth // local
        plan = (fsdp, seq, folds, local)
        own_units = partial(take_units, plan, where_here)
        packed_feed = lax.all_gather(own_units(hidden_in, hidden_out), "fsdp", axis=0, tiled=True)

        def feed_weights(block):
            per = model // block
            return (
                packed_feed,
                pl.BlockSpec((model, block), lambda at: (0, at)),
                packed_feed,
                pl.BlockSpec((block, model), lambda at: (at % per, folds + at // per)),
            )
    else:

        def own_units(matrix):
            kept = lax.dynamic_index_in_dim(matrix.reshape(-1, fsdp, seq, depth), spot, 2, False)
            return kept.reshape(-1, hidden)

        def all_units(matrix):
            return put(matrix.reshape(-1, fsdp, 1, depth), 2).reshape(-1, hidden_all)

        whole_in = lax.all_gather(own_units(hidden_in), "fsdp", axis=0, tiled=True)
        whole_out = lax.all_gather(pick(hidden_out, 0, depth), "fsdp", axis=0, tiled=True)

        def feed_weights(block):
            return (
                whole_in,
                pl.BlockSpec((model, block), lambda at: (0, at)),
                whole_out,
                pl.BlockSpec((block, model), lambda at: (at, 0)),
            )

    index_all = lax.all_to_all(jnp.broadcast_to(adapter_index, (fsdp,)), "fsdp", 0, 0, tiled=True)
    if pair:
        table = jnp.where(first_here, adapter_down, adapter_up)
        mine = join_pieces(lax.all_to_all(jnp.take(table, index_all, axis=0), "fsdp", 0, 0, tiled=True))
        down_all, upper_all = ordered(mine, swap(mine))
    else:
        table = jnp.concatenate([adapter_down, adapter_up], 1)
        chosen = join_pieces(lax.all_to_all(jnp.take(table, index_all, axis=0), "fsdp", 0, 0, tiled=True))
        down_all, upper_all = chosen[:rank], chosen[rank:]
    in_cuts = [0, 3 * model, 4 * model, 5 * model, 7 * model, 8 * model, 9 * model, 9 * model + hidden_all]
    out_cuts = [0, 3 * model, 4 * model, 5 * model, 7 * model, 8 * model, 8 * model + hidden_all, 9 * model + hidden_all]
    downs = [down_all[:, in_cuts[at] : in_cuts[at + 1]] for at in range(7)]
    uppers = [upper_all[:, out_cuts[at] : out_cuts[at + 1]] for at in range(7)]

    def part_down(matrix, parts):
        return jnp.concatenate([matrix[:, at * model : (at + 1) * model] for at in range(parts)], 0)

    def part_upper(matrix, parts):
        own = own_columns(matrix, parts)
        return jnp.stack(
            [jnp.pad(item, ((at * rank, (parts - 1 - at) * rank), (0, 0))) for at, item in enumerate(own)], 0
        )

    units = own_units(jnp.concatenate([uppers[5], downs[6]], 0))
    feed_adapters = (downs[5], units[:rank], units[rank:], uppers[6])
    square_adapters = jnp.concatenate([downs[1], uppers[1], downs[2], uppers[2], downs[4], uppers[4]], 0)
    down_qkv, upper_qkv = part_down(downs[0], 3), part_upper(uppers[0], 3)
    down_text, upper_text = part_down(downs[3], 2), part_upper(uppers[3], 2)
    flat_text = jnp.concatenate([upper_text[0], upper_text[1]], 1)

    frames_in = inputs[0]
    cot = cotangent[0]
    if pair:
        frames_parts = [frames_in, swap(frames_in)]
        cot_other = swap(after(cot, frames_parts[1]))
    else:
        frames_parts = [lax.all_gather(frames_in, "seq", axis=0, tiled=True)]
    norm_places = where_here if pair else jnp.zeros((4,), jnp.int32)
    if pair:
        frames_parts[1] = after(frames_parts[1], cot_other, units)
    normed1, lat_qkv = norm_project(norm_places, frames_parts, norm_gains[0:1], norm_biases[0:1], down_qkv)
    packed = after(packed, normed1)
    sources = [packed]
    if pair:
        half = model // 2
        straight = [swap(lax.dynamic_slice(packed, (core * half, at), (half, wide))) for at in edges[3:5]]
    triple = qkv_project(normed1, lat_qkv, upper_qkv, packed, start_in, 3 * wide)
    padded = -(-wide // LANES) * LANES
    if padded != wide:
        triple = jnp.pad(triple.reshape(frames, 3, wide), ((0, 0), (0, 0), (0, padded - wide)))
        triple = triple.reshape(frames, 3 * padded)
    text = after(text_states[0], triple)
    w_text = packed[:, start_text : start_text + 2 * wide]
    lat_text = mm_nt(text, down_text).astype(BF)
    memory = (mm(text, w_text) + mm(lat_text, flat_text)).astype(BF)
    head_out, probs, *leaving = attend(where_here, [size] * blocks if pair else [], after(triple, memory), padded)

    memory_all = gather(memory.reshape(-1, 2, wide), 2)
    keys, values = memory_all[:, 0], memory_all[:, 1]

    constants = (sources, squares_plan, square_adapters, norm_gains, norm_biases, keys, values)
    if pair:
        received = [swap(leaving[0])]
        for item in leaving[1:]:
            received.append(swap(after(item, received[-1])))
        neighbours = [(at, at ^ 1) for at in range(fsdp)]
        for item in straight:
            sources += [item, lax.ppermute(after(item, received[0], memory_all), "fsdp", neighbours)]
    else:
        natural = lax.all_to_all(head_out[:, :wide], "seq", split_axis=0, concat_axis=1, tiled=True)
    made = []
    for at in range(blocks):
        if pair:
            own, spec, others = head_out, (size, wide), [received[at]]
        else:
            own, spec, others = natural, (size, model), []
        ready = after(frames_in, made[-1][7]) if made else frames_in
        made.append(middle(where_here if pair else jnp.zeros((4,), jnp.int32), own, spec, others, ready, at, blocks, *constants))
    normed3 = [item[7] for item in made]
    resid2 = [item[6] for item in made]

    feed_tail = feed_adapters + (feed_weights, hidden)
    if pair:
        others = [swap(item) for item in normed3]
        ours = [feed_forward(normed3[:1], resid2[:1], cot, 0, *feed_tail, F32)]
        theirs = feed_forward([others[0], after(others[1], ours[0][0])] if blocks > 1 else others, [], cot_other, 0, *feed_tail, BF)
        out_leaving, gu_leaving = theirs[:blocks], theirs[blocks : 2 * blocks]
        gu_more = [swap(gu_leaving[0])]
        for at in range(1, blocks):
            ours.append(feed_forward([after(normed3[at], gu_leaving[0])], [resid2[at]], cot, at, *feed_tail, F32))
            gu_more.append(swap(after(gu_leaving[at], gu_more[-1], ours[-1][0])))
        gu = [item[1] for item in ours]
        out_more = []
        feed_grads = [item[2:] for item in ours] + [theirs[2 * blocks :]]
    else:
        wide_in = gather(jnp.concatenate(normed3, 0), 0)
        all_out = feed_forward([wide_in], [], gather(cot, 0), 0, *feed_tail, F32)
        summed = [
            lax.psum_scatter(item.astype(BF), "seq", scatter_dimension=0, tiled=True) for item in all_out[:2]
        ]
        output = (jnp.concatenate(resid2, 0) + summed[0].astype(F32)).astype(BF)
        gu = [summed[1][at * size : (at + 1) * size] for at in range(blocks)]
        gu_more = [jnp.zeros_like(item) for item in gu]
        feed_grads = [all_out[2:]]

    pieces, resid1_grads, memory_parts, square_parts = [], [], [], []
    for at in range(blocks):
        gu_here = gu[at] if at == 0 else after(gu[at], result[-3])
        kept = made[at][:7] + made[at][8:9]
        result = middle_back(
            where_here, 2 if pair else 1, at, cot, gu_here, gu_more[at],
            kept, sources, squares_plan, square_adapters, norm_gains, keys, values,
        )
        if pair:
            waited = [pieces[-1][1]] if at else []
            if at == 0:
                out_more.append(swap(after(out_leaving[0], result[0])))
            if at == blocks - 1:
                memory_part = sum(memory_parts, result[-2]).astype(BF)
                memory_other = swap(after(pick(memory_part, 2, wide, there), *out_more))
                waited.append(memory_other)
            pieces.append((result[0], swap(after(result[1], *waited) if waited else result[1])))
        else:
            pieces.append(result[0])
        resid1_grads.append(result[-3])
        memory_parts.append(result[-2])
        square_parts.append(result[-1])
    resid1_grad = jnp.concatenate(resid1_grads, 0)
    square_grads = sum(square_parts[1:], square_parts[0])

    if pair:
        early, early_leaving, text_low = collect(
            plan, where_here, memory_parts, square_parts, feed_grads, memory_other, lat_text, flat_text, down_text,
            text_states[0], packed, start_text,
        )
        grad_pieces = [item[0] for item in pieces] + [item[1] for item in pieces]
    else:
        head_grad = lax.all_to_all(jnp.concatenate(pieces, 0), "seq", split_axis=1, concat_axis=0, tiled=True)
        grad_pieces = [jnp.pad(head_grad, ((0, 0), (0, padded - wide)))]
    triple_grad = attend_back(where_here, triple, head_out, grad_pieces, probs, padded)[:, :, :wide]
    if pair:
        early_other = swap(after(early_leaving, pieces[-1][1]))
        for at in range(1, blocks):
            out_more.append(swap(after(out_leaving[at], pieces[-1][1])))
        glat_qkv, late, late_leaving = qkv_grads(
            where_here, triple_grad, normed1, lat_qkv, upper_qkv
        )
        late_other = swap(late_leaving)
    else:
        glat_qkv = sum(mm_nt(triple_grad[at], upper_qkv[at]) for at in range(3)).astype(BF)
        gdown_qkv = mm_tn(glat_qkv, normed1)
        gup_qkv = [mm_tn(lat_qkv[:, at * rank : (at + 1) * rank], triple_grad[at]) for at in range(3)]
    back = partial(qkv_back, gradient=triple_grad, glat=glat_qkv, down=down_qkv, packed=packed, start=start_in)
    if pair:
        for_them = back(after(there, early_other, *out_more)[None], rows, kind=BF)
        for_us = back(after(spot, for_them, *out_more)[None], rows, kind=F32)
        input_grad = last_norm(frames_in, for_us + swap(for_them).astype(F32), norm_gains[0:1], resid1_grads)
        output = jnp.concatenate(
            [(item[0] + other.astype(F32)).astype(BF) for item, other in zip(ours, out_more)], 0
        )
    else:
        full = back(jnp.zeros((1,), jnp.int32), frames, kind=BF)
        normed1_grad = lax.psum_scatter(full, "seq", scatter_dimension=0, tiled=True).astype(F32)
        resid1_grad = jnp.concatenate(resid1_grads, 0)
        input_grad = resid1_grad + norm_back(frames_in.astype(F32), norm_gains[0:1], normed1_grad)

    selector = (index_all[None, :] == jnp.arange(adapters, dtype=jnp.int32)[:, None]).astype(BF)

    def by_adapter(sent, *others):
        received = lax.all_to_all(sent, "fsdp", 0, 0, tiled=True)
        chooser = after(selector, *others) if others else selector
        return jnp.einsum("ac,crw->arw", chooser, received, preferred_element_type=F32)

    if pair:
        shares = by_adapter(split_sums([after(late, for_them), late_other, early, early_other], fsdp)).astype(BF)
        grad_down, grad_up = both_tables(where_here, after(shares, input_grad), swap(after(shares, for_us)))
        text_total = text_low.astype(F32) + swap(text_low).astype(F32)
    else:
        memory_part = sum(memory_parts[1:], memory_parts[0]).astype(BF)
        memory_grad = lax.psum_scatter(memory_part, "seq", scatter_dimension=2, tiled=True)
        memory_flat = jnp.concatenate([memory_grad[0], memory_grad[1]], 1)
        glat_text = mm_nt(memory_flat, flat_text).astype(BF)
        gup_text = mm_tn(lat_text, memory_flat)
        gdown_text = mm_tn(glat_text, text)
        text_low = (mm_nt(memory_flat, w_text) + mm(glat_text, down_text)).astype(BF)
        own_text = [gup_text[at * rank : (at + 1) * rank, at * wide : (at + 1) * wide] for at in range(2)]
        gdown_in, gup_in, gdown_out, gup_out = feed_grads[0]
        square_grads = sum(square_parts[1:], square_parts[0])
        squares = [square_grads[rank * at : rank * (at + 1)] for at in range(6)]
        down_sent = [flat_down(gdown_qkv, 3), squares[0], squares[2], flat_down(gdown_text, 2), squares[4], gdown_in]
        upper_sent = [flat_upper(gup_qkv), squares[1], squares[3], flat_upper(own_text), squares[5]]
        down_sent = jnp.concatenate(down_sent + [all_units(gdown_out)], 1)
        upper_sent = jnp.concatenate(upper_sent + [all_units(gup_in), gup_out], 1)
        sent = jnp.concatenate([down_sent, upper_sent], 0).astype(BF).reshape(2 * rank, fsdp, piece).transpose(1, 0, 2)
        shares = lax.psum(by_adapter(sent).astype(BF), "seq")
        grad_down, grad_up = shares[:, :rank], shares[:, rank:]
        text_total = lax.psum(text_low, "seq").astype(F32)
    return (output[None], input_grad[None], text_total[None], grad_down.astype(F32), grad_up.astype(F32))


def solution(mesh):
    return jax.shard_map(
        partial(body, sizes=(mesh.shape["seq"], mesh.shape["fsdp"])),
        mesh=mesh,
        in_specs=(
            P("fsdp", "seq", None),
            P("fsdp", None, None),
            P("fsdp"),
            P(),
            P(),
            P("fsdp", None),
            P("fsdp", None),
            P("fsdp", None),
            P("fsdp", None),
            P("fsdp", None),
            P("fsdp", None),
            P("fsdp", None),
            P(None, None, "fsdp"),
            P(None, None, "fsdp"),
            P("fsdp", "seq", None),
        ),
        out_specs=(
            P("fsdp", "seq", None),
            P("fsdp", "seq", None),
            P("fsdp", None, None),
            P(None, None, "fsdp"),
            P(None, None, "fsdp"),
        ),
        check_vma=False,
    )
```

```python
from functools import partial

import jax
import jax.numpy as jnp
from jax import lax
from jax.experimental import pallas as pl
from jax.experimental.pallas import tpu as pltpu
from jax.sharding import PartitionSpec as P

HEAD = 64
LANES = 128
QB = 256
BF = jnp.bfloat16
F32 = jnp.float32
SCALE = float(HEAD) ** (-0.5)
SQRT_HALF = 0.7071067811865476
INV_SQRT_2PI = 0.3989422804014327
MIB = 1024 * 1024
VMEM_LIMIT = 60 * MIB
COST = 1.0
FEED_BLOCK = 512


def mm(a, b):
    return lax.dot_general(a, b, (((1,), (0,)), ((), ())), preferred_element_type=F32)


def mm_nt(a, b):
    return lax.dot_general(a, b, (((1,), (1,)), ((), ())), preferred_element_type=F32)


def mm_tn(a, b):
    return lax.dot_general(a, b, (((0,), (0,)), ((), ())), preferred_element_type=F32)


def norm_stats(values):
    centered = values - jnp.mean(values, -1, keepdims=True)
    variance = jnp.mean(centered * centered, -1, keepdims=True)
    inverse = lax.rsqrt(variance + 1e-05)
    return centered * inverse, inverse


def layer_norm(values, gains, biases):
    unit, _ = norm_stats(values)
    return unit * gains + biases


def norm_back(values, gains, gradient):
    unit, inverse = norm_stats(values)
    scaled = gradient * gains
    mean_one = jnp.mean(scaled, -1, keepdims=True)
    mean_two = jnp.mean(scaled * unit, -1, keepdims=True)
    return inverse * (scaled - mean_one - unit * mean_two)


def whole(shape):
    return pl.BlockSpec(shape, lambda *_: (0,) * len(shape))


def once(shape):
    return pl.BlockSpec(shape, lambda *_: (0,) * len(shape), pipeline_mode=pl.Buffered(1))


def params(count=1, limit=None):
    return pltpu.CompilerParams(
        dimension_semantics=("arbitrary",) * count if count else None, vmem_limit_bytes=limit or VMEM_LIMIT
    )


def cost(flops, moved, special=0):
    return pl.CostEstimate(
        flops=int(flops * COST), bytes_accessed=int(moved * COST), transcendentals=int(special * COST)
    )


def window(packed, start, width, rows=None, steps=1, step=0):
    block = width // steps
    rows = packed.shape[0] if rows is None else rows
    if start % block == 0 and block % LANES == 0:
        base = start // block
        return packed, pl.BlockSpec((rows, block), lambda *at: (0, base + (at[step] if steps > 1 else 0)))
    return packed[:, start : start + width], pl.BlockSpec(
        (rows, block), lambda *at: (0, at[step] if steps > 1 else 0)
    )


def norm_kernel(place_ref, *refs):
    count = len(refs) - 5
    parts, (gain_ref, bias_ref, down_ref, normed_ref, lat_ref) = refs[:count], refs[count:]
    step = 128
    for index, part_ref in enumerate(parts):
        base = place_ref[index] * part_ref.shape[0]

        def some(at, carry):
            rows = pl.ds(pl.multiple_of(at * step, step), step)
            into = pl.ds(pl.multiple_of(base + at * step, step), step)
            normed = layer_norm(part_ref[rows, :].astype(F32), gain_ref[...], bias_ref[...]).astype(BF)
            normed_ref[into, :] = normed
            lat_ref[into, :] = mm_nt(normed, down_ref[...]).astype(BF)
            return carry

        lax.fori_loop(0, part_ref.shape[0] // step, some, 0)


def smem():
    return pl.BlockSpec(memory_space=pltpu.SMEM)


def norm_project(places, parts, gains, biases, down):
    model = parts[0].shape[1]
    frames = sum(part.shape[0] for part in parts)
    ranks = down.shape[0]
    return pl.pallas_call(
        norm_kernel,
        in_specs=[smem()] + [whole(item.shape) for item in parts + [gains, biases, down]],
        out_specs=[whole((frames, model)), whole((frames, ranks))],
        out_shape=[jax.ShapeDtypeStruct((frames, model), BF), jax.ShapeDtypeStruct((frames, ranks), BF)],
        grid=(1,),
        compiler_params=params(1),
        cost_estimate=cost(2 * frames * model * ranks, 4 * frames * model),
        name="norm_project",
    )(places, *parts, gains, biases, down)


def qkv_kernel(normed_ref, lat_ref, up_ref, w_ref, out_ref):
    step = 256

    def some(at, carry):
        rows = pl.ds(pl.multiple_of(at * step, step), step)
        out_ref[rows, :] = (mm(normed_ref[rows, :], w_ref[...]) + mm(lat_ref[rows, :], up_ref[...])).astype(BF)
        return carry

    lax.fori_loop(0, normed_ref.shape[0] // step, some, 0)


def qkv_project(normed, latent, up, packed, start, width):
    row_count, model = normed.shape
    ranks = latent.shape[1]
    steps = 3 if (width // 3) % LANES == 0 else 1
    operand, spec = window(packed, start, width, steps=steps)
    block = width // steps
    if steps == 3:
        up_spec = pl.BlockSpec((None, ranks, block), lambda at: (at, 0, 0))
    else:
        up = up.transpose(1, 0, 2).reshape(ranks, width)
        up_spec = whole(up.shape)
    return pl.pallas_call(
        qkv_kernel,
        grid=(steps,),
        in_specs=[whole(normed.shape), whole(latent.shape), up_spec, spec],
        out_specs=pl.BlockSpec((row_count, block), lambda at: (0, at)),
        out_shape=jax.ShapeDtypeStruct((row_count, width), BF),
        compiler_params=params(1, 42 * MIB),
        cost_estimate=cost(2 * row_count * model * width, 2 * (row_count + width) * model),
        name="qkv_project",
    )(normed, latent, up, operand)


def tri_start(at):
    return QB * at * (at + 1) // 2


def attend_kernel(place_ref, q_ref, k_ref, v_ref, out_ref, prob_ref, *refs):
    sent, (val_t_ref, out_t_ref) = refs[:-2], refs[-2:]
    frames = q_ref.shape[0]
    lane = lax.broadcasted_iota(jnp.int32, (1, LANES), 1) // HEAD
    val_t_ref[...] = v_ref[...].T
    square = (QB, QB)
    keep_tri = lax.broadcasted_iota(jnp.int32, square, 0) <= lax.broadcasted_iota(jnp.int32, square, 1)

    def scores(half, at):
        stop = (at + 1) * QB
        query = q_ref[at * QB : stop, :] * jnp.where(lane == half, SCALE, 0.0).astype(BF)
        last = jnp.where(keep_tri, mm_nt(k_ref[stop - QB : stop, :], query), -1e30)
        if at == 0:
            return last
        return jnp.concatenate([mm_nt(k_ref[0 : stop - QB, :], query), last], 0)

    turns = [(half, at) for at in range(frames // QB) for half in range(2)]
    score = scores(*turns[0])
    for index, (half, at) in enumerate(turns):
        stop = (at + 1) * QB
        own = slice(half * HEAD, (half + 1) * HEAD)
        later = scores(*turns[index + 1]) if index + 1 < len(turns) else None
        raised = jnp.exp(score - jnp.max(score, 0, keepdims=True))
        prob = (raised * (1.0 / jnp.sum(raised, 0, keepdims=True))).astype(BF)
        prob_ref[half, tri_start(at) : tri_start(at) + stop, :] = prob
        out_t_ref[own, at * QB : stop] = mm(val_t_ref[own, 0:stop], prob)
        score = later
    out_ref[...] = out_t_ref[...].T.astype(BF)
    for index, sent_ref in enumerate(sent):
        size = sent_ref.shape[0]
        at = place_ref[1] * len(sent) + index
        sent_ref[...] = out_ref[pl.ds(pl.multiple_of(at * size, size), size), :]


def pair_specs(frames, width):
    pairs = width // LANES
    return [pl.BlockSpec((frames, LANES), lambda at, part=part: (0, part * pairs + at)) for part in range(3)]


def attend(places, sizes, triple, width):
    frames = triple.shape[0]
    pairs = width // LANES
    tri = tri_start(frames // QB)
    return pl.pallas_call(
        attend_kernel,
        grid=(pairs,),
        in_specs=[smem()] + pair_specs(frames, width),
        out_specs=[
            pl.BlockSpec((frames, LANES), lambda at: (0, at)),
            pl.BlockSpec((2, tri, QB), lambda at: (at, 0, 0)),
        ]
        + [pl.BlockSpec((size, LANES), lambda at: (0, at)) for size in sizes],
        out_shape=[
            jax.ShapeDtypeStruct((frames, width), BF),
            jax.ShapeDtypeStruct((2 * pairs, tri, QB), BF),
        ]
        + [jax.ShapeDtypeStruct((size, width), BF) for size in sizes],
        scratch_shapes=[pltpu.VMEM((LANES, frames), BF), pltpu.VMEM((LANES, frames), F32)],
        compiler_params=params(1),
        cost_estimate=cost(
            8 * tri * QB * HEAD * pairs, 2 * (4 * frames * width + 2 * pairs * tri * QB), 2 * pairs * tri * QB
        ),
        name="attend",
    )(places, triple, triple, triple)


def attend_back_kernel(place_ref, q_ref, k_ref, v_ref, out_ref, prob_ref, *refs):
    pieces, (back_ref, grad_ref, key_t_ref, dq_t_ref, dk_acc, dv_acc) = refs[:-6], refs[-6:]
    frames = q_ref.shape[0]
    for index, piece_ref in enumerate(pieces):
        size = piece_ref.shape[0]
        count = max(len(pieces) // 2, 1)
        at = place_ref[index // count] * count + index % count if len(pieces) > 1 else 0
        grad_ref[pl.ds(pl.multiple_of(at * size, size), size), :] = piece_ref[...]
    lane = lax.broadcasted_iota(jnp.int32, (1, LANES), 1) // HEAD
    key_t_ref[...] = k_ref[...].T
    dk_acc[...] = jnp.zeros_like(dk_acc)
    dv_acc[...] = jnp.zeros_like(dv_acc)
    turns = [(half, at) for at in range(frames // QB) for half in range(2)]

    def start(half, at):
        rows = slice(at * QB, (at + 1) * QB)
        grad = grad_ref[rows, :] * jnp.where(lane == half, 1.0, 0.0).astype(BF)
        return grad, mm_nt(v_ref[0 : (at + 1) * QB, :], grad)

    ready = start(*turns[0])
    for index, (half, at) in enumerate(turns):
        stop = (at + 1) * QB
        rows = slice(at * QB, stop)
        own = slice(half * HEAD, (half + 1) * HEAD)
        grad, prob_grad = ready
        if half == 0:
            product = (out_ref[rows, :].astype(F32) * grad_ref[rows, :].astype(F32)).T
        if index + 1 < len(turns):
            ready = start(*turns[index + 1])
        query = q_ref[rows, :] * jnp.where(lane == half, SCALE, 0.0).astype(BF)
        delta = jnp.sum(product[own, :], 0, keepdims=True)
        prob = prob_ref[half, tri_start(at) : tri_start(at) + stop, :]
        dv_acc[0:stop, :] += mm(prob, grad)
        score_grad = (prob.astype(F32) * (prob_grad - delta)).astype(BF)
        dk_acc[0:stop, :] += mm(score_grad, query)
        dq_t_ref[own, rows] = mm(key_t_ref[own, 0:stop], score_grad)
    back_ref[0] = (dq_t_ref[...].T * SCALE).astype(BF)
    back_ref[1] = dk_acc[...].astype(BF)
    back_ref[2] = dv_acc[...].astype(BF)


def attend_back(places, triple, attended, pieces, probs, width):
    frames = triple.shape[0]
    pairs = width // LANES
    tri = tri_start(frames // QB)
    column = pl.BlockSpec((frames, LANES), lambda at: (0, at))
    return pl.pallas_call(
        attend_back_kernel,
        grid=(pairs,),
        in_specs=[smem()]
        + pair_specs(frames, width)
        + [column, pl.BlockSpec((2, tri, QB), lambda at: (at, 0, 0))]
        + [pl.BlockSpec((piece.shape[0], LANES), lambda at: (0, at)) for piece in pieces],
        out_specs=pl.BlockSpec((3, frames, LANES), lambda at: (0, 0, at)),
        out_shape=jax.ShapeDtypeStruct((3, frames, width), BF),
        scratch_shapes=[
            pltpu.VMEM((frames, LANES), BF),
            pltpu.VMEM((LANES, frames), BF),
            pltpu.VMEM((LANES, frames), F32),
            pltpu.VMEM((frames, LANES), F32),
            pltpu.VMEM((frames, LANES), F32),
        ],
        compiler_params=params(1, 42 * MIB),
        cost_estimate=cost(16 * tri * QB * HEAD * pairs, 2 * (8 * frames * width + 2 * pairs * tri * QB)),
        name="attend_back",
    )(places, triple, triple, triple, attended, probs, *pieces)


def feed_kernel(count, based, *refs):
    pieces, refs = refs[:count], refs[count:]
    bases, refs = refs[:based], refs[based:]
    cot_ref, down_in_ref, up_in_ref, down_out_ref, up_out_ref, w_in_ref, w_out_ref = refs[:7]
    out_refs, gu_refs, refs = refs[7 : 7 + count], refs[7 + count : 7 + 2 * count], refs[7 + 2 * count :]
    (
        gdown_in_ref, gup_in_ref, gdown_out_ref, gup_out_ref, normed_ref,
        out_acc, gu_acc, lat_in, glat_out, lat_acc, glat_acc, lat_t, glat_t,
    ) = refs
    at = pl.program_id(0)

    @pl.when(at == 0)
    def _():
        start = 0
        for piece_ref in pieces:
            normed_ref[start : start + piece_ref.shape[0], :] = piece_ref[...]
            start += piece_ref.shape[0]
        latent = mm_nt(normed_ref[...], down_in_ref[...]).astype(BF)
        glat = mm_nt(cot_ref[...], up_out_ref[...]).astype(BF)
        lat_in[...] = latent
        glat_out[...] = glat
        lat_t[...] = latent.astype(F32).T.astype(BF)
        glat_t[...] = glat.astype(F32).T.astype(BF)
        start = 0
        for base_ref in bases:
            out_acc[start : start + base_ref.shape[0], :] = base_ref[...]
            start += base_ref.shape[0]
        if not bases:
            out_acc[...] = jnp.zeros_like(out_acc)
        gu_acc[...] = jnp.zeros_like(gu_acc)
        lat_acc[...] = jnp.zeros_like(lat_acc)
        glat_acc[...] = jnp.zeros_like(glat_acc)

    w_in = w_in_ref[...]
    w_out = w_out_ref[...]
    pre = mm(normed_ref[...], w_in) + mm(lat_in[...], up_in_ref[...])
    act_grad = mm_nt(cot_ref[...], w_out) + mm(glat_out[...], down_out_ref[...])
    cdf = 0.5 * (1.0 + lax.erf(pre * SQRT_HALF))
    slope = cdf + pre * (jnp.exp(-0.5 * pre * pre) * INV_SQRT_2PI)
    act = (pre * cdf).astype(BF)
    pre_grad = (act_grad * slope).astype(BF)
    out_acc[...] += mm(act, w_out)
    gu_acc[...] += mm_nt(pre_grad, w_in)
    lat_acc[...] += mm_nt(act, down_out_ref[...])
    glat_acc[...] += mm_nt(pre_grad, up_in_ref[...])
    gup_in_ref[...] = mm(lat_t[...], pre_grad)
    gdown_out_ref[...] = mm(glat_t[...], act)

    @pl.when(at == pl.num_programs(0) - 1)
    def _():
        latent = lat_acc[...].astype(BF)
        glat = glat_acc[...].astype(BF)
        start = 0
        for out_ref, gu_ref in zip(out_refs, gu_refs):
            rows = slice(start, start + out_ref.shape[0])
            out_ref[...] = (out_acc[rows, :] + mm(latent[rows], up_out_ref[...])).astype(out_ref.dtype)
            gu_ref[...] = (gu_acc[rows, :] + mm(glat[rows], down_in_ref[...])).astype(gu_ref.dtype)
            start += out_ref.shape[0]
        gup_out_ref[...] = mm(latent.astype(F32).T.astype(BF), cot_ref[...])
        gdown_in_ref[...] = mm(glat.astype(F32).T.astype(BF), normed_ref[...])


def feed_forward(pieces, bases, cotangent, block_at, down_in, up_in, down_out, up_out, weights, hidden, kind):
    model = cotangent.shape[1]
    row_count = sum(item.shape[0] for item in pieces)
    rank = down_in.shape[0]
    block = FEED_BLOCK if hidden % FEED_BLOCK == 0 else hidden
    w_in, in_spec, w_out, out_spec = weights(block)
    main = pl.BlockSpec((row_count, model), lambda at: (block_at, 0))
    slim = pl.BlockSpec((rank, block), lambda at: (0, at))
    small = whole((rank, model))
    return pl.pallas_call(
        partial(feed_kernel, len(pieces), len(bases)),
        grid=(hidden // block,),
        in_specs=[once(item.shape) for item in pieces + bases]
        + [main, small, slim, slim, small, in_spec, out_spec],
        out_specs=[whole(item.shape) for item in pieces] * 2 + [small, slim, slim, small],
        out_shape=[jax.ShapeDtypeStruct(item.shape, kind) for item in pieces]
        + [jax.ShapeDtypeStruct(item.shape, BF) for item in pieces]
        + [
            jax.ShapeDtypeStruct((rank, model), F32),
            jax.ShapeDtypeStruct((rank, hidden), F32),
            jax.ShapeDtypeStruct((rank, hidden), F32),
            jax.ShapeDtypeStruct((rank, model), F32),
        ],
        scratch_shapes=[pltpu.VMEM((row_count, model), BF)]
        + [pltpu.VMEM((row_count, model), F32)] * 2
        + [pltpu.VMEM((row_count, rank), BF)] * 2
        + [pltpu.VMEM((row_count, rank), F32)] * 2
        + [pltpu.VMEM((rank, row_count), BF)] * 2,
        compiler_params=params(1),
        cost_estimate=cost(8 * row_count * model * hidden, 4 * hidden * model, 2 * row_count * hidden),
        name="feed_forward",
    )(*pieces, *bases, cotangent, down_in, up_in, down_out, up_out, w_in, w_out)


def spread_heads(rows_ref, into_ref, model):
    keys = rows_ref.shape[0]
    wide = 4 * HEAD
    row = lax.broadcasted_iota(jnp.int32, (4 * keys, wide), 0) // keys
    col = lax.broadcasted_iota(jnp.int32, (4 * keys, wide), 1) // HEAD
    mask = jnp.where(row == col, 1.0, 0.0).astype(BF)

    def some(group, carry):
        part = rows_ref[:, pl.ds(pl.multiple_of(group * wide, wide), wide)]
        into = pl.ds(pl.multiple_of(group * 4 * keys, 4 * keys), 4 * keys)
        into_ref[into, :] = jnp.concatenate([part] * 4, 0) * mask
        return carry

    lax.fori_loop(0, model // wide, some, 0)


def head_total(values, keys, reduce):
    split = values.reshape(4, keys, values.shape[1])
    return jnp.broadcast_to(reduce(split, 1, keepdims=True), split.shape).reshape(values.shape)


def each(count, step, work):
    def some(at, carry):
        work(pl.ds(pl.multiple_of(at * step, step), step))
        return carry

    lax.fori_loop(0, count // step, some, 0)


def pair_of(both, size):
    return [pl.ds(pl.multiple_of(both.start + at * size, size), size) for at in range(both.size // size)]


def weight_copies(plan, place_ref, sources, hold_ref, sem_ref):
    model = hold_ref.shape[1]
    groups = []
    for index, (start, extra) in enumerate(plan):
        if extra is None:
            parts = [slice(at * model // 2, (at + 1) * model // 2) for at in range(2)]
            pairs = [(sources[0].at[rows, pl.ds(start, model)], hold_ref.at[index, rows, :]) for rows in parts]
        else:
            half = model // 2
            here, there = [pl.ds(pl.multiple_of(place_ref[at] * half, half), half) for at in range(2)]
            pairs = [(sources[0].at[:, pl.ds(start, half)], hold_ref.at[index, :, here])]
            for at in range(2):
                rows = pl.ds(pl.multiple_of(place_ref[2 + at] * half, half), half)
                pairs.append((sources[extra + at], hold_ref.at[index, rows, there]))
        groups.append(
            [pltpu.make_async_copy(src, dst, sem_ref.at[index, at]) for at, (src, dst) in enumerate(pairs)]
        )
    return groups


def source_count(plan):
    return 1 + 2 * sum(extra is not None for _, extra in plan)


def start_all(copies):
    for copy in copies:
        copy.start()


def wait_all(copies):
    for copy in copies:
        copy.wait()


def middle_kernel(plan, place_ref, *refs):
    sources, refs = refs[: source_count(plan)], refs[source_count(plan) :]
    inputs_ref, adapt_ref, gain_ref, bias_ref, keys_ref, values_ref = refs[:6]
    pieces = refs[6:-20]
    away = refs[-20:-14]
    resid2_ref, normed3_ref, lat_ref, hold_ref, key_wide, value_wide, sem_ref = refs[-14:-7]
    kept, out_sem = refs[-7:-1], refs[-1]
    attended_ref, resid1_ref, normed2_ref, query_ref, probs_ref, crossed_ref = kept
    leaving = [pltpu.make_async_copy(kept[at], away[at], out_sem.at[at]) for at in range(6)]
    model = inputs_ref.shape[1]
    keys = keys_ref.shape[0]
    rows = inputs_ref.shape[0]
    wide = 4 * HEAD
    copies = weight_copies(plan, place_ref, sources, hold_ref, sem_ref)
    start_all(copies[0])
    for index, piece_ref in enumerate(pieces):
        size = piece_ref.shape[1]
        attended_ref[:, pl.ds(pl.multiple_of(place_ref[index] * size, size), size)] = piece_ref[...]
    spread_heads(keys_ref, key_wide, model)
    spread_heads(values_ref, value_wide, model)

    def adapted(moving_ref, index, store):
        latent = mm_nt(moving_ref[...], adapt_ref[32 * index : 32 * index + 16, :]).astype(BF)
        lat_ref[:, 16 * index : 16 * index + 16] = latent
        wait_all(copies[index])
        if index < 2:
            start_all(copies[index + 1])

        def some(cols):
            store(
                cols,
                mm(moving_ref[...], hold_ref[index, :, cols])
                + mm(latent, adapt_ref[32 * index + 16 : 32 * index + 32, cols]),
            )

        each(model, 512, some)

    def add_first(cols, value):
        resid1_ref[:, cols] = inputs_ref[:, cols].astype(F32) + value

    def add_second(cols, value):
        resid2_ref[:, cols] = resid1_ref[:, cols] + value

    def keep_query(cols, value):
        query_ref[:, cols] = value.astype(BF)

    def normed(values_at, into_ref, which):
        def some(part):
            into_ref[part, :] = layer_norm(
                values_at[part, :], gain_ref[which : which + 1, :], bias_ref[which : which + 1, :]
            ).astype(BF)

        each(rows, 128, some)

    def cross(both):
        groups = pair_of(both, wide)
        scores = [mm_nt(key_wide[lanes, :], query_ref[:, lanes]) * SCALE for lanes in groups]
        for lanes, score in zip(groups, scores):
            raised = jnp.exp(score - head_total(score, keys, jnp.max))
            prob = (raised / head_total(raised, keys, jnp.sum)).astype(BF)
            probs_ref[lanes, :] = prob
            crossed_ref[:, lanes] = mm_tn(prob, value_wide[lanes, :]).astype(BF)

    leaving[0].start()
    adapted(attended_ref, 0, add_first)
    leaving[1].start()
    normed(resid1_ref, normed2_ref, 1)
    leaving[2].start()
    adapted(normed2_ref, 1, keep_query)
    leaving[3].start()
    each(model, 3 * wide, cross)
    leaving[4].start()
    leaving[5].start()
    adapted(crossed_ref, 2, add_second)
    normed(resid2_ref, normed3_ref, 2)
    wait_all(leaving)


def middle(places, own, own_spec, others, inputs, at, blocks, sources, plan, adapters, gains, biases, keys, values):
    rows, model = own_spec[0], inputs.shape[1]
    spread = model // HEAD * keys.shape[0]
    shape = lambda kind, dims=(rows, model): jax.ShapeDtypeStruct(dims, kind)
    flat = lambda dims: pl.BlockSpec(dims, lambda _, ref: (0,) * len(dims))
    shapes = [shape(kind) for kind in (BF, F32, BF, BF)]
    shapes += [shape(BF, (spread, rows)), shape(BF), shape(F32), shape(BF), shape(BF, (rows, 48))]
    return pl.pallas_call(
        partial(middle_kernel, plan),
        grid_spec=pltpu.PrefetchScalarGridSpec(
            num_scalar_prefetch=1,
            grid=(1,),
            in_specs=[pl.BlockSpec(memory_space=pl.ANY)] * len(sources)
            + [pl.BlockSpec((rows, model), lambda _, ref: (at, 0))]
            + [flat(item.shape) for item in (adapters, gains, biases, keys, values)]
            + [pl.BlockSpec(own_spec, lambda _, ref: (ref[0] * blocks + at, 0) if others else (at, 0))]
            + [flat(item.shape) for item in others],
            out_specs=[pl.BlockSpec(memory_space=pl.ANY)] * 6 + [flat(item.shape) for item in shapes[6:]],
            scratch_shapes=[
                pltpu.VMEM((3, model, model), BF),
                pltpu.VMEM((spread, 4 * HEAD), BF),
                pltpu.VMEM((spread, 4 * HEAD), BF),
                pltpu.SemaphoreType.DMA((3, 3)),
            ]
            + [pltpu.VMEM(item.shape, item.dtype) for item in shapes[:6]]
            + [pltpu.SemaphoreType.DMA((6,))],
        ),
        out_shape=shapes,
        compiler_params=params(),
        cost_estimate=cost(6 * rows * model * model, 6 * model * model + 24 * rows * model),
        name="middle",
    )(places, *sources, inputs, adapters, gains, biases, keys, values, own, *others)


def middle_back_kernel(plan, split, place_ref, *refs):
    sources, refs = refs[: source_count(plan)], refs[source_count(plan) :]
    cot_ref, gu_ref, more_ref = refs[:3]
    far = refs[3:9]
    resid2_ref, lat_ref, adapt_ref, gain_ref, keys_ref, values_ref = refs[9:15]
    kept, in_sem = refs[-7:-1], refs[-1]
    attended_ref, resid1_ref, normed2_ref, query_ref, probs_ref, crossed_ref = kept
    coming = [pltpu.make_async_copy(far[at], kept[at], in_sem.at[at]) for at in range(6)]
    refs = refs[15:-7]
    outs = refs[: 2 if split else 1]
    resid1_grad_ref, memory_ref, small_ref, hold_ref, key_wide, value_wide, work_ref, low_ref, sem_ref = refs[len(outs) :]
    rows, model = cot_ref.shape
    keys = keys_ref.shape[0]
    wide = 4 * HEAD
    copies = weight_copies(plan, place_ref, sources, hold_ref, sem_ref)
    start_all(copies[2])
    coming[5].start()
    spread_heads(keys_ref, key_wide, model)
    spread_heads(values_ref, value_wide, model)

    def first(part):
        gradient = gu_ref[part, :].astype(F32) + more_ref[part, :].astype(F32)
        value = cot_ref[part, :].astype(F32) + norm_back(resid2_ref[part, :], gain_ref[2:3, :], gradient)
        resid1_grad_ref[part, :] = value
        low_ref[part, :] = value.astype(BF)

    def second(part):
        value = resid1_grad_ref[part, :] + norm_back(resid1_ref[part, :], gain_ref[1:2, :], work_ref[part, :])
        resid1_grad_ref[part, :] = value
        low_ref[part, :] = value.astype(BF)

    def back(moving_ref, index, store):
        down = slice(32 * index, 32 * index + 16)
        upper = slice(32 * index + 16, 32 * index + 32)
        glat = mm_nt(low_ref[...], adapt_ref[upper, :]).astype(BF)
        glat_t = glat.astype(F32).T.astype(BF)
        lat_t = lat_ref[:, 16 * index : 16 * index + 16].astype(F32).T.astype(BF)
        wait_all(copies[index])
        if index == 2:
            wait_all(coming[5:])
            start_all(coming[2:5])
        if index == 1:
            wait_all(coming[2:3])
            start_all(coming[:2])
        if index == 0:
            wait_all(coming[:1])
        if index:
            start_all(copies[index - 1])

        def some(cols):
            small_ref[down, cols] = mm(glat_t, moving_ref[:, cols])
            small_ref[upper, cols] = mm(lat_t, low_ref[:, cols])
            store(cols, mm_nt(low_ref[...], hold_ref[index, cols, :]) + mm(glat, adapt_ref[down, cols]))

        each(model, 512, some)

    def keep(cols, value):
        work_ref[:, cols] = value

    def cross(both):
        groups = pair_of(both, wide)
        parts = [work_ref[:, lanes].astype(BF) for lanes in groups]
        prob_grads = [mm_nt(value_wide[lanes, :], part) for lanes, part in zip(groups, parts)]
        for lanes, part, prob_grad in zip(groups, parts, prob_grads):
            cross_one(lanes, part, prob_grad)

    def cross_one(lanes, part, prob_grad):
        prob = probs_ref[lanes, :]
        wide_prob = prob.astype(F32)
        weighted = wide_prob * prob_grad
        score_grad = (weighted - wide_prob * head_total(weighted, keys, jnp.sum)).astype(BF)
        low_ref[:, lanes] = (mm_tn(score_grad, key_wide[lanes, :]) * SCALE).astype(BF)
        key_full = mm(score_grad, query_ref[:, lanes])
        value_full = mm(prob, part)
        col = lax.broadcasted_iota(jnp.int32, (keys, wide), 1) // HEAD
        key_sum, value_sum = key_full[:keys], value_full[:keys]
        for head in range(1, 4):
            rows_at = slice(head * keys, (head + 1) * keys)
            key_sum = jnp.where(col == head, key_full[rows_at], key_sum)
            value_sum = jnp.where(col == head, value_full[rows_at], value_sum)
        memory_ref[0, :, lanes] = key_sum * SCALE
        memory_ref[1, :, lanes] = value_sum

    each(rows, 128, first)
    back(crossed_ref, 2, keep)
    wait_all(coming[3:5])
    each(model, 3 * wide, cross)
    back(normed2_ref, 1, keep)
    wait_all(coming[1:2])
    each(rows, 128, second)
    back(attended_ref, 0, keep)
    if split:
        size = outs[0].shape[1]
        for out_ref, index in zip(outs, range(2)):
            out_ref[...] = work_ref[:, pl.ds(pl.multiple_of(place_ref[index] * size, size), size)].astype(BF)
    else:
        outs[0][...] = work_ref[...].astype(BF)


def middle_back(places, parts, at, cotangent, gu, more, kept, sources, plan, adapters, gains, keys, values):
    model = cotangent.shape[1]
    rows = kept[0].shape[0]
    spread = model // HEAD * keys.shape[0]
    flat = lambda dims: pl.BlockSpec(dims, lambda _, ref: (0,) * len(dims))
    block = pl.BlockSpec((rows, model), lambda _, ref: (at, 0))
    shapes = [jax.ShapeDtypeStruct((rows, model // parts), BF)] * parts + [
        jax.ShapeDtypeStruct((rows, model), F32),
        jax.ShapeDtypeStruct((2,) + keys.shape, F32),
        jax.ShapeDtypeStruct(adapters.shape, F32),
    ]
    return pl.pallas_call(
        partial(middle_back_kernel, plan, parts == 2),
        grid_spec=pltpu.PrefetchScalarGridSpec(
            num_scalar_prefetch=1,
            grid=(1,),
            in_specs=[pl.BlockSpec(memory_space=pl.ANY)] * len(sources)
            + [block, flat(gu.shape), flat(more.shape)]
            + [pl.BlockSpec(memory_space=pl.ANY)] * 6
            + [flat(item.shape) for item in kept[6:]]
            + [flat(item.shape) for item in (adapters, gains, keys, values)],
            out_specs=[flat(item.shape) for item in shapes],
            scratch_shapes=[
                pltpu.VMEM((3, model, model), BF),
                pltpu.VMEM((spread, 4 * HEAD), BF),
                pltpu.VMEM((spread, 4 * HEAD), BF),
                pltpu.VMEM((rows, model), F32),
                pltpu.VMEM((rows, model), BF),
                pltpu.SemaphoreType.DMA((3, 3)),
            ]
            + [pltpu.VMEM(item.shape, item.dtype) for item in kept[:6]]
            + [pltpu.SemaphoreType.DMA((6,))],
        ),
        out_shape=shapes,
        compiler_params=params(),
        cost_estimate=cost(6 * rows * model * model, 6 * model * model + 36 * rows * model),
        name="middle_back",
    )(places, *sources, cotangent, gu, more, *kept, adapters, gains, keys, values)


def qkv_grads_kernel(
    place_ref, grad_ref, normed_ref, lat_ref, up_ref, glat_ref, mine_ref, theirs_ref, glat_acc, gup_acc, down_acc,
    down_all, upper_all,
):
    at = pl.program_id(0)
    gradient = grad_ref[...]
    rank = mine_ref.shape[0]
    model = normed_ref.shape[1]
    width = gradient.shape[1]
    gup_acc[...] = mm_tn(lat_ref[...], gradient)

    @pl.when(at == 0)
    def _():
        glat_acc[...] = jnp.zeros_like(glat_acc)
        upper_all[...] = jnp.zeros_like(upper_all)

    into = pl.ds(pl.multiple_of(at * model + place_ref[0] * width, LANES), width)
    upper_all[:, into] = gup_acc[pl.ds(pl.multiple_of(at * rank, rank), rank), :].astype(BF)
    glat_acc[...] += mm_nt(gradient, up_ref[...])

    @pl.when(at == pl.num_programs(0) - 1)
    def _():
        low = glat_acc[...].astype(BF)
        glat_ref[...] = low
        down_acc[...] = mm_tn(low, normed_ref[...])
        for part in range(3):
            down_all[:, part * model : (part + 1) * model] = down_acc[part * rank : (part + 1) * rank, :].astype(BF)
        share(place_ref, down_all, upper_all, mine_ref, theirs_ref)


def share(place_ref, down_all, upper_all, mine_ref, theirs_ref):
    @pl.when(place_ref[0] == 0)
    def _():
        mine_ref[...] = down_all[...]
        theirs_ref[...] = upper_all[...]

    @pl.when(place_ref[0] != 0)
    def _():
        mine_ref[...] = upper_all[...]
        theirs_ref[...] = down_all[...]


def qkv_grads(places, gradient, normed, latent, up):
    frames, model = normed.shape
    parts, ranks, width = up.shape
    rank = ranks // parts
    table = jax.ShapeDtypeStruct((rank, parts * model), BF)
    return pl.pallas_call(
        qkv_grads_kernel,
        grid=(parts,),
        in_specs=[
            smem(),
            pl.BlockSpec((None, frames, width), lambda at: (at, 0, 0)),
            whole(normed.shape),
            whole(latent.shape),
            pl.BlockSpec((None, ranks, width), lambda at: (at, 0, 0)),
        ],
        out_specs=[whole(latent.shape), whole(table.shape), whole(table.shape)],
        out_shape=[jax.ShapeDtypeStruct(latent.shape, BF), table, table],
        scratch_shapes=[
            pltpu.VMEM(latent.shape, F32),
            pltpu.VMEM((ranks, width), F32),
            pltpu.VMEM((ranks, model), F32),
            pltpu.VMEM(table.shape, BF),
            pltpu.VMEM(table.shape, BF),
        ],
        compiler_params=params(1, 42 * MIB),
        cost_estimate=cost(8 * frames * ranks * width * parts, 2 * frames * (model + parts * width)),
        name="qkv_grads",
    )(places, gradient, normed, latent, up)


def qkv_back_kernel(place_ref, grad_ref, glat_ref, down_ref, w_ref, gu_ref, gu_acc):
    at = pl.program_id(0)
    model = gu_ref.shape[1]
    last = pl.num_programs(0) - 1

    def some(cols):
        direct = mm_nt(grad_ref[...], w_ref[cols, :])

        @pl.when(at == 0)
        def _():
            gu_acc[:, cols] = direct + mm(glat_ref[...], down_ref[:, cols])

        @pl.when(jnp.logical_and(at > 0, at < last))
        def _():
            gu_acc[:, cols] += direct

        @pl.when(at == last)
        def _():
            gu_ref[:, cols] = (gu_acc[:, cols] + direct).astype(gu_ref.dtype)

    each(model, 512, some)


def qkv_back(place, row_count, gradient, glat, down, packed, start, kind):
    ranks, model = down.shape
    width = gradient.shape[2]
    if start % width == 0 and width % LANES == 0:
        weight, spec = packed, pl.BlockSpec((model, width), lambda at, ref: (0, start // width + at))
    else:
        weight = packed[:, start : start + 3 * width].reshape(model, 3, width).transpose(1, 0, 2)
        spec = pl.BlockSpec((None, model, width), lambda at, ref: (at, 0, 0))
    return pl.pallas_call(
        qkv_back_kernel,
        grid_spec=pltpu.PrefetchScalarGridSpec(
            num_scalar_prefetch=1,
            grid=(3,),
            in_specs=[
                pl.BlockSpec((None, row_count, width), lambda at, ref: (at, ref[0], 0)),
                pl.BlockSpec((row_count, ranks), lambda at, ref: (ref[0], 0)),
                pl.BlockSpec(down.shape, lambda at, ref: (0, 0)),
                spec,
            ],
            out_specs=pl.BlockSpec((row_count, model), lambda at, ref: (0, 0)),
            scratch_shapes=[pltpu.VMEM((row_count, model), F32)],
        ),
        out_shape=jax.ShapeDtypeStruct((row_count, model), kind),
        compiler_params=params(1, 42 * MIB),
        cost_estimate=cost(6 * row_count * model * width, 6 * model * width + 8 * row_count * model),
        name="qkv_back",
    )(place, gradient, glat, down, weight)


def last_norm_kernel(blocks, frames_ref, gradient_ref, gain_ref, *refs):
    pieces, grad_ref = refs[:-1], refs[-1]
    at = pl.program_id(0)
    back = norm_back(frames_ref[...].astype(F32), gain_ref[...], gradient_ref[...])
    for index, piece_ref in enumerate(pieces):

        @pl.when(at // blocks == index)
        def _(piece_ref=piece_ref):
            grad_ref[...] = back + piece_ref[...]


def last_norm(frames, gradient, gains, pieces):
    rows, model = frames.shape
    step = min(128, rows)
    blocks = pieces[0].shape[0] // step
    block = pl.BlockSpec((step, model), lambda at: (at, 0))

    def piece_spec(index):
        return pl.BlockSpec((step, model), lambda at: (jnp.clip(at - index * blocks, 0, blocks - 1), 0))

    return pl.pallas_call(
        partial(last_norm_kernel, blocks),
        grid=(rows // step,),
        in_specs=[block, block, whole(gains.shape)] + [piece_spec(index) for index in range(len(pieces))],
        out_specs=block,
        out_shape=jax.ShapeDtypeStruct((rows, model), F32),
        compiler_params=params(1, 42 * MIB),
        cost_estimate=cost(20 * rows * model, 16 * rows * model),
        name="last_norm",
    )(frames, gradient, gains, *pieces)


def run_length(size):
    count = 1
    while count * size % LANES:
        count *= 2
    return count


def join_kernel(pieces_ref, flat_ref):
    count, _, size = pieces_ref.shape
    run = run_length(size)

    def some(at, carry):
        parts = [pieces_ref[at * run + index] for index in range(run)]
        into = pl.ds(pl.multiple_of(at * run * size, LANES), run * size)
        flat_ref[:, into] = jnp.concatenate(parts, 1)
        return carry

    lax.fori_loop(0, count // run, some, 0)


def join_pieces(pieces):
    count, rows, size = pieces.shape
    if count % run_length(size):
        return pieces.transpose(1, 0, 2).reshape(rows, count * size)
    return pl.pallas_call(
        join_kernel,
        out_shape=jax.ShapeDtypeStruct((rows, count * size), pieces.dtype),
        compiler_params=params(0),
        name="join_pieces",
    )(pieces)


def split_kernel(*refs):
    sources, pieces_ref, flat_ref = refs[:-2], refs[-2], refs[-1]
    count, _, size = pieces_ref.shape
    run = run_length(size)
    start = 0
    for first_ref, second_ref in zip(sources[::2], sources[1::2]):
        width = first_ref.shape[1]
        both = first_ref[...].astype(F32) + second_ref[...].astype(F32)
        flat_ref[:, start : start + width] = both.astype(BF)
        start += width

    def some(at, carry):
        block = flat_ref[:, pl.ds(pl.multiple_of(at * run * size, LANES), run * size)]
        for index in range(run):
            pieces_ref[at * run + index] = block[:, index * size : (index + 1) * size]
        return carry

    lax.fori_loop(0, count // run, some, 0)


def split_sums(pairs, count):
    rows = pairs[0].shape[0]
    total = sum(item.shape[1] for item in pairs[::2])
    return pl.pallas_call(
        split_kernel,
        out_shape=jax.ShapeDtypeStruct((count, rows, total // count), BF),
        scratch_shapes=[pltpu.VMEM((rows, total), BF)],
        compiler_params=params(0, 42 * MIB),
        name="split_sums",
    )(*pairs)


def unit_loop(plan, work):
    fsdp, seq, folds, local = plan
    run = run_length(local)

    def some(at, carry):
        span = run * seq * folds * local
        block = pl.ds(pl.multiple_of(at * span, LANES), span)
        folded = [
            pl.ds(pl.multiple_of(fold * fsdp * local + at * run * local, LANES), run * local) for fold in range(folds)
        ]
        work(run, block, folded)
        return carry

    lax.fori_loop(0, fsdp // run, some, 0)


def take_units_kernel(plan, place_ref, all_ref, *refs):
    own_ref = refs[-1]
    _, seq, folds, local = plan
    spot = place_ref[0]

    def work(run, block, folded):
        values = all_ref[:, block]
        for fold, into in enumerate(folded):
            parts = []
            for index in range(run):
                base = (index * seq * folds + fold) * local
                part = values[:, base : base + local]
                for other in range(1, seq):
                    shift = base + other * folds * local
                    part = jnp.where(spot == other, values[:, shift : shift + local], part)
                parts.append(part)
            own_ref[:, into] = jnp.concatenate(parts, 1)

    unit_loop(plan, work)
    if len(refs) == 2:
        model = refs[0].shape[1]
        hidden = own_ref.shape[1] - folds * model
        for fold in range(folds):
            rows = pl.ds(pl.multiple_of((spot * folds + fold) * local, 16), local)
            own_ref[:, hidden + fold * model : hidden + (fold + 1) * model] = refs[0][rows, :]


def take_units(plan, places, matrix, low=None):
    _, seq, folds, local = plan
    rows, width = matrix.shape
    extra = [] if low is None else [low]
    out_width = width // seq + sum(folds * item.shape[1] for item in extra)
    return pl.pallas_call(
        partial(take_units_kernel, plan),
        in_specs=[smem()] + [pl.BlockSpec(memory_space=pltpu.VMEM)] * (1 + len(extra)),
        out_shape=jax.ShapeDtypeStruct((rows, out_width), matrix.dtype),
        compiler_params=params(0),
        name="take_units",
    )(places, matrix, *extra)


def collect_kernel(plan, blocks, start_at, place_ref, *refs):
    parts, squares, refs = refs[:blocks], refs[blocks : 2 * blocks], refs[2 * blocks :]
    feeds = [refs[at : at + 4] for at in range(0, len(refs) - 14, 4)]
    (
        other_ref, lat_ref, flat_ref, down_text_ref, text_ref, w_ref,
        mine_ref, theirs_ref, text_grad_ref, down_all, upper_all, unit_acc, hold_ref, sem_ref,
    ) = refs[-14:]
    _, seq, folds, local = plan
    rank = mine_ref.shape[0]
    model = text_ref.shape[1]
    wide = other_ref.shape[2]
    spot = place_ref[0]
    own = pl.ds(pl.multiple_of(spot * wide, wide), wide)
    copy = pltpu.make_async_copy(w_ref.at[:, pl.ds(start_at, hold_ref.shape[1])], hold_ref, sem_ref)
    copy.start()

    def total(items, rows):
        value = items[0][rows, :]
        for item in items[1:]:
            value = value + item[rows, :]
        return value

    moved = []
    for part in range(2):
        value = parts[0][part, :, own]
        for item in parts[1:]:
            value = value + item[part, :, own]
        moved.append((value + other_ref[part].astype(F32)).astype(BF))
    moved = jnp.concatenate(moved, 1)
    glat = mm_nt(moved, flat_ref[...]).astype(BF)
    gup = mm_tn(lat_ref[...], moved)
    gdown = mm_tn(glat, text_ref[...])

    upper_all[:, 2 * model : 4 * model] = jnp.zeros((rank, 2 * model), BF)
    for part in range(2):
        rows = slice(part * rank, (part + 1) * rank)
        down_all[:, (2 + part) * model : (3 + part) * model] = gdown[rows].astype(BF)
        into = pl.ds(pl.multiple_of((2 + part) * model + spot * wide, LANES), wide)
        upper_all[:, into] = gup[rows, part * wide : (part + 1) * wide].astype(BF)
    for index, at in enumerate((0, 1, 4)):
        cols = slice(at * model, (at + 1) * model)
        down_all[:, cols] = total(squares, slice(2 * index * rank, (2 * index + 1) * rank)).astype(BF)
        upper_all[:, cols] = total(squares, slice((2 * index + 1) * rank, (2 * index + 2) * rank)).astype(BF)
    every = slice(0, rank)
    down_all[:, 5 * model : 6 * model] = total([item[0] for item in feeds], every).astype(BF)
    upper_all[:, upper_all.shape[1] - model :] = total([item[3] for item in feeds], every).astype(BF)
    for into_ref, start, which in ((upper_all, 5 * model, 1), (down_all, 6 * model, 2)):
        unit_acc[...] = total([item[which] for item in feeds], every)

        def work(run, block, folded):
            values = [unit_acc[:, cols] for cols in folded]
            spread = []
            for index in range(run):
                for other in range(seq):
                    for fold in range(folds):
                        part = values[fold][:, index * local : (index + 1) * local]
                        spread.append(jnp.where(spot == other, part, 0.0))
            at = pl.ds(pl.multiple_of(start + block.start, LANES), block.size)
            into_ref[:, at] = jnp.concatenate(spread, 1).astype(BF)

        unit_loop(plan, work)
    share(place_ref, down_all, upper_all, mine_ref, theirs_ref)
    copy.wait()
    text_grad_ref[...] = (mm_nt(moved, hold_ref[...]) + mm(glat, down_text_ref[...])).astype(BF)


def collect(plan, places, parts, squares, feeds, other, lat_text, flat_text, down_text, text, packed, start):
    rank = squares[0].shape[0] // 6
    model = text.shape[1]
    hidden = feeds[0][1].shape[1]
    wide2 = flat_text.shape[1]
    width = 6 * model + hidden * plan[1]
    feeds = [item for feed in feeds for item in feed]
    before = list(parts) + list(squares) + feeds + [other, lat_text, flat_text, down_text, text]
    table = jax.ShapeDtypeStruct((rank, width), BF)
    shapes = [table, table, jax.ShapeDtypeStruct(text.shape, BF)]
    return pl.pallas_call(
        partial(collect_kernel, plan, len(parts), start),
        grid=(1,),
        in_specs=[smem()] + [whole(item.shape) for item in before] + [pl.BlockSpec(memory_space=pl.ANY)],
        out_specs=[whole(item.shape) for item in shapes],
        out_shape=shapes,
        scratch_shapes=[pltpu.VMEM(table.shape, BF)] * 2
        + [pltpu.VMEM((rank, hidden), F32), pltpu.VMEM((model, wide2), BF), pltpu.SemaphoreType.DMA],
        compiler_params=params(1),
        cost_estimate=cost(4 * text.shape[0] * model * wide2, 2 * model * wide2),
        name="collect",
    )(places, *before, packed)


def both_kernel(place_ref, mine_ref, other_ref, down_ref, upper_ref):
    first = place_ref[0] == 0
    for at in range(mine_ref.shape[0]):
        mine, other = mine_ref[at].astype(F32), other_ref[at].astype(F32)
        down_ref[at] = jnp.where(first, mine, other)
        upper_ref[at] = jnp.where(first, other, mine)


def both_tables(places, mine, other):
    return pl.pallas_call(
        both_kernel,
        in_specs=[smem()] + [pl.BlockSpec(memory_space=pltpu.VMEM)] * 2,
        out_shape=[jax.ShapeDtypeStruct(mine.shape, F32)] * 2,
        compiler_params=params(0, 42 * MIB),
        name="both_tables",
    )(places, mine, other)


def body(
    inputs,
    text_states,
    adapter_index,
    norm_gains,
    norm_biases,
    self_in,
    self_out,
    cross_query,
    cross_text,
    cross_out,
    hidden_in,
    hidden_out,
    adapter_down,
    adapter_up,
    cotangent,
    *,
    sizes,
):
    seq, fsdp = sizes
    spot = lax.axis_index("seq")
    first_here = spot == 0
    there = (seq - 1) - spot
    local = self_in.shape[0]
    depth = hidden_out.shape[0] // seq
    pair = seq == 2 and depth % local == 0 and fsdp % run_length(local) == 0
    model = inputs.shape[2]
    rows = inputs.shape[1]
    frames = rows * seq
    wide = model // seq
    hidden_all = hidden_in.shape[1]
    hidden = hidden_all // seq
    adapters, rank, piece = adapter_down.shape
    total = piece * fsdp

    blocks = max(rows // 256, 1)
    size = rows // blocks

    def swap(value):
        return lax.ppermute(value, "seq", [(0, 1), (1, 0)])

    def pick(value, axis, extent, which=None):
        return lax.dynamic_slice_in_dim(value, (spot if which is None else which) * extent, extent, axis)

    def ordered(mine, other):
        return jnp.where(first_here, mine, other), jnp.where(first_here, other, mine)

    def gather(value, axis):
        if pair:
            return jnp.concatenate(ordered(value, swap(value)), axis)
        return lax.all_gather(value, "seq", axis=axis, tiled=True)

    def after(value, *others):
        return lax.optimization_barrier((value,) + others)[0]

    def put(value, axis):
        shape = list(value.shape)
        shape[axis] = seq
        return lax.dynamic_update_slice_in_dim(jnp.zeros(shape, value.dtype), value, spot, axis)

    def own_columns(matrix, parts):
        return [pick(matrix[:, at * model : (at + 1) * model], 1, wide) for at in range(parts)]

    def flat_down(grads, parts):
        return jnp.concatenate([grads[at * rank : (at + 1) * rank] for at in range(parts)], 1)

    def flat_upper(own):
        return put(jnp.stack(own, 1)[:, :, None], 2).reshape(rank, len(own) * model)

    halved = [pick(item, 1, wide) if pair else item for item in (self_out, cross_query)]
    first = [cross_out] + own_columns(cross_text, 2) + halved + own_columns(self_in, 3)
    edges = [0]
    for item in first:
        edges.append(edges[-1] + item.shape[1])
    start_in, start_text = edges[5], edges[1]
    packed = lax.all_gather(jnp.concatenate(first, 1), "fsdp", axis=0, tiled=True)
    squares_plan = ((edges[3], None), (edges[4], None), (edges[0], None))
    if pair:
        squares_plan = ((edges[3], 1), (edges[4], 3)) + squares_plan[2:]
    core = lax.rem(lax.axis_index("fsdp"), 2)
    where_here = jnp.stack([spot, there, core, 1 - core]).astype(jnp.int32)
    if pair:
        folds = depth // local
        plan = (fsdp, seq, folds, local)
        own_units = partial(take_units, plan, where_here)
        packed_feed = lax.all_gather(own_units(hidden_in, hidden_out), "fsdp", axis=0, tiled=True)

        def feed_weights(block):
            per = model // block
            return (
                packed_feed,
                pl.BlockSpec((model, block), lambda at: (0, at)),
                packed_feed,
                pl.BlockSpec((block, model), lambda at: (at % per, folds + at // per)),
            )
    else:

        def own_units(matrix):
            kept = lax.dynamic_index_in_dim(matrix.reshape(-1, fsdp, seq, depth), spot, 2, False)
            return kept.reshape(-1, hidden)

        def all_units(matrix):
            return put(matrix.reshape(-1, fsdp, 1, depth), 2).reshape(-1, hidden_all)

        whole_in = lax.all_gather(own_units(hidden_in), "fsdp", axis=0, tiled=True)
        whole_out = lax.all_gather(pick(hidden_out, 0, depth), "fsdp", axis=0, tiled=True)

        def feed_weights(block):
            return (
                whole_in,
                pl.BlockSpec((model, block), lambda at: (0, at)),
                whole_out,
                pl.BlockSpec((block, model), lambda at: (at, 0)),
            )

    index_all = lax.all_to_all(jnp.broadcast_to(adapter_index, (fsdp,)), "fsdp", 0, 0, tiled=True)
    if pair:
        table = jnp.where(first_here, adapter_down, adapter_up)
        mine = join_pieces(lax.all_to_all(jnp.take(table, index_all, axis=0), "fsdp", 0, 0, tiled=True))
        down_all, upper_all = ordered(mine, swap(mine))
    else:
        table = jnp.concatenate([adapter_down, adapter_up], 1)
        chosen = join_pieces(lax.all_to_all(jnp.take(table, index_all, axis=0), "fsdp", 0, 0, tiled=True))
        down_all, upper_all = chosen[:rank], chosen[rank:]
    in_cuts = [0, 3 * model, 4 * model, 5 * model, 7 * model, 8 * model, 9 * model, 9 * model + hidden_all]
    out_cuts = [0, 3 * model, 4 * model, 5 * model, 7 * model, 8 * model, 8 * model + hidden_all, 9 * model + hidden_all]
    downs = [down_all[:, in_cuts[at] : in_cuts[at + 1]] for at in range(7)]
    uppers = [upper_all[:, out_cuts[at] : out_cuts[at + 1]] for at in range(7)]

    def part_down(matrix, parts):
        return jnp.concatenate([matrix[:, at * model : (at + 1) * model] for at in range(parts)], 0)

    def part_upper(matrix, parts):
        own = own_columns(matrix, parts)
        return jnp.stack(
            [jnp.pad(item, ((at * rank, (parts - 1 - at) * rank), (0, 0))) for at, item in enumerate(own)], 0
        )

    units = own_units(jnp.concatenate([uppers[5], downs[6]], 0))
    feed_adapters = (downs[5], units[:rank], units[rank:], uppers[6])
    square_adapters = jnp.concatenate([downs[1], uppers[1], downs[2], uppers[2], downs[4], uppers[4]], 0)
    down_qkv, upper_qkv = part_down(downs[0], 3), part_upper(uppers[0], 3)
    down_text, upper_text = part_down(downs[3], 2), part_upper(uppers[3], 2)
    flat_text = jnp.concatenate([upper_text[0], upper_text[1]], 1)

    frames_in = inputs[0]
    cot = cotangent[0]
    if pair:
        frames_parts = [frames_in, swap(frames_in)]
        cot_other = swap(after(cot, frames_parts[1]))
    else:
        frames_parts = [lax.all_gather(frames_in, "seq", axis=0, tiled=True)]
    norm_places = where_here if pair else jnp.zeros((4,), jnp.int32)
    if pair:
        frames_parts[1] = after(frames_parts[1], cot_other, units)
    normed1, lat_qkv = norm_project(norm_places, frames_parts, norm_gains[0:1], norm_biases[0:1], down_qkv)
    packed = after(packed, normed1)
    sources = [packed]
    if pair:
        half = model // 2
        straight = [swap(lax.dynamic_slice(packed, (core * half, at), (half, wide))) for at in edges[3:5]]
    triple = qkv_project(normed1, lat_qkv, upper_qkv, packed, start_in, 3 * wide)
    padded = -(-wide // LANES) * LANES
    if padded != wide:
        triple = jnp.pad(triple.reshape(frames, 3, wide), ((0, 0), (0, 0), (0, padded - wide)))
        triple = triple.reshape(frames, 3 * padded)
    text = after(text_states[0], triple)
    w_text = packed[:, start_text : start_text + 2 * wide]
    lat_text = mm_nt(text, down_text).astype(BF)
    memory = (mm(text, w_text) + mm(lat_text, flat_text)).astype(BF)
    head_out, probs, *leaving = attend(where_here, [size] * blocks if pair else [], after(triple, memory), padded)

    memory_all = gather(memory.reshape(-1, 2, wide), 2)
    keys, values = memory_all[:, 0], memory_all[:, 1]

    constants = (sources, squares_plan, square_adapters, norm_gains, norm_biases, keys, values)
    if pair:
        received = [swap(leaving[0])]
        for item in leaving[1:]:
            received.append(swap(after(item, received[-1])))
        neighbours = [(at, at ^ 1) for at in range(fsdp)]
        for item in straight:
            sources += [item, lax.ppermute(after(item, received[0], memory_all), "fsdp", neighbours)]
    else:
        natural = lax.all_to_all(head_out[:, :wide], "seq", split_axis=0, concat_axis=1, tiled=True)
    made = []
    for at in range(blocks):
        if pair:
            own, spec, others = head_out, (size, wide), [received[at]]
        else:
            own, spec, others = natural, (size, model), []
        ready = after(frames_in, made[-1][7]) if made else frames_in
        made.append(middle(where_here if pair else jnp.zeros((4,), jnp.int32), own, spec, others, ready, at, blocks, *constants))
    normed3 = [item[7] for item in made]
    resid2 = [item[6] for item in made]

    feed_tail = feed_adapters + (feed_weights, hidden)
    if pair:
        others = [swap(item) for item in normed3]
        theirs, gu_more, out_more = [], [], []
        for at in range(blocks):
            ready = after(others[at], theirs[-1][0]) if at else others[at]
            theirs.append(feed_forward([ready], [], cot_other, at, *feed_tail, BF))
            gu_more.append(swap(after(theirs[at][1], *gu_more[-1:])))
        ours = feed_forward([after(normed3[0], theirs[-1][1])] + normed3[1:], resid2, cot, 0, *feed_tail, F32)
        for at in range(blocks):
            behind = [ours[0]] + out_more[-1:] if at else [theirs[-1][0], gu_more[0]]
            out_more.append(swap(after(theirs[at][0], *behind)))
        gu = ours[blocks : 2 * blocks]
        feed_grads = [ours[2 * blocks :]] + [item[2:] for item in theirs]
    else:
        wide_in = gather(jnp.concatenate(normed3, 0), 0)
        all_out = feed_forward([wide_in], [], gather(cot, 0), 0, *feed_tail, F32)
        summed = [
            lax.psum_scatter(item.astype(BF), "seq", scatter_dimension=0, tiled=True) for item in all_out[:2]
        ]
        output = (jnp.concatenate(resid2, 0) + summed[0].astype(F32)).astype(BF)
        gu = [summed[1][at * size : (at + 1) * size] for at in range(blocks)]
        gu_more = [jnp.zeros_like(item) for item in gu]
        feed_grads = [all_out[2:]]

    pieces, resid1_grads, memory_parts, square_parts = [], [], [], []
    for at in range(blocks):
        gu_here = gu[at] if at == 0 else after(gu[at], result[-3])
        kept = made[at][:7] + made[at][8:9]
        result = middle_back(
            where_here, 2 if pair else 1, at, cot, gu_here, gu_more[at],
            kept, sources, squares_plan, square_adapters, norm_gains, keys, values,
        )
        if pair:
            waited = [pieces[-1][1]] if at else []
            if at == blocks - 1:
                memory_part = sum(memory_parts, result[-2]).astype(BF)
                memory_other = swap(after(pick(memory_part, 2, wide, there), *out_more))
                waited.append(memory_other)
            pieces.append((result[0], swap(after(result[1], *waited) if waited else result[1])))
        else:
            pieces.append(result[0])
        resid1_grads.append(result[-3])
        memory_parts.append(result[-2])
        square_parts.append(result[-1])
    resid1_grad = jnp.concatenate(resid1_grads, 0)
    square_grads = sum(square_parts[1:], square_parts[0])

    if pair:
        early, early_leaving, text_low = collect(
            plan, where_here, memory_parts, square_parts, feed_grads, memory_other, lat_text, flat_text, down_text,
            text_states[0], packed, start_text,
        )
        grad_pieces = [item[0] for item in pieces] + [item[1] for item in pieces]
    else:
        head_grad = lax.all_to_all(jnp.concatenate(pieces, 0), "seq", split_axis=1, concat_axis=0, tiled=True)
        grad_pieces = [jnp.pad(head_grad, ((0, 0), (0, padded - wide)))]
    triple_grad = attend_back(where_here, triple, head_out, grad_pieces, probs, padded)[:, :, :wide]
    if pair:
        early_other = swap(after(early_leaving, pieces[-1][1]))
        glat_qkv, late, late_leaving = qkv_grads(
            where_here, triple_grad, normed1, lat_qkv, upper_qkv
        )
        late_other = swap(late_leaving)
    else:
        glat_qkv = sum(mm_nt(triple_grad[at], upper_qkv[at]) for at in range(3)).astype(BF)
        gdown_qkv = mm_tn(glat_qkv, normed1)
        gup_qkv = [mm_tn(lat_qkv[:, at * rank : (at + 1) * rank], triple_grad[at]) for at in range(3)]
    back = partial(qkv_back, gradient=triple_grad, glat=glat_qkv, down=down_qkv, packed=packed, start=start_in)
    if pair:
        for_them = back(after(there, early_other)[None], rows, kind=BF)
        for_us = back(after(spot, for_them, *out_more)[None], rows, kind=F32)
        input_grad = last_norm(frames_in, for_us + swap(for_them).astype(F32), norm_gains[0:1], resid1_grads)
        output = jnp.concatenate(
            [(after(item, for_them) + other.astype(F32)).astype(BF) for item, other in zip(ours[:blocks], out_more)], 0
        )
    else:
        full = back(jnp.zeros((1,), jnp.int32), frames, kind=BF)
        normed1_grad = lax.psum_scatter(full, "seq", scatter_dimension=0, tiled=True).astype(F32)
        resid1_grad = jnp.concatenate(resid1_grads, 0)
        input_grad = resid1_grad + norm_back(frames_in.astype(F32), norm_gains[0:1], normed1_grad)

    selector = (index_all[None, :] == jnp.arange(adapters, dtype=jnp.int32)[:, None]).astype(BF)

    def by_adapter(sent, *others):
        received = lax.all_to_all(sent, "fsdp", 0, 0, tiled=True)
        chooser = after(selector, *others) if others else selector
        return jnp.einsum("ac,crw->arw", chooser, received, preferred_element_type=F32)

    if pair:
        shares = by_adapter(split_sums([after(late, for_them), late_other, early, early_other], fsdp)).astype(BF)
        grad_down, grad_up = both_tables(where_here, after(shares, input_grad), swap(after(shares, for_us)))
        text_total = text_low.astype(F32) + swap(text_low).astype(F32)
    else:
        memory_part = sum(memory_parts[1:], memory_parts[0]).astype(BF)
        memory_grad = lax.psum_scatter(memory_part, "seq", scatter_dimension=2, tiled=True)
        memory_flat = jnp.concatenate([memory_grad[0], memory_grad[1]], 1)
        glat_text = mm_nt(memory_flat, flat_text).astype(BF)
        gup_text = mm_tn(lat_text, memory_flat)
        gdown_text = mm_tn(glat_text, text)
        text_low = (mm_nt(memory_flat, w_text) + mm(glat_text, down_text)).astype(BF)
        own_text = [gup_text[at * rank : (at + 1) * rank, at * wide : (at + 1) * wide] for at in range(2)]
        gdown_in, gup_in, gdown_out, gup_out = feed_grads[0]
        square_grads = sum(square_parts[1:], square_parts[0])
        squares = [square_grads[rank * at : rank * (at + 1)] for at in range(6)]
        down_sent = [flat_down(gdown_qkv, 3), squares[0], squares[2], flat_down(gdown_text, 2), squares[4], gdown_in]
        upper_sent = [flat_upper(gup_qkv), squares[1], squares[3], flat_upper(own_text), squares[5]]
        down_sent = jnp.concatenate(down_sent + [all_units(gdown_out)], 1)
        upper_sent = jnp.concatenate(upper_sent + [all_units(gup_in), gup_out], 1)
        sent = jnp.concatenate([down_sent, upper_sent], 0).astype(BF).reshape(2 * rank, fsdp, piece).transpose(1, 0, 2)
        shares = lax.psum(by_adapter(sent).astype(BF), "seq")
        grad_down, grad_up = shares[:, :rank], shares[:, rank:]
        text_total = lax.psum(text_low, "seq").astype(F32)
    return (output[None], input_grad[None], text_total[None], grad_down.astype(F32), grad_up.astype(F32))


def solution(mesh):
    return jax.shard_map(
        partial(body, sizes=(mesh.shape["seq"], mesh.shape["fsdp"])),
        mesh=mesh,
        in_specs=(
            P("fsdp", "seq", None),
            P("fsdp", None, None),
            P("fsdp"),
            P(),
            P(),
            P("fsdp", None),
            P("fsdp", None),
            P("fsdp", None),
            P("fsdp", None),
            P("fsdp", None),
            P("fsdp", None),
            P("fsdp", None),
            P(None, None, "fsdp"),
            P(None, None, "fsdp"),
            P("fsdp", "seq", None),
        ),
        out_specs=(
            P("fsdp", "seq", None),
            P("fsdp", "seq", None),
            P("fsdp", None, None),
            P(None, None, "fsdp"),
            P(None, None, "fsdp"),
        ),
        check_vma=False,
    )
```

```python
from functools import partial

import jax
import jax.numpy as jnp
from jax import lax
from jax.experimental import pallas as pl
from jax.experimental.pallas import tpu as pltpu
from jax.sharding import PartitionSpec as P

HEAD = 64
LANES = 128
QB = 256
BF = jnp.bfloat16
F32 = jnp.float32
SCALE = float(HEAD) ** (-0.5)
SQRT_HALF = 0.7071067811865476
INV_SQRT_2PI = 0.3989422804014327
MIB = 1024 * 1024
VMEM_LIMIT = 60 * MIB
COST = 1.0
FEED_BLOCK = 512


def mm(a, b):
    return lax.dot_general(a, b, (((1,), (0,)), ((), ())), preferred_element_type=F32)


def mm_nt(a, b):
    return lax.dot_general(a, b, (((1,), (1,)), ((), ())), preferred_element_type=F32)


def mm_tn(a, b):
    return lax.dot_general(a, b, (((0,), (0,)), ((), ())), preferred_element_type=F32)


def norm_stats(values):
    centered = values - jnp.mean(values, -1, keepdims=True)
    variance = jnp.mean(centered * centered, -1, keepdims=True)
    inverse = lax.rsqrt(variance + 1e-05)
    return centered * inverse, inverse


def layer_norm(values, gains, biases):
    unit, _ = norm_stats(values)
    return unit * gains + biases


def norm_back(values, gains, gradient):
    unit, inverse = norm_stats(values)
    scaled = gradient * gains
    mean_one = jnp.mean(scaled, -1, keepdims=True)
    mean_two = jnp.mean(scaled * unit, -1, keepdims=True)
    return inverse * (scaled - mean_one - unit * mean_two)


def whole(shape):
    return pl.BlockSpec(shape, lambda *_: (0,) * len(shape))


def once(shape):
    return pl.BlockSpec(shape, lambda *_: (0,) * len(shape), pipeline_mode=pl.Buffered(1))


def params(count=1, limit=None):
    return pltpu.CompilerParams(
        dimension_semantics=("arbitrary",) * count if count else None, vmem_limit_bytes=limit or VMEM_LIMIT
    )


def cost(flops, moved, special=0):
    return pl.CostEstimate(
        flops=int(flops * COST), bytes_accessed=int(moved * COST), transcendentals=int(special * COST)
    )


def window(packed, start, width, rows=None, steps=1, step=0):
    block = width // steps
    rows = packed.shape[0] if rows is None else rows
    if start % block == 0 and block % LANES == 0:
        base = start // block
        return packed, pl.BlockSpec((rows, block), lambda *at: (0, base + (at[step] if steps > 1 else 0)))
    return packed[:, start : start + width], pl.BlockSpec(
        (rows, block), lambda *at: (0, at[step] if steps > 1 else 0)
    )


def norm_kernel(place_ref, *refs):
    count = len(refs) - 5
    parts, (gain_ref, bias_ref, down_ref, normed_ref, lat_ref) = refs[:count], refs[count:]
    step = 128
    for index, part_ref in enumerate(parts):
        base = place_ref[index] * part_ref.shape[0]

        def some(at, carry):
            rows = pl.ds(pl.multiple_of(at * step, step), step)
            into = pl.ds(pl.multiple_of(base + at * step, step), step)
            normed = layer_norm(part_ref[rows, :].astype(F32), gain_ref[...], bias_ref[...]).astype(BF)
            normed_ref[into, :] = normed
            lat_ref[into, :] = mm_nt(normed, down_ref[...]).astype(BF)
            return carry

        lax.fori_loop(0, part_ref.shape[0] // step, some, 0)


def smem():
    return pl.BlockSpec(memory_space=pltpu.SMEM)


def norm_project(places, parts, gains, biases, down):
    model = parts[0].shape[1]
    frames = sum(part.shape[0] for part in parts)
    ranks = down.shape[0]
    return pl.pallas_call(
        norm_kernel,
        in_specs=[smem()] + [whole(item.shape) for item in parts + [gains, biases, down]],
        out_specs=[whole((frames, model)), whole((frames, ranks))],
        out_shape=[jax.ShapeDtypeStruct((frames, model), BF), jax.ShapeDtypeStruct((frames, ranks), BF)],
        grid=(1,),
        compiler_params=params(1),
        cost_estimate=cost(2 * frames * model * ranks, 4 * frames * model),
        name="norm_project",
    )(places, *parts, gains, biases, down)


def qkv_kernel(normed_ref, lat_ref, up_ref, w_ref, out_ref):
    step = 256

    def some(at, carry):
        rows = pl.ds(pl.multiple_of(at * step, step), step)
        out_ref[rows, :] = (mm(normed_ref[rows, :], w_ref[...]) + mm(lat_ref[rows, :], up_ref[...])).astype(BF)
        return carry

    lax.fori_loop(0, normed_ref.shape[0] // step, some, 0)


def qkv_project(normed, latent, up, packed, start, width):
    row_count, model = normed.shape
    ranks = latent.shape[1]
    steps = 3 if (width // 3) % LANES == 0 else 1
    operand, spec = window(packed, start, width, steps=steps)
    block = width // steps
    if steps == 3:
        up_spec = pl.BlockSpec((None, ranks, block), lambda at: (at, 0, 0))
    else:
        up = up.transpose(1, 0, 2).reshape(ranks, width)
        up_spec = whole(up.shape)
    return pl.pallas_call(
        qkv_kernel,
        grid=(steps,),
        in_specs=[whole(normed.shape), whole(latent.shape), up_spec, spec],
        out_specs=pl.BlockSpec((row_count, block), lambda at: (0, at)),
        out_shape=jax.ShapeDtypeStruct((row_count, width), BF),
        compiler_params=params(1, 42 * MIB),
        cost_estimate=cost(2 * row_count * model * width, 2 * (row_count + width) * model),
        name="qkv_project",
    )(normed, latent, up, operand)


def tri_start(at):
    return QB * at * (at + 1) // 2


def attend_kernel(place_ref, q_ref, k_ref, v_ref, out_ref, prob_ref, *refs):
    sent, (val_t_ref, out_t_ref) = refs[:-2], refs[-2:]
    frames = q_ref.shape[0]
    lane = lax.broadcasted_iota(jnp.int32, (1, LANES), 1) // HEAD
    val_t_ref[...] = v_ref[...].T
    square = (QB, QB)
    keep_tri = lax.broadcasted_iota(jnp.int32, square, 0) <= lax.broadcasted_iota(jnp.int32, square, 1)

    def scores(half, at):
        stop = (at + 1) * QB
        query = q_ref[at * QB : stop, :] * jnp.where(lane == half, SCALE, 0.0).astype(BF)
        last = jnp.where(keep_tri, mm_nt(k_ref[stop - QB : stop, :], query), -1e30)
        if at == 0:
            return last
        return jnp.concatenate([mm_nt(k_ref[0 : stop - QB, :], query), last], 0)

    turns = [(half, at) for at in range(frames // QB) for half in range(2)]
    score = scores(*turns[0])
    for index, (half, at) in enumerate(turns):
        stop = (at + 1) * QB
        own = slice(half * HEAD, (half + 1) * HEAD)
        later = scores(*turns[index + 1]) if index + 1 < len(turns) else None
        raised = jnp.exp(score - jnp.max(score, 0, keepdims=True))
        prob = (raised * (1.0 / jnp.sum(raised, 0, keepdims=True))).astype(BF)
        prob_ref[half, tri_start(at) : tri_start(at) + stop, :] = prob
        out_t_ref[own, at * QB : stop] = mm(val_t_ref[own, 0:stop], prob)
        score = later
    out_ref[...] = out_t_ref[...].T.astype(BF)
    for index, sent_ref in enumerate(sent):
        size = sent_ref.shape[0]
        at = place_ref[1] * len(sent) + index
        sent_ref[...] = out_ref[pl.ds(pl.multiple_of(at * size, size), size), :]


def pair_specs(frames, width):
    pairs = width // LANES
    return [pl.BlockSpec((frames, LANES), lambda at, part=part: (0, part * pairs + at)) for part in range(3)]


def attend(places, sizes, triple, width):
    frames = triple.shape[0]
    pairs = width // LANES
    tri = tri_start(frames // QB)
    return pl.pallas_call(
        attend_kernel,
        grid=(pairs,),
        in_specs=[smem()] + pair_specs(frames, width),
        out_specs=[
            pl.BlockSpec((frames, LANES), lambda at: (0, at)),
            pl.BlockSpec((2, tri, QB), lambda at: (at, 0, 0)),
        ]
        + [pl.BlockSpec((size, LANES), lambda at: (0, at)) for size in sizes],
        out_shape=[
            jax.ShapeDtypeStruct((frames, width), BF),
            jax.ShapeDtypeStruct((2 * pairs, tri, QB), BF),
        ]
        + [jax.ShapeDtypeStruct((size, width), BF) for size in sizes],
        scratch_shapes=[pltpu.VMEM((LANES, frames), BF), pltpu.VMEM((LANES, frames), F32)],
        compiler_params=params(1),
        cost_estimate=cost(
            8 * tri * QB * HEAD * pairs, 2 * (4 * frames * width + 2 * pairs * tri * QB), 2 * pairs * tri * QB
        ),
        name="attend",
    )(places, triple, triple, triple)


def attend_back_kernel(place_ref, q_ref, k_ref, v_ref, out_ref, prob_ref, *refs):
    pieces, (back_ref, grad_ref, key_t_ref, dq_t_ref, dk_acc, dv_acc) = refs[:-6], refs[-6:]
    frames = q_ref.shape[0]
    for index, piece_ref in enumerate(pieces):
        size = piece_ref.shape[0]
        count = max(len(pieces) // 2, 1)
        at = place_ref[index // count] * count + index % count if len(pieces) > 1 else 0
        grad_ref[pl.ds(pl.multiple_of(at * size, size), size), :] = piece_ref[...]
    lane = lax.broadcasted_iota(jnp.int32, (1, LANES), 1) // HEAD
    key_t_ref[...] = k_ref[...].T
    dk_acc[...] = jnp.zeros_like(dk_acc)
    dv_acc[...] = jnp.zeros_like(dv_acc)
    turns = [(half, at) for at in range(frames // QB) for half in range(2)]

    def start(half, at):
        rows = slice(at * QB, (at + 1) * QB)
        grad = grad_ref[rows, :] * jnp.where(lane == half, 1.0, 0.0).astype(BF)
        return grad, mm_nt(v_ref[0 : (at + 1) * QB, :], grad)

    ready = start(*turns[0])
    for index, (half, at) in enumerate(turns):
        stop = (at + 1) * QB
        rows = slice(at * QB, stop)
        own = slice(half * HEAD, (half + 1) * HEAD)
        grad, prob_grad = ready
        if half == 0:
            product = (out_ref[rows, :].astype(F32) * grad_ref[rows, :].astype(F32)).T
        if index + 1 < len(turns):
            ready = start(*turns[index + 1])
        query = q_ref[rows, :] * jnp.where(lane == half, SCALE, 0.0).astype(BF)
        delta = jnp.sum(product[own, :], 0, keepdims=True)
        prob = prob_ref[half, tri_start(at) : tri_start(at) + stop, :]
        dv_acc[0:stop, :] += mm(prob, grad)
        score_grad = (prob.astype(F32) * (prob_grad - delta)).astype(BF)
        dk_acc[0:stop, :] += mm(score_grad, query)
        dq_t_ref[own, rows] = mm(key_t_ref[own, 0:stop], score_grad)
    back_ref[0] = (dq_t_ref[...].T * SCALE).astype(BF)
    back_ref[1] = dk_acc[...].astype(BF)
    back_ref[2] = dv_acc[...].astype(BF)


def attend_back(places, triple, attended, pieces, probs, width):
    frames = triple.shape[0]
    pairs = width // LANES
    tri = tri_start(frames // QB)
    column = pl.BlockSpec((frames, LANES), lambda at: (0, at))
    return pl.pallas_call(
        attend_back_kernel,
        grid=(pairs,),
        in_specs=[smem()]
        + pair_specs(frames, width)
        + [column, pl.BlockSpec((2, tri, QB), lambda at: (at, 0, 0))]
        + [pl.BlockSpec((piece.shape[0], LANES), lambda at: (0, at)) for piece in pieces],
        out_specs=pl.BlockSpec((3, frames, LANES), lambda at: (0, 0, at)),
        out_shape=jax.ShapeDtypeStruct((3, frames, width), BF),
        scratch_shapes=[
            pltpu.VMEM((frames, LANES), BF),
            pltpu.VMEM((LANES, frames), BF),
            pltpu.VMEM((LANES, frames), F32),
            pltpu.VMEM((frames, LANES), F32),
            pltpu.VMEM((frames, LANES), F32),
        ],
        compiler_params=params(1, 42 * MIB),
        cost_estimate=cost(16 * tri * QB * HEAD * pairs, 2 * (8 * frames * width + 2 * pairs * tri * QB)),
        name="attend_back",
    )(places, triple, triple, triple, attended, probs, *pieces)


def feed_kernel(count, based, *refs):
    pieces, refs = refs[:count], refs[count:]
    bases, refs = refs[:based], refs[based:]
    cot_ref, down_in_ref, up_in_ref, down_out_ref, up_out_ref, w_in_ref, w_out_ref = refs[:7]
    out_refs, gu_refs, refs = refs[7 : 7 + count], refs[7 + count : 7 + 2 * count], refs[7 + 2 * count :]
    (
        gdown_in_ref, gup_in_ref, gdown_out_ref, gup_out_ref, normed_ref,
        out_acc, gu_acc, lat_in, glat_out, lat_acc, glat_acc, lat_t, glat_t,
    ) = refs
    at = pl.program_id(0)

    @pl.when(at == 0)
    def _():
        start = 0
        for piece_ref in pieces:
            normed_ref[start : start + piece_ref.shape[0], :] = piece_ref[...]
            start += piece_ref.shape[0]
        latent = mm_nt(normed_ref[...], down_in_ref[...]).astype(BF)
        glat = mm_nt(cot_ref[...], up_out_ref[...]).astype(BF)
        lat_in[...] = latent
        glat_out[...] = glat
        lat_t[...] = latent.astype(F32).T.astype(BF)
        glat_t[...] = glat.astype(F32).T.astype(BF)
        start = 0
        for base_ref in bases:
            out_acc[start : start + base_ref.shape[0], :] = base_ref[...]
            start += base_ref.shape[0]
        if not bases:
            out_acc[...] = jnp.zeros_like(out_acc)
        gu_acc[...] = jnp.zeros_like(gu_acc)
        lat_acc[...] = jnp.zeros_like(lat_acc)
        glat_acc[...] = jnp.zeros_like(glat_acc)

    w_in = w_in_ref[...]
    w_out = w_out_ref[...]
    pre = mm(normed_ref[...], w_in) + mm(lat_in[...], up_in_ref[...])
    act_grad = mm_nt(cot_ref[...], w_out) + mm(glat_out[...], down_out_ref[...])
    cdf = 0.5 * (1.0 + lax.erf(pre * SQRT_HALF))
    slope = cdf + pre * (jnp.exp(-0.5 * pre * pre) * INV_SQRT_2PI)
    act = (pre * cdf).astype(BF)
    pre_grad = (act_grad * slope).astype(BF)
    out_acc[...] += mm(act, w_out)
    gu_acc[...] += mm_nt(pre_grad, w_in)
    lat_acc[...] += mm_nt(act, down_out_ref[...])
    glat_acc[...] += mm_nt(pre_grad, up_in_ref[...])
    gup_in_ref[...] = mm(lat_t[...], pre_grad)
    gdown_out_ref[...] = mm(glat_t[...], act)

    @pl.when(at == pl.num_programs(0) - 1)
    def _():
        latent = lat_acc[...].astype(BF)
        glat = glat_acc[...].astype(BF)
        start = 0
        for out_ref, gu_ref in zip(out_refs, gu_refs):
            rows = slice(start, start + out_ref.shape[0])
            out_ref[...] = (out_acc[rows, :] + mm(latent[rows], up_out_ref[...])).astype(out_ref.dtype)
            gu_ref[...] = (gu_acc[rows, :] + mm(glat[rows], down_in_ref[...])).astype(gu_ref.dtype)
            start += out_ref.shape[0]
        gup_out_ref[...] = mm(latent.astype(F32).T.astype(BF), cot_ref[...])
        gdown_in_ref[...] = mm(glat.astype(F32).T.astype(BF), normed_ref[...])


def feed_forward(pieces, bases, cotangent, block_at, down_in, up_in, down_out, up_out, weights, hidden, kind):
    model = cotangent.shape[1]
    row_count = sum(item.shape[0] for item in pieces)
    rank = down_in.shape[0]
    block = FEED_BLOCK if hidden % FEED_BLOCK == 0 else hidden
    w_in, in_spec, w_out, out_spec = weights(block)
    main = pl.BlockSpec((row_count, model), lambda at: (block_at, 0))
    slim = pl.BlockSpec((rank, block), lambda at: (0, at))
    small = whole((rank, model))
    return pl.pallas_call(
        partial(feed_kernel, len(pieces), len(bases)),
        grid=(hidden // block,),
        in_specs=[once(item.shape) for item in pieces + bases]
        + [main, small, slim, slim, small, in_spec, out_spec],
        out_specs=[whole(item.shape) for item in pieces] * 2 + [small, slim, slim, small],
        out_shape=[jax.ShapeDtypeStruct(item.shape, kind) for item in pieces]
        + [jax.ShapeDtypeStruct(item.shape, BF) for item in pieces]
        + [
            jax.ShapeDtypeStruct((rank, model), F32),
            jax.ShapeDtypeStruct((rank, hidden), F32),
            jax.ShapeDtypeStruct((rank, hidden), F32),
            jax.ShapeDtypeStruct((rank, model), F32),
        ],
        scratch_shapes=[pltpu.VMEM((row_count, model), BF)]
        + [pltpu.VMEM((row_count, model), F32)] * 2
        + [pltpu.VMEM((row_count, rank), BF)] * 2
        + [pltpu.VMEM((row_count, rank), F32)] * 2
        + [pltpu.VMEM((rank, row_count), BF)] * 2,
        compiler_params=params(1),
        cost_estimate=cost(8 * row_count * model * hidden, 4 * hidden * model, 2 * row_count * hidden),
        name="feed_forward",
    )(*pieces, *bases, cotangent, down_in, up_in, down_out, up_out, w_in, w_out)


def spread_heads(rows_ref, into_ref, model):
    keys = rows_ref.shape[0]
    wide = 4 * HEAD
    row = lax.broadcasted_iota(jnp.int32, (4 * keys, wide), 0) // keys
    col = lax.broadcasted_iota(jnp.int32, (4 * keys, wide), 1) // HEAD
    mask = jnp.where(row == col, 1.0, 0.0).astype(BF)

    def some(group, carry):
        part = rows_ref[:, pl.ds(pl.multiple_of(group * wide, wide), wide)]
        into = pl.ds(pl.multiple_of(group * 4 * keys, 4 * keys), 4 * keys)
        into_ref[into, :] = jnp.concatenate([part] * 4, 0) * mask
        return carry

    lax.fori_loop(0, model // wide, some, 0)


def head_total(values, keys, reduce):
    split = values.reshape(4, keys, values.shape[1])
    return jnp.broadcast_to(reduce(split, 1, keepdims=True), split.shape).reshape(values.shape)


def each(count, step, work):
    def some(at, carry):
        work(pl.ds(pl.multiple_of(at * step, step), step))
        return carry

    lax.fori_loop(0, count // step, some, 0)


def pair_of(both, size):
    return [pl.ds(pl.multiple_of(both.start + at * size, size), size) for at in range(both.size // size)]


def weight_copies(plan, place_ref, sources, hold_ref, sem_ref):
    model = hold_ref.shape[1]
    groups = []
    for index, (start, extra) in enumerate(plan):
        if extra is None:
            parts = [slice(at * model // 2, (at + 1) * model // 2) for at in range(2)]
            pairs = [(sources[0].at[rows, pl.ds(start, model)], hold_ref.at[index, rows, :]) for rows in parts]
        else:
            half = model // 2
            here, there = [pl.ds(pl.multiple_of(place_ref[at] * half, half), half) for at in range(2)]
            pairs = [(sources[0].at[:, pl.ds(start, half)], hold_ref.at[index, :, here])]
            for at in range(2):
                rows = pl.ds(pl.multiple_of(place_ref[2 + at] * half, half), half)
                pairs.append((sources[extra + at], hold_ref.at[index, rows, there]))
        groups.append(
            [pltpu.make_async_copy(src, dst, sem_ref.at[index, at]) for at, (src, dst) in enumerate(pairs)]
        )
    return groups


def source_count(plan):
    return 1 + 2 * sum(extra is not None for _, extra in plan)


def start_all(copies):
    for copy in copies:
        copy.start()


def wait_all(copies):
    for copy in copies:
        copy.wait()


def middle_kernel(plan, place_ref, *refs):
    sources, refs = refs[: source_count(plan)], refs[source_count(plan) :]
    inputs_ref, adapt_ref, gain_ref, bias_ref, keys_ref, values_ref = refs[:6]
    pieces = refs[6:-20]
    away = refs[-20:-14]
    resid2_ref, normed3_ref, lat_ref, hold_ref, key_wide, value_wide, sem_ref = refs[-14:-7]
    kept, out_sem = refs[-7:-1], refs[-1]
    attended_ref, resid1_ref, normed2_ref, query_ref, probs_ref, crossed_ref = kept
    leaving = [pltpu.make_async_copy(kept[at], away[at], out_sem.at[at]) for at in range(6)]
    model = inputs_ref.shape[1]
    keys = keys_ref.shape[0]
    rows = inputs_ref.shape[0]
    wide = 4 * HEAD
    copies = weight_copies(plan, place_ref, sources, hold_ref, sem_ref)
    start_all(copies[0])
    for index, piece_ref in enumerate(pieces):
        size = piece_ref.shape[1]
        attended_ref[:, pl.ds(pl.multiple_of(place_ref[index] * size, size), size)] = piece_ref[...]
    spread_heads(keys_ref, key_wide, model)
    spread_heads(values_ref, value_wide, model)

    def adapted(moving_ref, index, store):
        latent = mm_nt(moving_ref[...], adapt_ref[32 * index : 32 * index + 16, :]).astype(BF)
        lat_ref[:, 16 * index : 16 * index + 16] = latent
        wait_all(copies[index])
        if index < 2:
            start_all(copies[index + 1])

        def some(cols):
            store(
                cols,
                mm(moving_ref[...], hold_ref[index, :, cols])
                + mm(latent, adapt_ref[32 * index + 16 : 32 * index + 32, cols]),
            )

        each(model, 512, some)

    def add_first(cols, value):
        resid1_ref[:, cols] = inputs_ref[:, cols].astype(F32) + value

    def add_second(cols, value):
        resid2_ref[:, cols] = resid1_ref[:, cols] + value

    def keep_query(cols, value):
        query_ref[:, cols] = value.astype(BF)

    def normed(values_at, into_ref, which):
        def some(part):
            into_ref[part, :] = layer_norm(
                values_at[part, :], gain_ref[which : which + 1, :], bias_ref[which : which + 1, :]
            ).astype(BF)

        each(rows, 128, some)

    def cross(both):
        groups = pair_of(both, wide)
        scores = [mm_nt(key_wide[lanes, :], query_ref[:, lanes]) * SCALE for lanes in groups]
        for lanes, score in zip(groups, scores):
            raised = jnp.exp(score - head_total(score, keys, jnp.max))
            prob = (raised / head_total(raised, keys, jnp.sum)).astype(BF)
            probs_ref[lanes, :] = prob
            crossed_ref[:, lanes] = mm_tn(prob, value_wide[lanes, :]).astype(BF)

    leaving[0].start()
    adapted(attended_ref, 0, add_first)
    leaving[1].start()
    normed(resid1_ref, normed2_ref, 1)
    leaving[2].start()
    adapted(normed2_ref, 1, keep_query)
    leaving[3].start()
    each(model, 3 * wide, cross)
    leaving[4].start()
    leaving[5].start()
    adapted(crossed_ref, 2, add_second)
    normed(resid2_ref, normed3_ref, 2)
    wait_all(leaving)


def middle(places, own, own_spec, others, inputs, at, blocks, sources, plan, adapters, gains, biases, keys, values):
    rows, model = own_spec[0], inputs.shape[1]
    spread = model // HEAD * keys.shape[0]
    shape = lambda kind, dims=(rows, model): jax.ShapeDtypeStruct(dims, kind)
    flat = lambda dims: pl.BlockSpec(dims, lambda _, ref: (0,) * len(dims))
    shapes = [shape(kind) for kind in (BF, F32, BF, BF)]
    shapes += [shape(BF, (spread, rows)), shape(BF), shape(F32), shape(BF), shape(BF, (rows, 48))]
    return pl.pallas_call(
        partial(middle_kernel, plan),
        grid_spec=pltpu.PrefetchScalarGridSpec(
            num_scalar_prefetch=1,
            grid=(1,),
            in_specs=[pl.BlockSpec(memory_space=pl.ANY)] * len(sources)
            + [pl.BlockSpec((rows, model), lambda _, ref: (at, 0))]
            + [flat(item.shape) for item in (adapters, gains, biases, keys, values)]
            + [pl.BlockSpec(own_spec, lambda _, ref: (ref[0] * blocks + at, 0) if others else (at, 0))]
            + [flat(item.shape) for item in others],
            out_specs=[pl.BlockSpec(memory_space=pl.ANY)] * 6 + [flat(item.shape) for item in shapes[6:]],
            scratch_shapes=[
                pltpu.VMEM((3, model, model), BF),
                pltpu.VMEM((spread, 4 * HEAD), BF),
                pltpu.VMEM((spread, 4 * HEAD), BF),
                pltpu.SemaphoreType.DMA((3, 3)),
            ]
            + [pltpu.VMEM(item.shape, item.dtype) for item in shapes[:6]]
            + [pltpu.SemaphoreType.DMA((6,))],
        ),
        out_shape=shapes,
        compiler_params=params(),
        cost_estimate=cost(6 * rows * model * model, 6 * model * model + 24 * rows * model),
        name="middle",
    )(places, *sources, inputs, adapters, gains, biases, keys, values, own, *others)


def middle_back_kernel(plan, split, place_ref, *refs):
    sources, refs = refs[: source_count(plan)], refs[source_count(plan) :]
    cot_ref, gu_ref, more_ref = refs[:3]
    far = refs[3:9]
    resid2_ref, lat_ref, adapt_ref, gain_ref, keys_ref, values_ref = refs[9:15]
    kept, in_sem = refs[-7:-1], refs[-1]
    attended_ref, resid1_ref, normed2_ref, query_ref, probs_ref, crossed_ref = kept
    coming = [pltpu.make_async_copy(far[at], kept[at], in_sem.at[at]) for at in range(6)]
    refs = refs[15:-7]
    outs = refs[: 2 if split else 1]
    resid1_grad_ref, memory_ref, small_ref, hold_ref, key_wide, value_wide, work_ref, low_ref, sem_ref = refs[len(outs) :]
    rows, model = cot_ref.shape
    keys = keys_ref.shape[0]
    wide = 4 * HEAD
    copies = weight_copies(plan, place_ref, sources, hold_ref, sem_ref)
    start_all(copies[2])
    coming[5].start()
    spread_heads(keys_ref, key_wide, model)
    spread_heads(values_ref, value_wide, model)

    def first(part):
        gradient = gu_ref[part, :].astype(F32) + more_ref[part, :].astype(F32)
        value = cot_ref[part, :].astype(F32) + norm_back(resid2_ref[part, :], gain_ref[2:3, :], gradient)
        resid1_grad_ref[part, :] = value
        low_ref[part, :] = value.astype(BF)

    def second(part):
        value = resid1_grad_ref[part, :] + norm_back(resid1_ref[part, :], gain_ref[1:2, :], work_ref[part, :])
        resid1_grad_ref[part, :] = value
        low_ref[part, :] = value.astype(BF)

    def back(moving_ref, index, store):
        down = slice(32 * index, 32 * index + 16)
        upper = slice(32 * index + 16, 32 * index + 32)
        glat = mm_nt(low_ref[...], adapt_ref[upper, :]).astype(BF)
        glat_t = glat.astype(F32).T.astype(BF)
        lat_t = lat_ref[:, 16 * index : 16 * index + 16].astype(F32).T.astype(BF)
        wait_all(copies[index])
        if index == 2:
            wait_all(coming[5:])
            start_all(coming[2:5])
        if index == 1:
            wait_all(coming[2:3])
            start_all(coming[:2])
        if index == 0:
            wait_all(coming[:1])
        if index:
            start_all(copies[index - 1])

        def some(cols):
            small_ref[down, cols] = mm(glat_t, moving_ref[:, cols])
            small_ref[upper, cols] = mm(lat_t, low_ref[:, cols])
            store(cols, mm_nt(low_ref[...], hold_ref[index, cols, :]) + mm(glat, adapt_ref[down, cols]))

        each(model, 512, some)

    def keep(cols, value):
        work_ref[:, cols] = value

    def cross(both):
        groups = pair_of(both, wide)
        parts = [work_ref[:, lanes].astype(BF) for lanes in groups]
        prob_grads = [mm_nt(value_wide[lanes, :], part) for lanes, part in zip(groups, parts)]
        for lanes, part, prob_grad in zip(groups, parts, prob_grads):
            cross_one(lanes, part, prob_grad)

    def cross_one(lanes, part, prob_grad):
        prob = probs_ref[lanes, :]
        wide_prob = prob.astype(F32)
        weighted = wide_prob * prob_grad
        score_grad = (weighted - wide_prob * head_total(weighted, keys, jnp.sum)).astype(BF)
        low_ref[:, lanes] = (mm_tn(score_grad, key_wide[lanes, :]) * SCALE).astype(BF)
        key_full = mm(score_grad, query_ref[:, lanes])
        value_full = mm(prob, part)
        col = lax.broadcasted_iota(jnp.int32, (keys, wide), 1) // HEAD
        key_sum, value_sum = key_full[:keys], value_full[:keys]
        for head in range(1, 4):
            rows_at = slice(head * keys, (head + 1) * keys)
            key_sum = jnp.where(col == head, key_full[rows_at], key_sum)
            value_sum = jnp.where(col == head, value_full[rows_at], value_sum)
        memory_ref[0, :, lanes] = key_sum * SCALE
        memory_ref[1, :, lanes] = value_sum

    each(rows, 128, first)
    back(crossed_ref, 2, keep)
    wait_all(coming[3:5])
    each(model, 3 * wide, cross)
    back(normed2_ref, 1, keep)
    wait_all(coming[1:2])
    each(rows, 128, second)
    back(attended_ref, 0, keep)
    if split:
        size = outs[0].shape[1]
        for out_ref, index in zip(outs, range(2)):
            out_ref[...] = work_ref[:, pl.ds(pl.multiple_of(place_ref[index] * size, size), size)].astype(BF)
    else:
        outs[0][...] = work_ref[...].astype(BF)


def middle_back(places, parts, at, cotangent, gu, more, kept, sources, plan, adapters, gains, keys, values):
    model = cotangent.shape[1]
    rows = kept[0].shape[0]
    spread = model // HEAD * keys.shape[0]
    flat = lambda dims: pl.BlockSpec(dims, lambda _, ref: (0,) * len(dims))
    block = pl.BlockSpec((rows, model), lambda _, ref: (at, 0))
    shapes = [jax.ShapeDtypeStruct((rows, model // parts), BF)] * parts + [
        jax.ShapeDtypeStruct((rows, model), F32),
        jax.ShapeDtypeStruct((2,) + keys.shape, F32),
        jax.ShapeDtypeStruct(adapters.shape, F32),
    ]
    return pl.pallas_call(
        partial(middle_back_kernel, plan, parts == 2),
        grid_spec=pltpu.PrefetchScalarGridSpec(
            num_scalar_prefetch=1,
            grid=(1,),
            in_specs=[pl.BlockSpec(memory_space=pl.ANY)] * len(sources)
            + [block, flat(gu.shape), flat(more.shape)]
            + [pl.BlockSpec(memory_space=pl.ANY)] * 6
            + [flat(item.shape) for item in kept[6:]]
            + [flat(item.shape) for item in (adapters, gains, keys, values)],
            out_specs=[flat(item.shape) for item in shapes],
            scratch_shapes=[
                pltpu.VMEM((3, model, model), BF),
                pltpu.VMEM((spread, 4 * HEAD), BF),
                pltpu.VMEM((spread, 4 * HEAD), BF),
                pltpu.VMEM((rows, model), F32),
                pltpu.VMEM((rows, model), BF),
                pltpu.SemaphoreType.DMA((3, 3)),
            ]
            + [pltpu.VMEM(item.shape, item.dtype) for item in kept[:6]]
            + [pltpu.SemaphoreType.DMA((6,))],
        ),
        out_shape=shapes,
        compiler_params=params(),
        cost_estimate=cost(6 * rows * model * model, 6 * model * model + 36 * rows * model),
        name="middle_back",
    )(places, *sources, cotangent, gu, more, *kept, adapters, gains, keys, values)


def qkv_grads_kernel(
    place_ref, grad_ref, normed_ref, lat_ref, up_ref, glat_ref, mine_ref, theirs_ref, glat_acc, gup_acc, down_acc,
    down_all, upper_all,
):
    at = pl.program_id(0)
    gradient = grad_ref[...]
    rank = mine_ref.shape[0]
    model = normed_ref.shape[1]
    width = gradient.shape[1]
    gup_acc[...] = mm_tn(lat_ref[...], gradient)

    @pl.when(at == 0)
    def _():
        glat_acc[...] = jnp.zeros_like(glat_acc)
        upper_all[...] = jnp.zeros_like(upper_all)

    into = pl.ds(pl.multiple_of(at * model + place_ref[0] * width, LANES), width)
    upper_all[:, into] = gup_acc[pl.ds(pl.multiple_of(at * rank, rank), rank), :].astype(BF)
    glat_acc[...] += mm_nt(gradient, up_ref[...])

    @pl.when(at == pl.num_programs(0) - 1)
    def _():
        low = glat_acc[...].astype(BF)
        glat_ref[...] = low
        down_acc[...] = mm_tn(low, normed_ref[...])
        for part in range(3):
            down_all[:, part * model : (part + 1) * model] = down_acc[part * rank : (part + 1) * rank, :].astype(BF)
        share(place_ref, down_all, upper_all, mine_ref, theirs_ref)


def share(place_ref, down_all, upper_all, mine_ref, theirs_ref):
    @pl.when(place_ref[0] == 0)
    def _():
        mine_ref[...] = down_all[...]
        theirs_ref[...] = upper_all[...]

    @pl.when(place_ref[0] != 0)
    def _():
        mine_ref[...] = upper_all[...]
        theirs_ref[...] = down_all[...]


def qkv_grads(places, gradient, normed, latent, up):
    frames, model = normed.shape
    parts, ranks, width = up.shape
    rank = ranks // parts
    table = jax.ShapeDtypeStruct((rank, parts * model), BF)
    return pl.pallas_call(
        qkv_grads_kernel,
        grid=(parts,),
        in_specs=[
            smem(),
            pl.BlockSpec((None, frames, width), lambda at: (at, 0, 0)),
            whole(normed.shape),
            whole(latent.shape),
            pl.BlockSpec((None, ranks, width), lambda at: (at, 0, 0)),
        ],
        out_specs=[whole(latent.shape), whole(table.shape), whole(table.shape)],
        out_shape=[jax.ShapeDtypeStruct(latent.shape, BF), table, table],
        scratch_shapes=[
            pltpu.VMEM(latent.shape, F32),
            pltpu.VMEM((ranks, width), F32),
            pltpu.VMEM((ranks, model), F32),
            pltpu.VMEM(table.shape, BF),
            pltpu.VMEM(table.shape, BF),
        ],
        compiler_params=params(1, 42 * MIB),
        cost_estimate=cost(8 * frames * ranks * width * parts, 2 * frames * (model + parts * width)),
        name="qkv_grads",
    )(places, gradient, normed, latent, up)


def qkv_back_kernel(place_ref, grad_ref, glat_ref, down_ref, w_ref, gu_ref, gu_acc):
    at = pl.program_id(0)
    model = gu_ref.shape[1]
    last = pl.num_programs(0) - 1

    def some(cols):
        direct = mm_nt(grad_ref[...], w_ref[cols, :])

        @pl.when(at == 0)
        def _():
            gu_acc[:, cols] = direct + mm(glat_ref[...], down_ref[:, cols])

        @pl.when(jnp.logical_and(at > 0, at < last))
        def _():
            gu_acc[:, cols] += direct

        @pl.when(at == last)
        def _():
            gu_ref[:, cols] = (gu_acc[:, cols] + direct).astype(gu_ref.dtype)

    each(model, 512, some)


def qkv_back(place, row_count, gradient, glat, down, packed, start, kind):
    ranks, model = down.shape
    width = gradient.shape[2]
    if start % width == 0 and width % LANES == 0:
        weight, spec = packed, pl.BlockSpec((model, width), lambda at, ref: (0, start // width + at))
    else:
        weight = packed[:, start : start + 3 * width].reshape(model, 3, width).transpose(1, 0, 2)
        spec = pl.BlockSpec((None, model, width), lambda at, ref: (at, 0, 0))
    return pl.pallas_call(
        qkv_back_kernel,
        grid_spec=pltpu.PrefetchScalarGridSpec(
            num_scalar_prefetch=1,
            grid=(3,),
            in_specs=[
                pl.BlockSpec((None, row_count, width), lambda at, ref: (at, ref[0], 0)),
                pl.BlockSpec((row_count, ranks), lambda at, ref: (ref[0], 0)),
                pl.BlockSpec(down.shape, lambda at, ref: (0, 0)),
                spec,
            ],
            out_specs=pl.BlockSpec((row_count, model), lambda at, ref: (0, 0)),
            scratch_shapes=[pltpu.VMEM((row_count, model), F32)],
        ),
        out_shape=jax.ShapeDtypeStruct((row_count, model), kind),
        compiler_params=params(1, 42 * MIB),
        cost_estimate=cost(6 * row_count * model * width, 6 * model * width + 8 * row_count * model),
        name="qkv_back",
    )(place, gradient, glat, down, weight)


def last_norm_kernel(blocks, frames_ref, gradient_ref, gain_ref, *refs):
    pieces, grad_ref = refs[:-1], refs[-1]
    at = pl.program_id(0)
    back = norm_back(frames_ref[...].astype(F32), gain_ref[...], gradient_ref[...])
    for index, piece_ref in enumerate(pieces):

        @pl.when(at // blocks == index)
        def _(piece_ref=piece_ref):
            grad_ref[...] = back + piece_ref[...]


def last_norm(frames, gradient, gains, pieces):
    rows, model = frames.shape
    step = min(128, rows)
    blocks = pieces[0].shape[0] // step
    block = pl.BlockSpec((step, model), lambda at: (at, 0))

    def piece_spec(index):
        return pl.BlockSpec((step, model), lambda at: (jnp.clip(at - index * blocks, 0, blocks - 1), 0))

    return pl.pallas_call(
        partial(last_norm_kernel, blocks),
        grid=(rows // step,),
        in_specs=[block, block, whole(gains.shape)] + [piece_spec(index) for index in range(len(pieces))],
        out_specs=block,
        out_shape=jax.ShapeDtypeStruct((rows, model), F32),
        compiler_params=params(1, 42 * MIB),
        cost_estimate=cost(20 * rows * model, 16 * rows * model),
        name="last_norm",
    )(frames, gradient, gains, *pieces)


def run_length(size):
    count = 1
    while count * size % LANES:
        count *= 2
    return count


def join_kernel(pieces_ref, flat_ref):
    count, _, size = pieces_ref.shape
    run = run_length(size)

    def some(at, carry):
        parts = [pieces_ref[at * run + index] for index in range(run)]
        into = pl.ds(pl.multiple_of(at * run * size, LANES), run * size)
        flat_ref[:, into] = jnp.concatenate(parts, 1)
        return carry

    lax.fori_loop(0, count // run, some, 0)


def join_pieces(pieces):
    count, rows, size = pieces.shape
    if count % run_length(size):
        return pieces.transpose(1, 0, 2).reshape(rows, count * size)
    return pl.pallas_call(
        join_kernel,
        out_shape=jax.ShapeDtypeStruct((rows, count * size), pieces.dtype),
        compiler_params=params(0),
        name="join_pieces",
    )(pieces)


def split_kernel(*refs):
    sources, pieces_ref, flat_ref = refs[:-2], refs[-2], refs[-1]
    count, _, size = pieces_ref.shape
    run = run_length(size)
    start = 0
    for first_ref, second_ref in zip(sources[::2], sources[1::2]):
        width = first_ref.shape[1]
        both = first_ref[...].astype(F32) + second_ref[...].astype(F32)
        flat_ref[:, start : start + width] = both.astype(BF)
        start += width

    def some(at, carry):
        block = flat_ref[:, pl.ds(pl.multiple_of(at * run * size, LANES), run * size)]
        for index in range(run):
            pieces_ref[at * run + index] = block[:, index * size : (index + 1) * size]
        return carry

    lax.fori_loop(0, count // run, some, 0)


def split_sums(pairs, count):
    rows = pairs[0].shape[0]
    total = sum(item.shape[1] for item in pairs[::2])
    return pl.pallas_call(
        split_kernel,
        out_shape=jax.ShapeDtypeStruct((count, rows, total // count), BF),
        scratch_shapes=[pltpu.VMEM((rows, total), BF)],
        compiler_params=params(0, 42 * MIB),
        name="split_sums",
    )(*pairs)


def unit_loop(plan, work):
    fsdp, seq, folds, local = plan
    run = run_length(local)

    def some(at, carry):
        span = run * seq * folds * local
        block = pl.ds(pl.multiple_of(at * span, LANES), span)
        folded = [
            pl.ds(pl.multiple_of(fold * fsdp * local + at * run * local, LANES), run * local) for fold in range(folds)
        ]
        work(run, block, folded)
        return carry

    lax.fori_loop(0, fsdp // run, some, 0)


def take_units_kernel(plan, place_ref, all_ref, *refs):
    own_ref = refs[-1]
    _, seq, folds, local = plan
    spot = place_ref[0]

    def work(run, block, folded):
        values = all_ref[:, block]
        for fold, into in enumerate(folded):
            parts = []
            for index in range(run):
                base = (index * seq * folds + fold) * local
                part = values[:, base : base + local]
                for other in range(1, seq):
                    shift = base + other * folds * local
                    part = jnp.where(spot == other, values[:, shift : shift + local], part)
                parts.append(part)
            own_ref[:, into] = jnp.concatenate(parts, 1)

    unit_loop(plan, work)
    if len(refs) == 2:
        model = refs[0].shape[1]
        hidden = own_ref.shape[1] - folds * model
        for fold in range(folds):
            rows = pl.ds(pl.multiple_of((spot * folds + fold) * local, 16), local)
            own_ref[:, hidden + fold * model : hidden + (fold + 1) * model] = refs[0][rows, :]


def take_units(plan, places, matrix, low=None):
    _, seq, folds, local = plan
    rows, width = matrix.shape
    extra = [] if low is None else [low]
    out_width = width // seq + sum(folds * item.shape[1] for item in extra)
    return pl.pallas_call(
        partial(take_units_kernel, plan),
        in_specs=[smem()] + [pl.BlockSpec(memory_space=pltpu.VMEM)] * (1 + len(extra)),
        out_shape=jax.ShapeDtypeStruct((rows, out_width), matrix.dtype),
        compiler_params=params(0),
        name="take_units",
    )(places, matrix, *extra)


def collect_kernel(plan, blocks, start_at, place_ref, *refs):
    parts, squares, refs = refs[:blocks], refs[blocks : 2 * blocks], refs[2 * blocks :]
    feeds = [refs[at : at + 4] for at in range(0, len(refs) - 14, 4)]
    (
        other_ref, lat_ref, flat_ref, down_text_ref, text_ref, w_ref,
        mine_ref, theirs_ref, text_grad_ref, down_all, upper_all, unit_acc, hold_ref, sem_ref,
    ) = refs[-14:]
    _, seq, folds, local = plan
    rank = mine_ref.shape[0]
    model = text_ref.shape[1]
    wide = other_ref.shape[2]
    spot = place_ref[0]
    own = pl.ds(pl.multiple_of(spot * wide, wide), wide)
    copy = pltpu.make_async_copy(w_ref.at[:, pl.ds(start_at, hold_ref.shape[1])], hold_ref, sem_ref)
    copy.start()

    def total(items, rows):
        value = items[0][rows, :]
        for item in items[1:]:
            value = value + item[rows, :]
        return value

    moved = []
    for part in range(2):
        value = parts[0][part, :, own]
        for item in parts[1:]:
            value = value + item[part, :, own]
        moved.append((value + other_ref[part].astype(F32)).astype(BF))
    moved = jnp.concatenate(moved, 1)
    glat = mm_nt(moved, flat_ref[...]).astype(BF)
    gup = mm_tn(lat_ref[...], moved)
    gdown = mm_tn(glat, text_ref[...])

    upper_all[:, 2 * model : 4 * model] = jnp.zeros((rank, 2 * model), BF)
    for part in range(2):
        rows = slice(part * rank, (part + 1) * rank)
        down_all[:, (2 + part) * model : (3 + part) * model] = gdown[rows].astype(BF)
        into = pl.ds(pl.multiple_of((2 + part) * model + spot * wide, LANES), wide)
        upper_all[:, into] = gup[rows, part * wide : (part + 1) * wide].astype(BF)
    for index, at in enumerate((0, 1, 4)):
        cols = slice(at * model, (at + 1) * model)
        down_all[:, cols] = total(squares, slice(2 * index * rank, (2 * index + 1) * rank)).astype(BF)
        upper_all[:, cols] = total(squares, slice((2 * index + 1) * rank, (2 * index + 2) * rank)).astype(BF)
    every = slice(0, rank)
    down_all[:, 5 * model : 6 * model] = total([item[0] for item in feeds], every).astype(BF)
    upper_all[:, upper_all.shape[1] - model :] = total([item[3] for item in feeds], every).astype(BF)
    for into_ref, start, which in ((upper_all, 5 * model, 1), (down_all, 6 * model, 2)):
        unit_acc[...] = total([item[which] for item in feeds], every)

        def work(run, block, folded):
            values = [unit_acc[:, cols] for cols in folded]
            spread = []
            for index in range(run):
                for other in range(seq):
                    for fold in range(folds):
                        part = values[fold][:, index * local : (index + 1) * local]
                        spread.append(jnp.where(spot == other, part, 0.0))
            at = pl.ds(pl.multiple_of(start + block.start, LANES), block.size)
            into_ref[:, at] = jnp.concatenate(spread, 1).astype(BF)

        unit_loop(plan, work)
    share(place_ref, down_all, upper_all, mine_ref, theirs_ref)
    copy.wait()
    text_grad_ref[...] = (mm_nt(moved, hold_ref[...]) + mm(glat, down_text_ref[...])).astype(BF)


def collect(plan, places, parts, squares, feeds, other, lat_text, flat_text, down_text, text, packed, start):
    rank = squares[0].shape[0] // 6
    model = text.shape[1]
    hidden = feeds[0][1].shape[1]
    wide2 = flat_text.shape[1]
    width = 6 * model + hidden * plan[1]
    feeds = [item for feed in feeds for item in feed]
    before = list(parts) + list(squares) + feeds + [other, lat_text, flat_text, down_text, text]
    table = jax.ShapeDtypeStruct((rank, width), BF)
    shapes = [table, table, jax.ShapeDtypeStruct(text.shape, BF)]
    return pl.pallas_call(
        partial(collect_kernel, plan, len(parts), start),
        grid=(1,),
        in_specs=[smem()] + [whole(item.shape) for item in before] + [pl.BlockSpec(memory_space=pl.ANY)],
        out_specs=[whole(item.shape) for item in shapes],
        out_shape=shapes,
        scratch_shapes=[pltpu.VMEM(table.shape, BF)] * 2
        + [pltpu.VMEM((rank, hidden), F32), pltpu.VMEM((model, wide2), BF), pltpu.SemaphoreType.DMA],
        compiler_params=params(1),
        cost_estimate=cost(4 * text.shape[0] * model * wide2, 2 * model * wide2),
        name="collect",
    )(places, *before, packed)


def both_kernel(place_ref, mine_ref, other_ref, down_ref, upper_ref):
    first = place_ref[0] == 0
    for at in range(mine_ref.shape[0]):
        mine, other = mine_ref[at].astype(F32), other_ref[at].astype(F32)
        down_ref[at] = jnp.where(first, mine, other)
        upper_ref[at] = jnp.where(first, other, mine)


def both_tables(places, mine, other):
    return pl.pallas_call(
        both_kernel,
        in_specs=[smem()] + [pl.BlockSpec(memory_space=pltpu.VMEM)] * 2,
        out_shape=[jax.ShapeDtypeStruct(mine.shape, F32)] * 2,
        compiler_params=params(0, 42 * MIB),
        name="both_tables",
    )(places, mine, other)


def body(
    inputs,
    text_states,
    adapter_index,
    norm_gains,
    norm_biases,
    self_in,
    self_out,
    cross_query,
    cross_text,
    cross_out,
    hidden_in,
    hidden_out,
    adapter_down,
    adapter_up,
    cotangent,
    *,
    sizes,
):
    seq, fsdp = sizes
    spot = lax.axis_index("seq")
    first_here = spot == 0
    there = (seq - 1) - spot
    local = self_in.shape[0]
    depth = hidden_out.shape[0] // seq
    pair = seq == 2 and depth % local == 0 and fsdp % run_length(local) == 0
    model = inputs.shape[2]
    rows = inputs.shape[1]
    frames = rows * seq
    wide = model // seq
    hidden_all = hidden_in.shape[1]
    hidden = hidden_all // seq
    adapters, rank, piece = adapter_down.shape
    total = piece * fsdp

    blocks = max(rows // 256, 1)
    size = rows // blocks

    def swap(value):
        return lax.ppermute(value, "seq", [(0, 1), (1, 0)])

    def pick(value, axis, extent, which=None):
        return lax.dynamic_slice_in_dim(value, (spot if which is None else which) * extent, extent, axis)

    def ordered(mine, other):
        return jnp.where(first_here, mine, other), jnp.where(first_here, other, mine)

    def gather(value, axis):
        if pair:
            return jnp.concatenate(ordered(value, swap(value)), axis)
        return lax.all_gather(value, "seq", axis=axis, tiled=True)

    def after(value, *others):
        return lax.optimization_barrier((value,) + others)[0]

    def put(value, axis):
        shape = list(value.shape)
        shape[axis] = seq
        return lax.dynamic_update_slice_in_dim(jnp.zeros(shape, value.dtype), value, spot, axis)

    def own_columns(matrix, parts):
        return [pick(matrix[:, at * model : (at + 1) * model], 1, wide) for at in range(parts)]

    def flat_down(grads, parts):
        return jnp.concatenate([grads[at * rank : (at + 1) * rank] for at in range(parts)], 1)

    def flat_upper(own):
        return put(jnp.stack(own, 1)[:, :, None], 2).reshape(rank, len(own) * model)

    halved = [pick(item, 1, wide) if pair else item for item in (self_out, cross_query)]
    first = [cross_out] + own_columns(cross_text, 2) + halved + own_columns(self_in, 3)
    edges = [0]
    for item in first:
        edges.append(edges[-1] + item.shape[1])
    start_in, start_text = edges[5], edges[1]
    packed = lax.all_gather(jnp.concatenate(first, 1), "fsdp", axis=0, tiled=True)
    squares_plan = ((edges[3], None), (edges[4], None), (edges[0], None))
    if pair:
        squares_plan = ((edges[3], 1), (edges[4], 3)) + squares_plan[2:]
    core = lax.rem(lax.axis_index("fsdp"), 2)
    where_here = jnp.stack([spot, there, core, 1 - core]).astype(jnp.int32)
    if pair:
        folds = depth // local
        plan = (fsdp, seq, folds, local)
        own_units = partial(take_units, plan, where_here)
        packed_feed = lax.all_gather(own_units(hidden_in, hidden_out), "fsdp", axis=0, tiled=True)

        def feed_weights(block):
            per = model // block
            return (
                packed_feed,
                pl.BlockSpec((model, block), lambda at: (0, at)),
                packed_feed,
                pl.BlockSpec((block, model), lambda at: (at % per, folds + at // per)),
            )
    else:

        def own_units(matrix):
            kept = lax.dynamic_index_in_dim(matrix.reshape(-1, fsdp, seq, depth), spot, 2, False)
            return kept.reshape(-1, hidden)

        def all_units(matrix):
            return put(matrix.reshape(-1, fsdp, 1, depth), 2).reshape(-1, hidden_all)

        whole_in = lax.all_gather(own_units(hidden_in), "fsdp", axis=0, tiled=True)
        whole_out = lax.all_gather(pick(hidden_out, 0, depth), "fsdp", axis=0, tiled=True)

        def feed_weights(block):
            return (
                whole_in,
                pl.BlockSpec((model, block), lambda at: (0, at)),
                whole_out,
                pl.BlockSpec((block, model), lambda at: (at, 0)),
            )

    index_all = lax.all_to_all(jnp.broadcast_to(adapter_index, (fsdp,)), "fsdp", 0, 0, tiled=True)
    if pair:
        table = jnp.where(first_here, adapter_down, adapter_up)
        mine = join_pieces(lax.all_to_all(jnp.take(table, index_all, axis=0), "fsdp", 0, 0, tiled=True))
        down_all, upper_all = ordered(mine, swap(mine))
    else:
        table = jnp.concatenate([adapter_down, adapter_up], 1)
        chosen = join_pieces(lax.all_to_all(jnp.take(table, index_all, axis=0), "fsdp", 0, 0, tiled=True))
        down_all, upper_all = chosen[:rank], chosen[rank:]
    in_cuts = [0, 3 * model, 4 * model, 5 * model, 7 * model, 8 * model, 9 * model, 9 * model + hidden_all]
    out_cuts = [0, 3 * model, 4 * model, 5 * model, 7 * model, 8 * model, 8 * model + hidden_all, 9 * model + hidden_all]
    downs = [down_all[:, in_cuts[at] : in_cuts[at + 1]] for at in range(7)]
    uppers = [upper_all[:, out_cuts[at] : out_cuts[at + 1]] for at in range(7)]

    def part_down(matrix, parts):
        return jnp.concatenate([matrix[:, at * model : (at + 1) * model] for at in range(parts)], 0)

    def part_upper(matrix, parts):
        own = own_columns(matrix, parts)
        return jnp.stack(
            [jnp.pad(item, ((at * rank, (parts - 1 - at) * rank), (0, 0))) for at, item in enumerate(own)], 0
        )

    units = own_units(jnp.concatenate([uppers[5], downs[6]], 0))
    feed_adapters = (downs[5], units[:rank], units[rank:], uppers[6])
    square_adapters = jnp.concatenate([downs[1], uppers[1], downs[2], uppers[2], downs[4], uppers[4]], 0)
    down_qkv, upper_qkv = part_down(downs[0], 3), part_upper(uppers[0], 3)
    down_text, upper_text = part_down(downs[3], 2), part_upper(uppers[3], 2)
    flat_text = jnp.concatenate([upper_text[0], upper_text[1]], 1)

    frames_in = inputs[0]
    cot = cotangent[0]
    if pair:
        frames_parts = [frames_in, swap(frames_in)]
        cot_other = swap(after(cot, frames_parts[1]))
    else:
        frames_parts = [lax.all_gather(frames_in, "seq", axis=0, tiled=True)]
    norm_places = where_here if pair else jnp.zeros((4,), jnp.int32)
    if pair:
        frames_parts[1] = after(frames_parts[1], cot_other, units)
    normed1, lat_qkv = norm_project(norm_places, frames_parts, norm_gains[0:1], norm_biases[0:1], down_qkv)
    packed = after(packed, normed1)
    sources = [packed]
    if pair:
        half = model // 2
        cut = [lax.dynamic_slice(packed, (core * half, at), (half, wide)) for at in edges[3:5]]
        straight = [swap(item) for item in cut]
        normed1 = after(normed1, *cut)
    triple = qkv_project(normed1, lat_qkv, upper_qkv, packed, start_in, 3 * wide)
    padded = -(-wide // LANES) * LANES
    if padded != wide:
        triple = jnp.pad(triple.reshape(frames, 3, wide), ((0, 0), (0, 0), (0, padded - wide)))
        triple = triple.reshape(frames, 3 * padded)
    text = after(text_states[0], triple)
    w_text = packed[:, start_text : start_text + 2 * wide]
    lat_text = mm_nt(text, down_text).astype(BF)
    memory = (mm(text, w_text) + mm(lat_text, flat_text)).astype(BF)
    head_out, probs, *leaving = attend(where_here, [size] * blocks if pair else [], after(triple, memory), padded)

    memory_all = gather(memory.reshape(-1, 2, wide), 2)
    keys, values = memory_all[:, 0], memory_all[:, 1]

    constants = (sources, squares_plan, square_adapters, norm_gains, norm_biases, keys, values)
    if pair:
        received = [swap(leaving[0])]
        for item in leaving[1:]:
            received.append(swap(after(item, received[-1])))
        neighbours = [(at, at ^ 1) for at in range(fsdp)]
        for item in straight:
            sources += [item, lax.ppermute(after(item, received[0], memory_all), "fsdp", neighbours)]
    else:
        natural = lax.all_to_all(head_out[:, :wide], "seq", split_axis=0, concat_axis=1, tiled=True)
    made = []
    for at in range(blocks):
        if pair:
            own, spec, others = head_out, (size, wide), [received[at]]
        else:
            own, spec, others = natural, (size, model), []
        ready = after(frames_in, made[-1][7]) if made else frames_in
        made.append(middle(where_here if pair else jnp.zeros((4,), jnp.int32), own, spec, others, ready, at, blocks, *constants))
    normed3 = [item[7] for item in made]
    resid2 = [item[6] for item in made]

    feed_tail = feed_adapters + (feed_weights, hidden)
    if pair:
        others = [swap(item) for item in normed3]
        theirs, gu_more, out_more = [], [], []
        for at in range(blocks):
            ready = after(others[at], theirs[-1][0]) if at else others[at]
            theirs.append(feed_forward([ready], [], cot_other, at, *feed_tail, BF))
            gu_more.append(swap(after(theirs[at][1], *gu_more[-1:])))
        ours = feed_forward([after(normed3[0], theirs[-1][1])] + normed3[1:], resid2, cot, 0, *feed_tail, F32)
        for at in range(blocks):
            behind = [ours[0]] + out_more[-1:] if at else [theirs[-1][0], gu_more[0]]
            out_more.append(swap(after(theirs[at][0], *behind)))
        gu = ours[blocks : 2 * blocks]
        feed_grads = [ours[2 * blocks :]] + [item[2:] for item in theirs]
    else:
        wide_in = gather(jnp.concatenate(normed3, 0), 0)
        all_out = feed_forward([wide_in], [], gather(cot, 0), 0, *feed_tail, F32)
        summed = [
            lax.psum_scatter(item.astype(BF), "seq", scatter_dimension=0, tiled=True) for item in all_out[:2]
        ]
        output = (jnp.concatenate(resid2, 0) + summed[0].astype(F32)).astype(BF)
        gu = [summed[1][at * size : (at + 1) * size] for at in range(blocks)]
        gu_more = [jnp.zeros_like(item) for item in gu]
        feed_grads = [all_out[2:]]

    pieces, resid1_grads, memory_parts, square_parts = [], [], [], []
    for at in range(blocks):
        gu_here = gu[at] if at == 0 else after(gu[at], result[-3])
        kept = made[at][:7] + made[at][8:9]
        result = middle_back(
            where_here, 2 if pair else 1, at, cot, gu_here, gu_more[at],
            kept, sources, squares_plan, square_adapters, norm_gains, keys, values,
        )
        if pair:
            waited = [pieces[-1][1]] if at else []
            if at == blocks - 1:
                memory_part = sum(memory_parts, result[-2]).astype(BF)
                memory_other = swap(after(pick(memory_part, 2, wide, there), *out_more))
                waited.append(memory_other)
            pieces.append((result[0], swap(after(result[1], *waited) if waited else result[1])))
        else:
            pieces.append(result[0])
        resid1_grads.append(result[-3])
        memory_parts.append(result[-2])
        square_parts.append(result[-1])
    resid1_grad = jnp.concatenate(resid1_grads, 0)
    square_grads = sum(square_parts[1:], square_parts[0])

    if pair:
        early, early_leaving, text_low = collect(
            plan, where_here, memory_parts, square_parts, feed_grads, memory_other, lat_text, flat_text, down_text,
            text_states[0], packed, start_text,
        )
        grad_pieces = [item[0] for item in pieces] + [item[1] for item in pieces]
    else:
        head_grad = lax.all_to_all(jnp.concatenate(pieces, 0), "seq", split_axis=1, concat_axis=0, tiled=True)
        grad_pieces = [jnp.pad(head_grad, ((0, 0), (0, padded - wide)))]
    triple_grad = attend_back(where_here, triple, head_out, grad_pieces, probs, padded)[:, :, :wide]
    if pair:
        early_other = swap(after(early_leaving, pieces[-1][1]))
        glat_qkv, late, late_leaving = qkv_grads(
            where_here, triple_grad, normed1, lat_qkv, upper_qkv
        )
        late_other = swap(late_leaving)
    else:
        glat_qkv = sum(mm_nt(triple_grad[at], upper_qkv[at]) for at in range(3)).astype(BF)
        gdown_qkv = mm_tn(glat_qkv, normed1)
        gup_qkv = [mm_tn(lat_qkv[:, at * rank : (at + 1) * rank], triple_grad[at]) for at in range(3)]
    back = partial(qkv_back, gradient=triple_grad, glat=glat_qkv, down=down_qkv, packed=packed, start=start_in)
    if pair:
        for_them = back(after(there, early_other)[None], rows, kind=BF)
        for_us = back(after(spot, for_them, *out_more)[None], rows, kind=F32)
        input_grad = last_norm(frames_in, for_us + swap(for_them).astype(F32), norm_gains[0:1], resid1_grads)
        output = jnp.concatenate(
            [(after(item, for_them) + other.astype(F32)).astype(BF) for item, other in zip(ours[:blocks], out_more)], 0
        )
    else:
        full = back(jnp.zeros((1,), jnp.int32), frames, kind=BF)
        normed1_grad = lax.psum_scatter(full, "seq", scatter_dimension=0, tiled=True).astype(F32)
        resid1_grad = jnp.concatenate(resid1_grads, 0)
        input_grad = resid1_grad + norm_back(frames_in.astype(F32), norm_gains[0:1], normed1_grad)

    selector = (index_all[None, :] == jnp.arange(adapters, dtype=jnp.int32)[:, None]).astype(BF)

    def by_adapter(sent, *others):
        received = lax.all_to_all(sent, "fsdp", 0, 0, tiled=True)
        chooser = after(selector, *others) if others else selector
        return jnp.einsum("ac,crw->arw", chooser, received, preferred_element_type=F32)

    if pair:
        shares = by_adapter(split_sums([after(late, for_them), late_other, early, early_other], fsdp)).astype(BF)
        grad_down, grad_up = both_tables(where_here, after(shares, input_grad), swap(after(shares, for_us)))
        text_total = text_low.astype(F32) + swap(after(text_low, for_them)).astype(F32)
    else:
        memory_part = sum(memory_parts[1:], memory_parts[0]).astype(BF)
        memory_grad = lax.psum_scatter(memory_part, "seq", scatter_dimension=2, tiled=True)
        memory_flat = jnp.concatenate([memory_grad[0], memory_grad[1]], 1)
        glat_text = mm_nt(memory_flat, flat_text).astype(BF)
        gup_text = mm_tn(lat_text, memory_flat)
        gdown_text = mm_tn(glat_text, text)
        text_low = (mm_nt(memory_flat, w_text) + mm(glat_text, down_text)).astype(BF)
        own_text = [gup_text[at * rank : (at + 1) * rank, at * wide : (at + 1) * wide] for at in range(2)]
        gdown_in, gup_in, gdown_out, gup_out = feed_grads[0]
        square_grads = sum(square_parts[1:], square_parts[0])
        squares = [square_grads[rank * at : rank * (at + 1)] for at in range(6)]
        down_sent = [flat_down(gdown_qkv, 3), squares[0], squares[2], flat_down(gdown_text, 2), squares[4], gdown_in]
        upper_sent = [flat_upper(gup_qkv), squares[1], squares[3], flat_upper(own_text), squares[5]]
        down_sent = jnp.concatenate(down_sent + [all_units(gdown_out)], 1)
        upper_sent = jnp.concatenate(upper_sent + [all_units(gup_in), gup_out], 1)
        sent = jnp.concatenate([down_sent, upper_sent], 0).astype(BF).reshape(2 * rank, fsdp, piece).transpose(1, 0, 2)
        shares = lax.psum(by_adapter(sent).astype(BF), "seq")
        grad_down, grad_up = shares[:, :rank], shares[:, rank:]
        text_total = lax.psum(text_low, "seq").astype(F32)
    return (output[None], input_grad[None], text_total[None], grad_down.astype(F32), grad_up.astype(F32))


def solution(mesh):
    return jax.shard_map(
        partial(body, sizes=(mesh.shape["seq"], mesh.shape["fsdp"])),
        mesh=mesh,
        in_specs=(
            P("fsdp", "seq", None),
            P("fsdp", None, None),
            P("fsdp"),
            P(),
            P(),
            P("fsdp", None),
            P("fsdp", None),
            P("fsdp", None),
            P("fsdp", None),
            P("fsdp", None),
            P("fsdp", None),
            P("fsdp", None),
            P(None, None, "fsdp"),
            P(None, None, "fsdp"),
            P("fsdp", "seq", None),
        ),
        out_specs=(
            P("fsdp", "seq", None),
            P("fsdp", "seq", None),
            P("fsdp", None, None),
            P(None, None, "fsdp"),
            P(None, None, "fsdp"),
        ),
        check_vma=False,
    )
```

```python
from functools import partial

import jax
import jax.numpy as jnp
from jax import lax
from jax.experimental import pallas as pl
from jax.experimental.pallas import tpu as pltpu
from jax.sharding import PartitionSpec as P

HEAD = 64
LANES = 128
QB = 256
BF = jnp.bfloat16
F32 = jnp.float32
SCALE = float(HEAD) ** (-0.5)
SQRT_HALF = 0.7071067811865476
INV_SQRT_2PI = 0.3989422804014327
MIB = 1024 * 1024
VMEM_LIMIT = 60 * MIB
COST = 1.0
FEED_BLOCK = 512


def mm(a, b):
    return lax.dot_general(a, b, (((1,), (0,)), ((), ())), preferred_element_type=F32)


def mm_nt(a, b):
    return lax.dot_general(a, b, (((1,), (1,)), ((), ())), preferred_element_type=F32)


def mm_tn(a, b):
    return lax.dot_general(a, b, (((0,), (0,)), ((), ())), preferred_element_type=F32)


def norm_stats(values):
    centered = values - jnp.mean(values, -1, keepdims=True)
    variance = jnp.mean(centered * centered, -1, keepdims=True)
    inverse = lax.rsqrt(variance + 1e-05)
    return centered * inverse, inverse


def layer_norm(values, gains, biases):
    unit, _ = norm_stats(values)
    return unit * gains + biases


def norm_back(values, gains, gradient):
    unit, inverse = norm_stats(values)
    scaled = gradient * gains
    mean_one = jnp.mean(scaled, -1, keepdims=True)
    mean_two = jnp.mean(scaled * unit, -1, keepdims=True)
    return inverse * (scaled - mean_one - unit * mean_two)


def whole(shape):
    return pl.BlockSpec(shape, lambda *_: (0,) * len(shape))


def once(shape):
    return pl.BlockSpec(shape, lambda *_: (0,) * len(shape), pipeline_mode=pl.Buffered(1))


def params(count=1, limit=None):
    return pltpu.CompilerParams(
        dimension_semantics=("arbitrary",) * count if count else None, vmem_limit_bytes=limit or VMEM_LIMIT
    )


def cost(flops, moved, special=0):
    return pl.CostEstimate(
        flops=int(flops * COST), bytes_accessed=int(moved * COST), transcendentals=int(special * COST)
    )


def window(packed, start, width, rows=None, steps=1, step=0):
    block = width // steps
    rows = packed.shape[0] if rows is None else rows
    if start % block == 0 and block % LANES == 0:
        base = start // block
        return packed, pl.BlockSpec((rows, block), lambda *at: (0, base + (at[step] if steps > 1 else 0)))
    return packed[:, start : start + width], pl.BlockSpec(
        (rows, block), lambda *at: (0, at[step] if steps > 1 else 0)
    )


def norm_kernel(place_ref, *refs):
    count = len(refs) - 5
    parts, (gain_ref, bias_ref, down_ref, normed_ref, lat_ref) = refs[:count], refs[count:]
    step = 128
    for index, part_ref in enumerate(parts):
        base = place_ref[index] * part_ref.shape[0]

        def some(at, carry):
            rows = pl.ds(pl.multiple_of(at * step, step), step)
            into = pl.ds(pl.multiple_of(base + at * step, step), step)
            normed = layer_norm(part_ref[rows, :].astype(F32), gain_ref[...], bias_ref[...]).astype(BF)
            normed_ref[into, :] = normed
            lat_ref[into, :] = mm_nt(normed, down_ref[...]).astype(BF)
            return carry

        lax.fori_loop(0, part_ref.shape[0] // step, some, 0)


def smem():
    return pl.BlockSpec(memory_space=pltpu.SMEM)


def norm_project(places, parts, gains, biases, down):
    model = parts[0].shape[1]
    frames = sum(part.shape[0] for part in parts)
    ranks = down.shape[0]
    return pl.pallas_call(
        norm_kernel,
        in_specs=[smem()] + [whole(item.shape) for item in parts + [gains, biases, down]],
        out_specs=[whole((frames, model)), whole((frames, ranks))],
        out_shape=[jax.ShapeDtypeStruct((frames, model), BF), jax.ShapeDtypeStruct((frames, ranks), BF)],
        grid=(1,),
        compiler_params=params(1),
        cost_estimate=cost(2 * frames * model * ranks, 4 * frames * model),
        name="norm_project",
    )(places, *parts, gains, biases, down)


def qkv_kernel(normed_ref, lat_ref, up_ref, w_ref, out_ref):
    step = 256

    def some(at, carry):
        rows = pl.ds(pl.multiple_of(at * step, step), step)
        out_ref[rows, :] = (mm(normed_ref[rows, :], w_ref[...]) + mm(lat_ref[rows, :], up_ref[...])).astype(BF)
        return carry

    lax.fori_loop(0, normed_ref.shape[0] // step, some, 0)


def qkv_project(normed, latent, up, packed, start, width):
    row_count, model = normed.shape
    ranks = latent.shape[1]
    steps = 3 if (width // 3) % LANES == 0 else 1
    operand, spec = window(packed, start, width, steps=steps)
    block = width // steps
    if steps == 3:
        up_spec = pl.BlockSpec((None, ranks, block), lambda at: (at, 0, 0))
    else:
        up = up.transpose(1, 0, 2).reshape(ranks, width)
        up_spec = whole(up.shape)
    return pl.pallas_call(
        qkv_kernel,
        grid=(steps,),
        in_specs=[whole(normed.shape), whole(latent.shape), up_spec, spec],
        out_specs=pl.BlockSpec((row_count, block), lambda at: (0, at)),
        out_shape=jax.ShapeDtypeStruct((row_count, width), BF),
        compiler_params=params(1, 42 * MIB),
        cost_estimate=cost(2 * row_count * model * width, 2 * (row_count + width) * model),
        name="qkv_project",
    )(normed, latent, up, operand)


def tri_start(at):
    return QB * at * (at + 1) // 2


def attend_kernel(place_ref, q_ref, k_ref, v_ref, out_ref, prob_ref, *refs):
    sent, (val_t_ref, out_t_ref) = refs[:-2], refs[-2:]
    frames = q_ref.shape[0]
    lane = lax.broadcasted_iota(jnp.int32, (1, LANES), 1) // HEAD
    val_t_ref[...] = v_ref[...].T
    square = (QB, QB)
    keep_tri = lax.broadcasted_iota(jnp.int32, square, 0) <= lax.broadcasted_iota(jnp.int32, square, 1)

    def scores(half, at):
        stop = (at + 1) * QB
        query = q_ref[at * QB : stop, :] * jnp.where(lane == half, SCALE, 0.0).astype(BF)
        last = jnp.where(keep_tri, mm_nt(k_ref[stop - QB : stop, :], query), -1e30)
        if at == 0:
            return last
        return jnp.concatenate([mm_nt(k_ref[0 : stop - QB, :], query), last], 0)

    turns = [(half, at) for at in range(frames // QB) for half in range(2)]
    score = scores(*turns[0])
    for index, (half, at) in enumerate(turns):
        stop = (at + 1) * QB
        own = slice(half * HEAD, (half + 1) * HEAD)
        later = scores(*turns[index + 1]) if index + 1 < len(turns) else None
        raised = jnp.exp(score - jnp.max(score, 0, keepdims=True))
        prob = (raised * (1.0 / jnp.sum(raised, 0, keepdims=True))).astype(BF)
        prob_ref[half, tri_start(at) : tri_start(at) + stop, :] = prob
        out_t_ref[own, at * QB : stop] = mm(val_t_ref[own, 0:stop], prob)
        score = later
    out_ref[...] = out_t_ref[...].T.astype(BF)
    for index, sent_ref in enumerate(sent):
        size = sent_ref.shape[0]
        at = place_ref[1] * len(sent) + index
        sent_ref[...] = out_ref[pl.ds(pl.multiple_of(at * size, size), size), :]


def pair_specs(frames, width):
    pairs = width // LANES
    return [pl.BlockSpec((frames, LANES), lambda at, part=part: (0, part * pairs + at)) for part in range(3)]


def attend(places, sizes, triple, width):
    frames = triple.shape[0]
    pairs = width // LANES
    tri = tri_start(frames // QB)
    return pl.pallas_call(
        attend_kernel,
        grid=(pairs,),
        in_specs=[smem()] + pair_specs(frames, width),
        out_specs=[
            pl.BlockSpec((frames, LANES), lambda at: (0, at)),
            pl.BlockSpec((2, tri, QB), lambda at: (at, 0, 0)),
        ]
        + [pl.BlockSpec((size, LANES), lambda at: (0, at)) for size in sizes],
        out_shape=[
            jax.ShapeDtypeStruct((frames, width), BF),
            jax.ShapeDtypeStruct((2 * pairs, tri, QB), BF),
        ]
        + [jax.ShapeDtypeStruct((size, width), BF) for size in sizes],
        scratch_shapes=[pltpu.VMEM((LANES, frames), BF), pltpu.VMEM((LANES, frames), F32)],
        compiler_params=params(1),
        cost_estimate=cost(
            8 * tri * QB * HEAD * pairs, 2 * (4 * frames * width + 2 * pairs * tri * QB), 2 * pairs * tri * QB
        ),
        name="attend",
    )(places, triple, triple, triple)


def attend_back_kernel(place_ref, q_ref, k_ref, v_ref, out_ref, prob_ref, *refs):
    pieces, (back_ref, grad_ref, key_t_ref, dq_t_ref, dk_acc, dv_acc) = refs[:-6], refs[-6:]
    frames = q_ref.shape[0]
    for index, piece_ref in enumerate(pieces):
        size = piece_ref.shape[0]
        count = max(len(pieces) // 2, 1)
        at = place_ref[index // count] * count + index % count if len(pieces) > 1 else 0
        grad_ref[pl.ds(pl.multiple_of(at * size, size), size), :] = piece_ref[...]
    lane = lax.broadcasted_iota(jnp.int32, (1, LANES), 1) // HEAD
    key_t_ref[...] = k_ref[...].T
    dk_acc[...] = jnp.zeros_like(dk_acc)
    dv_acc[...] = jnp.zeros_like(dv_acc)
    turns = [(half, at) for at in range(frames // QB) for half in range(2)]

    def start(half, at):
        rows = slice(at * QB, (at + 1) * QB)
        grad = grad_ref[rows, :] * jnp.where(lane == half, 1.0, 0.0).astype(BF)
        return grad, mm_nt(v_ref[0 : (at + 1) * QB, :], grad)

    ready = start(*turns[0])
    for index, (half, at) in enumerate(turns):
        stop = (at + 1) * QB
        rows = slice(at * QB, stop)
        own = slice(half * HEAD, (half + 1) * HEAD)
        grad, prob_grad = ready
        if half == 0:
            product = (out_ref[rows, :].astype(F32) * grad_ref[rows, :].astype(F32)).T
        if index + 1 < len(turns):
            ready = start(*turns[index + 1])
        query = q_ref[rows, :] * jnp.where(lane == half, SCALE, 0.0).astype(BF)
        delta = jnp.sum(product[own, :], 0, keepdims=True)
        prob = prob_ref[half, tri_start(at) : tri_start(at) + stop, :]
        dv_acc[0:stop, :] += mm(prob, grad)
        score_grad = (prob.astype(F32) * (prob_grad - delta)).astype(BF)
        dk_acc[0:stop, :] += mm(score_grad, query)
        dq_t_ref[own, rows] = mm(key_t_ref[own, 0:stop], score_grad)
    back_ref[0] = (dq_t_ref[...].T * SCALE).astype(BF)
    back_ref[1] = dk_acc[...].astype(BF)
    back_ref[2] = dv_acc[...].astype(BF)


def attend_back(places, triple, attended, pieces, probs, width):
    frames = triple.shape[0]
    pairs = width // LANES
    tri = tri_start(frames // QB)
    column = pl.BlockSpec((frames, LANES), lambda at: (0, at))
    return pl.pallas_call(
        attend_back_kernel,
        grid=(pairs,),
        in_specs=[smem()]
        + pair_specs(frames, width)
        + [column, pl.BlockSpec((2, tri, QB), lambda at: (at, 0, 0))]
        + [pl.BlockSpec((piece.shape[0], LANES), lambda at: (0, at)) for piece in pieces],
        out_specs=pl.BlockSpec((3, frames, LANES), lambda at: (0, 0, at)),
        out_shape=jax.ShapeDtypeStruct((3, frames, width), BF),
        scratch_shapes=[
            pltpu.VMEM((frames, LANES), BF),
            pltpu.VMEM((LANES, frames), BF),
            pltpu.VMEM((LANES, frames), F32),
            pltpu.VMEM((frames, LANES), F32),
            pltpu.VMEM((frames, LANES), F32),
        ],
        compiler_params=params(1, 42 * MIB),
        cost_estimate=cost(16 * tri * QB * HEAD * pairs, 2 * (8 * frames * width + 2 * pairs * tri * QB)),
        name="attend_back",
    )(places, triple, triple, triple, attended, probs, *pieces)


def feed_kernel(count, based, *refs):
    pieces, refs = refs[:count], refs[count:]
    bases, refs = refs[:based], refs[based:]
    cot_ref, down_in_ref, up_in_ref, down_out_ref, up_out_ref, w_in_ref, w_out_ref = refs[:7]
    out_refs, gu_refs, refs = refs[7 : 7 + count], refs[7 + count : 7 + 2 * count], refs[7 + 2 * count :]
    (
        gdown_in_ref, gup_in_ref, gdown_out_ref, gup_out_ref, normed_ref,
        out_acc, gu_acc, lat_in, glat_out, lat_acc, glat_acc, lat_t, glat_t,
    ) = refs
    at = pl.program_id(0)

    @pl.when(at == 0)
    def _():
        start = 0
        for piece_ref in pieces:
            normed_ref[start : start + piece_ref.shape[0], :] = piece_ref[...]
            start += piece_ref.shape[0]
        latent = mm_nt(normed_ref[...], down_in_ref[...]).astype(BF)
        glat = mm_nt(cot_ref[...], up_out_ref[...]).astype(BF)
        lat_in[...] = latent
        glat_out[...] = glat
        lat_t[...] = latent.astype(F32).T.astype(BF)
        glat_t[...] = glat.astype(F32).T.astype(BF)
        start = 0
        for base_ref in bases:
            out_acc[start : start + base_ref.shape[0], :] = base_ref[...]
            start += base_ref.shape[0]
        if not bases:
            out_acc[...] = jnp.zeros_like(out_acc)
        gu_acc[...] = jnp.zeros_like(gu_acc)
        lat_acc[...] = jnp.zeros_like(lat_acc)
        glat_acc[...] = jnp.zeros_like(glat_acc)

    w_in = w_in_ref[...]
    w_out = w_out_ref[...]
    pre = mm(normed_ref[...], w_in) + mm(lat_in[...], up_in_ref[...])
    act_grad = mm_nt(cot_ref[...], w_out) + mm(glat_out[...], down_out_ref[...])
    cdf = 0.5 * (1.0 + lax.erf(pre * SQRT_HALF))
    slope = cdf + pre * (jnp.exp(-0.5 * pre * pre) * INV_SQRT_2PI)
    act = (pre * cdf).astype(BF)
    pre_grad = (act_grad * slope).astype(BF)
    out_acc[...] += mm(act, w_out)
    gu_acc[...] += mm_nt(pre_grad, w_in)
    lat_acc[...] += mm_nt(act, down_out_ref[...])
    glat_acc[...] += mm_nt(pre_grad, up_in_ref[...])
    gup_in_ref[...] = mm(lat_t[...], pre_grad)
    gdown_out_ref[...] = mm(glat_t[...], act)

    @pl.when(at == pl.num_programs(0) - 1)
    def _():
        latent = lat_acc[...].astype(BF)
        glat = glat_acc[...].astype(BF)
        start = 0
        for out_ref, gu_ref in zip(out_refs, gu_refs):
            rows = slice(start, start + out_ref.shape[0])
            out_ref[...] = (out_acc[rows, :] + mm(latent[rows], up_out_ref[...])).astype(out_ref.dtype)
            gu_ref[...] = (gu_acc[rows, :] + mm(glat[rows], down_in_ref[...])).astype(gu_ref.dtype)
            start += out_ref.shape[0]
        gup_out_ref[...] = mm(latent.astype(F32).T.astype(BF), cot_ref[...])
        gdown_in_ref[...] = mm(glat.astype(F32).T.astype(BF), normed_ref[...])


def feed_forward(pieces, bases, cotangent, block_at, down_in, up_in, down_out, up_out, weights, hidden, kind):
    model = cotangent.shape[1]
    row_count = sum(item.shape[0] for item in pieces)
    rank = down_in.shape[0]
    block = FEED_BLOCK if hidden % FEED_BLOCK == 0 else hidden
    w_in, in_spec, w_out, out_spec = weights(block)
    main = pl.BlockSpec((row_count, model), lambda at: (block_at, 0))
    slim = pl.BlockSpec((rank, block), lambda at: (0, at))
    small = whole((rank, model))
    return pl.pallas_call(
        partial(feed_kernel, len(pieces), len(bases)),
        grid=(hidden // block,),
        in_specs=[once(item.shape) for item in pieces + bases]
        + [main, small, slim, slim, small, in_spec, out_spec],
        out_specs=[whole(item.shape) for item in pieces] * 2 + [small, slim, slim, small],
        out_shape=[jax.ShapeDtypeStruct(item.shape, kind) for item in pieces]
        + [jax.ShapeDtypeStruct(item.shape, BF) for item in pieces]
        + [
            jax.ShapeDtypeStruct((rank, model), F32),
            jax.ShapeDtypeStruct((rank, hidden), F32),
            jax.ShapeDtypeStruct((rank, hidden), F32),
            jax.ShapeDtypeStruct((rank, model), F32),
        ],
        scratch_shapes=[pltpu.VMEM((row_count, model), BF)]
        + [pltpu.VMEM((row_count, model), F32)] * 2
        + [pltpu.VMEM((row_count, rank), BF)] * 2
        + [pltpu.VMEM((row_count, rank), F32)] * 2
        + [pltpu.VMEM((rank, row_count), BF)] * 2,
        compiler_params=params(1),
        cost_estimate=cost(8 * row_count * model * hidden, 4 * hidden * model, 2 * row_count * hidden),
        name="feed_forward",
    )(*pieces, *bases, cotangent, down_in, up_in, down_out, up_out, w_in, w_out)


def spread_heads(rows_ref, into_ref, model):
    keys = rows_ref.shape[0]
    wide = 4 * HEAD
    row = lax.broadcasted_iota(jnp.int32, (4 * keys, wide), 0) // keys
    col = lax.broadcasted_iota(jnp.int32, (4 * keys, wide), 1) // HEAD
    mask = jnp.where(row == col, 1.0, 0.0).astype(BF)

    def some(group, carry):
        part = rows_ref[:, pl.ds(pl.multiple_of(group * wide, wide), wide)]
        into = pl.ds(pl.multiple_of(group * 4 * keys, 4 * keys), 4 * keys)
        into_ref[into, :] = jnp.concatenate([part] * 4, 0) * mask
        return carry

    lax.fori_loop(0, model // wide, some, 0)


def head_total(values, keys, reduce):
    split = values.reshape(4, keys, values.shape[1])
    return jnp.broadcast_to(reduce(split, 1, keepdims=True), split.shape).reshape(values.shape)


def each(count, step, work):
    def some(at, carry):
        work(pl.ds(pl.multiple_of(at * step, step), step))
        return carry

    lax.fori_loop(0, count // step, some, 0)


def pair_of(both, size):
    return [pl.ds(pl.multiple_of(both.start + at * size, size), size) for at in range(both.size // size)]


def weight_copies(plan, place_ref, sources, hold_ref, sem_ref):
    model = hold_ref.shape[1]
    groups = []
    for index, (start, extra) in enumerate(plan):
        if extra is None:
            parts = [slice(at * model // 2, (at + 1) * model // 2) for at in range(2)]
            pairs = [(sources[0].at[rows, pl.ds(start, model)], hold_ref.at[index, rows, :]) for rows in parts]
        else:
            half = model // 2
            here, there = [pl.ds(pl.multiple_of(place_ref[at] * half, half), half) for at in range(2)]
            pairs = [(sources[0].at[:, pl.ds(start, half)], hold_ref.at[index, :, here])]
            for at in range(2):
                rows = pl.ds(pl.multiple_of(place_ref[2 + at] * half, half), half)
                pairs.append((sources[extra + at], hold_ref.at[index, rows, there]))
        groups.append(
            [pltpu.make_async_copy(src, dst, sem_ref.at[index, at]) for at, (src, dst) in enumerate(pairs)]
        )
    return groups


def source_count(plan):
    return 1 + 2 * sum(extra is not None for _, extra in plan)


def start_all(copies):
    for copy in copies:
        copy.start()


def wait_all(copies):
    for copy in copies:
        copy.wait()


def middle_kernel(plan, place_ref, *refs):
    sources, refs = refs[: source_count(plan)], refs[source_count(plan) :]
    inputs_ref, adapt_ref, gain_ref, bias_ref, keys_ref, values_ref = refs[:6]
    pieces = refs[6:-20]
    away = refs[-20:-14]
    resid2_ref, normed3_ref, lat_ref, hold_ref, key_wide, value_wide, sem_ref = refs[-14:-7]
    kept, out_sem = refs[-7:-1], refs[-1]
    attended_ref, resid1_ref, normed2_ref, query_ref, probs_ref, crossed_ref = kept
    leaving = [pltpu.make_async_copy(kept[at], away[at], out_sem.at[at]) for at in range(6)]
    model = inputs_ref.shape[1]
    keys = keys_ref.shape[0]
    rows = inputs_ref.shape[0]
    wide = 4 * HEAD
    copies = weight_copies(plan, place_ref, sources, hold_ref, sem_ref)
    start_all(copies[0])
    for index, piece_ref in enumerate(pieces):
        size = piece_ref.shape[1]
        attended_ref[:, pl.ds(pl.multiple_of(place_ref[index] * size, size), size)] = piece_ref[...]
    spread_heads(keys_ref, key_wide, model)
    spread_heads(values_ref, value_wide, model)

    def adapted(moving_ref, index, store):
        latent = mm_nt(moving_ref[...], adapt_ref[32 * index : 32 * index + 16, :]).astype(BF)
        lat_ref[:, 16 * index : 16 * index + 16] = latent
        wait_all(copies[index])
        if index < 2:
            start_all(copies[index + 1])

        def some(cols):
            store(
                cols,
                mm(moving_ref[...], hold_ref[index, :, cols])
                + mm(latent, adapt_ref[32 * index + 16 : 32 * index + 32, cols]),
            )

        each(model, 512, some)

    def add_first(cols, value):
        resid1_ref[:, cols] = inputs_ref[:, cols].astype(F32) + value

    def add_second(cols, value):
        resid2_ref[:, cols] = resid1_ref[:, cols] + value

    def keep_query(cols, value):
        query_ref[:, cols] = value.astype(BF)

    def normed(values_at, into_ref, which):
        def some(part):
            into_ref[part, :] = layer_norm(
                values_at[part, :], gain_ref[which : which + 1, :], bias_ref[which : which + 1, :]
            ).astype(BF)

        each(rows, 128, some)

    def cross(both):
        groups = pair_of(both, wide)
        scores = [mm_nt(key_wide[lanes, :], query_ref[:, lanes]) * SCALE for lanes in groups]
        for lanes, score in zip(groups, scores):
            raised = jnp.exp(score - head_total(score, keys, jnp.max))
            prob = (raised / head_total(raised, keys, jnp.sum)).astype(BF)
            probs_ref[lanes, :] = prob
            crossed_ref[:, lanes] = mm_tn(prob, value_wide[lanes, :]).astype(BF)

    leaving[0].start()
    adapted(attended_ref, 0, add_first)
    leaving[1].start()
    normed(resid1_ref, normed2_ref, 1)
    leaving[2].start()
    adapted(normed2_ref, 1, keep_query)
    leaving[3].start()
    each(model, 3 * wide, cross)
    leaving[4].start()
    leaving[5].start()
    adapted(crossed_ref, 2, add_second)
    normed(resid2_ref, normed3_ref, 2)
    wait_all(leaving)


def middle(places, own, own_spec, others, inputs, at, blocks, sources, plan, adapters, gains, biases, keys, values):
    rows, model = own_spec[0], inputs.shape[1]
    spread = model // HEAD * keys.shape[0]
    shape = lambda kind, dims=(rows, model): jax.ShapeDtypeStruct(dims, kind)
    flat = lambda dims: pl.BlockSpec(dims, lambda _, ref: (0,) * len(dims))
    shapes = [shape(kind) for kind in (BF, F32, BF, BF)]
    shapes += [shape(BF, (spread, rows)), shape(BF), shape(F32), shape(BF), shape(BF, (rows, 48))]
    return pl.pallas_call(
        partial(middle_kernel, plan),
        grid_spec=pltpu.PrefetchScalarGridSpec(
            num_scalar_prefetch=1,
            grid=(1,),
            in_specs=[pl.BlockSpec(memory_space=pl.ANY)] * len(sources)
            + [pl.BlockSpec((rows, model), lambda _, ref: (at, 0))]
            + [flat(item.shape) for item in (adapters, gains, biases, keys, values)]
            + [pl.BlockSpec(own_spec, lambda _, ref: (ref[0] * blocks + at, 0) if others else (at, 0))]
            + [flat(item.shape) for item in others],
            out_specs=[pl.BlockSpec(memory_space=pl.ANY)] * 6 + [flat(item.shape) for item in shapes[6:]],
            scratch_shapes=[
                pltpu.VMEM((3, model, model), BF),
                pltpu.VMEM((spread, 4 * HEAD), BF),
                pltpu.VMEM((spread, 4 * HEAD), BF),
                pltpu.SemaphoreType.DMA((3, 3)),
            ]
            + [pltpu.VMEM(item.shape, item.dtype) for item in shapes[:6]]
            + [pltpu.SemaphoreType.DMA((6,))],
        ),
        out_shape=shapes,
        compiler_params=params(),
        cost_estimate=cost(6 * rows * model * model, 6 * model * model + 24 * rows * model),
        name="middle",
    )(places, *sources, inputs, adapters, gains, biases, keys, values, own, *others)


def middle_back_kernel(plan, split, place_ref, *refs):
    sources, refs = refs[: source_count(plan)], refs[source_count(plan) :]
    cot_ref, gu_ref, more_ref = refs[:3]
    far = refs[3:9]
    resid2_ref, lat_ref, adapt_ref, gain_ref, keys_ref, values_ref = refs[9:15]
    kept, in_sem = refs[-7:-1], refs[-1]
    attended_ref, resid1_ref, normed2_ref, query_ref, probs_ref, crossed_ref = kept
    coming = [pltpu.make_async_copy(far[at], kept[at], in_sem.at[at]) for at in range(6)]
    refs = refs[15:-7]
    outs = refs[: 2 if split else 1]
    resid1_grad_ref, memory_ref, small_ref, hold_ref, key_wide, value_wide, work_ref, low_ref, sem_ref = refs[len(outs) :]
    rows, model = cot_ref.shape
    keys = keys_ref.shape[0]
    wide = 4 * HEAD
    copies = weight_copies(plan, place_ref, sources, hold_ref, sem_ref)
    start_all(copies[2])
    coming[5].start()
    spread_heads(keys_ref, key_wide, model)
    spread_heads(values_ref, value_wide, model)

    def first(part):
        gradient = gu_ref[part, :].astype(F32) + more_ref[part, :].astype(F32)
        value = cot_ref[part, :].astype(F32) + norm_back(resid2_ref[part, :], gain_ref[2:3, :], gradient)
        resid1_grad_ref[part, :] = value
        low_ref[part, :] = value.astype(BF)

    def second(part):
        value = resid1_grad_ref[part, :] + norm_back(resid1_ref[part, :], gain_ref[1:2, :], work_ref[part, :])
        resid1_grad_ref[part, :] = value
        low_ref[part, :] = value.astype(BF)

    def back(moving_ref, index, store):
        down = slice(32 * index, 32 * index + 16)
        upper = slice(32 * index + 16, 32 * index + 32)
        glat = mm_nt(low_ref[...], adapt_ref[upper, :]).astype(BF)
        glat_t = glat.astype(F32).T.astype(BF)
        lat_t = lat_ref[:, 16 * index : 16 * index + 16].astype(F32).T.astype(BF)
        wait_all(copies[index])
        if index == 2:
            wait_all(coming[5:])
            start_all(coming[2:5])
        if index == 1:
            wait_all(coming[2:3])
            start_all(coming[:2])
        if index == 0:
            wait_all(coming[:1])
        if index:
            start_all(copies[index - 1])

        def some(cols):
            small_ref[down, cols] = mm(glat_t, moving_ref[:, cols])
            small_ref[upper, cols] = mm(lat_t, low_ref[:, cols])
            store(cols, mm_nt(low_ref[...], hold_ref[index, cols, :]) + mm(glat, adapt_ref[down, cols]))

        each(model, 512, some)

    def keep(cols, value):
        work_ref[:, cols] = value

    def cross(both):
        groups = pair_of(both, wide)
        parts = [work_ref[:, lanes].astype(BF) for lanes in groups]
        prob_grads = [mm_nt(value_wide[lanes, :], part) for lanes, part in zip(groups, parts)]
        for lanes, part, prob_grad in zip(groups, parts, prob_grads):
            cross_one(lanes, part, prob_grad)

    def cross_one(lanes, part, prob_grad):
        prob = probs_ref[lanes, :]
        wide_prob = prob.astype(F32)
        weighted = wide_prob * prob_grad
        score_grad = (weighted - wide_prob * head_total(weighted, keys, jnp.sum)).astype(BF)
        low_ref[:, lanes] = (mm_tn(score_grad, key_wide[lanes, :]) * SCALE).astype(BF)
        key_full = mm(score_grad, query_ref[:, lanes])
        value_full = mm(prob, part)
        col = lax.broadcasted_iota(jnp.int32, (keys, wide), 1) // HEAD
        key_sum, value_sum = key_full[:keys], value_full[:keys]
        for head in range(1, 4):
            rows_at = slice(head * keys, (head + 1) * keys)
            key_sum = jnp.where(col == head, key_full[rows_at], key_sum)
            value_sum = jnp.where(col == head, value_full[rows_at], value_sum)
        memory_ref[0, :, lanes] = key_sum * SCALE
        memory_ref[1, :, lanes] = value_sum

    each(rows, 128, first)
    back(crossed_ref, 2, keep)
    wait_all(coming[3:5])
    each(model, 3 * wide, cross)
    back(normed2_ref, 1, keep)
    wait_all(coming[1:2])
    each(rows, 128, second)
    back(attended_ref, 0, keep)
    if split:
        size = outs[0].shape[1]
        for out_ref, index in zip(outs, range(2)):
            out_ref[...] = work_ref[:, pl.ds(pl.multiple_of(place_ref[index] * size, size), size)].astype(BF)
    else:
        outs[0][...] = work_ref[...].astype(BF)


def middle_back(places, parts, at, cotangent, gu, more, kept, sources, plan, adapters, gains, keys, values):
    model = cotangent.shape[1]
    rows = kept[0].shape[0]
    spread = model // HEAD * keys.shape[0]
    flat = lambda dims: pl.BlockSpec(dims, lambda _, ref: (0,) * len(dims))
    block = pl.BlockSpec((rows, model), lambda _, ref: (at, 0))
    shapes = [jax.ShapeDtypeStruct((rows, model // parts), BF)] * parts + [
        jax.ShapeDtypeStruct((rows, model), F32),
        jax.ShapeDtypeStruct((2,) + keys.shape, F32),
        jax.ShapeDtypeStruct(adapters.shape, F32),
    ]
    return pl.pallas_call(
        partial(middle_back_kernel, plan, parts == 2),
        grid_spec=pltpu.PrefetchScalarGridSpec(
            num_scalar_prefetch=1,
            grid=(1,),
            in_specs=[pl.BlockSpec(memory_space=pl.ANY)] * len(sources)
            + [block, flat(gu.shape), flat(more.shape)]
            + [pl.BlockSpec(memory_space=pl.ANY)] * 6
            + [flat(item.shape) for item in kept[6:]]
            + [flat(item.shape) for item in (adapters, gains, keys, values)],
            out_specs=[flat(item.shape) for item in shapes],
            scratch_shapes=[
                pltpu.VMEM((3, model, model), BF),
                pltpu.VMEM((spread, 4 * HEAD), BF),
                pltpu.VMEM((spread, 4 * HEAD), BF),
                pltpu.VMEM((rows, model), F32),
                pltpu.VMEM((rows, model), BF),
                pltpu.SemaphoreType.DMA((3, 3)),
            ]
            + [pltpu.VMEM(item.shape, item.dtype) for item in kept[:6]]
            + [pltpu.SemaphoreType.DMA((6,))],
        ),
        out_shape=shapes,
        compiler_params=params(),
        cost_estimate=cost(6 * rows * model * model, 6 * model * model + 36 * rows * model),
        name="middle_back",
    )(places, *sources, cotangent, gu, more, *kept, adapters, gains, keys, values)


def qkv_grads_kernel(
    place_ref, grad_ref, normed_ref, lat_ref, up_ref, glat_ref, mine_ref, theirs_ref, glat_acc, gup_acc, down_acc,
    down_all, upper_all,
):
    at = pl.program_id(0)
    gradient = grad_ref[...]
    rank = mine_ref.shape[0]
    model = normed_ref.shape[1]
    width = gradient.shape[1]
    gup_acc[...] = mm_tn(lat_ref[...], gradient)

    @pl.when(at == 0)
    def _():
        glat_acc[...] = jnp.zeros_like(glat_acc)
        upper_all[...] = jnp.zeros_like(upper_all)

    into = pl.ds(pl.multiple_of(at * model + place_ref[0] * width, LANES), width)
    upper_all[:, into] = gup_acc[pl.ds(pl.multiple_of(at * rank, rank), rank), :].astype(BF)
    glat_acc[...] += mm_nt(gradient, up_ref[...])

    @pl.when(at == pl.num_programs(0) - 1)
    def _():
        low = glat_acc[...].astype(BF)
        glat_ref[...] = low
        down_acc[...] = mm_tn(low, normed_ref[...])
        for part in range(3):
            down_all[:, part * model : (part + 1) * model] = down_acc[part * rank : (part + 1) * rank, :].astype(BF)
        share(place_ref, down_all, upper_all, mine_ref, theirs_ref)


def share(place_ref, down_all, upper_all, mine_ref, theirs_ref):
    @pl.when(place_ref[0] == 0)
    def _():
        mine_ref[...] = down_all[...]
        theirs_ref[...] = upper_all[...]

    @pl.when(place_ref[0] != 0)
    def _():
        mine_ref[...] = upper_all[...]
        theirs_ref[...] = down_all[...]


def qkv_grads(places, gradient, normed, latent, up):
    frames, model = normed.shape
    parts, ranks, width = up.shape
    rank = ranks // parts
    table = jax.ShapeDtypeStruct((rank, parts * model), BF)
    return pl.pallas_call(
        qkv_grads_kernel,
        grid=(parts,),
        in_specs=[
            smem(),
            pl.BlockSpec((None, frames, width), lambda at: (at, 0, 0)),
            whole(normed.shape),
            whole(latent.shape),
            pl.BlockSpec((None, ranks, width), lambda at: (at, 0, 0)),
        ],
        out_specs=[whole(latent.shape), whole(table.shape), whole(table.shape)],
        out_shape=[jax.ShapeDtypeStruct(latent.shape, BF), table, table],
        scratch_shapes=[
            pltpu.VMEM(latent.shape, F32),
            pltpu.VMEM((ranks, width), F32),
            pltpu.VMEM((ranks, model), F32),
            pltpu.VMEM(table.shape, BF),
            pltpu.VMEM(table.shape, BF),
        ],
        compiler_params=params(1, 42 * MIB),
        cost_estimate=cost(8 * frames * ranks * width * parts, 2 * frames * (model + parts * width)),
        name="qkv_grads",
    )(places, gradient, normed, latent, up)


def qkv_back_kernel(place_ref, grad_ref, glat_ref, down_ref, w_ref, gu_ref, gu_acc):
    at = pl.program_id(0)
    model = gu_ref.shape[1]
    last = pl.num_programs(0) - 1

    def some(cols):
        direct = mm_nt(grad_ref[...], w_ref[cols, :])

        @pl.when(at == 0)
        def _():
            gu_acc[:, cols] = direct + mm(glat_ref[...], down_ref[:, cols])

        @pl.when(jnp.logical_and(at > 0, at < last))
        def _():
            gu_acc[:, cols] += direct

        @pl.when(at == last)
        def _():
            gu_ref[:, cols] = (gu_acc[:, cols] + direct).astype(gu_ref.dtype)

    each(model, 512, some)


def qkv_back(place, row_count, gradient, glat, down, packed, start, kind):
    ranks, model = down.shape
    width = gradient.shape[2]
    if start % width == 0 and width % LANES == 0:
        weight, spec = packed, pl.BlockSpec((model, width), lambda at, ref: (0, start // width + at))
    else:
        weight = packed[:, start : start + 3 * width].reshape(model, 3, width).transpose(1, 0, 2)
        spec = pl.BlockSpec((None, model, width), lambda at, ref: (at, 0, 0))
    return pl.pallas_call(
        qkv_back_kernel,
        grid_spec=pltpu.PrefetchScalarGridSpec(
            num_scalar_prefetch=1,
            grid=(3,),
            in_specs=[
                pl.BlockSpec((None, row_count, width), lambda at, ref: (at, ref[0], 0)),
                pl.BlockSpec((row_count, ranks), lambda at, ref: (ref[0], 0)),
                pl.BlockSpec(down.shape, lambda at, ref: (0, 0)),
                spec,
            ],
            out_specs=pl.BlockSpec((row_count, model), lambda at, ref: (0, 0)),
            scratch_shapes=[pltpu.VMEM((row_count, model), F32)],
        ),
        out_shape=jax.ShapeDtypeStruct((row_count, model), kind),
        compiler_params=params(1, 42 * MIB),
        cost_estimate=cost(6 * row_count * model * width, 6 * model * width + 8 * row_count * model),
        name="qkv_back",
    )(place, gradient, glat, down, weight)


def last_norm_kernel(blocks, frames_ref, gradient_ref, gain_ref, *refs):
    pieces, grad_ref = refs[:-1], refs[-1]
    at = pl.program_id(0)
    back = norm_back(frames_ref[...].astype(F32), gain_ref[...], gradient_ref[...])
    for index, piece_ref in enumerate(pieces):

        @pl.when(at // blocks == index)
        def _(piece_ref=piece_ref):
            grad_ref[...] = back + piece_ref[...]


def last_norm(frames, gradient, gains, pieces):
    rows, model = frames.shape
    step = min(128, rows)
    blocks = pieces[0].shape[0] // step
    block = pl.BlockSpec((step, model), lambda at: (at, 0))

    def piece_spec(index):
        return pl.BlockSpec((step, model), lambda at: (jnp.clip(at - index * blocks, 0, blocks - 1), 0))

    return pl.pallas_call(
        partial(last_norm_kernel, blocks),
        grid=(rows // step,),
        in_specs=[block, block, whole(gains.shape)] + [piece_spec(index) for index in range(len(pieces))],
        out_specs=block,
        out_shape=jax.ShapeDtypeStruct((rows, model), F32),
        compiler_params=params(1, 42 * MIB),
        cost_estimate=cost(20 * rows * model, 16 * rows * model),
        name="last_norm",
    )(frames, gradient, gains, *pieces)


def run_length(size):
    count = 1
    while count * size % LANES:
        count *= 2
    return count


def join_kernel(pieces_ref, flat_ref):
    count, _, size = pieces_ref.shape
    run = run_length(size)

    def some(at, carry):
        parts = [pieces_ref[at * run + index] for index in range(run)]
        into = pl.ds(pl.multiple_of(at * run * size, LANES), run * size)
        flat_ref[:, into] = jnp.concatenate(parts, 1)
        return carry

    lax.fori_loop(0, count // run, some, 0)


def join_pieces(pieces):
    count, rows, size = pieces.shape
    if count % run_length(size):
        return pieces.transpose(1, 0, 2).reshape(rows, count * size)
    return pl.pallas_call(
        join_kernel,
        out_shape=jax.ShapeDtypeStruct((rows, count * size), pieces.dtype),
        compiler_params=params(0),
        name="join_pieces",
    )(pieces)


def split_kernel(*refs):
    sources, pieces_ref, flat_ref = refs[:-2], refs[-2], refs[-1]
    count, _, size = pieces_ref.shape
    run = run_length(size)
    start = 0
    for first_ref, second_ref in zip(sources[::2], sources[1::2]):
        width = first_ref.shape[1]
        both = first_ref[...].astype(F32) + second_ref[...].astype(F32)
        flat_ref[:, start : start + width] = both.astype(BF)
        start += width

    def some(at, carry):
        block = flat_ref[:, pl.ds(pl.multiple_of(at * run * size, LANES), run * size)]
        for index in range(run):
            pieces_ref[at * run + index] = block[:, index * size : (index + 1) * size]
        return carry

    lax.fori_loop(0, count // run, some, 0)


def split_sums(pairs, count):
    rows = pairs[0].shape[0]
    total = sum(item.shape[1] for item in pairs[::2])
    return pl.pallas_call(
        split_kernel,
        out_shape=jax.ShapeDtypeStruct((count, rows, total // count), BF),
        scratch_shapes=[pltpu.VMEM((rows, total), BF)],
        compiler_params=params(0, 42 * MIB),
        name="split_sums",
    )(*pairs)


def unit_loop(plan, work):
    fsdp, seq, folds, local = plan
    run = run_length(local)

    def some(at, carry):
        span = run * seq * folds * local
        block = pl.ds(pl.multiple_of(at * span, LANES), span)
        folded = [
            pl.ds(pl.multiple_of(fold * fsdp * local + at * run * local, LANES), run * local) for fold in range(folds)
        ]
        work(run, block, folded)
        return carry

    lax.fori_loop(0, fsdp // run, some, 0)


def take_units_kernel(plan, place_ref, all_ref, *refs):
    own_ref = refs[-1]
    _, seq, folds, local = plan
    spot = place_ref[0]

    def work(run, block, folded):
        values = all_ref[:, block]
        for fold, into in enumerate(folded):
            parts = []
            for index in range(run):
                base = (index * seq * folds + fold) * local
                part = values[:, base : base + local]
                for other in range(1, seq):
                    shift = base + other * folds * local
                    part = jnp.where(spot == other, values[:, shift : shift + local], part)
                parts.append(part)
            own_ref[:, into] = jnp.concatenate(parts, 1)

    unit_loop(plan, work)
    if len(refs) == 2:
        model = refs[0].shape[1]
        hidden = own_ref.shape[1] - folds * model
        for fold in range(folds):
            rows = pl.ds(pl.multiple_of((spot * folds + fold) * local, 16), local)
            own_ref[:, hidden + fold * model : hidden + (fold + 1) * model] = refs[0][rows, :]


def take_units(plan, places, matrix, low=None):
    _, seq, folds, local = plan
    rows, width = matrix.shape
    extra = [] if low is None else [low]
    out_width = width // seq + sum(folds * item.shape[1] for item in extra)
    return pl.pallas_call(
        partial(take_units_kernel, plan),
        in_specs=[smem()] + [pl.BlockSpec(memory_space=pltpu.VMEM)] * (1 + len(extra)),
        out_shape=jax.ShapeDtypeStruct((rows, out_width), matrix.dtype),
        compiler_params=params(0),
        name="take_units",
    )(places, matrix, *extra)


def collect_kernel(plan, blocks, start_at, place_ref, *refs):
    parts, squares, refs = refs[:blocks], refs[blocks : 2 * blocks], refs[2 * blocks :]
    feeds = [refs[at : at + 4] for at in range(0, len(refs) - 14, 4)]
    (
        other_ref, lat_ref, flat_ref, down_text_ref, text_ref, w_ref,
        mine_ref, theirs_ref, text_grad_ref, down_all, upper_all, unit_acc, hold_ref, sem_ref,
    ) = refs[-14:]
    _, seq, folds, local = plan
    rank = mine_ref.shape[0]
    model = text_ref.shape[1]
    wide = other_ref.shape[2]
    spot = place_ref[0]
    own = pl.ds(pl.multiple_of(spot * wide, wide), wide)
    copy = pltpu.make_async_copy(w_ref.at[:, pl.ds(start_at, hold_ref.shape[1])], hold_ref, sem_ref)
    copy.start()

    def total(items, rows):
        value = items[0][rows, :]
        for item in items[1:]:
            value = value + item[rows, :]
        return value

    moved = []
    for part in range(2):
        value = parts[0][part, :, own]
        for item in parts[1:]:
            value = value + item[part, :, own]
        moved.append((value + other_ref[part].astype(F32)).astype(BF))
    moved = jnp.concatenate(moved, 1)
    glat = mm_nt(moved, flat_ref[...]).astype(BF)
    gup = mm_tn(lat_ref[...], moved)
    gdown = mm_tn(glat, text_ref[...])

    upper_all[:, 2 * model : 4 * model] = jnp.zeros((rank, 2 * model), BF)
    for part in range(2):
        rows = slice(part * rank, (part + 1) * rank)
        down_all[:, (2 + part) * model : (3 + part) * model] = gdown[rows].astype(BF)
        into = pl.ds(pl.multiple_of((2 + part) * model + spot * wide, LANES), wide)
        upper_all[:, into] = gup[rows, part * wide : (part + 1) * wide].astype(BF)
    for index, at in enumerate((0, 1, 4)):
        cols = slice(at * model, (at + 1) * model)
        down_all[:, cols] = total(squares, slice(2 * index * rank, (2 * index + 1) * rank)).astype(BF)
        upper_all[:, cols] = total(squares, slice((2 * index + 1) * rank, (2 * index + 2) * rank)).astype(BF)
    every = slice(0, rank)
    down_all[:, 5 * model : 6 * model] = total([item[0] for item in feeds], every).astype(BF)
    upper_all[:, upper_all.shape[1] - model :] = total([item[3] for item in feeds], every).astype(BF)
    for into_ref, start, which in ((upper_all, 5 * model, 1), (down_all, 6 * model, 2)):
        unit_acc[...] = total([item[which] for item in feeds], every)

        def work(run, block, folded):
            values = [unit_acc[:, cols] for cols in folded]
            spread = []
            for index in range(run):
                for other in range(seq):
                    for fold in range(folds):
                        part = values[fold][:, index * local : (index + 1) * local]
                        spread.append(jnp.where(spot == other, part, 0.0))
            at = pl.ds(pl.multiple_of(start + block.start, LANES), block.size)
            into_ref[:, at] = jnp.concatenate(spread, 1).astype(BF)

        unit_loop(plan, work)
    share(place_ref, down_all, upper_all, mine_ref, theirs_ref)
    copy.wait()
    text_grad_ref[...] = (mm_nt(moved, hold_ref[...]) + mm(glat, down_text_ref[...])).astype(BF)


def collect(plan, places, parts, squares, feeds, other, lat_text, flat_text, down_text, text, packed, start):
    rank = squares[0].shape[0] // 6
    model = text.shape[1]
    hidden = feeds[0][1].shape[1]
    wide2 = flat_text.shape[1]
    width = 6 * model + hidden * plan[1]
    feeds = [item for feed in feeds for item in feed]
    before = list(parts) + list(squares) + feeds + [other, lat_text, flat_text, down_text, text]
    table = jax.ShapeDtypeStruct((rank, width), BF)
    shapes = [table, table, jax.ShapeDtypeStruct(text.shape, BF)]
    return pl.pallas_call(
        partial(collect_kernel, plan, len(parts), start),
        grid=(1,),
        in_specs=[smem()] + [whole(item.shape) for item in before] + [pl.BlockSpec(memory_space=pl.ANY)],
        out_specs=[whole(item.shape) for item in shapes],
        out_shape=shapes,
        scratch_shapes=[pltpu.VMEM(table.shape, BF)] * 2
        + [pltpu.VMEM((rank, hidden), F32), pltpu.VMEM((model, wide2), BF), pltpu.SemaphoreType.DMA],
        compiler_params=params(1),
        cost_estimate=cost(4 * text.shape[0] * model * wide2, 2 * model * wide2),
        name="collect",
    )(places, *before, packed)


def both_kernel(place_ref, mine_ref, other_ref, down_ref, upper_ref):
    first = place_ref[0] == 0
    for at in range(mine_ref.shape[0]):
        mine, other = mine_ref[at].astype(F32), other_ref[at].astype(F32)
        down_ref[at] = jnp.where(first, mine, other)
        upper_ref[at] = jnp.where(first, other, mine)


def both_tables(places, mine, other):
    return pl.pallas_call(
        both_kernel,
        in_specs=[smem()] + [pl.BlockSpec(memory_space=pltpu.VMEM)] * 2,
        out_shape=[jax.ShapeDtypeStruct(mine.shape, F32)] * 2,
        compiler_params=params(0, 42 * MIB),
        name="both_tables",
    )(places, mine, other)


def body(
    inputs,
    text_states,
    adapter_index,
    norm_gains,
    norm_biases,
    self_in,
    self_out,
    cross_query,
    cross_text,
    cross_out,
    hidden_in,
    hidden_out,
    adapter_down,
    adapter_up,
    cotangent,
    *,
    sizes,
):
    seq, fsdp = sizes
    spot = lax.axis_index("seq")
    first_here = spot == 0
    there = (seq - 1) - spot
    local = self_in.shape[0]
    depth = hidden_out.shape[0] // seq
    pair = seq == 2 and depth % local == 0 and fsdp % run_length(local) == 0
    model = inputs.shape[2]
    rows = inputs.shape[1]
    frames = rows * seq
    wide = model // seq
    hidden_all = hidden_in.shape[1]
    hidden = hidden_all // seq
    adapters, rank, piece = adapter_down.shape
    total = piece * fsdp

    blocks = max(rows // 256, 1)
    size = rows // blocks

    def swap(value):
        return lax.ppermute(value, "seq", [(0, 1), (1, 0)])

    def pick(value, axis, extent, which=None):
        return lax.dynamic_slice_in_dim(value, (spot if which is None else which) * extent, extent, axis)

    def ordered(mine, other):
        return jnp.where(first_here, mine, other), jnp.where(first_here, other, mine)

    def gather(value, axis):
        if pair:
            return jnp.concatenate(ordered(value, swap(value)), axis)
        return lax.all_gather(value, "seq", axis=axis, tiled=True)

    def after(value, *others):
        return lax.optimization_barrier((value,) + others)[0]

    def put(value, axis):
        shape = list(value.shape)
        shape[axis] = seq
        return lax.dynamic_update_slice_in_dim(jnp.zeros(shape, value.dtype), value, spot, axis)

    def own_columns(matrix, parts):
        return [pick(matrix[:, at * model : (at + 1) * model], 1, wide) for at in range(parts)]

    def flat_down(grads, parts):
        return jnp.concatenate([grads[at * rank : (at + 1) * rank] for at in range(parts)], 1)

    def flat_upper(own):
        return put(jnp.stack(own, 1)[:, :, None], 2).reshape(rank, len(own) * model)

    halved = [pick(item, 1, wide) if pair else item for item in (self_out, cross_query)]
    first = [cross_out] + own_columns(cross_text, 2) + halved + own_columns(self_in, 3)
    edges = [0]
    for item in first:
        edges.append(edges[-1] + item.shape[1])
    start_in, start_text = edges[5], edges[1]
    packed = lax.all_gather(jnp.concatenate(first, 1), "fsdp", axis=0, tiled=True)
    squares_plan = ((edges[3], None), (edges[4], None), (edges[0], None))
    if pair:
        squares_plan = ((edges[3], 1), (edges[4], 3)) + squares_plan[2:]
    core = lax.rem(lax.axis_index("fsdp"), 2)
    where_here = jnp.stack([spot, there, core, 1 - core]).astype(jnp.int32)
    if pair:
        folds = depth // local
        plan = (fsdp, seq, folds, local)
        own_units = partial(take_units, plan, where_here)
        packed_feed = lax.all_gather(own_units(hidden_in, hidden_out), "fsdp", axis=0, tiled=True)

        def feed_weights(block):
            per = model // block
            return (
                packed_feed,
                pl.BlockSpec((model, block), lambda at: (0, at)),
                packed_feed,
                pl.BlockSpec((block, model), lambda at: (at % per, folds + at // per)),
            )
    else:

        def own_units(matrix):
            kept = lax.dynamic_index_in_dim(matrix.reshape(-1, fsdp, seq, depth), spot, 2, False)
            return kept.reshape(-1, hidden)

        def all_units(matrix):
            return put(matrix.reshape(-1, fsdp, 1, depth), 2).reshape(-1, hidden_all)

        whole_in = lax.all_gather(own_units(hidden_in), "fsdp", axis=0, tiled=True)
        whole_out = lax.all_gather(pick(hidden_out, 0, depth), "fsdp", axis=0, tiled=True)

        def feed_weights(block):
            return (
                whole_in,
                pl.BlockSpec((model, block), lambda at: (0, at)),
                whole_out,
                pl.BlockSpec((block, model), lambda at: (at, 0)),
            )

    index_all = lax.all_to_all(jnp.broadcast_to(adapter_index, (fsdp,)), "fsdp", 0, 0, tiled=True)
    if pair:
        table = jnp.where(first_here, adapter_down, adapter_up)
        mine = join_pieces(lax.all_to_all(jnp.take(table, index_all, axis=0), "fsdp", 0, 0, tiled=True))
        down_all, upper_all = ordered(mine, swap(mine))
    else:
        table = jnp.concatenate([adapter_down, adapter_up], 1)
        chosen = join_pieces(lax.all_to_all(jnp.take(table, index_all, axis=0), "fsdp", 0, 0, tiled=True))
        down_all, upper_all = chosen[:rank], chosen[rank:]
    in_cuts = [0, 3 * model, 4 * model, 5 * model, 7 * model, 8 * model, 9 * model, 9 * model + hidden_all]
    out_cuts = [0, 3 * model, 4 * model, 5 * model, 7 * model, 8 * model, 8 * model + hidden_all, 9 * model + hidden_all]
    downs = [down_all[:, in_cuts[at] : in_cuts[at + 1]] for at in range(7)]
    uppers = [upper_all[:, out_cuts[at] : out_cuts[at + 1]] for at in range(7)]

    def part_down(matrix, parts):
        return jnp.concatenate([matrix[:, at * model : (at + 1) * model] for at in range(parts)], 0)

    def part_upper(matrix, parts):
        own = own_columns(matrix, parts)
        return jnp.stack(
            [jnp.pad(item, ((at * rank, (parts - 1 - at) * rank), (0, 0))) for at, item in enumerate(own)], 0
        )

    units = own_units(jnp.concatenate([uppers[5], downs[6]], 0))
    feed_adapters = (downs[5], units[:rank], units[rank:], uppers[6])
    square_adapters = jnp.concatenate([downs[1], uppers[1], downs[2], uppers[2], downs[4], uppers[4]], 0)
    down_qkv, upper_qkv = part_down(downs[0], 3), part_upper(uppers[0], 3)
    down_text, upper_text = part_down(downs[3], 2), part_upper(uppers[3], 2)
    flat_text = jnp.concatenate([upper_text[0], upper_text[1]], 1)

    frames_in = inputs[0]
    cot = cotangent[0]
    if pair:
        frames_parts = [frames_in, swap(frames_in)]
        cot_other = swap(after(cot, frames_parts[1]))
    else:
        frames_parts = [lax.all_gather(frames_in, "seq", axis=0, tiled=True)]
    norm_places = where_here if pair else jnp.zeros((4,), jnp.int32)
    if pair:
        frames_parts[1] = after(frames_parts[1], cot_other, units)
    normed1, lat_qkv = norm_project(norm_places, frames_parts, norm_gains[0:1], norm_biases[0:1], down_qkv)
    packed = after(packed, normed1)
    sources = [packed]
    if pair:
        half = model // 2
        cut = [lax.dynamic_slice(packed, (core * half, at), (half, wide)) for at in edges[3:5]]
        straight = [swap(item) for item in cut]
        normed1 = after(normed1, *cut)
    triple = qkv_project(normed1, lat_qkv, upper_qkv, packed, start_in, 3 * wide)
    padded = -(-wide // LANES) * LANES
    if padded != wide:
        triple = jnp.pad(triple.reshape(frames, 3, wide), ((0, 0), (0, 0), (0, padded - wide)))
        triple = triple.reshape(frames, 3 * padded)
    text = after(text_states[0], triple)
    w_text = packed[:, start_text : start_text + 2 * wide]
    lat_text = mm_nt(text, down_text).astype(BF)
    memory = (mm(text, w_text) + mm(lat_text, flat_text)).astype(BF)
    head_out, probs, *leaving = attend(where_here, [size] * blocks if pair else [], after(triple, memory), padded)

    memory_all = gather(memory.reshape(-1, 2, wide), 2)
    keys, values = memory_all[:, 0], memory_all[:, 1]

    constants = (sources, squares_plan, square_adapters, norm_gains, norm_biases, keys, values)
    if pair:
        received = [swap(leaving[0])]
        for item in leaving[1:]:
            received.append(swap(after(item, received[-1])))
        neighbours = [(at, at ^ 1) for at in range(fsdp)]
        for item in straight:
            sources += [item, lax.ppermute(after(item, received[0], memory_all), "fsdp", neighbours)]
    else:
        natural = lax.all_to_all(head_out[:, :wide], "seq", split_axis=0, concat_axis=1, tiled=True)
    made = []
    for at in range(blocks):
        if pair:
            own, spec, others = head_out, (size, wide), [received[at]]
        else:
            own, spec, others = natural, (size, model), []
        ready = after(frames_in, made[-1][7]) if made else frames_in
        made.append(middle(where_here if pair else jnp.zeros((4,), jnp.int32), own, spec, others, ready, at, blocks, *constants))
    normed3 = [item[7] for item in made]
    resid2 = [item[6] for item in made]

    feed_tail = feed_adapters + (feed_weights, hidden)
    if pair:
        others = [swap(item) for item in normed3]
        theirs, gu_more, out_more = [], [], []
        for at in range(blocks):
            ready = after(others[at], theirs[-1][0]) if at else others[at]
            theirs.append(feed_forward([ready], [], cot_other, at, *feed_tail, BF))
            gu_more.append(swap(after(theirs[at][1], *gu_more[-1:])))
        ours = feed_forward([after(normed3[0], theirs[-1][1])] + normed3[1:], resid2, cot, 0, *feed_tail, F32)
        for at in range(blocks):
            behind = [ours[0]] + out_more[-1:] if at else [theirs[-1][0], gu_more[0]]
            out_more.append(swap(after(theirs[at][0], *behind)))
        gu = ours[blocks : 2 * blocks]
        feed_grads = [ours[2 * blocks :]] + [item[2:] for item in theirs]
    else:
        wide_in = gather(jnp.concatenate(normed3, 0), 0)
        all_out = feed_forward([wide_in], [], gather(cot, 0), 0, *feed_tail, F32)
        summed = [
            lax.psum_scatter(item.astype(BF), "seq", scatter_dimension=0, tiled=True) for item in all_out[:2]
        ]
        output = (jnp.concatenate(resid2, 0) + summed[0].astype(F32)).astype(BF)
        gu = [summed[1][at * size : (at + 1) * size] for at in range(blocks)]
        gu_more = [jnp.zeros_like(item) for item in gu]
        feed_grads = [all_out[2:]]

    pieces, resid1_grads, memory_parts, square_parts = [], [], [], []
    for at in range(blocks):
        gu_here = gu[at] if at == 0 else after(gu[at], result[-3])
        kept = made[at][:7] + made[at][8:9]
        result = middle_back(
            where_here, 2 if pair else 1, at, cot, gu_here, gu_more[at],
            kept, sources, squares_plan, square_adapters, norm_gains, keys, values,
        )
        if pair:
            waited = [pieces[-1][1]] if at else []
            if at == blocks - 1:
                memory_part = sum(memory_parts, result[-2]).astype(BF)
                memory_other = swap(after(pick(memory_part, 2, wide, there), *out_more))
                waited.append(memory_other)
            pieces.append((result[0], swap(after(result[1], *waited) if waited else result[1])))
        else:
            pieces.append(result[0])
        resid1_grads.append(result[-3])
        memory_parts.append(result[-2])
        square_parts.append(result[-1])
    resid1_grad = jnp.concatenate(resid1_grads, 0)
    square_grads = sum(square_parts[1:], square_parts[0])

    if pair:
        early, early_leaving, text_low = collect(
            plan, where_here, memory_parts, square_parts, feed_grads, memory_other, lat_text, flat_text, down_text,
            text_states[0], packed, start_text,
        )
        grad_pieces = [item[0] for item in pieces] + [item[1] for item in pieces]
    else:
        head_grad = lax.all_to_all(jnp.concatenate(pieces, 0), "seq", split_axis=1, concat_axis=0, tiled=True)
        grad_pieces = [jnp.pad(head_grad, ((0, 0), (0, padded - wide)))]
    triple_grad = attend_back(where_here, triple, head_out, grad_pieces, probs, padded)[:, :, :wide]
    if pair:
        early_other = swap(after(early_leaving, pieces[-1][1]))
        text_other = swap(after(text_low, early_other, triple_grad))
        glat_qkv, late, late_leaving = qkv_grads(
            where_here, after(triple_grad, early_other), normed1, lat_qkv, upper_qkv
        )
        late_other = swap(late_leaving)
    else:
        glat_qkv = sum(mm_nt(triple_grad[at], upper_qkv[at]) for at in range(3)).astype(BF)
        gdown_qkv = mm_tn(glat_qkv, normed1)
        gup_qkv = [mm_tn(lat_qkv[:, at * rank : (at + 1) * rank], triple_grad[at]) for at in range(3)]
    back = partial(qkv_back, gradient=triple_grad, glat=glat_qkv, down=down_qkv, packed=packed, start=start_in)
    if pair:
        for_them = back(after(there, early_other, text_other)[None], rows, kind=BF)
        for_us = back(after(spot, for_them, *out_more)[None], rows, kind=F32)
        input_grad = last_norm(frames_in, for_us + swap(for_them).astype(F32), norm_gains[0:1], resid1_grads)
        output = jnp.concatenate(
            [(after(item, for_them) + other.astype(F32)).astype(BF) for item, other in zip(ours[:blocks], out_more)], 0
        )
    else:
        full = back(jnp.zeros((1,), jnp.int32), frames, kind=BF)
        normed1_grad = lax.psum_scatter(full, "seq", scatter_dimension=0, tiled=True).astype(F32)
        resid1_grad = jnp.concatenate(resid1_grads, 0)
        input_grad = resid1_grad + norm_back(frames_in.astype(F32), norm_gains[0:1], normed1_grad)

    selector = (index_all[None, :] == jnp.arange(adapters, dtype=jnp.int32)[:, None]).astype(BF)

    def by_adapter(sent, *others):
        received = lax.all_to_all(sent, "fsdp", 0, 0, tiled=True)
        chooser = after(selector, *others) if others else selector
        return jnp.einsum("ac,crw->arw", chooser, received, preferred_element_type=F32)

    if pair:
        shares = by_adapter(split_sums([after(late, for_them), late_other, early, early_other], fsdp)).astype(BF)
        grad_down, grad_up = both_tables(where_here, after(shares, input_grad), swap(after(shares, for_us)))
        text_total = text_low.astype(F32) + text_other.astype(F32)
    else:
        memory_part = sum(memory_parts[1:], memory_parts[0]).astype(BF)
        memory_grad = lax.psum_scatter(memory_part, "seq", scatter_dimension=2, tiled=True)
        memory_flat = jnp.concatenate([memory_grad[0], memory_grad[1]], 1)
        glat_text = mm_nt(memory_flat, flat_text).astype(BF)
        gup_text = mm_tn(lat_text, memory_flat)
        gdown_text = mm_tn(glat_text, text)
        text_low = (mm_nt(memory_flat, w_text) + mm(glat_text, down_text)).astype(BF)
        own_text = [gup_text[at * rank : (at + 1) * rank, at * wide : (at + 1) * wide] for at in range(2)]
        gdown_in, gup_in, gdown_out, gup_out = feed_grads[0]
        square_grads = sum(square_parts[1:], square_parts[0])
        squares = [square_grads[rank * at : rank * (at + 1)] for at in range(6)]
        down_sent = [flat_down(gdown_qkv, 3), squares[0], squares[2], flat_down(gdown_text, 2), squares[4], gdown_in]
        upper_sent = [flat_upper(gup_qkv), squares[1], squares[3], flat_upper(own_text), squares[5]]
        down_sent = jnp.concatenate(down_sent + [all_units(gdown_out)], 1)
        upper_sent = jnp.concatenate(upper_sent + [all_units(gup_in), gup_out], 1)
        sent = jnp.concatenate([down_sent, upper_sent], 0).astype(BF).reshape(2 * rank, fsdp, piece).transpose(1, 0, 2)
        shares = lax.psum(by_adapter(sent).astype(BF), "seq")
        grad_down, grad_up = shares[:, :rank], shares[:, rank:]
        text_total = lax.psum(text_low, "seq").astype(F32)
    return (output[None], input_grad[None], text_total[None], grad_down.astype(F32), grad_up.astype(F32))


def solution(mesh):
    return jax.shard_map(
        partial(body, sizes=(mesh.shape["seq"], mesh.shape["fsdp"])),
        mesh=mesh,
        in_specs=(
            P("fsdp", "seq", None),
            P("fsdp", None, None),
            P("fsdp"),
            P(),
            P(),
            P("fsdp", None),
            P("fsdp", None),
            P("fsdp", None),
            P("fsdp", None),
            P("fsdp", None),
            P("fsdp", None),
            P("fsdp", None),
            P(None, None, "fsdp"),
            P(None, None, "fsdp"),
            P("fsdp", "seq", None),
        ),
        out_specs=(
            P("fsdp", "seq", None),
            P("fsdp", "seq", None),
            P("fsdp", None, None),
            P(None, None, "fsdp"),
            P(None, None, "fsdp"),
        ),
        check_vma=False,
    )
```

```python
from functools import partial

import jax
import jax.numpy as jnp
from jax import lax
from jax.experimental import pallas as pl
from jax.experimental.pallas import tpu as pltpu
from jax.sharding import PartitionSpec as P

HEAD = 64
LANES = 128
QB = 256
BF = jnp.bfloat16
F32 = jnp.float32
SCALE = float(HEAD) ** (-0.5)
SQRT_HALF = 0.7071067811865476
INV_SQRT_2PI = 0.3989422804014327
MIB = 1024 * 1024
VMEM_LIMIT = 60 * MIB
COST = 1.0
FEED_BLOCK = 512


def mm(a, b):
    return lax.dot_general(a, b, (((1,), (0,)), ((), ())), preferred_element_type=F32)


def mm_nt(a, b):
    return lax.dot_general(a, b, (((1,), (1,)), ((), ())), preferred_element_type=F32)


def mm_tn(a, b):
    return lax.dot_general(a, b, (((0,), (0,)), ((), ())), preferred_element_type=F32)


def norm_stats(values):
    centered = values - jnp.mean(values, -1, keepdims=True)
    variance = jnp.mean(centered * centered, -1, keepdims=True)
    inverse = lax.rsqrt(variance + 1e-05)
    return centered * inverse, inverse


def layer_norm(values, gains, biases):
    unit, _ = norm_stats(values)
    return unit * gains + biases


def norm_back(values, gains, gradient):
    unit, inverse = norm_stats(values)
    scaled = gradient * gains
    mean_one = jnp.mean(scaled, -1, keepdims=True)
    mean_two = jnp.mean(scaled * unit, -1, keepdims=True)
    return inverse * (scaled - mean_one - unit * mean_two)


def whole(shape):
    return pl.BlockSpec(shape, lambda *_: (0,) * len(shape))


def once(shape):
    return pl.BlockSpec(shape, lambda *_: (0,) * len(shape), pipeline_mode=pl.Buffered(1))


def params(count=1, limit=None):
    return pltpu.CompilerParams(
        dimension_semantics=("arbitrary",) * count if count else None, vmem_limit_bytes=limit or VMEM_LIMIT
    )


def cost(flops, moved, special=0):
    return pl.CostEstimate(
        flops=int(flops * COST), bytes_accessed=int(moved * COST), transcendentals=int(special * COST)
    )


def window(packed, start, width, rows=None, steps=1, step=0):
    block = width // steps
    rows = packed.shape[0] if rows is None else rows
    if start % block == 0 and block % LANES == 0:
        base = start // block
        return packed, pl.BlockSpec((rows, block), lambda *at: (0, base + (at[step] if steps > 1 else 0)))
    return packed[:, start : start + width], pl.BlockSpec(
        (rows, block), lambda *at: (0, at[step] if steps > 1 else 0)
    )


def norm_kernel(place_ref, *refs):
    count = len(refs) - 5
    parts, (gain_ref, bias_ref, down_ref, normed_ref, lat_ref) = refs[:count], refs[count:]
    step = 128
    for index, part_ref in enumerate(parts):
        base = place_ref[index] * part_ref.shape[0]

        def some(at, carry):
            rows = pl.ds(pl.multiple_of(at * step, step), step)
            into = pl.ds(pl.multiple_of(base + at * step, step), step)
            normed = layer_norm(part_ref[rows, :].astype(F32), gain_ref[...], bias_ref[...]).astype(BF)
            normed_ref[into, :] = normed
            lat_ref[into, :] = mm_nt(normed, down_ref[...]).astype(BF)
            return carry

        lax.fori_loop(0, part_ref.shape[0] // step, some, 0)


def smem():
    return pl.BlockSpec(memory_space=pltpu.SMEM)


def norm_project(places, parts, gains, biases, down):
    model = parts[0].shape[1]
    frames = sum(part.shape[0] for part in parts)
    ranks = down.shape[0]
    return pl.pallas_call(
        norm_kernel,
        in_specs=[smem()] + [whole(item.shape) for item in parts + [gains, biases, down]],
        out_specs=[whole((frames, model)), whole((frames, ranks))],
        out_shape=[jax.ShapeDtypeStruct((frames, model), BF), jax.ShapeDtypeStruct((frames, ranks), BF)],
        grid=(1,),
        compiler_params=params(1),
        cost_estimate=cost(2 * frames * model * ranks, 4 * frames * model),
        name="norm_project",
    )(places, *parts, gains, biases, down)


def qkv_kernel(normed_ref, lat_ref, up_ref, w_ref, out_ref):
    step = 256

    def some(at, carry):
        rows = pl.ds(pl.multiple_of(at * step, step), step)
        out_ref[rows, :] = (mm(normed_ref[rows, :], w_ref[...]) + mm(lat_ref[rows, :], up_ref[...])).astype(BF)
        return carry

    lax.fori_loop(0, normed_ref.shape[0] // step, some, 0)


def qkv_project(normed, latent, up, packed, start, width):
    row_count, model = normed.shape
    ranks = latent.shape[1]
    steps = 3 if (width // 3) % LANES == 0 else 1
    operand, spec = window(packed, start, width, steps=steps)
    block = width // steps
    if steps == 3:
        up_spec = pl.BlockSpec((None, ranks, block), lambda at: (at, 0, 0))
    else:
        up = up.transpose(1, 0, 2).reshape(ranks, width)
        up_spec = whole(up.shape)
    return pl.pallas_call(
        qkv_kernel,
        grid=(steps,),
        in_specs=[whole(normed.shape), whole(latent.shape), up_spec, spec],
        out_specs=pl.BlockSpec((row_count, block), lambda at: (0, at)),
        out_shape=jax.ShapeDtypeStruct((row_count, width), BF),
        compiler_params=params(1, 42 * MIB),
        cost_estimate=cost(2 * row_count * model * width, 2 * (row_count + width) * model),
        name="qkv_project",
    )(normed, latent, up, operand)


def tri_start(at):
    return QB * at * (at + 1) // 2


def attend_kernel(place_ref, q_ref, k_ref, v_ref, out_ref, prob_ref, *refs):
    sent, (val_t_ref, out_t_ref) = refs[:-2], refs[-2:]
    frames = q_ref.shape[0]
    lane = lax.broadcasted_iota(jnp.int32, (1, LANES), 1) // HEAD
    val_t_ref[...] = v_ref[...].T
    square = (QB, QB)
    keep_tri = lax.broadcasted_iota(jnp.int32, square, 0) <= lax.broadcasted_iota(jnp.int32, square, 1)

    def scores(half, at):
        stop = (at + 1) * QB
        query = q_ref[at * QB : stop, :] * jnp.where(lane == half, SCALE, 0.0).astype(BF)
        last = jnp.where(keep_tri, mm_nt(k_ref[stop - QB : stop, :], query), -1e30)
        if at == 0:
            return last
        return jnp.concatenate([mm_nt(k_ref[0 : stop - QB, :], query), last], 0)

    turns = [(half, at) for at in range(frames // QB) for half in range(2)]
    score = scores(*turns[0])
    for index, (half, at) in enumerate(turns):
        stop = (at + 1) * QB
        own = slice(half * HEAD, (half + 1) * HEAD)
        later = scores(*turns[index + 1]) if index + 1 < len(turns) else None
        raised = jnp.exp(score - jnp.max(score, 0, keepdims=True))
        prob = (raised * (1.0 / jnp.sum(raised, 0, keepdims=True))).astype(BF)
        prob_ref[half, tri_start(at) : tri_start(at) + stop, :] = prob
        out_t_ref[own, at * QB : stop] = mm(val_t_ref[own, 0:stop], prob)
        score = later
    out_ref[...] = out_t_ref[...].T.astype(BF)
    for index, sent_ref in enumerate(sent):
        size = sent_ref.shape[0]
        at = place_ref[1] * len(sent) + index
        sent_ref[...] = out_ref[pl.ds(pl.multiple_of(at * size, size), size), :]


def pair_specs(frames, width):
    pairs = width // LANES
    return [pl.BlockSpec((frames, LANES), lambda at, part=part: (0, part * pairs + at)) for part in range(3)]


def attend(places, sizes, triple, width):
    frames = triple.shape[0]
    pairs = width // LANES
    tri = tri_start(frames // QB)
    return pl.pallas_call(
        attend_kernel,
        grid=(pairs,),
        in_specs=[smem()] + pair_specs(frames, width),
        out_specs=[
            pl.BlockSpec((frames, LANES), lambda at: (0, at)),
            pl.BlockSpec((2, tri, QB), lambda at: (at, 0, 0)),
        ]
        + [pl.BlockSpec((size, LANES), lambda at: (0, at)) for size in sizes],
        out_shape=[
            jax.ShapeDtypeStruct((frames, width), BF),
            jax.ShapeDtypeStruct((2 * pairs, tri, QB), BF),
        ]
        + [jax.ShapeDtypeStruct((size, width), BF) for size in sizes],
        scratch_shapes=[pltpu.VMEM((LANES, frames), BF), pltpu.VMEM((LANES, frames), F32)],
        compiler_params=params(1),
        cost_estimate=cost(
            8 * tri * QB * HEAD * pairs, 2 * (4 * frames * width + 2 * pairs * tri * QB), 2 * pairs * tri * QB
        ),
        name="attend",
    )(places, triple, triple, triple)


def attend_back_kernel(place_ref, q_ref, k_ref, v_ref, out_ref, prob_ref, *refs):
    pieces, (back_ref, grad_ref, key_t_ref, dq_t_ref, dk_acc, dv_acc) = refs[:-6], refs[-6:]
    frames = q_ref.shape[0]
    for index, piece_ref in enumerate(pieces):
        size = piece_ref.shape[0]
        count = max(len(pieces) // 2, 1)
        at = place_ref[index // count] * count + index % count if len(pieces) > 1 else 0
        grad_ref[pl.ds(pl.multiple_of(at * size, size), size), :] = piece_ref[...]
    lane = lax.broadcasted_iota(jnp.int32, (1, LANES), 1) // HEAD
    key_t_ref[...] = k_ref[...].T
    dk_acc[...] = jnp.zeros_like(dk_acc)
    dv_acc[...] = jnp.zeros_like(dv_acc)
    turns = [(half, at) for at in range(frames // QB) for half in range(2)]

    def start(half, at):
        rows = slice(at * QB, (at + 1) * QB)
        grad = grad_ref[rows, :] * jnp.where(lane == half, 1.0, 0.0).astype(BF)
        return grad, mm_nt(v_ref[0 : (at + 1) * QB, :], grad)

    ready = start(*turns[0])
    for index, (half, at) in enumerate(turns):
        stop = (at + 1) * QB
        rows = slice(at * QB, stop)
        own = slice(half * HEAD, (half + 1) * HEAD)
        grad, prob_grad = ready
        if half == 0:
            product = (out_ref[rows, :].astype(F32) * grad_ref[rows, :].astype(F32)).T
        if index + 1 < len(turns):
            ready = start(*turns[index + 1])
        query = q_ref[rows, :] * jnp.where(lane == half, SCALE, 0.0).astype(BF)
        delta = jnp.sum(product[own, :], 0, keepdims=True)
        prob = prob_ref[half, tri_start(at) : tri_start(at) + stop, :]
        dv_acc[0:stop, :] += mm(prob, grad)
        score_grad = (prob.astype(F32) * (prob_grad - delta)).astype(BF)
        dk_acc[0:stop, :] += mm(score_grad, query)
        dq_t_ref[own, rows] = mm(key_t_ref[own, 0:stop], score_grad)
    back_ref[0] = (dq_t_ref[...].T * SCALE).astype(BF)
    back_ref[1] = dk_acc[...].astype(BF)
    back_ref[2] = dv_acc[...].astype(BF)


def attend_back(places, triple, attended, pieces, probs, width):
    frames = triple.shape[0]
    pairs = width // LANES
    tri = tri_start(frames // QB)
    column = pl.BlockSpec((frames, LANES), lambda at: (0, at))
    return pl.pallas_call(
        attend_back_kernel,
        grid=(pairs,),
        in_specs=[smem()]
        + pair_specs(frames, width)
        + [column, pl.BlockSpec((2, tri, QB), lambda at: (at, 0, 0))]
        + [pl.BlockSpec((piece.shape[0], LANES), lambda at: (0, at)) for piece in pieces],
        out_specs=pl.BlockSpec((3, frames, LANES), lambda at: (0, 0, at)),
        out_shape=jax.ShapeDtypeStruct((3, frames, width), BF),
        scratch_shapes=[
            pltpu.VMEM((frames, LANES), BF),
            pltpu.VMEM((LANES, frames), BF),
            pltpu.VMEM((LANES, frames), F32),
            pltpu.VMEM((frames, LANES), F32),
            pltpu.VMEM((frames, LANES), F32),
        ],
        compiler_params=params(1, 42 * MIB),
        cost_estimate=cost(16 * tri * QB * HEAD * pairs, 2 * (8 * frames * width + 2 * pairs * tri * QB)),
        name="attend_back",
    )(places, triple, triple, triple, attended, probs, *pieces)


def feed_kernel(count, based, *refs):
    pieces, refs = refs[:count], refs[count:]
    bases, refs = refs[:based], refs[based:]
    cot_ref, down_in_ref, up_in_ref, down_out_ref, up_out_ref, w_in_ref, w_out_ref = refs[:7]
    out_refs, gu_refs, refs = refs[7 : 7 + count], refs[7 + count : 7 + 2 * count], refs[7 + 2 * count :]
    (
        gdown_in_ref, gup_in_ref, gdown_out_ref, gup_out_ref, normed_ref,
        out_acc, gu_acc, lat_in, glat_out, lat_acc, glat_acc, lat_t, glat_t,
    ) = refs
    at = pl.program_id(0)

    @pl.when(at == 0)
    def _():
        start = 0
        for piece_ref in pieces:
            normed_ref[start : start + piece_ref.shape[0], :] = piece_ref[...]
            start += piece_ref.shape[0]
        latent = mm_nt(normed_ref[...], down_in_ref[...]).astype(BF)
        glat = mm_nt(cot_ref[...], up_out_ref[...]).astype(BF)
        lat_in[...] = latent
        glat_out[...] = glat
        lat_t[...] = latent.astype(F32).T.astype(BF)
        glat_t[...] = glat.astype(F32).T.astype(BF)
        start = 0
        for base_ref in bases:
            out_acc[start : start + base_ref.shape[0], :] = base_ref[...]
            start += base_ref.shape[0]
        if not bases:
            out_acc[...] = jnp.zeros_like(out_acc)
        gu_acc[...] = jnp.zeros_like(gu_acc)
        lat_acc[...] = jnp.zeros_like(lat_acc)
        glat_acc[...] = jnp.zeros_like(glat_acc)

    w_in = w_in_ref[...]
    w_out = w_out_ref[...]
    pre = mm(normed_ref[...], w_in) + mm(lat_in[...], up_in_ref[...])
    act_grad = mm_nt(cot_ref[...], w_out) + mm(glat_out[...], down_out_ref[...])
    cdf = 0.5 * (1.0 + lax.erf(pre * SQRT_HALF))
    slope = cdf + pre * (jnp.exp(-0.5 * pre * pre) * INV_SQRT_2PI)
    act = (pre * cdf).astype(BF)
    pre_grad = (act_grad * slope).astype(BF)
    out_acc[...] += mm(act, w_out)
    gu_acc[...] += mm_nt(pre_grad, w_in)
    lat_acc[...] += mm_nt(act, down_out_ref[...])
    glat_acc[...] += mm_nt(pre_grad, up_in_ref[...])
    gup_in_ref[...] = mm(lat_t[...], pre_grad)
    gdown_out_ref[...] = mm(glat_t[...], act)

    @pl.when(at == pl.num_programs(0) - 1)
    def _():
        latent = lat_acc[...].astype(BF)
        glat = glat_acc[...].astype(BF)
        start = 0
        for out_ref, gu_ref in zip(out_refs, gu_refs):
            rows = slice(start, start + out_ref.shape[0])
            out_ref[...] = (out_acc[rows, :] + mm(latent[rows], up_out_ref[...])).astype(out_ref.dtype)
            gu_ref[...] = (gu_acc[rows, :] + mm(glat[rows], down_in_ref[...])).astype(gu_ref.dtype)
            start += out_ref.shape[0]
        gup_out_ref[...] = mm(latent.astype(F32).T.astype(BF), cot_ref[...])
        gdown_in_ref[...] = mm(glat.astype(F32).T.astype(BF), normed_ref[...])


def feed_forward(pieces, bases, cotangent, block_at, down_in, up_in, down_out, up_out, weights, hidden, kind):
    model = cotangent.shape[1]
    row_count = sum(item.shape[0] for item in pieces)
    rank = down_in.shape[0]
    block = FEED_BLOCK if hidden % FEED_BLOCK == 0 else hidden
    w_in, in_spec, w_out, out_spec = weights(block)
    main = pl.BlockSpec((row_count, model), lambda at: (block_at, 0))
    slim = pl.BlockSpec((rank, block), lambda at: (0, at))
    small = whole((rank, model))
    return pl.pallas_call(
        partial(feed_kernel, len(pieces), len(bases)),
        grid=(hidden // block,),
        in_specs=[once(item.shape) for item in pieces + bases]
        + [main, small, slim, slim, small, in_spec, out_spec],
        out_specs=[whole(item.shape) for item in pieces] * 2 + [small, slim, slim, small],
        out_shape=[jax.ShapeDtypeStruct(item.shape, kind) for item in pieces]
        + [jax.ShapeDtypeStruct(item.shape, BF) for item in pieces]
        + [
            jax.ShapeDtypeStruct((rank, model), F32),
            jax.ShapeDtypeStruct((rank, hidden), F32),
            jax.ShapeDtypeStruct((rank, hidden), F32),
            jax.ShapeDtypeStruct((rank, model), F32),
        ],
        scratch_shapes=[pltpu.VMEM((row_count, model), BF)]
        + [pltpu.VMEM((row_count, model), F32)] * 2
        + [pltpu.VMEM((row_count, rank), BF)] * 2
        + [pltpu.VMEM((row_count, rank), F32)] * 2
        + [pltpu.VMEM((rank, row_count), BF)] * 2,
        compiler_params=params(1),
        cost_estimate=cost(8 * row_count * model * hidden, 4 * hidden * model, 2 * row_count * hidden),
        name="feed_forward",
    )(*pieces, *bases, cotangent, down_in, up_in, down_out, up_out, w_in, w_out)


def spread_heads(rows_ref, into_ref, model):
    keys = rows_ref.shape[0]
    wide = 4 * HEAD
    row = lax.broadcasted_iota(jnp.int32, (4 * keys, wide), 0) // keys
    col = lax.broadcasted_iota(jnp.int32, (4 * keys, wide), 1) // HEAD
    mask = jnp.where(row == col, 1.0, 0.0).astype(BF)

    def some(group, carry):
        part = rows_ref[:, pl.ds(pl.multiple_of(group * wide, wide), wide)]
        into = pl.ds(pl.multiple_of(group * 4 * keys, 4 * keys), 4 * keys)
        into_ref[into, :] = jnp.concatenate([part] * 4, 0) * mask
        return carry

    lax.fori_loop(0, model // wide, some, 0)


def head_total(values, keys, reduce):
    split = values.reshape(4, keys, values.shape[1])
    return jnp.broadcast_to(reduce(split, 1, keepdims=True), split.shape).reshape(values.shape)


def each(count, step, work):
    def some(at, carry):
        work(pl.ds(pl.multiple_of(at * step, step), step))
        return carry

    lax.fori_loop(0, count // step, some, 0)


def pair_of(both, size):
    return [pl.ds(pl.multiple_of(both.start + at * size, size), size) for at in range(both.size // size)]


def weight_copies(plan, place_ref, sources, hold_ref, sem_ref):
    model = hold_ref.shape[1]
    groups = []
    for index, (start, extra) in enumerate(plan):
        if extra is None:
            parts = [slice(at * model // 2, (at + 1) * model // 2) for at in range(2)]
            pairs = [(sources[0].at[rows, pl.ds(start, model)], hold_ref.at[index, rows, :]) for rows in parts]
        else:
            half = model // 2
            here, there = [pl.ds(pl.multiple_of(place_ref[at] * half, half), half) for at in range(2)]
            pairs = [(sources[0].at[:, pl.ds(start, half)], hold_ref.at[index, :, here])]
            for at in range(2):
                rows = pl.ds(pl.multiple_of(place_ref[2 + at] * half, half), half)
                pairs.append((sources[extra + at], hold_ref.at[index, rows, there]))
        groups.append(
            [pltpu.make_async_copy(src, dst, sem_ref.at[index, at]) for at, (src, dst) in enumerate(pairs)]
        )
    return groups


def source_count(plan):
    return 1 + 2 * sum(extra is not None for _, extra in plan)


def start_all(copies):
    for copy in copies:
        copy.start()


def wait_all(copies):
    for copy in copies:
        copy.wait()


def middle_kernel(plan, place_ref, *refs):
    sources, refs = refs[: source_count(plan)], refs[source_count(plan) :]
    inputs_ref, adapt_ref, gain_ref, bias_ref, keys_ref, values_ref = refs[:6]
    pieces = refs[6:-20]
    away = refs[-20:-14]
    resid2_ref, normed3_ref, lat_ref, hold_ref, key_wide, value_wide, sem_ref = refs[-14:-7]
    kept, out_sem = refs[-7:-1], refs[-1]
    attended_ref, resid1_ref, normed2_ref, query_ref, probs_ref, crossed_ref = kept
    leaving = [pltpu.make_async_copy(kept[at], away[at], out_sem.at[at]) for at in range(6)]
    model = inputs_ref.shape[1]
    keys = keys_ref.shape[0]
    rows = inputs_ref.shape[0]
    wide = 4 * HEAD
    copies = weight_copies(plan, place_ref, sources, hold_ref, sem_ref)
    start_all(copies[0])
    for index, piece_ref in enumerate(pieces):
        size = piece_ref.shape[1]
        attended_ref[:, pl.ds(pl.multiple_of(place_ref[index] * size, size), size)] = piece_ref[...]
    spread_heads(keys_ref, key_wide, model)
    spread_heads(values_ref, value_wide, model)

    def adapted(moving_ref, index, store):
        latent = mm_nt(moving_ref[...], adapt_ref[32 * index : 32 * index + 16, :]).astype(BF)
        lat_ref[:, 16 * index : 16 * index + 16] = latent
        wait_all(copies[index])
        if index < 2:
            start_all(copies[index + 1])

        def some(cols):
            store(
                cols,
                mm(moving_ref[...], hold_ref[index, :, cols])
                + mm(latent, adapt_ref[32 * index + 16 : 32 * index + 32, cols]),
            )

        each(model, 512, some)

    def add_first(cols, value):
        resid1_ref[:, cols] = inputs_ref[:, cols].astype(F32) + value

    def add_second(cols, value):
        resid2_ref[:, cols] = resid1_ref[:, cols] + value

    def keep_query(cols, value):
        query_ref[:, cols] = value.astype(BF)

    def normed(values_at, into_ref, which):
        def some(part):
            into_ref[part, :] = layer_norm(
                values_at[part, :], gain_ref[which : which + 1, :], bias_ref[which : which + 1, :]
            ).astype(BF)

        each(rows, 128, some)

    def cross(both):
        groups = pair_of(both, wide)
        scores = [mm_nt(key_wide[lanes, :], query_ref[:, lanes]) * SCALE for lanes in groups]
        for lanes, score in zip(groups, scores):
            raised = jnp.exp(score - head_total(score, keys, jnp.max))
            prob = (raised / head_total(raised, keys, jnp.sum)).astype(BF)
            probs_ref[lanes, :] = prob
            crossed_ref[:, lanes] = mm_tn(prob, value_wide[lanes, :]).astype(BF)

    leaving[0].start()
    adapted(attended_ref, 0, add_first)
    leaving[1].start()
    normed(resid1_ref, normed2_ref, 1)
    leaving[2].start()
    adapted(normed2_ref, 1, keep_query)
    leaving[3].start()
    each(model, 3 * wide, cross)
    leaving[4].start()
    leaving[5].start()
    adapted(crossed_ref, 2, add_second)
    normed(resid2_ref, normed3_ref, 2)
    wait_all(leaving)


def middle(places, own, own_spec, others, inputs, at, blocks, sources, plan, adapters, gains, biases, keys, values):
    rows, model = own_spec[0], inputs.shape[1]
    spread = model // HEAD * keys.shape[0]
    shape = lambda kind, dims=(rows, model): jax.ShapeDtypeStruct(dims, kind)
    flat = lambda dims: pl.BlockSpec(dims, lambda _, ref: (0,) * len(dims))
    shapes = [shape(kind) for kind in (BF, F32, BF, BF)]
    shapes += [shape(BF, (spread, rows)), shape(BF), shape(F32), shape(BF), shape(BF, (rows, 48))]
    return pl.pallas_call(
        partial(middle_kernel, plan),
        grid_spec=pltpu.PrefetchScalarGridSpec(
            num_scalar_prefetch=1,
            grid=(1,),
            in_specs=[pl.BlockSpec(memory_space=pl.ANY)] * len(sources)
            + [pl.BlockSpec((rows, model), lambda _, ref: (at, 0))]
            + [flat(item.shape) for item in (adapters, gains, biases, keys, values)]
            + [pl.BlockSpec(own_spec, lambda _, ref: (ref[0] * blocks + at, 0) if others else (at, 0))]
            + [flat(item.shape) for item in others],
            out_specs=[pl.BlockSpec(memory_space=pl.ANY)] * 6 + [flat(item.shape) for item in shapes[6:]],
            scratch_shapes=[
                pltpu.VMEM((3, model, model), BF),
                pltpu.VMEM((spread, 4 * HEAD), BF),
                pltpu.VMEM((spread, 4 * HEAD), BF),
                pltpu.SemaphoreType.DMA((3, 3)),
            ]
            + [pltpu.VMEM(item.shape, item.dtype) for item in shapes[:6]]
            + [pltpu.SemaphoreType.DMA((6,))],
        ),
        out_shape=shapes,
        compiler_params=params(),
        cost_estimate=cost(6 * rows * model * model, 6 * model * model + 24 * rows * model),
        name="middle",
    )(places, *sources, inputs, adapters, gains, biases, keys, values, own, *others)


def middle_back_kernel(plan, split, place_ref, *refs):
    sources, refs = refs[: source_count(plan)], refs[source_count(plan) :]
    cot_ref, gu_ref, more_ref = refs[:3]
    far = refs[3:9]
    resid2_ref, lat_ref, adapt_ref, gain_ref, keys_ref, values_ref = refs[9:15]
    kept, in_sem = refs[-7:-1], refs[-1]
    attended_ref, resid1_ref, normed2_ref, query_ref, probs_ref, crossed_ref = kept
    coming = [pltpu.make_async_copy(far[at], kept[at], in_sem.at[at]) for at in range(6)]
    refs = refs[15:-7]
    outs = refs[: 2 if split else 1]
    resid1_grad_ref, memory_ref, small_ref, hold_ref, key_wide, value_wide, work_ref, low_ref, sem_ref = refs[len(outs) :]
    rows, model = cot_ref.shape
    keys = keys_ref.shape[0]
    wide = 4 * HEAD
    copies = weight_copies(plan, place_ref, sources, hold_ref, sem_ref)
    start_all(copies[2])
    coming[5].start()
    spread_heads(keys_ref, key_wide, model)
    spread_heads(values_ref, value_wide, model)

    def first(part):
        gradient = gu_ref[part, :].astype(F32) + more_ref[part, :].astype(F32)
        value = cot_ref[part, :].astype(F32) + norm_back(resid2_ref[part, :], gain_ref[2:3, :], gradient)
        resid1_grad_ref[part, :] = value
        low_ref[part, :] = value.astype(BF)

    def second(part):
        value = resid1_grad_ref[part, :] + norm_back(resid1_ref[part, :], gain_ref[1:2, :], work_ref[part, :])
        resid1_grad_ref[part, :] = value
        low_ref[part, :] = value.astype(BF)

    def back(moving_ref, index, store):
        down = slice(32 * index, 32 * index + 16)
        upper = slice(32 * index + 16, 32 * index + 32)
        glat = mm_nt(low_ref[...], adapt_ref[upper, :]).astype(BF)
        glat_t = glat.astype(F32).T.astype(BF)
        lat_t = lat_ref[:, 16 * index : 16 * index + 16].astype(F32).T.astype(BF)
        wait_all(copies[index])
        if index == 2:
            wait_all(coming[5:])
            start_all(coming[2:5])
        if index == 1:
            wait_all(coming[2:3])
            start_all(coming[:2])
        if index == 0:
            wait_all(coming[:1])
        if index:
            start_all(copies[index - 1])

        def some(cols):
            small_ref[down, cols] = mm(glat_t, moving_ref[:, cols])
            small_ref[upper, cols] = mm(lat_t, low_ref[:, cols])
            store(cols, mm_nt(low_ref[...], hold_ref[index, cols, :]) + mm(glat, adapt_ref[down, cols]))

        each(model, 512, some)

    def keep(cols, value):
        work_ref[:, cols] = value

    def cross(both):
        groups = pair_of(both, wide)
        parts = [work_ref[:, lanes].astype(BF) for lanes in groups]
        prob_grads = [mm_nt(value_wide[lanes, :], part) for lanes, part in zip(groups, parts)]
        for lanes, part, prob_grad in zip(groups, parts, prob_grads):
            cross_one(lanes, part, prob_grad)

    def cross_one(lanes, part, prob_grad):
        prob = probs_ref[lanes, :]
        wide_prob = prob.astype(F32)
        weighted = wide_prob * prob_grad
        score_grad = (weighted - wide_prob * head_total(weighted, keys, jnp.sum)).astype(BF)
        low_ref[:, lanes] = (mm_tn(score_grad, key_wide[lanes, :]) * SCALE).astype(BF)
        key_full = mm(score_grad, query_ref[:, lanes])
        value_full = mm(prob, part)
        col = lax.broadcasted_iota(jnp.int32, (keys, wide), 1) // HEAD
        key_sum, value_sum = key_full[:keys], value_full[:keys]
        for head in range(1, 4):
            rows_at = slice(head * keys, (head + 1) * keys)
            key_sum = jnp.where(col == head, key_full[rows_at], key_sum)
            value_sum = jnp.where(col == head, value_full[rows_at], value_sum)
        memory_ref[0, :, lanes] = key_sum * SCALE
        memory_ref[1, :, lanes] = value_sum

    each(rows, 128, first)
    back(crossed_ref, 2, keep)
    wait_all(coming[3:5])
    each(model, 3 * wide, cross)
    back(normed2_ref, 1, keep)
    wait_all(coming[1:2])
    each(rows, 128, second)
    back(attended_ref, 0, keep)
    if split:
        size = outs[0].shape[1]
        for out_ref, index in zip(outs, range(2)):
            out_ref[...] = work_ref[:, pl.ds(pl.multiple_of(place_ref[index] * size, size), size)].astype(BF)
    else:
        outs[0][...] = work_ref[...].astype(BF)


def middle_back(places, parts, at, cotangent, gu, more, kept, sources, plan, adapters, gains, keys, values):
    model = cotangent.shape[1]
    rows = kept[0].shape[0]
    spread = model // HEAD * keys.shape[0]
    flat = lambda dims: pl.BlockSpec(dims, lambda _, ref: (0,) * len(dims))
    block = pl.BlockSpec((rows, model), lambda _, ref: (at, 0))
    shapes = [jax.ShapeDtypeStruct((rows, model // parts), BF)] * parts + [
        jax.ShapeDtypeStruct((rows, model), F32),
        jax.ShapeDtypeStruct((2,) + keys.shape, F32),
        jax.ShapeDtypeStruct(adapters.shape, F32),
    ]
    return pl.pallas_call(
        partial(middle_back_kernel, plan, parts == 2),
        grid_spec=pltpu.PrefetchScalarGridSpec(
            num_scalar_prefetch=1,
            grid=(1,),
            in_specs=[pl.BlockSpec(memory_space=pl.ANY)] * len(sources)
            + [block, flat(gu.shape), flat(more.shape)]
            + [pl.BlockSpec(memory_space=pl.ANY)] * 6
            + [flat(item.shape) for item in kept[6:]]
            + [flat(item.shape) for item in (adapters, gains, keys, values)],
            out_specs=[flat(item.shape) for item in shapes],
            scratch_shapes=[
                pltpu.VMEM((3, model, model), BF),
                pltpu.VMEM((spread, 4 * HEAD), BF),
                pltpu.VMEM((spread, 4 * HEAD), BF),
                pltpu.VMEM((rows, model), F32),
                pltpu.VMEM((rows, model), BF),
                pltpu.SemaphoreType.DMA((3, 3)),
            ]
            + [pltpu.VMEM(item.shape, item.dtype) for item in kept[:6]]
            + [pltpu.SemaphoreType.DMA((6,))],
        ),
        out_shape=shapes,
        compiler_params=params(),
        cost_estimate=cost(6 * rows * model * model, 6 * model * model + 36 * rows * model),
        name="middle_back",
    )(places, *sources, cotangent, gu, more, *kept, adapters, gains, keys, values)


def qkv_grads_kernel(
    place_ref, grad_ref, normed_ref, lat_ref, up_ref, glat_ref, mine_ref, theirs_ref, glat_acc, gup_acc, down_acc,
    down_all, upper_all,
):
    at = pl.program_id(0)
    gradient = grad_ref[...]
    rank = mine_ref.shape[0]
    model = normed_ref.shape[1]
    width = gradient.shape[1]
    gup_acc[...] = mm_tn(lat_ref[...], gradient)

    @pl.when(at == 0)
    def _():
        glat_acc[...] = jnp.zeros_like(glat_acc)
        upper_all[...] = jnp.zeros_like(upper_all)

    into = pl.ds(pl.multiple_of(at * model + place_ref[0] * width, LANES), width)
    upper_all[:, into] = gup_acc[pl.ds(pl.multiple_of(at * rank, rank), rank), :].astype(BF)
    glat_acc[...] += mm_nt(gradient, up_ref[...])

    @pl.when(at == pl.num_programs(0) - 1)
    def _():
        low = glat_acc[...].astype(BF)
        glat_ref[...] = low
        down_acc[...] = mm_tn(low, normed_ref[...])
        for part in range(3):
            down_all[:, part * model : (part + 1) * model] = down_acc[part * rank : (part + 1) * rank, :].astype(BF)
        share(place_ref, down_all, upper_all, mine_ref, theirs_ref)


def share(place_ref, down_all, upper_all, mine_ref, theirs_ref):
    @pl.when(place_ref[0] == 0)
    def _():
        mine_ref[...] = down_all[...]
        theirs_ref[...] = upper_all[...]

    @pl.when(place_ref[0] != 0)
    def _():
        mine_ref[...] = upper_all[...]
        theirs_ref[...] = down_all[...]


def qkv_grads(places, gradient, normed, latent, up):
    frames, model = normed.shape
    parts, ranks, width = up.shape
    rank = ranks // parts
    table = jax.ShapeDtypeStruct((rank, parts * model), BF)
    return pl.pallas_call(
        qkv_grads_kernel,
        grid=(parts,),
        in_specs=[
            smem(),
            pl.BlockSpec((None, frames, width), lambda at: (at, 0, 0)),
            whole(normed.shape),
            whole(latent.shape),
            pl.BlockSpec((None, ranks, width), lambda at: (at, 0, 0)),
        ],
        out_specs=[whole(latent.shape), whole(table.shape), whole(table.shape)],
        out_shape=[jax.ShapeDtypeStruct(latent.shape, BF), table, table],
        scratch_shapes=[
            pltpu.VMEM(latent.shape, F32),
            pltpu.VMEM((ranks, width), F32),
            pltpu.VMEM((ranks, model), F32),
            pltpu.VMEM(table.shape, BF),
            pltpu.VMEM(table.shape, BF),
        ],
        compiler_params=params(1, 42 * MIB),
        cost_estimate=cost(8 * frames * ranks * width * parts, 2 * frames * (model + parts * width)),
        name="qkv_grads",
    )(places, gradient, normed, latent, up)


def qkv_back_kernel(place_ref, grad_ref, glat_ref, down_ref, w_ref, gu_ref, gu_acc):
    at = pl.program_id(0)
    model = gu_ref.shape[1]
    last = pl.num_programs(0) - 1

    def some(cols):
        direct = mm_nt(grad_ref[...], w_ref[cols, :])

        @pl.when(at == 0)
        def _():
            gu_acc[:, cols] = direct + mm(glat_ref[...], down_ref[:, cols])

        @pl.when(jnp.logical_and(at > 0, at < last))
        def _():
            gu_acc[:, cols] += direct

        @pl.when(at == last)
        def _():
            gu_ref[:, cols] = (gu_acc[:, cols] + direct).astype(gu_ref.dtype)

    each(model, 512, some)


def qkv_back(place, row_count, gradient, glat, down, packed, start, kind):
    ranks, model = down.shape
    width = gradient.shape[2]
    if start % width == 0 and width % LANES == 0:
        weight, spec = packed, pl.BlockSpec((model, width), lambda at, ref: (0, start // width + at))
    else:
        weight = packed[:, start : start + 3 * width].reshape(model, 3, width).transpose(1, 0, 2)
        spec = pl.BlockSpec((None, model, width), lambda at, ref: (at, 0, 0))
    return pl.pallas_call(
        qkv_back_kernel,
        grid_spec=pltpu.PrefetchScalarGridSpec(
            num_scalar_prefetch=1,
            grid=(3,),
            in_specs=[
                pl.BlockSpec((None, row_count, width), lambda at, ref: (at, ref[0], 0)),
                pl.BlockSpec((row_count, ranks), lambda at, ref: (ref[0], 0)),
                pl.BlockSpec(down.shape, lambda at, ref: (0, 0)),
                spec,
            ],
            out_specs=pl.BlockSpec((row_count, model), lambda at, ref: (0, 0)),
            scratch_shapes=[pltpu.VMEM((row_count, model), F32)],
        ),
        out_shape=jax.ShapeDtypeStruct((row_count, model), kind),
        compiler_params=params(1, 42 * MIB),
        cost_estimate=cost(6 * row_count * model * width, 6 * model * width + 8 * row_count * model),
        name="qkv_back",
    )(place, gradient, glat, down, weight)


def last_norm_kernel(blocks, frames_ref, ours_ref, theirs_ref, gain_ref, *refs):
    pieces, grad_ref = refs[:-1], refs[-1]
    at = pl.program_id(0)
    gradient = ours_ref[...] + theirs_ref[...].astype(F32)
    back = norm_back(frames_ref[...].astype(F32), gain_ref[...], gradient)
    for index, piece_ref in enumerate(pieces):

        @pl.when(at // blocks == index)
        def _(piece_ref=piece_ref):
            grad_ref[...] = back + piece_ref[...]


def last_norm(frames, ours, theirs, gains, pieces):
    rows, model = frames.shape
    step = min(128, rows)
    blocks = pieces[0].shape[0] // step
    block = pl.BlockSpec((step, model), lambda at: (at, 0))

    def piece_spec(index):
        return pl.BlockSpec((step, model), lambda at: (jnp.clip(at - index * blocks, 0, blocks - 1), 0))

    return pl.pallas_call(
        partial(last_norm_kernel, blocks),
        grid=(rows // step,),
        in_specs=[block, block, block, whole(gains.shape)] + [piece_spec(index) for index in range(len(pieces))],
        out_specs=block,
        out_shape=jax.ShapeDtypeStruct((rows, model), F32),
        compiler_params=params(1, 42 * MIB),
        cost_estimate=cost(20 * rows * model, 16 * rows * model),
        name="last_norm",
    )(frames, ours, theirs, gains, *pieces)


def run_length(size):
    count = 1
    while count * size % LANES:
        count *= 2
    return count


def join_kernel(pieces_ref, flat_ref):
    count, _, size = pieces_ref.shape
    run = run_length(size)

    def some(at, carry):
        parts = [pieces_ref[at * run + index] for index in range(run)]
        into = pl.ds(pl.multiple_of(at * run * size, LANES), run * size)
        flat_ref[:, into] = jnp.concatenate(parts, 1)
        return carry

    lax.fori_loop(0, count // run, some, 0)


def join_pieces(pieces):
    count, rows, size = pieces.shape
    if count % run_length(size):
        return pieces.transpose(1, 0, 2).reshape(rows, count * size)
    return pl.pallas_call(
        join_kernel,
        out_shape=jax.ShapeDtypeStruct((rows, count * size), pieces.dtype),
        compiler_params=params(0),
        name="join_pieces",
    )(pieces)


def split_kernel(*refs):
    sources, pieces_ref, flat_ref = refs[:-2], refs[-2], refs[-1]
    count, _, size = pieces_ref.shape
    run = run_length(size)
    start = 0
    for first_ref, second_ref in zip(sources[::2], sources[1::2]):
        width = first_ref.shape[1]
        both = first_ref[...].astype(F32) + second_ref[...].astype(F32)
        flat_ref[:, start : start + width] = both.astype(BF)
        start += width

    def some(at, carry):
        block = flat_ref[:, pl.ds(pl.multiple_of(at * run * size, LANES), run * size)]
        for index in range(run):
            pieces_ref[at * run + index] = block[:, index * size : (index + 1) * size]
        return carry

    lax.fori_loop(0, count // run, some, 0)


def split_sums(pairs, count):
    rows = pairs[0].shape[0]
    total = sum(item.shape[1] for item in pairs[::2])
    return pl.pallas_call(
        split_kernel,
        out_shape=jax.ShapeDtypeStruct((count, rows, total // count), BF),
        scratch_shapes=[pltpu.VMEM((rows, total), BF)],
        compiler_params=params(0, 42 * MIB),
        name="split_sums",
    )(*pairs)


def unit_loop(plan, work):
    fsdp, seq, folds, local = plan
    run = run_length(local)

    def some(at, carry):
        span = run * seq * folds * local
        block = pl.ds(pl.multiple_of(at * span, LANES), span)
        folded = [
            pl.ds(pl.multiple_of(fold * fsdp * local + at * run * local, LANES), run * local) for fold in range(folds)
        ]
        work(run, block, folded)
        return carry

    lax.fori_loop(0, fsdp // run, some, 0)


def take_units_kernel(plan, place_ref, all_ref, *refs):
    own_ref = refs[-1]
    _, seq, folds, local = plan
    spot = place_ref[0]

    def work(run, block, folded):
        values = all_ref[:, block]
        for fold, into in enumerate(folded):
            parts = []
            for index in range(run):
                base = (index * seq * folds + fold) * local
                part = values[:, base : base + local]
                for other in range(1, seq):
                    shift = base + other * folds * local
                    part = jnp.where(spot == other, values[:, shift : shift + local], part)
                parts.append(part)
            own_ref[:, into] = jnp.concatenate(parts, 1)

    unit_loop(plan, work)
    if len(refs) == 2:
        model = refs[0].shape[1]
        hidden = own_ref.shape[1] - folds * model
        for fold in range(folds):
            rows = pl.ds(pl.multiple_of((spot * folds + fold) * local, 16), local)
            own_ref[:, hidden + fold * model : hidden + (fold + 1) * model] = refs[0][rows, :]


def take_units(plan, places, matrix, low=None):
    _, seq, folds, local = plan
    rows, width = matrix.shape
    extra = [] if low is None else [low]
    out_width = width // seq + sum(folds * item.shape[1] for item in extra)
    return pl.pallas_call(
        partial(take_units_kernel, plan),
        in_specs=[smem()] + [pl.BlockSpec(memory_space=pltpu.VMEM)] * (1 + len(extra)),
        out_shape=jax.ShapeDtypeStruct((rows, out_width), matrix.dtype),
        compiler_params=params(0),
        name="take_units",
    )(places, matrix, *extra)


def collect_kernel(plan, blocks, start_at, place_ref, *refs):
    parts, squares, refs = refs[:blocks], refs[blocks : 2 * blocks], refs[2 * blocks :]
    feeds = [refs[at : at + 4] for at in range(0, len(refs) - 14, 4)]
    (
        other_ref, lat_ref, flat_ref, down_text_ref, text_ref, w_ref,
        mine_ref, theirs_ref, text_grad_ref, down_all, upper_all, unit_acc, hold_ref, sem_ref,
    ) = refs[-14:]
    _, seq, folds, local = plan
    rank = mine_ref.shape[0]
    model = text_ref.shape[1]
    wide = other_ref.shape[2]
    spot = place_ref[0]
    own = pl.ds(pl.multiple_of(spot * wide, wide), wide)
    copy = pltpu.make_async_copy(w_ref.at[:, pl.ds(start_at, hold_ref.shape[1])], hold_ref, sem_ref)
    copy.start()

    def total(items, rows):
        value = items[0][rows, :]
        for item in items[1:]:
            value = value + item[rows, :]
        return value

    moved = []
    for part in range(2):
        value = parts[0][part, :, own]
        for item in parts[1:]:
            value = value + item[part, :, own]
        moved.append((value + other_ref[part].astype(F32)).astype(BF))
    moved = jnp.concatenate(moved, 1)
    glat = mm_nt(moved, flat_ref[...]).astype(BF)
    gup = mm_tn(lat_ref[...], moved)
    gdown = mm_tn(glat, text_ref[...])

    upper_all[:, 2 * model : 4 * model] = jnp.zeros((rank, 2 * model), BF)
    for part in range(2):
        rows = slice(part * rank, (part + 1) * rank)
        down_all[:, (2 + part) * model : (3 + part) * model] = gdown[rows].astype(BF)
        into = pl.ds(pl.multiple_of((2 + part) * model + spot * wide, LANES), wide)
        upper_all[:, into] = gup[rows, part * wide : (part + 1) * wide].astype(BF)
    for index, at in enumerate((0, 1, 4)):
        cols = slice(at * model, (at + 1) * model)
        down_all[:, cols] = total(squares, slice(2 * index * rank, (2 * index + 1) * rank)).astype(BF)
        upper_all[:, cols] = total(squares, slice((2 * index + 1) * rank, (2 * index + 2) * rank)).astype(BF)
    every = slice(0, rank)
    down_all[:, 5 * model : 6 * model] = total([item[0] for item in feeds], every).astype(BF)
    upper_all[:, upper_all.shape[1] - model :] = total([item[3] for item in feeds], every).astype(BF)
    for into_ref, start, which in ((upper_all, 5 * model, 1), (down_all, 6 * model, 2)):
        unit_acc[...] = total([item[which] for item in feeds], every)

        def work(run, block, folded):
            values = [unit_acc[:, cols] for cols in folded]
            spread = []
            for index in range(run):
                for other in range(seq):
                    for fold in range(folds):
                        part = values[fold][:, index * local : (index + 1) * local]
                        spread.append(jnp.where(spot == other, part, 0.0))
            at = pl.ds(pl.multiple_of(start + block.start, LANES), block.size)
            into_ref[:, at] = jnp.concatenate(spread, 1).astype(BF)

        unit_loop(plan, work)
    share(place_ref, down_all, upper_all, mine_ref, theirs_ref)
    copy.wait()
    text_grad_ref[...] = (mm_nt(moved, hold_ref[...]) + mm(glat, down_text_ref[...])).astype(BF)


def collect(plan, places, parts, squares, feeds, other, lat_text, flat_text, down_text, text, packed, start):
    rank = squares[0].shape[0] // 6
    model = text.shape[1]
    hidden = feeds[0][1].shape[1]
    wide2 = flat_text.shape[1]
    width = 6 * model + hidden * plan[1]
    feeds = [item for feed in feeds for item in feed]
    before = list(parts) + list(squares) + feeds + [other, lat_text, flat_text, down_text, text]
    table = jax.ShapeDtypeStruct((rank, width), BF)
    shapes = [table, table, jax.ShapeDtypeStruct(text.shape, BF)]
    return pl.pallas_call(
        partial(collect_kernel, plan, len(parts), start),
        grid=(1,),
        in_specs=[smem()] + [whole(item.shape) for item in before] + [pl.BlockSpec(memory_space=pl.ANY)],
        out_specs=[whole(item.shape) for item in shapes],
        out_shape=shapes,
        scratch_shapes=[pltpu.VMEM(table.shape, BF)] * 2
        + [pltpu.VMEM((rank, hidden), F32), pltpu.VMEM((model, wide2), BF), pltpu.SemaphoreType.DMA],
        compiler_params=params(1),
        cost_estimate=cost(4 * text.shape[0] * model * wide2, 2 * model * wide2),
        name="collect",
    )(places, *before, packed)


def both_kernel(place_ref, mine_ref, other_ref, down_ref, upper_ref):
    first = place_ref[0] == 0
    for at in range(mine_ref.shape[0]):
        mine, other = mine_ref[at].astype(F32), other_ref[at].astype(F32)
        down_ref[at] = jnp.where(first, mine, other)
        upper_ref[at] = jnp.where(first, other, mine)


def both_tables(places, mine, other):
    return pl.pallas_call(
        both_kernel,
        in_specs=[smem()] + [pl.BlockSpec(memory_space=pltpu.VMEM)] * 2,
        out_shape=[jax.ShapeDtypeStruct(mine.shape, F32)] * 2,
        compiler_params=params(0, 42 * MIB),
        name="both_tables",
    )(places, mine, other)


def body(
    inputs,
    text_states,
    adapter_index,
    norm_gains,
    norm_biases,
    self_in,
    self_out,
    cross_query,
    cross_text,
    cross_out,
    hidden_in,
    hidden_out,
    adapter_down,
    adapter_up,
    cotangent,
    *,
    sizes,
):
    seq, fsdp = sizes
    spot = lax.axis_index("seq")
    first_here = spot == 0
    there = (seq - 1) - spot
    local = self_in.shape[0]
    depth = hidden_out.shape[0] // seq
    pair = seq == 2 and depth % local == 0 and fsdp % run_length(local) == 0
    model = inputs.shape[2]
    rows = inputs.shape[1]
    frames = rows * seq
    wide = model // seq
    hidden_all = hidden_in.shape[1]
    hidden = hidden_all // seq
    adapters, rank, piece = adapter_down.shape
    total = piece * fsdp

    blocks = max(rows // 256, 1)
    size = rows // blocks

    def swap(value):
        return lax.ppermute(value, "seq", [(0, 1), (1, 0)])

    def pick(value, axis, extent, which=None):
        return lax.dynamic_slice_in_dim(value, (spot if which is None else which) * extent, extent, axis)

    def ordered(mine, other):
        return jnp.where(first_here, mine, other), jnp.where(first_here, other, mine)

    def gather(value, axis):
        if pair:
            return jnp.concatenate(ordered(value, swap(value)), axis)
        return lax.all_gather(value, "seq", axis=axis, tiled=True)

    def after(value, *others):
        return lax.optimization_barrier((value,) + others)[0]

    def put(value, axis):
        shape = list(value.shape)
        shape[axis] = seq
        return lax.dynamic_update_slice_in_dim(jnp.zeros(shape, value.dtype), value, spot, axis)

    def own_columns(matrix, parts):
        return [pick(matrix[:, at * model : (at + 1) * model], 1, wide) for at in range(parts)]

    def flat_down(grads, parts):
        return jnp.concatenate([grads[at * rank : (at + 1) * rank] for at in range(parts)], 1)

    def flat_upper(own):
        return put(jnp.stack(own, 1)[:, :, None], 2).reshape(rank, len(own) * model)

    halved = [pick(item, 1, wide) if pair else item for item in (self_out, cross_query)]
    first = [cross_out] + own_columns(cross_text, 2) + halved + own_columns(self_in, 3)
    edges = [0]
    for item in first:
        edges.append(edges[-1] + item.shape[1])
    start_in, start_text = edges[5], edges[1]
    packed = lax.all_gather(jnp.concatenate(first, 1), "fsdp", axis=0, tiled=True)
    squares_plan = ((edges[3], None), (edges[4], None), (edges[0], None))
    if pair:
        squares_plan = ((edges[3], 1), (edges[4], 3)) + squares_plan[2:]
    core = lax.rem(lax.axis_index("fsdp"), 2)
    where_here = jnp.stack([spot, there, core, 1 - core]).astype(jnp.int32)
    if pair:
        folds = depth // local
        plan = (fsdp, seq, folds, local)
        own_units = partial(take_units, plan, where_here)
        packed_feed = lax.all_gather(own_units(hidden_in, hidden_out), "fsdp", axis=0, tiled=True)

        def feed_weights(block):
            per = model // block
            return (
                packed_feed,
                pl.BlockSpec((model, block), lambda at: (0, at)),
                packed_feed,
                pl.BlockSpec((block, model), lambda at: (at % per, folds + at // per)),
            )
    else:

        def own_units(matrix):
            kept = lax.dynamic_index_in_dim(matrix.reshape(-1, fsdp, seq, depth), spot, 2, False)
            return kept.reshape(-1, hidden)

        def all_units(matrix):
            return put(matrix.reshape(-1, fsdp, 1, depth), 2).reshape(-1, hidden_all)

        whole_in = lax.all_gather(own_units(hidden_in), "fsdp", axis=0, tiled=True)
        whole_out = lax.all_gather(pick(hidden_out, 0, depth), "fsdp", axis=0, tiled=True)

        def feed_weights(block):
            return (
                whole_in,
                pl.BlockSpec((model, block), lambda at: (0, at)),
                whole_out,
                pl.BlockSpec((block, model), lambda at: (at, 0)),
            )

    index_all = lax.all_to_all(jnp.broadcast_to(adapter_index, (fsdp,)), "fsdp", 0, 0, tiled=True)
    if pair:
        table = jnp.where(first_here, adapter_down, adapter_up)
        mine = join_pieces(lax.all_to_all(jnp.take(table, index_all, axis=0), "fsdp", 0, 0, tiled=True))
        down_all, upper_all = ordered(mine, swap(mine))
    else:
        table = jnp.concatenate([adapter_down, adapter_up], 1)
        chosen = join_pieces(lax.all_to_all(jnp.take(table, index_all, axis=0), "fsdp", 0, 0, tiled=True))
        down_all, upper_all = chosen[:rank], chosen[rank:]
    in_cuts = [0, 3 * model, 4 * model, 5 * model, 7 * model, 8 * model, 9 * model, 9 * model + hidden_all]
    out_cuts = [0, 3 * model, 4 * model, 5 * model, 7 * model, 8 * model, 8 * model + hidden_all, 9 * model + hidden_all]
    downs = [down_all[:, in_cuts[at] : in_cuts[at + 1]] for at in range(7)]
    uppers = [upper_all[:, out_cuts[at] : out_cuts[at + 1]] for at in range(7)]

    def part_down(matrix, parts):
        return jnp.concatenate([matrix[:, at * model : (at + 1) * model] for at in range(parts)], 0)

    def part_upper(matrix, parts):
        own = own_columns(matrix, parts)
        return jnp.stack(
            [jnp.pad(item, ((at * rank, (parts - 1 - at) * rank), (0, 0))) for at, item in enumerate(own)], 0
        )

    units = own_units(jnp.concatenate([uppers[5], downs[6]], 0))
    feed_adapters = (downs[5], units[:rank], units[rank:], uppers[6])
    square_adapters = jnp.concatenate([downs[1], uppers[1], downs[2], uppers[2], downs[4], uppers[4]], 0)
    down_qkv, upper_qkv = part_down(downs[0], 3), part_upper(uppers[0], 3)
    down_text, upper_text = part_down(downs[3], 2), part_upper(uppers[3], 2)
    flat_text = jnp.concatenate([upper_text[0], upper_text[1]], 1)

    frames_in = inputs[0]
    cot = cotangent[0]
    if pair:
        frames_parts = [frames_in, swap(frames_in)]
        cot_other = swap(after(cot, frames_parts[1]))
    else:
        frames_parts = [lax.all_gather(frames_in, "seq", axis=0, tiled=True)]
    norm_places = where_here if pair else jnp.zeros((4,), jnp.int32)
    if pair:
        frames_parts[1] = after(frames_parts[1], cot_other, units)
    normed1, lat_qkv = norm_project(norm_places, frames_parts, norm_gains[0:1], norm_biases[0:1], down_qkv)
    packed = after(packed, normed1)
    sources = [packed]
    if pair:
        half = model // 2
        cut = [lax.dynamic_slice(packed, (core * half, at), (half, wide)) for at in edges[3:5]]
        straight = [swap(item) for item in cut]
        normed1 = after(normed1, *cut)
    triple = qkv_project(normed1, lat_qkv, upper_qkv, packed, start_in, 3 * wide)
    padded = -(-wide // LANES) * LANES
    if padded != wide:
        triple = jnp.pad(triple.reshape(frames, 3, wide), ((0, 0), (0, 0), (0, padded - wide)))
        triple = triple.reshape(frames, 3 * padded)
    text = after(text_states[0], triple)
    w_text = packed[:, start_text : start_text + 2 * wide]
    lat_text = mm_nt(text, down_text).astype(BF)
    memory = (mm(text, w_text) + mm(lat_text, flat_text)).astype(BF)
    head_out, probs, *leaving = attend(where_here, [size] * blocks if pair else [], after(triple, memory), padded)

    memory_all = gather(memory.reshape(-1, 2, wide), 2)
    keys, values = memory_all[:, 0], memory_all[:, 1]

    constants = (sources, squares_plan, square_adapters, norm_gains, norm_biases, keys, values)
    if pair:
        received = [swap(leaving[0])]
        for item in leaving[1:]:
            received.append(swap(after(item, received[-1])))
        neighbours = [(at, at ^ 1) for at in range(fsdp)]
        for item in straight:
            sources += [item, lax.ppermute(after(item, received[0], memory_all), "fsdp", neighbours)]
    else:
        natural = lax.all_to_all(head_out[:, :wide], "seq", split_axis=0, concat_axis=1, tiled=True)
    made = []
    for at in range(blocks):
        if pair:
            own, spec, others = head_out, (size, wide), [received[at]]
        else:
            own, spec, others = natural, (size, model), []
        ready = after(frames_in, made[-1][7]) if made else frames_in
        made.append(middle(where_here if pair else jnp.zeros((4,), jnp.int32), own, spec, others, ready, at, blocks, *constants))
    normed3 = [item[7] for item in made]
    resid2 = [item[6] for item in made]

    feed_tail = feed_adapters + (feed_weights, hidden)
    if pair:
        others = [swap(item) for item in normed3]
        theirs, gu_more, out_more = [], [], []
        for at in range(blocks):
            ready = after(others[at], theirs[-1][0]) if at else others[at]
            theirs.append(feed_forward([ready], [], cot_other, at, *feed_tail, BF))
            gu_more.append(swap(after(theirs[at][1], *gu_more[-1:])))
        ours = feed_forward([after(normed3[0], theirs[-1][1])] + normed3[1:], resid2, cot, 0, *feed_tail, F32)
        for at in range(blocks):
            behind = [ours[0]] + out_more[-1:] if at else [theirs[-1][0], gu_more[0]]
            out_more.append(swap(after(theirs[at][0], *behind)))
        gu = ours[blocks : 2 * blocks]
        feed_grads = [ours[2 * blocks :]] + [item[2:] for item in theirs]
    else:
        wide_in = gather(jnp.concatenate(normed3, 0), 0)
        all_out = feed_forward([wide_in], [], gather(cot, 0), 0, *feed_tail, F32)
        summed = [
            lax.psum_scatter(item.astype(BF), "seq", scatter_dimension=0, tiled=True) for item in all_out[:2]
        ]
        output = (jnp.concatenate(resid2, 0) + summed[0].astype(F32)).astype(BF)
        gu = [summed[1][at * size : (at + 1) * size] for at in range(blocks)]
        gu_more = [jnp.zeros_like(item) for item in gu]
        feed_grads = [all_out[2:]]

    pieces, resid1_grads, memory_parts, square_parts = [], [], [], []
    for at in range(blocks):
        gu_here = gu[at] if at == 0 else after(gu[at], result[-3])
        kept = made[at][:7] + made[at][8:9]
        result = middle_back(
            where_here, 2 if pair else 1, at, cot, gu_here, gu_more[at],
            kept, sources, squares_plan, square_adapters, norm_gains, keys, values,
        )
        if pair:
            waited = [pieces[-1][1]] if at else []
            if at == blocks - 1:
                memory_part = sum(memory_parts, result[-2]).astype(BF)
                memory_other = swap(after(pick(memory_part, 2, wide, there), *out_more))
                waited.append(memory_other)
            pieces.append((result[0], swap(after(result[1], *waited) if waited else result[1])))
        else:
            pieces.append(result[0])
        resid1_grads.append(result[-3])
        memory_parts.append(result[-2])
        square_parts.append(result[-1])
    resid1_grad = jnp.concatenate(resid1_grads, 0)
    square_grads = sum(square_parts[1:], square_parts[0])

    if pair:
        early, early_leaving, text_low = collect(
            plan, where_here, memory_parts, square_parts, feed_grads, memory_other, lat_text, flat_text, down_text,
            text_states[0], packed, start_text,
        )
        grad_pieces = [item[0] for item in pieces] + [item[1] for item in pieces]
    else:
        head_grad = lax.all_to_all(jnp.concatenate(pieces, 0), "seq", split_axis=1, concat_axis=0, tiled=True)
        grad_pieces = [jnp.pad(head_grad, ((0, 0), (0, padded - wide)))]
    triple_grad = attend_back(where_here, triple, head_out, grad_pieces, probs, padded)[:, :, :wide]
    if pair:
        early_other = swap(after(early_leaving, pieces[-1][1]))
        text_other = swap(after(text_low, early_other, triple_grad))
        glat_qkv, late, late_leaving = qkv_grads(
            where_here, after(triple_grad, early_other), normed1, lat_qkv, upper_qkv
        )
        late_other = swap(late_leaving)
    else:
        glat_qkv = sum(mm_nt(triple_grad[at], upper_qkv[at]) for at in range(3)).astype(BF)
        gdown_qkv = mm_tn(glat_qkv, normed1)
        gup_qkv = [mm_tn(lat_qkv[:, at * rank : (at + 1) * rank], triple_grad[at]) for at in range(3)]
    back = partial(qkv_back, gradient=triple_grad, glat=glat_qkv, down=down_qkv, packed=packed, start=start_in)
    if pair:
        for_them = back(after(there, early_other, text_other)[None], rows, kind=BF)
        for_us = back(after(spot, for_them, *out_more)[None], rows, kind=F32)
        input_grad = last_norm(frames_in, for_us, swap(for_them), norm_gains[0:1], resid1_grads)
        output = jnp.concatenate(
            [(after(item, for_them) + other.astype(F32)).astype(BF) for item, other in zip(ours[:blocks], out_more)], 0
        )
    else:
        full = back(jnp.zeros((1,), jnp.int32), frames, kind=BF)
        normed1_grad = lax.psum_scatter(full, "seq", scatter_dimension=0, tiled=True).astype(F32)
        resid1_grad = jnp.concatenate(resid1_grads, 0)
        input_grad = resid1_grad + norm_back(frames_in.astype(F32), norm_gains[0:1], normed1_grad)

    selector = (index_all[None, :] == jnp.arange(adapters, dtype=jnp.int32)[:, None]).astype(BF)

    def by_adapter(sent, *others):
        received = lax.all_to_all(sent, "fsdp", 0, 0, tiled=True)
        chooser = after(selector, *others) if others else selector
        return jnp.einsum("ac,crw->arw", chooser, received, preferred_element_type=F32)

    if pair:
        shares = by_adapter(split_sums([after(late, for_them), late_other, early, early_other], fsdp)).astype(BF)
        grad_down, grad_up = both_tables(where_here, after(shares, input_grad), swap(after(shares, for_us)))
        text_total = text_low.astype(F32) + text_other.astype(F32)
    else:
        memory_part = sum(memory_parts[1:], memory_parts[0]).astype(BF)
        memory_grad = lax.psum_scatter(memory_part, "seq", scatter_dimension=2, tiled=True)
        memory_flat = jnp.concatenate([memory_grad[0], memory_grad[1]], 1)
        glat_text = mm_nt(memory_flat, flat_text).astype(BF)
        gup_text = mm_tn(lat_text, memory_flat)
        gdown_text = mm_tn(glat_text, text)
        text_low = (mm_nt(memory_flat, w_text) + mm(glat_text, down_text)).astype(BF)
        own_text = [gup_text[at * rank : (at + 1) * rank, at * wide : (at + 1) * wide] for at in range(2)]
        gdown_in, gup_in, gdown_out, gup_out = feed_grads[0]
        square_grads = sum(square_parts[1:], square_parts[0])
        squares = [square_grads[rank * at : rank * (at + 1)] for at in range(6)]
        down_sent = [flat_down(gdown_qkv, 3), squares[0], squares[2], flat_down(gdown_text, 2), squares[4], gdown_in]
        upper_sent = [flat_upper(gup_qkv), squares[1], squares[3], flat_upper(own_text), squares[5]]
        down_sent = jnp.concatenate(down_sent + [all_units(gdown_out)], 1)
        upper_sent = jnp.concatenate(upper_sent + [all_units(gup_in), gup_out], 1)
        sent = jnp.concatenate([down_sent, upper_sent], 0).astype(BF).reshape(2 * rank, fsdp, piece).transpose(1, 0, 2)
        shares = lax.psum(by_adapter(sent).astype(BF), "seq")
        grad_down, grad_up = shares[:, :rank], shares[:, rank:]
        text_total = lax.psum(text_low, "seq").astype(F32)
    return (output[None], input_grad[None], text_total[None], grad_down.astype(F32), grad_up.astype(F32))


def solution(mesh):
    return jax.shard_map(
        partial(body, sizes=(mesh.shape["seq"], mesh.shape["fsdp"])),
        mesh=mesh,
        in_specs=(
            P("fsdp", "seq", None),
            P("fsdp", None, None),
            P("fsdp"),
            P(),
            P(),
            P("fsdp", None),
            P("fsdp", None),
            P("fsdp", None),
            P("fsdp", None),
            P("fsdp", None),
            P("fsdp", None),
            P("fsdp", None),
            P(None, None, "fsdp"),
            P(None, None, "fsdp"),
            P("fsdp", "seq", None),
        ),
        out_specs=(
            P("fsdp", "seq", None),
            P("fsdp", "seq", None),
            P("fsdp", None, None),
            P(None, None, "fsdp"),
            P(None, None, "fsdp"),
        ),
        check_vma=False,
    )
```

```python
from functools import partial

import jax
import jax.numpy as jnp
from jax import lax
from jax.experimental import pallas as pl
from jax.experimental.pallas import tpu as pltpu
from jax.sharding import PartitionSpec as P

HEAD = 64
LANES = 128
QB = 256
BF = jnp.bfloat16
F32 = jnp.float32
SCALE = float(HEAD) ** (-0.5)
SQRT_HALF = 0.7071067811865476
INV_SQRT_2PI = 0.3989422804014327
MIB = 1024 * 1024
VMEM_LIMIT = 60 * MIB
COST = 1.0
FEED_BLOCK = 512


def mm(a, b):
    return lax.dot_general(a, b, (((1,), (0,)), ((), ())), preferred_element_type=F32)


def mm_nt(a, b):
    return lax.dot_general(a, b, (((1,), (1,)), ((), ())), preferred_element_type=F32)


def mm_tn(a, b):
    return lax.dot_general(a, b, (((0,), (0,)), ((), ())), preferred_element_type=F32)


def norm_stats(values):
    centered = values - jnp.mean(values, -1, keepdims=True)
    variance = jnp.mean(centered * centered, -1, keepdims=True)
    inverse = lax.rsqrt(variance + 1e-05)
    return centered * inverse, inverse


def layer_norm(values, gains, biases):
    unit, _ = norm_stats(values)
    return unit * gains + biases


def norm_back(values, gains, gradient):
    unit, inverse = norm_stats(values)
    scaled = gradient * gains
    mean_one = jnp.mean(scaled, -1, keepdims=True)
    mean_two = jnp.mean(scaled * unit, -1, keepdims=True)
    return inverse * (scaled - mean_one - unit * mean_two)


def whole(shape):
    return pl.BlockSpec(shape, lambda *_: (0,) * len(shape))


def once(shape):
    return pl.BlockSpec(shape, lambda *_: (0,) * len(shape), pipeline_mode=pl.Buffered(1))


def params(count=1, limit=None):
    return pltpu.CompilerParams(
        dimension_semantics=("arbitrary",) * count if count else None, vmem_limit_bytes=limit or VMEM_LIMIT
    )


def cost(flops, moved, special=0):
    return pl.CostEstimate(
        flops=int(flops * COST), bytes_accessed=int(moved * COST), transcendentals=int(special * COST)
    )


def window(packed, start, width, rows=None, steps=1, step=0):
    block = width // steps
    rows = packed.shape[0] if rows is None else rows
    if start % block == 0 and block % LANES == 0:
        base = start // block
        return packed, pl.BlockSpec((rows, block), lambda *at: (0, base + (at[step] if steps > 1 else 0)))
    return packed[:, start : start + width], pl.BlockSpec(
        (rows, block), lambda *at: (0, at[step] if steps > 1 else 0)
    )


def norm_kernel(place_ref, *refs):
    count = len(refs) - 5
    parts, (gain_ref, bias_ref, down_ref, normed_ref, lat_ref) = refs[:count], refs[count:]
    step = 128
    for index, part_ref in enumerate(parts):
        base = place_ref[index] * part_ref.shape[0]

        def some(at, carry):
            rows = pl.ds(pl.multiple_of(at * step, step), step)
            into = pl.ds(pl.multiple_of(base + at * step, step), step)
            normed = layer_norm(part_ref[rows, :].astype(F32), gain_ref[...], bias_ref[...]).astype(BF)
            normed_ref[into, :] = normed
            lat_ref[into, :] = mm_nt(normed, down_ref[...]).astype(BF)
            return carry

        lax.fori_loop(0, part_ref.shape[0] // step, some, 0)


def smem():
    return pl.BlockSpec(memory_space=pltpu.SMEM)


def norm_project(places, parts, gains, biases, down):
    model = parts[0].shape[1]
    frames = sum(part.shape[0] for part in parts)
    ranks = down.shape[0]
    return pl.pallas_call(
        norm_kernel,
        in_specs=[smem()] + [whole(item.shape) for item in parts + [gains, biases, down]],
        out_specs=[whole((frames, model)), whole((frames, ranks))],
        out_shape=[jax.ShapeDtypeStruct((frames, model), BF), jax.ShapeDtypeStruct((frames, ranks), BF)],
        grid=(1,),
        compiler_params=params(1),
        cost_estimate=cost(2 * frames * model * ranks, 4 * frames * model),
        name="norm_project",
    )(places, *parts, gains, biases, down)


def qkv_kernel(normed_ref, lat_ref, up_ref, w_ref, out_ref):
    step = 256

    def some(at, carry):
        rows = pl.ds(pl.multiple_of(at * step, step), step)
        out_ref[rows, :] = (mm(normed_ref[rows, :], w_ref[...]) + mm(lat_ref[rows, :], up_ref[...])).astype(BF)
        return carry

    lax.fori_loop(0, normed_ref.shape[0] // step, some, 0)


def qkv_project(normed, latent, up, packed, start, width):
    row_count, model = normed.shape
    ranks = latent.shape[1]
    steps = 3 if (width // 3) % LANES == 0 else 1
    operand, spec = window(packed, start, width, steps=steps)
    block = width // steps
    if steps == 3:
        up_spec = pl.BlockSpec((None, ranks, block), lambda at: (at, 0, 0))
    else:
        up = up.transpose(1, 0, 2).reshape(ranks, width)
        up_spec = whole(up.shape)
    return pl.pallas_call(
        qkv_kernel,
        grid=(steps,),
        in_specs=[whole(normed.shape), whole(latent.shape), up_spec, spec],
        out_specs=pl.BlockSpec((row_count, block), lambda at: (0, at)),
        out_shape=jax.ShapeDtypeStruct((row_count, width), BF),
        compiler_params=params(1, 42 * MIB),
        cost_estimate=cost(2 * row_count * model * width, 2 * (row_count + width) * model),
        name="qkv_project",
    )(normed, latent, up, operand)


def tri_start(at):
    return QB * at * (at + 1) // 2


def attend_kernel(place_ref, q_ref, k_ref, v_ref, out_ref, prob_ref, *refs):
    sent, (val_t_ref, out_t_ref) = refs[:-2], refs[-2:]
    frames = q_ref.shape[0]
    lane = lax.broadcasted_iota(jnp.int32, (1, LANES), 1) // HEAD
    val_t_ref[...] = v_ref[...].T
    square = (QB, QB)
    keep_tri = lax.broadcasted_iota(jnp.int32, square, 0) <= lax.broadcasted_iota(jnp.int32, square, 1)

    def scores(half, at):
        stop = (at + 1) * QB
        query = q_ref[at * QB : stop, :] * jnp.where(lane == half, SCALE, 0.0).astype(BF)
        last = jnp.where(keep_tri, mm_nt(k_ref[stop - QB : stop, :], query), -1e30)
        if at == 0:
            return last
        return jnp.concatenate([mm_nt(k_ref[0 : stop - QB, :], query), last], 0)

    turns = [(half, at) for at in range(frames // QB) for half in range(2)]
    score = scores(*turns[0])
    for index, (half, at) in enumerate(turns):
        stop = (at + 1) * QB
        own = slice(half * HEAD, (half + 1) * HEAD)
        later = scores(*turns[index + 1]) if index + 1 < len(turns) else None
        raised = jnp.exp(score - jnp.max(score, 0, keepdims=True))
        prob = (raised * (1.0 / jnp.sum(raised, 0, keepdims=True))).astype(BF)
        prob_ref[half, tri_start(at) : tri_start(at) + stop, :] = prob
        out_t_ref[own, at * QB : stop] = mm(val_t_ref[own, 0:stop], prob)
        score = later
    out_ref[...] = out_t_ref[...].T.astype(BF)
    for index, sent_ref in enumerate(sent):
        size = sent_ref.shape[0]
        at = place_ref[1] * len(sent) + index
        sent_ref[...] = out_ref[pl.ds(pl.multiple_of(at * size, size), size), :]


def pair_specs(frames, width):
    pairs = width // LANES
    return [pl.BlockSpec((frames, LANES), lambda at, part=part: (0, part * pairs + at)) for part in range(3)]


def attend(places, sizes, triple, width):
    frames = triple.shape[0]
    pairs = width // LANES
    tri = tri_start(frames // QB)
    return pl.pallas_call(
        attend_kernel,
        grid=(pairs,),
        in_specs=[smem()] + pair_specs(frames, width),
        out_specs=[
            pl.BlockSpec((frames, LANES), lambda at: (0, at)),
            pl.BlockSpec((2, tri, QB), lambda at: (at, 0, 0)),
        ]
        + [pl.BlockSpec((size, LANES), lambda at: (0, at)) for size in sizes],
        out_shape=[
            jax.ShapeDtypeStruct((frames, width), BF),
            jax.ShapeDtypeStruct((2 * pairs, tri, QB), BF),
        ]
        + [jax.ShapeDtypeStruct((size, width), BF) for size in sizes],
        scratch_shapes=[pltpu.VMEM((LANES, frames), BF), pltpu.VMEM((LANES, frames), F32)],
        compiler_params=params(1),
        cost_estimate=cost(
            8 * tri * QB * HEAD * pairs, 2 * (4 * frames * width + 2 * pairs * tri * QB), 2 * pairs * tri * QB
        ),
        name="attend",
    )(places, triple, triple, triple)


def attend_back_kernel(place_ref, q_ref, k_ref, v_ref, out_ref, prob_ref, *refs):
    pieces, (back_ref, grad_ref, key_t_ref, dq_t_ref, dk_acc, dv_acc) = refs[:-6], refs[-6:]
    frames = q_ref.shape[0]
    for index, piece_ref in enumerate(pieces):
        size = piece_ref.shape[0]
        count = max(len(pieces) // 2, 1)
        at = place_ref[index // count] * count + index % count if len(pieces) > 1 else 0
        grad_ref[pl.ds(pl.multiple_of(at * size, size), size), :] = piece_ref[...]
    lane = lax.broadcasted_iota(jnp.int32, (1, LANES), 1) // HEAD
    key_t_ref[...] = k_ref[...].T
    dk_acc[...] = jnp.zeros_like(dk_acc)
    dv_acc[...] = jnp.zeros_like(dv_acc)
    turns = [(half, at) for at in range(frames // QB) for half in range(2)]

    def start(half, at):
        rows = slice(at * QB, (at + 1) * QB)
        grad = grad_ref[rows, :] * jnp.where(lane == half, 1.0, 0.0).astype(BF)
        return grad, mm_nt(v_ref[0 : (at + 1) * QB, :], grad)

    ready = start(*turns[0])
    for index, (half, at) in enumerate(turns):
        stop = (at + 1) * QB
        rows = slice(at * QB, stop)
        own = slice(half * HEAD, (half + 1) * HEAD)
        grad, prob_grad = ready
        if half == 0:
            product = (out_ref[rows, :].astype(F32) * grad_ref[rows, :].astype(F32)).T
        if index + 1 < len(turns):
            ready = start(*turns[index + 1])
        query = q_ref[rows, :] * jnp.where(lane == half, SCALE, 0.0).astype(BF)
        delta = jnp.sum(product[own, :], 0, keepdims=True)
        prob = prob_ref[half, tri_start(at) : tri_start(at) + stop, :]
        dv_acc[0:stop, :] += mm(prob, grad)
        score_grad = (prob.astype(F32) * (prob_grad - delta)).astype(BF)
        dk_acc[0:stop, :] += mm(score_grad, query)
        dq_t_ref[own, rows] = mm(key_t_ref[own, 0:stop], score_grad)
    back_ref[0] = (dq_t_ref[...].T * SCALE).astype(BF)
    back_ref[1] = dk_acc[...].astype(BF)
    back_ref[2] = dv_acc[...].astype(BF)


def attend_back(places, triple, attended, pieces, probs, width):
    frames = triple.shape[0]
    pairs = width // LANES
    tri = tri_start(frames // QB)
    column = pl.BlockSpec((frames, LANES), lambda at: (0, at))
    return pl.pallas_call(
        attend_back_kernel,
        grid=(pairs,),
        in_specs=[smem()]
        + pair_specs(frames, width)
        + [column, pl.BlockSpec((2, tri, QB), lambda at: (at, 0, 0))]
        + [pl.BlockSpec((piece.shape[0], LANES), lambda at: (0, at)) for piece in pieces],
        out_specs=pl.BlockSpec((3, frames, LANES), lambda at: (0, 0, at)),
        out_shape=jax.ShapeDtypeStruct((3, frames, width), BF),
        scratch_shapes=[
            pltpu.VMEM((frames, LANES), BF),
            pltpu.VMEM((LANES, frames), BF),
            pltpu.VMEM((LANES, frames), F32),
            pltpu.VMEM((frames, LANES), F32),
            pltpu.VMEM((frames, LANES), F32),
        ],
        compiler_params=params(1, 42 * MIB),
        cost_estimate=cost(16 * tri * QB * HEAD * pairs, 2 * (8 * frames * width + 2 * pairs * tri * QB)),
        name="attend_back",
    )(places, triple, triple, triple, attended, probs, *pieces)


def feed_kernel(count, based, *refs):
    pieces, refs = refs[:count], refs[count:]
    bases, refs = refs[:based], refs[based:]
    cot_ref, down_in_ref, up_in_ref, down_out_ref, up_out_ref, w_in_ref, w_out_ref = refs[:7]
    out_refs, gu_refs, refs = refs[7 : 7 + count], refs[7 + count : 7 + 2 * count], refs[7 + 2 * count :]
    (
        gdown_in_ref, gup_in_ref, gdown_out_ref, gup_out_ref, normed_ref,
        out_acc, gu_acc, lat_in, glat_out, lat_acc, glat_acc, lat_t, glat_t,
    ) = refs
    at = pl.program_id(0)

    @pl.when(at == 0)
    def _():
        start = 0
        for piece_ref in pieces:
            normed_ref[start : start + piece_ref.shape[0], :] = piece_ref[...]
            start += piece_ref.shape[0]
        latent = mm_nt(normed_ref[...], down_in_ref[...]).astype(BF)
        glat = mm_nt(cot_ref[...], up_out_ref[...]).astype(BF)
        lat_in[...] = latent
        glat_out[...] = glat
        lat_t[...] = latent.astype(F32).T.astype(BF)
        glat_t[...] = glat.astype(F32).T.astype(BF)
        start = 0
        for base_ref in bases:
            out_acc[start : start + base_ref.shape[0], :] = base_ref[...]
            start += base_ref.shape[0]
        if not bases:
            out_acc[...] = jnp.zeros_like(out_acc)
        gu_acc[...] = jnp.zeros_like(gu_acc)
        lat_acc[...] = jnp.zeros_like(lat_acc)
        glat_acc[...] = jnp.zeros_like(glat_acc)

    w_in = w_in_ref[...]
    w_out = w_out_ref[...]
    pre = mm(normed_ref[...], w_in) + mm(lat_in[...], up_in_ref[...])
    act_grad = mm_nt(cot_ref[...], w_out) + mm(glat_out[...], down_out_ref[...])
    cdf = 0.5 * (1.0 + lax.erf(pre * SQRT_HALF))
    slope = cdf + pre * (jnp.exp(-0.5 * pre * pre) * INV_SQRT_2PI)
    act = (pre * cdf).astype(BF)
    pre_grad = (act_grad * slope).astype(BF)
    out_acc[...] += mm(act, w_out)
    gu_acc[...] += mm_nt(pre_grad, w_in)
    lat_acc[...] += mm_nt(act, down_out_ref[...])
    glat_acc[...] += mm_nt(pre_grad, up_in_ref[...])
    gup_in_ref[...] = mm(lat_t[...], pre_grad)
    gdown_out_ref[...] = mm(glat_t[...], act)

    @pl.when(at == pl.num_programs(0) - 1)
    def _():
        latent = lat_acc[...].astype(BF)
        glat = glat_acc[...].astype(BF)
        start = 0
        for out_ref, gu_ref in zip(out_refs, gu_refs):
            rows = slice(start, start + out_ref.shape[0])
            out_ref[...] = (out_acc[rows, :] + mm(latent[rows], up_out_ref[...])).astype(out_ref.dtype)
            gu_ref[...] = (gu_acc[rows, :] + mm(glat[rows], down_in_ref[...])).astype(gu_ref.dtype)
            start += out_ref.shape[0]
        gup_out_ref[...] = mm(latent.astype(F32).T.astype(BF), cot_ref[...])
        gdown_in_ref[...] = mm(glat.astype(F32).T.astype(BF), normed_ref[...])


def feed_forward(pieces, bases, cotangent, block_at, down_in, up_in, down_out, up_out, weights, hidden, kind):
    model = cotangent.shape[1]
    row_count = sum(item.shape[0] for item in pieces)
    rank = down_in.shape[0]
    block = FEED_BLOCK if hidden % FEED_BLOCK == 0 else hidden
    w_in, in_spec, w_out, out_spec = weights(block)
    main = pl.BlockSpec((row_count, model), lambda at: (block_at, 0))
    slim = pl.BlockSpec((rank, block), lambda at: (0, at))
    small = whole((rank, model))
    return pl.pallas_call(
        partial(feed_kernel, len(pieces), len(bases)),
        grid=(hidden // block,),
        in_specs=[once(item.shape) for item in pieces + bases]
        + [main, small, slim, slim, small, in_spec, out_spec],
        out_specs=[whole(item.shape) for item in pieces] * 2 + [small, slim, slim, small],
        out_shape=[jax.ShapeDtypeStruct(item.shape, kind) for item in pieces]
        + [jax.ShapeDtypeStruct(item.shape, BF) for item in pieces]
        + [
            jax.ShapeDtypeStruct((rank, model), F32),
            jax.ShapeDtypeStruct((rank, hidden), F32),
            jax.ShapeDtypeStruct((rank, hidden), F32),
            jax.ShapeDtypeStruct((rank, model), F32),
        ],
        scratch_shapes=[pltpu.VMEM((row_count, model), BF)]
        + [pltpu.VMEM((row_count, model), F32)] * 2
        + [pltpu.VMEM((row_count, rank), BF)] * 2
        + [pltpu.VMEM((row_count, rank), F32)] * 2
        + [pltpu.VMEM((rank, row_count), BF)] * 2,
        compiler_params=params(1),
        cost_estimate=cost(8 * row_count * model * hidden, 4 * hidden * model, 2 * row_count * hidden),
        name="feed_forward",
    )(*pieces, *bases, cotangent, down_in, up_in, down_out, up_out, w_in, w_out)


def spread_heads(rows_ref, into_ref, model):
    keys = rows_ref.shape[0]
    wide = 4 * HEAD
    row = lax.broadcasted_iota(jnp.int32, (4 * keys, wide), 0) // keys
    col = lax.broadcasted_iota(jnp.int32, (4 * keys, wide), 1) // HEAD
    mask = jnp.where(row == col, 1.0, 0.0).astype(BF)

    def some(group, carry):
        part = rows_ref[:, pl.ds(pl.multiple_of(group * wide, wide), wide)]
        into = pl.ds(pl.multiple_of(group * 4 * keys, 4 * keys), 4 * keys)
        into_ref[into, :] = jnp.concatenate([part] * 4, 0) * mask
        return carry

    lax.fori_loop(0, model // wide, some, 0)


def head_total(values, keys, reduce):
    split = values.reshape(4, keys, values.shape[1])
    return jnp.broadcast_to(reduce(split, 1, keepdims=True), split.shape).reshape(values.shape)


def each(count, step, work):
    def some(at, carry):
        work(pl.ds(pl.multiple_of(at * step, step), step))
        return carry

    lax.fori_loop(0, count // step, some, 0)


def pair_of(both, size):
    return [pl.ds(pl.multiple_of(both.start + at * size, size), size) for at in range(both.size // size)]


def weight_copies(plan, place_ref, sources, hold_ref, sem_ref):
    model = hold_ref.shape[1]
    groups = []
    for index, (start, extra) in enumerate(plan):
        if extra is None:
            parts = [slice(at * model // 2, (at + 1) * model // 2) for at in range(2)]
            pairs = [(sources[0].at[rows, pl.ds(start, model)], hold_ref.at[index, rows, :]) for rows in parts]
        else:
            half = model // 2
            here, there = [pl.ds(pl.multiple_of(place_ref[at] * half, half), half) for at in range(2)]
            pairs = [(sources[0].at[:, pl.ds(start, half)], hold_ref.at[index, :, here])]
            for at in range(2):
                rows = pl.ds(pl.multiple_of(place_ref[2 + at] * half, half), half)
                pairs.append((sources[extra + at], hold_ref.at[index, rows, there]))
        groups.append(
            [pltpu.make_async_copy(src, dst, sem_ref.at[index, at]) for at, (src, dst) in enumerate(pairs)]
        )
    return groups


def source_count(plan):
    return 1 + 2 * sum(extra is not None for _, extra in plan)


def start_all(copies):
    for copy in copies:
        copy.start()


def wait_all(copies):
    for copy in copies:
        copy.wait()


def middle_kernel(plan, place_ref, *refs):
    sources, refs = refs[: source_count(plan)], refs[source_count(plan) :]
    inputs_ref, adapt_ref, gain_ref, bias_ref, keys_ref, values_ref = refs[:6]
    pieces = refs[6:-20]
    away = refs[-20:-14]
    resid2_ref, normed3_ref, lat_ref, hold_ref, key_wide, value_wide, sem_ref = refs[-14:-7]
    kept, out_sem = refs[-7:-1], refs[-1]
    attended_ref, resid1_ref, normed2_ref, query_ref, probs_ref, crossed_ref = kept
    leaving = [pltpu.make_async_copy(kept[at], away[at], out_sem.at[at]) for at in range(6)]
    model = inputs_ref.shape[1]
    keys = keys_ref.shape[0]
    rows = inputs_ref.shape[0]
    wide = 4 * HEAD
    copies = weight_copies(plan, place_ref, sources, hold_ref, sem_ref)
    start_all(copies[0])
    for index, piece_ref in enumerate(pieces):
        size = piece_ref.shape[1]
        attended_ref[:, pl.ds(pl.multiple_of(place_ref[index] * size, size), size)] = piece_ref[...]
    spread_heads(keys_ref, key_wide, model)
    spread_heads(values_ref, value_wide, model)

    def adapted(moving_ref, index, store):
        latent = mm_nt(moving_ref[...], adapt_ref[32 * index : 32 * index + 16, :]).astype(BF)
        lat_ref[:, 16 * index : 16 * index + 16] = latent
        wait_all(copies[index])
        if index < 2:
            start_all(copies[index + 1])

        def some(cols):
            store(
                cols,
                mm(moving_ref[...], hold_ref[index, :, cols])
                + mm(latent, adapt_ref[32 * index + 16 : 32 * index + 32, cols]),
            )

        each(model, 512, some)

    def add_first(cols, value):
        resid1_ref[:, cols] = inputs_ref[:, cols].astype(F32) + value

    def add_second(cols, value):
        resid2_ref[:, cols] = resid1_ref[:, cols] + value

    def keep_query(cols, value):
        query_ref[:, cols] = value.astype(BF)

    def normed(values_at, into_ref, which):
        def some(part):
            into_ref[part, :] = layer_norm(
                values_at[part, :], gain_ref[which : which + 1, :], bias_ref[which : which + 1, :]
            ).astype(BF)

        each(rows, 128, some)

    def cross(both):
        groups = pair_of(both, wide)
        scores = [mm_nt(key_wide[lanes, :], query_ref[:, lanes]) * SCALE for lanes in groups]
        for lanes, score in zip(groups, scores):
            raised = jnp.exp(score - head_total(score, keys, jnp.max))
            prob = (raised / head_total(raised, keys, jnp.sum)).astype(BF)
            probs_ref[lanes, :] = prob
            crossed_ref[:, lanes] = mm_tn(prob, value_wide[lanes, :]).astype(BF)

    leaving[0].start()
    adapted(attended_ref, 0, add_first)
    leaving[1].start()
    normed(resid1_ref, normed2_ref, 1)
    leaving[2].start()
    adapted(normed2_ref, 1, keep_query)
    leaving[3].start()
    each(model, 6 * wide, cross)
    leaving[4].start()
    leaving[5].start()
    adapted(crossed_ref, 2, add_second)
    normed(resid2_ref, normed3_ref, 2)
    wait_all(leaving)


def middle(places, own, own_spec, others, inputs, at, blocks, sources, plan, adapters, gains, biases, keys, values):
    rows, model = own_spec[0], inputs.shape[1]
    spread = model // HEAD * keys.shape[0]
    shape = lambda kind, dims=(rows, model): jax.ShapeDtypeStruct(dims, kind)
    flat = lambda dims: pl.BlockSpec(dims, lambda _, ref: (0,) * len(dims))
    shapes = [shape(kind) for kind in (BF, F32, BF, BF)]
    shapes += [shape(BF, (spread, rows)), shape(BF), shape(F32), shape(BF), shape(BF, (rows, 48))]
    return pl.pallas_call(
        partial(middle_kernel, plan),
        grid_spec=pltpu.PrefetchScalarGridSpec(
            num_scalar_prefetch=1,
            grid=(1,),
            in_specs=[pl.BlockSpec(memory_space=pl.ANY)] * len(sources)
            + [pl.BlockSpec((rows, model), lambda _, ref: (at, 0))]
            + [flat(item.shape) for item in (adapters, gains, biases, keys, values)]
            + [pl.BlockSpec(own_spec, lambda _, ref: (ref[0] * blocks + at, 0) if others else (at, 0))]
            + [flat(item.shape) for item in others],
            out_specs=[pl.BlockSpec(memory_space=pl.ANY)] * 6 + [flat(item.shape) for item in shapes[6:]],
            scratch_shapes=[
                pltpu.VMEM((3, model, model), BF),
                pltpu.VMEM((spread, 4 * HEAD), BF),
                pltpu.VMEM((spread, 4 * HEAD), BF),
                pltpu.SemaphoreType.DMA((3, 3)),
            ]
            + [pltpu.VMEM(item.shape, item.dtype) for item in shapes[:6]]
            + [pltpu.SemaphoreType.DMA((6,))],
        ),
        out_shape=shapes,
        compiler_params=params(),
        cost_estimate=cost(6 * rows * model * model, 6 * model * model + 24 * rows * model),
        name="middle",
    )(places, *sources, inputs, adapters, gains, biases, keys, values, own, *others)


def middle_back_kernel(plan, split, place_ref, *refs):
    sources, refs = refs[: source_count(plan)], refs[source_count(plan) :]
    cot_ref, gu_ref, more_ref = refs[:3]
    far = refs[3:9]
    resid2_ref, lat_ref, adapt_ref, gain_ref, keys_ref, values_ref = refs[9:15]
    kept, in_sem = refs[-7:-1], refs[-1]
    attended_ref, resid1_ref, normed2_ref, query_ref, probs_ref, crossed_ref = kept
    coming = [pltpu.make_async_copy(far[at], kept[at], in_sem.at[at]) for at in range(6)]
    refs = refs[15:-7]
    outs = refs[: 2 if split else 1]
    resid1_grad_ref, memory_ref, small_ref, hold_ref, key_wide, value_wide, work_ref, low_ref, sem_ref = refs[len(outs) :]
    rows, model = cot_ref.shape
    keys = keys_ref.shape[0]
    wide = 4 * HEAD
    copies = weight_copies(plan, place_ref, sources, hold_ref, sem_ref)
    start_all(copies[2])
    coming[5].start()
    spread_heads(keys_ref, key_wide, model)
    spread_heads(values_ref, value_wide, model)

    def first(part):
        gradient = gu_ref[part, :].astype(F32) + more_ref[part, :].astype(F32)
        value = cot_ref[part, :].astype(F32) + norm_back(resid2_ref[part, :], gain_ref[2:3, :], gradient)
        resid1_grad_ref[part, :] = value
        low_ref[part, :] = value.astype(BF)

    def second(part):
        value = resid1_grad_ref[part, :] + norm_back(resid1_ref[part, :], gain_ref[1:2, :], work_ref[part, :])
        resid1_grad_ref[part, :] = value
        low_ref[part, :] = value.astype(BF)

    def back(moving_ref, index, store):
        down = slice(32 * index, 32 * index + 16)
        upper = slice(32 * index + 16, 32 * index + 32)
        glat = mm_nt(low_ref[...], adapt_ref[upper, :]).astype(BF)
        glat_t = glat.astype(F32).T.astype(BF)
        lat_t = lat_ref[:, 16 * index : 16 * index + 16].astype(F32).T.astype(BF)
        wait_all(copies[index])
        if index == 2:
            wait_all(coming[5:])
            start_all(coming[2:5])
        if index == 1:
            wait_all(coming[2:3])
            start_all(coming[:2])
        if index == 0:
            wait_all(coming[:1])
        if index:
            start_all(copies[index - 1])

        def some(cols):
            small_ref[down, cols] = mm(glat_t, moving_ref[:, cols])
            small_ref[upper, cols] = mm(lat_t, low_ref[:, cols])
            store(cols, mm_nt(low_ref[...], hold_ref[index, cols, :]) + mm(glat, adapt_ref[down, cols]))

        each(model, 512, some)

    def keep(cols, value):
        work_ref[:, cols] = value

    def cross(both):
        groups = pair_of(both, wide)
        parts = [work_ref[:, lanes].astype(BF) for lanes in groups]
        prob_grads = [mm_nt(value_wide[lanes, :], part) for lanes, part in zip(groups, parts)]
        for lanes, part, prob_grad in zip(groups, parts, prob_grads):
            cross_one(lanes, part, prob_grad)

    def cross_one(lanes, part, prob_grad):
        prob = probs_ref[lanes, :]
        wide_prob = prob.astype(F32)
        weighted = wide_prob * prob_grad
        score_grad = (weighted - wide_prob * head_total(weighted, keys, jnp.sum)).astype(BF)
        low_ref[:, lanes] = (mm_tn(score_grad, key_wide[lanes, :]) * SCALE).astype(BF)
        key_full = mm(score_grad, query_ref[:, lanes])
        value_full = mm(prob, part)
        col = lax.broadcasted_iota(jnp.int32, (keys, wide), 1) // HEAD
        key_sum, value_sum = key_full[:keys], value_full[:keys]
        for head in range(1, 4):
            rows_at = slice(head * keys, (head + 1) * keys)
            key_sum = jnp.where(col == head, key_full[rows_at], key_sum)
            value_sum = jnp.where(col == head, value_full[rows_at], value_sum)
        memory_ref[0, :, lanes] = key_sum * SCALE
        memory_ref[1, :, lanes] = value_sum

    each(rows, 128, first)
    back(crossed_ref, 2, keep)
    wait_all(coming[3:5])
    each(model, 6 * wide, cross)
    back(normed2_ref, 1, keep)
    wait_all(coming[1:2])
    each(rows, 128, second)
    back(attended_ref, 0, keep)
    if split:
        size = outs[0].shape[1]
        for out_ref, index in zip(outs, range(2)):
            out_ref[...] = work_ref[:, pl.ds(pl.multiple_of(place_ref[index] * size, size), size)].astype(BF)
    else:
        outs[0][...] = work_ref[...].astype(BF)


def middle_back(places, parts, at, cotangent, gu, more, kept, sources, plan, adapters, gains, keys, values):
    model = cotangent.shape[1]
    rows = kept[0].shape[0]
    spread = model // HEAD * keys.shape[0]
    flat = lambda dims: pl.BlockSpec(dims, lambda _, ref: (0,) * len(dims))
    block = pl.BlockSpec((rows, model), lambda _, ref: (at, 0))
    shapes = [jax.ShapeDtypeStruct((rows, model // parts), BF)] * parts + [
        jax.ShapeDtypeStruct((rows, model), F32),
        jax.ShapeDtypeStruct((2,) + keys.shape, F32),
        jax.ShapeDtypeStruct(adapters.shape, F32),
    ]
    return pl.pallas_call(
        partial(middle_back_kernel, plan, parts == 2),
        grid_spec=pltpu.PrefetchScalarGridSpec(
            num_scalar_prefetch=1,
            grid=(1,),
            in_specs=[pl.BlockSpec(memory_space=pl.ANY)] * len(sources)
            + [block, flat(gu.shape), flat(more.shape)]
            + [pl.BlockSpec(memory_space=pl.ANY)] * 6
            + [flat(item.shape) for item in kept[6:]]
            + [flat(item.shape) for item in (adapters, gains, keys, values)],
            out_specs=[flat(item.shape) for item in shapes],
            scratch_shapes=[
                pltpu.VMEM((3, model, model), BF),
                pltpu.VMEM((spread, 4 * HEAD), BF),
                pltpu.VMEM((spread, 4 * HEAD), BF),
                pltpu.VMEM((rows, model), F32),
                pltpu.VMEM((rows, model), BF),
                pltpu.SemaphoreType.DMA((3, 3)),
            ]
            + [pltpu.VMEM(item.shape, item.dtype) for item in kept[:6]]
            + [pltpu.SemaphoreType.DMA((6,))],
        ),
        out_shape=shapes,
        compiler_params=params(),
        cost_estimate=cost(6 * rows * model * model, 6 * model * model + 36 * rows * model),
        name="middle_back",
    )(places, *sources, cotangent, gu, more, *kept, adapters, gains, keys, values)


def qkv_grads_kernel(
    place_ref, grad_ref, normed_ref, lat_ref, up_ref, glat_ref, mine_ref, theirs_ref, glat_acc, gup_acc, down_acc,
    down_all, upper_all,
):
    at = pl.program_id(0)
    gradient = grad_ref[...]
    rank = mine_ref.shape[0]
    model = normed_ref.shape[1]
    width = gradient.shape[1]
    gup_acc[...] = mm_tn(lat_ref[...], gradient)

    @pl.when(at == 0)
    def _():
        glat_acc[...] = jnp.zeros_like(glat_acc)
        upper_all[...] = jnp.zeros_like(upper_all)

    into = pl.ds(pl.multiple_of(at * model + place_ref[0] * width, LANES), width)
    upper_all[:, into] = gup_acc[pl.ds(pl.multiple_of(at * rank, rank), rank), :].astype(BF)
    glat_acc[...] += mm_nt(gradient, up_ref[...])

    @pl.when(at == pl.num_programs(0) - 1)
    def _():
        low = glat_acc[...].astype(BF)
        glat_ref[...] = low
        down_acc[...] = mm_tn(low, normed_ref[...])
        for part in range(3):
            down_all[:, part * model : (part + 1) * model] = down_acc[part * rank : (part + 1) * rank, :].astype(BF)
        share(place_ref, down_all, upper_all, mine_ref, theirs_ref)


def share(place_ref, down_all, upper_all, mine_ref, theirs_ref):
    @pl.when(place_ref[0] == 0)
    def _():
        mine_ref[...] = down_all[...]
        theirs_ref[...] = upper_all[...]

    @pl.when(place_ref[0] != 0)
    def _():
        mine_ref[...] = upper_all[...]
        theirs_ref[...] = down_all[...]


def qkv_grads(places, gradient, normed, latent, up):
    frames, model = normed.shape
    parts, ranks, width = up.shape
    rank = ranks // parts
    table = jax.ShapeDtypeStruct((rank, parts * model), BF)
    return pl.pallas_call(
        qkv_grads_kernel,
        grid=(parts,),
        in_specs=[
            smem(),
            pl.BlockSpec((None, frames, width), lambda at: (at, 0, 0)),
            whole(normed.shape),
            whole(latent.shape),
            pl.BlockSpec((None, ranks, width), lambda at: (at, 0, 0)),
        ],
        out_specs=[whole(latent.shape), whole(table.shape), whole(table.shape)],
        out_shape=[jax.ShapeDtypeStruct(latent.shape, BF), table, table],
        scratch_shapes=[
            pltpu.VMEM(latent.shape, F32),
            pltpu.VMEM((ranks, width), F32),
            pltpu.VMEM((ranks, model), F32),
            pltpu.VMEM(table.shape, BF),
            pltpu.VMEM(table.shape, BF),
        ],
        compiler_params=params(1, 42 * MIB),
        cost_estimate=cost(8 * frames * ranks * width * parts, 2 * frames * (model + parts * width)),
        name="qkv_grads",
    )(places, gradient, normed, latent, up)


def qkv_back_kernel(place_ref, grad_ref, glat_ref, down_ref, w_ref, gu_ref, gu_acc):
    at = pl.program_id(0)
    model = gu_ref.shape[1]
    last = pl.num_programs(0) - 1

    def some(cols):
        direct = mm_nt(grad_ref[...], w_ref[cols, :])

        @pl.when(at == 0)
        def _():
            gu_acc[:, cols] = direct + mm(glat_ref[...], down_ref[:, cols])

        @pl.when(jnp.logical_and(at > 0, at < last))
        def _():
            gu_acc[:, cols] += direct

        @pl.when(at == last)
        def _():
            gu_ref[:, cols] = (gu_acc[:, cols] + direct).astype(gu_ref.dtype)

    each(model, 512, some)


def qkv_back(place, row_count, gradient, glat, down, packed, start, kind):
    ranks, model = down.shape
    width = gradient.shape[2]
    if start % width == 0 and width % LANES == 0:
        weight, spec = packed, pl.BlockSpec((model, width), lambda at, ref: (0, start // width + at))
    else:
        weight = packed[:, start : start + 3 * width].reshape(model, 3, width).transpose(1, 0, 2)
        spec = pl.BlockSpec((None, model, width), lambda at, ref: (at, 0, 0))
    return pl.pallas_call(
        qkv_back_kernel,
        grid_spec=pltpu.PrefetchScalarGridSpec(
            num_scalar_prefetch=1,
            grid=(3,),
            in_specs=[
                pl.BlockSpec((None, row_count, width), lambda at, ref: (at, ref[0], 0)),
                pl.BlockSpec((row_count, ranks), lambda at, ref: (ref[0], 0)),
                pl.BlockSpec(down.shape, lambda at, ref: (0, 0)),
                spec,
            ],
            out_specs=pl.BlockSpec((row_count, model), lambda at, ref: (0, 0)),
            scratch_shapes=[pltpu.VMEM((row_count, model), F32)],
        ),
        out_shape=jax.ShapeDtypeStruct((row_count, model), kind),
        compiler_params=params(1, 42 * MIB),
        cost_estimate=cost(6 * row_count * model * width, 6 * model * width + 8 * row_count * model),
        name="qkv_back",
    )(place, gradient, glat, down, weight)


def last_norm_kernel(blocks, frames_ref, gradient_ref, gain_ref, *refs):
    pieces, grad_ref = refs[:-1], refs[-1]
    at = pl.program_id(0)
    back = norm_back(frames_ref[...].astype(F32), gain_ref[...], gradient_ref[...])
    for index, piece_ref in enumerate(pieces):

        @pl.when(at // blocks == index)
        def _(piece_ref=piece_ref):
            grad_ref[...] = back + piece_ref[...]


def last_norm(frames, gradient, gains, pieces):
    rows, model = frames.shape
    step = min(128, rows)
    blocks = pieces[0].shape[0] // step
    block = pl.BlockSpec((step, model), lambda at: (at, 0))

    def piece_spec(index):
        return pl.BlockSpec((step, model), lambda at: (jnp.clip(at - index * blocks, 0, blocks - 1), 0))

    return pl.pallas_call(
        partial(last_norm_kernel, blocks),
        grid=(rows // step,),
        in_specs=[block, block, whole(gains.shape)] + [piece_spec(index) for index in range(len(pieces))],
        out_specs=block,
        out_shape=jax.ShapeDtypeStruct((rows, model), F32),
        compiler_params=params(1, 42 * MIB),
        cost_estimate=cost(20 * rows * model, 16 * rows * model),
        name="last_norm",
    )(frames, gradient, gains, *pieces)


def run_length(size):
    count = 1
    while count * size % LANES:
        count *= 2
    return count


def join_kernel(pieces_ref, flat_ref):
    count, _, size = pieces_ref.shape
    run = run_length(size)

    def some(at, carry):
        parts = [pieces_ref[at * run + index] for index in range(run)]
        into = pl.ds(pl.multiple_of(at * run * size, LANES), run * size)
        flat_ref[:, into] = jnp.concatenate(parts, 1)
        return carry

    lax.fori_loop(0, count // run, some, 0)


def join_pieces(pieces):
    count, rows, size = pieces.shape
    if count % run_length(size):
        return pieces.transpose(1, 0, 2).reshape(rows, count * size)
    return pl.pallas_call(
        join_kernel,
        out_shape=jax.ShapeDtypeStruct((rows, count * size), pieces.dtype),
        compiler_params=params(0),
        name="join_pieces",
    )(pieces)


def split_kernel(*refs):
    sources, pieces_ref, flat_ref = refs[:-2], refs[-2], refs[-1]
    count, _, size = pieces_ref.shape
    run = run_length(size)
    start = 0
    for first_ref, second_ref in zip(sources[::2], sources[1::2]):
        width = first_ref.shape[1]
        both = first_ref[...].astype(F32) + second_ref[...].astype(F32)
        flat_ref[:, start : start + width] = both.astype(BF)
        start += width

    def some(at, carry):
        block = flat_ref[:, pl.ds(pl.multiple_of(at * run * size, LANES), run * size)]
        for index in range(run):
            pieces_ref[at * run + index] = block[:, index * size : (index + 1) * size]
        return carry

    lax.fori_loop(0, count // run, some, 0)


def split_sums(pairs, count):
    rows = pairs[0].shape[0]
    total = sum(item.shape[1] for item in pairs[::2])
    return pl.pallas_call(
        split_kernel,
        out_shape=jax.ShapeDtypeStruct((count, rows, total // count), BF),
        scratch_shapes=[pltpu.VMEM((rows, total), BF)],
        compiler_params=params(0, 42 * MIB),
        name="split_sums",
    )(*pairs)


def unit_loop(plan, work):
    fsdp, seq, folds, local = plan
    run = run_length(local)

    def some(at, carry):
        span = run * seq * folds * local
        block = pl.ds(pl.multiple_of(at * span, LANES), span)
        folded = [
            pl.ds(pl.multiple_of(fold * fsdp * local + at * run * local, LANES), run * local) for fold in range(folds)
        ]
        work(run, block, folded)
        return carry

    lax.fori_loop(0, fsdp // run, some, 0)


def take_units_kernel(plan, place_ref, all_ref, *refs):
    own_ref = refs[-1]
    _, seq, folds, local = plan
    spot = place_ref[0]

    def work(run, block, folded):
        values = all_ref[:, block]
        for fold, into in enumerate(folded):
            parts = []
            for index in range(run):
                base = (index * seq * folds + fold) * local
                part = values[:, base : base + local]
                for other in range(1, seq):
                    shift = base + other * folds * local
                    part = jnp.where(spot == other, values[:, shift : shift + local], part)
                parts.append(part)
            own_ref[:, into] = jnp.concatenate(parts, 1)

    unit_loop(plan, work)
    if len(refs) == 2:
        model = refs[0].shape[1]
        hidden = own_ref.shape[1] - folds * model
        for fold in range(folds):
            rows = pl.ds(pl.multiple_of((spot * folds + fold) * local, 16), local)
            own_ref[:, hidden + fold * model : hidden + (fold + 1) * model] = refs[0][rows, :]


def take_units(plan, places, matrix, low=None):
    _, seq, folds, local = plan
    rows, width = matrix.shape
    extra = [] if low is None else [low]
    out_width = width // seq + sum(folds * item.shape[1] for item in extra)
    return pl.pallas_call(
        partial(take_units_kernel, plan),
        in_specs=[smem()] + [pl.BlockSpec(memory_space=pltpu.VMEM)] * (1 + len(extra)),
        out_shape=jax.ShapeDtypeStruct((rows, out_width), matrix.dtype),
        compiler_params=params(0),
        name="take_units",
    )(places, matrix, *extra)


def collect_kernel(plan, blocks, start_at, place_ref, *refs):
    parts, squares, refs = refs[:blocks], refs[blocks : 2 * blocks], refs[2 * blocks :]
    feeds = [refs[at : at + 4] for at in range(0, len(refs) - 14, 4)]
    (
        other_ref, lat_ref, flat_ref, down_text_ref, text_ref, w_ref,
        mine_ref, theirs_ref, text_grad_ref, down_all, upper_all, unit_acc, hold_ref, sem_ref,
    ) = refs[-14:]
    _, seq, folds, local = plan
    rank = mine_ref.shape[0]
    model = text_ref.shape[1]
    wide = other_ref.shape[2]
    spot = place_ref[0]
    own = pl.ds(pl.multiple_of(spot * wide, wide), wide)
    copy = pltpu.make_async_copy(w_ref.at[:, pl.ds(start_at, hold_ref.shape[1])], hold_ref, sem_ref)
    copy.start()

    def total(items, rows):
        value = items[0][rows, :]
        for item in items[1:]:
            value = value + item[rows, :]
        return value

    moved = []
    for part in range(2):
        value = parts[0][part, :, own]
        for item in parts[1:]:
            value = value + item[part, :, own]
        moved.append((value + other_ref[part].astype(F32)).astype(BF))
    moved = jnp.concatenate(moved, 1)
    glat = mm_nt(moved, flat_ref[...]).astype(BF)
    gup = mm_tn(lat_ref[...], moved)
    gdown = mm_tn(glat, text_ref[...])

    upper_all[:, 2 * model : 4 * model] = jnp.zeros((rank, 2 * model), BF)
    for part in range(2):
        rows = slice(part * rank, (part + 1) * rank)
        down_all[:, (2 + part) * model : (3 + part) * model] = gdown[rows].astype(BF)
        into = pl.ds(pl.multiple_of((2 + part) * model + spot * wide, LANES), wide)
        upper_all[:, into] = gup[rows, part * wide : (part + 1) * wide].astype(BF)
    for index, at in enumerate((0, 1, 4)):
        cols = slice(at * model, (at + 1) * model)
        down_all[:, cols] = total(squares, slice(2 * index * rank, (2 * index + 1) * rank)).astype(BF)
        upper_all[:, cols] = total(squares, slice((2 * index + 1) * rank, (2 * index + 2) * rank)).astype(BF)
    every = slice(0, rank)
    down_all[:, 5 * model : 6 * model] = total([item[0] for item in feeds], every).astype(BF)
    upper_all[:, upper_all.shape[1] - model :] = total([item[3] for item in feeds], every).astype(BF)
    for into_ref, start, which in ((upper_all, 5 * model, 1), (down_all, 6 * model, 2)):
        unit_acc[...] = total([item[which] for item in feeds], every)

        def work(run, block, folded):
            values = [unit_acc[:, cols] for cols in folded]
            spread = []
            for index in range(run):
                for other in range(seq):
                    for fold in range(folds):
                        part = values[fold][:, index * local : (index + 1) * local]
                        spread.append(jnp.where(spot == other, part, 0.0))
            at = pl.ds(pl.multiple_of(start + block.start, LANES), block.size)
            into_ref[:, at] = jnp.concatenate(spread, 1).astype(BF)

        unit_loop(plan, work)
    share(place_ref, down_all, upper_all, mine_ref, theirs_ref)
    copy.wait()
    text_grad_ref[...] = (mm_nt(moved, hold_ref[...]) + mm(glat, down_text_ref[...])).astype(BF)


def collect(plan, places, parts, squares, feeds, other, lat_text, flat_text, down_text, text, packed, start):
    rank = squares[0].shape[0] // 6
    model = text.shape[1]
    hidden = feeds[0][1].shape[1]
    wide2 = flat_text.shape[1]
    width = 6 * model + hidden * plan[1]
    feeds = [item for feed in feeds for item in feed]
    before = list(parts) + list(squares) + feeds + [other, lat_text, flat_text, down_text, text]
    table = jax.ShapeDtypeStruct((rank, width), BF)
    shapes = [table, table, jax.ShapeDtypeStruct(text.shape, BF)]
    return pl.pallas_call(
        partial(collect_kernel, plan, len(parts), start),
        grid=(1,),
        in_specs=[smem()] + [whole(item.shape) for item in before] + [pl.BlockSpec(memory_space=pl.ANY)],
        out_specs=[whole(item.shape) for item in shapes],
        out_shape=shapes,
        scratch_shapes=[pltpu.VMEM(table.shape, BF)] * 2
        + [pltpu.VMEM((rank, hidden), F32), pltpu.VMEM((model, wide2), BF), pltpu.SemaphoreType.DMA],
        compiler_params=params(1),
        cost_estimate=cost(4 * text.shape[0] * model * wide2, 2 * model * wide2),
        name="collect",
    )(places, *before, packed)


def both_kernel(place_ref, mine_ref, other_ref, down_ref, upper_ref):
    first = place_ref[0] == 0
    for at in range(mine_ref.shape[0]):
        mine, other = mine_ref[at].astype(F32), other_ref[at].astype(F32)
        down_ref[at] = jnp.where(first, mine, other)
        upper_ref[at] = jnp.where(first, other, mine)


def both_tables(places, mine, other):
    return pl.pallas_call(
        both_kernel,
        in_specs=[smem()] + [pl.BlockSpec(memory_space=pltpu.VMEM)] * 2,
        out_shape=[jax.ShapeDtypeStruct(mine.shape, F32)] * 2,
        compiler_params=params(0, 42 * MIB),
        name="both_tables",
    )(places, mine, other)


def body(
    inputs,
    text_states,
    adapter_index,
    norm_gains,
    norm_biases,
    self_in,
    self_out,
    cross_query,
    cross_text,
    cross_out,
    hidden_in,
    hidden_out,
    adapter_down,
    adapter_up,
    cotangent,
    *,
    sizes,
):
    seq, fsdp = sizes
    spot = lax.axis_index("seq")
    first_here = spot == 0
    there = (seq - 1) - spot
    local = self_in.shape[0]
    depth = hidden_out.shape[0] // seq
    pair = seq == 2 and depth % local == 0 and fsdp % run_length(local) == 0
    model = inputs.shape[2]
    rows = inputs.shape[1]
    frames = rows * seq
    wide = model // seq
    hidden_all = hidden_in.shape[1]
    hidden = hidden_all // seq
    adapters, rank, piece = adapter_down.shape
    total = piece * fsdp

    blocks = max(rows // 256, 1)
    size = rows // blocks

    def swap(value):
        return lax.ppermute(value, "seq", [(0, 1), (1, 0)])

    def pick(value, axis, extent, which=None):
        return lax.dynamic_slice_in_dim(value, (spot if which is None else which) * extent, extent, axis)

    def ordered(mine, other):
        return jnp.where(first_here, mine, other), jnp.where(first_here, other, mine)

    def gather(value, axis):
        if pair:
            return jnp.concatenate(ordered(value, swap(value)), axis)
        return lax.all_gather(value, "seq", axis=axis, tiled=True)

    def after(value, *others):
        return lax.optimization_barrier((value,) + others)[0]

    def put(value, axis):
        shape = list(value.shape)
        shape[axis] = seq
        return lax.dynamic_update_slice_in_dim(jnp.zeros(shape, value.dtype), value, spot, axis)

    def own_columns(matrix, parts):
        return [pick(matrix[:, at * model : (at + 1) * model], 1, wide) for at in range(parts)]

    def flat_down(grads, parts):
        return jnp.concatenate([grads[at * rank : (at + 1) * rank] for at in range(parts)], 1)

    def flat_upper(own):
        return put(jnp.stack(own, 1)[:, :, None], 2).reshape(rank, len(own) * model)

    halved = [pick(item, 1, wide) if pair else item for item in (self_out, cross_query)]
    first = [cross_out] + own_columns(cross_text, 2) + halved + own_columns(self_in, 3)
    edges = [0]
    for item in first:
        edges.append(edges[-1] + item.shape[1])
    start_in, start_text = edges[5], edges[1]
    packed = lax.all_gather(jnp.concatenate(first, 1), "fsdp", axis=0, tiled=True)
    squares_plan = ((edges[3], None), (edges[4], None), (edges[0], None))
    if pair:
        squares_plan = ((edges[3], 1), (edges[4], 3)) + squares_plan[2:]
    core = lax.rem(lax.axis_index("fsdp"), 2)
    where_here = jnp.stack([spot, there, core, 1 - core]).astype(jnp.int32)
    if pair:
        folds = depth // local
        plan = (fsdp, seq, folds, local)
        own_units = partial(take_units, plan, where_here)
        packed_feed = lax.all_gather(own_units(hidden_in, hidden_out), "fsdp", axis=0, tiled=True)

        def feed_weights(block):
            per = model // block
            return (
                packed_feed,
                pl.BlockSpec((model, block), lambda at: (0, at)),
                packed_feed,
                pl.BlockSpec((block, model), lambda at: (at % per, folds + at // per)),
            )
    else:

        def own_units(matrix):
            kept = lax.dynamic_index_in_dim(matrix.reshape(-1, fsdp, seq, depth), spot, 2, False)
            return kept.reshape(-1, hidden)

        def all_units(matrix):
            return put(matrix.reshape(-1, fsdp, 1, depth), 2).reshape(-1, hidden_all)

        whole_in = lax.all_gather(own_units(hidden_in), "fsdp", axis=0, tiled=True)
        whole_out = lax.all_gather(pick(hidden_out, 0, depth), "fsdp", axis=0, tiled=True)

        def feed_weights(block):
            return (
                whole_in,
                pl.BlockSpec((model, block), lambda at: (0, at)),
                whole_out,
                pl.BlockSpec((block, model), lambda at: (at, 0)),
            )

    index_all = lax.all_to_all(jnp.broadcast_to(adapter_index, (fsdp,)), "fsdp", 0, 0, tiled=True)
    if pair:
        table = jnp.where(first_here, adapter_down, adapter_up)
        mine = join_pieces(lax.all_to_all(jnp.take(table, index_all, axis=0), "fsdp", 0, 0, tiled=True))
        down_all, upper_all = ordered(mine, swap(mine))
    else:
        table = jnp.concatenate([adapter_down, adapter_up], 1)
        chosen = join_pieces(lax.all_to_all(jnp.take(table, index_all, axis=0), "fsdp", 0, 0, tiled=True))
        down_all, upper_all = chosen[:rank], chosen[rank:]
    in_cuts = [0, 3 * model, 4 * model, 5 * model, 7 * model, 8 * model, 9 * model, 9 * model + hidden_all]
    out_cuts = [0, 3 * model, 4 * model, 5 * model, 7 * model, 8 * model, 8 * model + hidden_all, 9 * model + hidden_all]
    downs = [down_all[:, in_cuts[at] : in_cuts[at + 1]] for at in range(7)]
    uppers = [upper_all[:, out_cuts[at] : out_cuts[at + 1]] for at in range(7)]

    def part_down(matrix, parts):
        return jnp.concatenate([matrix[:, at * model : (at + 1) * model] for at in range(parts)], 0)

    def part_upper(matrix, parts):
        own = own_columns(matrix, parts)
        return jnp.stack(
            [jnp.pad(item, ((at * rank, (parts - 1 - at) * rank), (0, 0))) for at, item in enumerate(own)], 0
        )

    units = own_units(jnp.concatenate([uppers[5], downs[6]], 0))
    feed_adapters = (downs[5], units[:rank], units[rank:], uppers[6])
    square_adapters = jnp.concatenate([downs[1], uppers[1], downs[2], uppers[2], downs[4], uppers[4]], 0)
    down_qkv, upper_qkv = part_down(downs[0], 3), part_upper(uppers[0], 3)
    down_text, upper_text = part_down(downs[3], 2), part_upper(uppers[3], 2)
    flat_text = jnp.concatenate([upper_text[0], upper_text[1]], 1)

    frames_in = inputs[0]
    cot = cotangent[0]
    if pair:
        frames_parts = [frames_in, swap(frames_in)]
        cot_other = swap(after(cot, frames_parts[1]))
    else:
        frames_parts = [lax.all_gather(frames_in, "seq", axis=0, tiled=True)]
    norm_places = where_here if pair else jnp.zeros((4,), jnp.int32)
    if pair:
        frames_parts[1] = after(frames_parts[1], cot_other, units)
    normed1, lat_qkv = norm_project(norm_places, frames_parts, norm_gains[0:1], norm_biases[0:1], down_qkv)
    packed = after(packed, normed1)
    sources = [packed]
    if pair:
        half = model // 2
        cut = [lax.dynamic_slice(packed, (core * half, at), (half, wide)) for at in edges[3:5]]
        straight = [swap(item) for item in cut]
        normed1 = after(normed1, *cut)
    triple = qkv_project(normed1, lat_qkv, upper_qkv, packed, start_in, 3 * wide)
    padded = -(-wide // LANES) * LANES
    if padded != wide:
        triple = jnp.pad(triple.reshape(frames, 3, wide), ((0, 0), (0, 0), (0, padded - wide)))
        triple = triple.reshape(frames, 3 * padded)
    text = after(text_states[0], triple)
    w_text = packed[:, start_text : start_text + 2 * wide]
    lat_text = mm_nt(text, down_text).astype(BF)
    memory = (mm(text, w_text) + mm(lat_text, flat_text)).astype(BF)
    head_out, probs, *leaving = attend(where_here, [size] * blocks if pair else [], after(triple, memory), padded)

    memory_all = gather(memory.reshape(-1, 2, wide), 2)
    keys, values = memory_all[:, 0], memory_all[:, 1]

    constants = (sources, squares_plan, square_adapters, norm_gains, norm_biases, keys, values)
    if pair:
        received = [swap(leaving[0])]
        for item in leaving[1:]:
            received.append(swap(after(item, received[-1])))
        neighbours = [(at, at ^ 1) for at in range(fsdp)]
        for item in straight:
            sources += [item, lax.ppermute(after(item, received[0], memory_all), "fsdp", neighbours)]
    else:
        natural = lax.all_to_all(head_out[:, :wide], "seq", split_axis=0, concat_axis=1, tiled=True)
    made = []
    for at in range(blocks):
        if pair:
            own, spec, others = head_out, (size, wide), [received[at]]
        else:
            own, spec, others = natural, (size, model), []
        ready = after(frames_in, made[-1][7]) if made else frames_in
        made.append(middle(where_here if pair else jnp.zeros((4,), jnp.int32), own, spec, others, ready, at, blocks, *constants))
    normed3 = [item[7] for item in made]
    resid2 = [item[6] for item in made]

    feed_tail = feed_adapters + (feed_weights, hidden)
    if pair:
        others = [swap(item) for item in normed3]
        theirs, gu_more, out_more = [], [], []
        for at in range(blocks):
            ready = after(others[at], theirs[-1][0]) if at else others[at]
            theirs.append(feed_forward([ready], [], cot_other, at, *feed_tail, BF))
            gu_more.append(swap(after(theirs[at][1], *gu_more[-1:])))
        ours = feed_forward([after(normed3[0], theirs[-1][1])] + normed3[1:], resid2, cot, 0, *feed_tail, F32)
        for at in range(blocks):
            behind = [ours[0]] + out_more[-1:] if at else [theirs[-1][0], gu_more[0]]
            out_more.append(swap(after(theirs[at][0], *behind)))
        gu = ours[blocks : 2 * blocks]
        feed_grads = [ours[2 * blocks :]] + [item[2:] for item in theirs]
    else:
        wide_in = gather(jnp.concatenate(normed3, 0), 0)
        all_out = feed_forward([wide_in], [], gather(cot, 0), 0, *feed_tail, F32)
        summed = [
            lax.psum_scatter(item.astype(BF), "seq", scatter_dimension=0, tiled=True) for item in all_out[:2]
        ]
        output = (jnp.concatenate(resid2, 0) + summed[0].astype(F32)).astype(BF)
        gu = [summed[1][at * size : (at + 1) * size] for at in range(blocks)]
        gu_more = [jnp.zeros_like(item) for item in gu]
        feed_grads = [all_out[2:]]

    pieces, resid1_grads, memory_parts, square_parts = [], [], [], []
    for at in range(blocks):
        gu_here = gu[at] if at == 0 else after(gu[at], result[-3])
        kept = made[at][:7] + made[at][8:9]
        result = middle_back(
            where_here, 2 if pair else 1, at, cot, gu_here, gu_more[at],
            kept, sources, squares_plan, square_adapters, norm_gains, keys, values,
        )
        if pair:
            waited = [pieces[-1][1]] if at else []
            if at == blocks - 1:
                memory_part = sum(memory_parts, result[-2]).astype(BF)
                memory_other = swap(after(pick(memory_part, 2, wide, there), *out_more))
                waited.append(memory_other)
            pieces.append((result[0], swap(after(result[1], *waited) if waited else result[1])))
        else:
            pieces.append(result[0])
        resid1_grads.append(result[-3])
        memory_parts.append(result[-2])
        square_parts.append(result[-1])
    resid1_grad = jnp.concatenate(resid1_grads, 0)
    square_grads = sum(square_parts[1:], square_parts[0])

    if pair:
        early, early_leaving, text_low = collect(
            plan, where_here, memory_parts, square_parts, feed_grads, memory_other, lat_text, flat_text, down_text,
            text_states[0], packed, start_text,
        )
        grad_pieces = [item[0] for item in pieces] + [item[1] for item in pieces]
    else:
        head_grad = lax.all_to_all(jnp.concatenate(pieces, 0), "seq", split_axis=1, concat_axis=0, tiled=True)
        grad_pieces = [jnp.pad(head_grad, ((0, 0), (0, padded - wide)))]
    triple_grad = attend_back(where_here, triple, head_out, grad_pieces, probs, padded)[:, :, :wide]
    if pair:
        early_other = swap(after(early_leaving, pieces[-1][1]))
        text_other = swap(after(text_low, early_other, triple_grad))
        glat_qkv, late, late_leaving = qkv_grads(
            where_here, after(triple_grad, early_other), normed1, lat_qkv, upper_qkv
        )
        late_other = swap(late_leaving)
    else:
        glat_qkv = sum(mm_nt(triple_grad[at], upper_qkv[at]) for at in range(3)).astype(BF)
        gdown_qkv = mm_tn(glat_qkv, normed1)
        gup_qkv = [mm_tn(lat_qkv[:, at * rank : (at + 1) * rank], triple_grad[at]) for at in range(3)]
    back = partial(qkv_back, gradient=triple_grad, glat=glat_qkv, down=down_qkv, packed=packed, start=start_in)
    if pair:
        for_them = back(after(there, early_other, text_other)[None], rows, kind=BF)
        for_us = back(after(spot, for_them, *out_more)[None], rows, kind=F32)
        input_grad = last_norm(frames_in, for_us + swap(for_them).astype(F32), norm_gains[0:1], resid1_grads)
        output = jnp.concatenate(
            [(after(item, for_them) + other.astype(F32)).astype(BF) for item, other in zip(ours[:blocks], out_more)], 0
        )
    else:
        full = back(jnp.zeros((1,), jnp.int32), frames, kind=BF)
        normed1_grad = lax.psum_scatter(full, "seq", scatter_dimension=0, tiled=True).astype(F32)
        resid1_grad = jnp.concatenate(resid1_grads, 0)
        input_grad = resid1_grad + norm_back(frames_in.astype(F32), norm_gains[0:1], normed1_grad)

    selector = (index_all[None, :] == jnp.arange(adapters, dtype=jnp.int32)[:, None]).astype(BF)

    def by_adapter(sent, *others):
        received = lax.all_to_all(sent, "fsdp", 0, 0, tiled=True)
        chooser = after(selector, *others) if others else selector
        return jnp.einsum("ac,crw->arw", chooser, received, preferred_element_type=F32)

    if pair:
        shares = by_adapter(split_sums([after(late, for_them), late_other, early, early_other], fsdp)).astype(BF)
        grad_down, grad_up = both_tables(where_here, after(shares, input_grad), swap(after(shares, for_us)))
        text_total = text_low.astype(F32) + text_other.astype(F32)
    else:
        memory_part = sum(memory_parts[1:], memory_parts[0]).astype(BF)
        memory_grad = lax.psum_scatter(memory_part, "seq", scatter_dimension=2, tiled=True)
        memory_flat = jnp.concatenate([memory_grad[0], memory_grad[1]], 1)
        glat_text = mm_nt(memory_flat, flat_text).astype(BF)
        gup_text = mm_tn(lat_text, memory_flat)
        gdown_text = mm_tn(glat_text, text)
        text_low = (mm_nt(memory_flat, w_text) + mm(glat_text, down_text)).astype(BF)
        own_text = [gup_text[at * rank : (at + 1) * rank, at * wide : (at + 1) * wide] for at in range(2)]
        gdown_in, gup_in, gdown_out, gup_out = feed_grads[0]
        square_grads = sum(square_parts[1:], square_parts[0])
        squares = [square_grads[rank * at : rank * (at + 1)] for at in range(6)]
        down_sent = [flat_down(gdown_qkv, 3), squares[0], squares[2], flat_down(gdown_text, 2), squares[4], gdown_in]
        upper_sent = [flat_upper(gup_qkv), squares[1], squares[3], flat_upper(own_text), squares[5]]
        down_sent = jnp.concatenate(down_sent + [all_units(gdown_out)], 1)
        upper_sent = jnp.concatenate(upper_sent + [all_units(gup_in), gup_out], 1)
        sent = jnp.concatenate([down_sent, upper_sent], 0).astype(BF).reshape(2 * rank, fsdp, piece).transpose(1, 0, 2)
        shares = lax.psum(by_adapter(sent).astype(BF), "seq")
        grad_down, grad_up = shares[:, :rank], shares[:, rank:]
        text_total = lax.psum(text_low, "seq").astype(F32)
    return (output[None], input_grad[None], text_total[None], grad_down.astype(F32), grad_up.astype(F32))


def solution(mesh):
    return jax.shard_map(
        partial(body, sizes=(mesh.shape["seq"], mesh.shape["fsdp"])),
        mesh=mesh,
        in_specs=(
            P("fsdp", "seq", None),
            P("fsdp", None, None),
            P("fsdp"),
            P(),
            P(),
            P("fsdp", None),
            P("fsdp", None),
            P("fsdp", None),
            P("fsdp", None),
            P("fsdp", None),
            P("fsdp", None),
            P("fsdp", None),
            P(None, None, "fsdp"),
            P(None, None, "fsdp"),
            P("fsdp", "seq", None),
        ),
        out_specs=(
            P("fsdp", "seq", None),
            P("fsdp", "seq", None),
            P("fsdp", None, None),
            P(None, None, "fsdp"),
            P(None, None, "fsdp"),
        ),
        check_vma=False,
    )
```
